32 devices in a mesh: wide: 8 (over y, x, core), narrow: 4 (over z).
Axes of the slice: x: 2, y: 2, z: 4, core: 2. Of those that a mesh axis runs over, the one named last changes fastest.
Arguments:
- tokens: bfloat16 [32768, 512], P('wide'), may hold values from -6 to 6
- cotangent: bfloat16 [32768, 512], P('wide'), may hold values from -6 to 6
- segment_ids: int32 [8, 4096], P('wide'), may hold values from 0 to 3, never falling along the last dimension, each value on 1 to 2560 neighbouring positions
- pad_mask: int32 [8, 4096], P('wide'), may hold values 0 or 1
- owner_order: int32 [192], replicated, may hold values from 0 to 191, as said below
- weights: float32 [4, 192, 64, 64], P('narrow', 'wide')
- first_moment: float32 [4, 192, 64, 64], P('narrow', 'wide')
- second_moment: float32 [4, 192, 64, 64], P('narrow', 'wide'), as said below
- average: float32 [4, 192, 64, 64], P('narrow', 'wide')
- stats: float32 [4, 192, 2, 64, 64], P('narrow', 'wide'), as said below
- bases: float32 [4, 192, 2, 64, 64], P('narrow', 'wide'), as said below
- gains: float32 [1024], P('wide'), may hold values from 0.5 to 1.5
- gain_first: float32 [1024], P('wide'), may hold values from -128 to 128
- gain_second: float32 [1024], P('wide'), may hold values from 1723.5968 to 6881.28
- gain_average: float32 [1024], P('wide'), may hold values from 0.5 to 1.5
Outputs:
- output: bfloat16 [32768, 512], P('wide')
- input_grad: float32 [32768, 512], P('wide')
- new_weights: float32 [4, 192, 64, 64], P('narrow', 'wide')
- new_first: float32 [4, 192, 64, 64], P('narrow', 'wide')
- new_second: float32 [4, 192, 64, 64], P('narrow', 'wide')
- new_average: float32 [4, 192, 64, 64], P('narrow', 'wide')
- new_stats: float32 [4, 192, 2, 64, 64], P('narrow', 'wide')
- new_bases: float32 [4, 192, 2, 64, 64], P('narrow', 'wide')
- new_gains: float32 [1024], P('wide')
- gain_moment: float32 [1024], P('wide')
- gain_square: float32 [1024], P('wide')
- gain_mean: float32 [1024], P('wide')
The draws below stay inside these ranges and needn't reach their ends.
Inputs may be any that keep to these rules, and one draw needn't show every extreme that they name: `segment_ids`: within a row segment numbers never fall; a segment holds at most 2560 positions. `owner_order`: each block number appears exactly once. `second_moment`: Positive. `stats`: each matrix is symmetric positive definite. `bases`: each matrix is orthogonal.
All inputs are finite; a program needn't handle non-finite values. No bound on the sum of `pad_mask` on one device may be relied on, other than what follows from the above.
Results may differ from the reference program's by a relative error of at most 0.025.
Values may be sent and summed in bfloat16 or wider, within the bound.
A program may use at most 192 MiB of HBM per device.

```python
import math
from functools import partial
import jax
import jax.numpy as jnp
import numpy as np
from jax import lax

D = 512
HEADS = 8
HD = 64
FF = 2048
TOK_DEV = 4096
BLK = 64
SEG_COUNT = 4
HN = 2
FN = 512
WO_FAN = 1
NB = 192
PACKS = 8
TOKENS = 32768
GAINS = 1024
SEG_MOST = 2560
N_NARROW = 4


def slot_blocks(key):
    return jax.random.permutation(jax.random.fold_in(key, 11), NB).astype(jnp.int32)


def slot_kinds(key):
    blocks = slot_blocks(key)
    first_end = D // BLK * (3 * HN * HD // BLK)
    second_end = first_end + HN * HD // BLK * (D // BLK)
    third_end = second_end + D // BLK * (FN // BLK)
    return (blocks >= first_end).astype(jnp.int32) + (blocks >= second_end).astype(jnp.int32) + (blocks >= third_end).astype(jnp.int32)


def by_kind(key, entries):
    kinds = slot_kinds(key)
    table = jnp.array(entries, jnp.float32)
    picked = jnp.where(kinds[:, None] == jnp.arange(4, dtype=jnp.int32)[None, :], table[None, :], 0.0)
    return jnp.sum(picked, axis=1)


def gradient_size(key):
    root = math.sqrt(TOKENS)
    return by_kind(key, [root, root * math.sqrt(10.0 / TOK_DEV), 0.3 * root, 0.6 * root])


def weight_size(key):
    return by_kind(key, [D ** (-0.5), WO_FAN ** (-0.5), D ** (-0.5), FF ** (-0.5)])


def log_uniform(key, shape, low_end, high_end):
    return jnp.exp(jax.random.uniform(key, shape, jnp.float32, math.log(low_end), math.log(high_end)))


def draw_owner_order(key, part):
    return slot_blocks(key)


def draw_weights(key, part):
    noise = jax.random.truncated_normal(jax.random.fold_in(key, 21), -3.0, 3.0, (N_NARROW, NB, BLK, BLK), jnp.float32)
    return noise * weight_size(key)[None, :, None, None]


def draw_average(key, part):
    noise = jax.random.truncated_normal(jax.random.fold_in(key, 22), -3.0, 3.0, (N_NARROW, NB, BLK, BLK), jnp.float32)
    return noise * weight_size(key)[None, :, None, None]


def draw_first_moment(key, part):
    noise = jax.random.truncated_normal(jax.random.fold_in(key, 23), -3.0, 3.0, (N_NARROW, NB, BLK, BLK), jnp.float32)
    return noise * (gradient_size(key) / 9.0)[None, :, None, None]


def draw_second_moment(key, part):
    square = gradient_size(key) ** 2 * (0.05 / 0.95)
    per_block = log_uniform(jax.random.fold_in(key, 24), (N_NARROW, NB, 1, 1), 1.0, 4.0)
    per_entry = log_uniform(jax.random.fold_in(key, 25), (N_NARROW, NB, BLK, BLK), 0.5, 2.0)
    return square[None, :, None, None] * per_block * per_entry


def draw_stats(key, part):
    square = gradient_size(key) ** 2 * (0.05 / 0.95) * BLK
    level = square[None, :, None, None, None] * log_uniform(jax.random.fold_in(key, 26), (N_NARROW, NB, 2, 1, 1), 1.0, 4.0)
    noise = jax.random.uniform(jax.random.fold_in(key, 27), (N_NARROW, NB, 2, BLK, BLK), jnp.float32, -1.0, 1.0)
    mirror = 0.5 * (noise + jnp.swapaxes(noise, -1, -2))
    return level * (jnp.eye(BLK, dtype=jnp.float32) + 0.9 / BLK * mirror)


def reflect(matrix, vector):
    length = jnp.sum(vector * vector, axis=-1)
    inner = jnp.sum(vector[..., :, None] * matrix, axis=-2)
    return matrix - (2.0 / length)[..., None, None] * vector[..., :, None] * inner[..., None, :]


def draw_bases(key, part):
    result = jnp.broadcast_to(jnp.eye(BLK, dtype=jnp.float32), (N_NARROW, NB, 2, BLK, BLK))
    for turn in range(3):
        raw = jax.random.uniform(jax.random.fold_in(key, 28 + turn), (N_NARROW, NB, 2, BLK), jnp.float32, -1.0, 1.0)
        vector = raw + 0.1 * jnp.where(raw >= 0.0, 1.0, -1.0)
        result = reflect(result, vector)
    return result


def place_ends(values, own_key, smallest, largest):
    place = [jax.random.randint(jax.random.fold_in(own_key, axis), (), 0, length) for axis, length in enumerate(values.shape)]
    widest = values.shape.index(max(values.shape))
    beside = place[:widest] + [(place[widest] + 1) % values.shape[widest]] + place[widest + 1:]
    return values.at[tuple(place)].set(smallest).at[tuple(beside)].set(largest)


def block_scale(stream_key, extent, cuts, smallest, largest):
    def one(axis_at, parts):
        steps = jax.random.uniform(jax.random.fold_in(jax.random.fold_in(stream_key, 6), axis_at), (parts,), jnp.float32, smallest / len(cuts), largest / len(cuts))
        return jnp.repeat(jnp.exp(steps), extent[axis_at] // parts).reshape((-1,) + (1,) * (len(extent) - axis_at - 1))

    level = one(*cuts[0])
    for cut in cuts[1:]:
        level = level * one(*cut)
    return level


def split_up(amount, total, reach, skew):
    loads = [(1 << 20) // math.isqrt(standing ** skew) + 1 for standing in range(2, amount + 1)]
    rest, given = total - reach - (amount - 1), [1] * (amount - 1)
    while rest > 0:
        movable = [i for i in range(amount - 1) if given[i] < reach]
        pool, remaining = sum([loads[i] for i in movable]), rest
        for i in movable:
            more = min(reach - given[i], max(1, remaining * loads[i] // pool), rest)
            given[i] = given[i] + more
            rest = rest - more
    return np.array([reach] + given)


def uneven_parts(key, count, total, limit, slope):
    if count == 2:
        one = jax.random.randint(key, (), max(1, total - limit), min(limit, total - 1) + 1)
        return jnp.stack([one, total - one])
    lengths = jnp.asarray(split_up(count, total, limit, slope), jnp.int32)
    couples = (count - 1) // 2
    source_of, receiver = lengths[1:1 + 2 * couples:2], lengths[2:2 + 2 * couples:2]
    slack = jnp.minimum(source_of - 1, limit - receiver)
    passed = jax.random.randint(jax.random.fold_in(key, 1), (couples,), 0, 1 << 20) % (slack + 1)
    lengths = lengths.at[1:1 + 2 * couples:2].set(source_of - passed).at[2:2 + 2 * couples:2].set(receiver + passed)
    return lengths[jax.random.permutation(jax.random.fold_in(key, 2), count)]


def bell_draw(rng, extent, spread, most, shards=(), kind=jnp.bfloat16):
    values = jax.random.normal(rng, extent, jnp.float32) * spread
    if len(shards) > 0:
        values = block_scale(rng, extent, shards, -0.22, 0.18) * values
    return jnp.clip(values, min=-most, max=most).astype(kind)


def setup_inputs(seed: int = 0) -> dict:
    splits = jax.random.split(jax.random.key(seed), 16)
    tokens = bell_draw(splits[0], (TOKENS, D), 1.0, 6.0, ((0, 8),))
    cotangent = bell_draw(splits[1], (TOKENS, D), 1.0, 6.0, ((0, 8),))
    segment_ids = jax.vmap(lambda own: jnp.searchsorted(jnp.cumsum(uneven_parts(own, SEG_COUNT, TOK_DEV, SEG_MOST, 0)), jnp.arange(TOK_DEV), side="right"))(jax.random.split(splits[2], PACKS)).reshape((PACKS, TOK_DEV)).astype(jnp.int32)
    pad_mask = place_ends((jax.random.randint(splits[3], (PACKS, TOK_DEV), 0, 8) < 7).astype(jnp.int32), jax.random.fold_in(splits[3], 1), 0, 1)
    owner_order = draw_owner_order(jax.random.fold_in(splits[15], 71), 0)
    weights = draw_weights(jax.random.fold_in(splits[15], 71), 0)
    first_moment = draw_first_moment(jax.random.fold_in(splits[15], 71), 0)
    second_moment = draw_second_moment(jax.random.fold_in(splits[15], 71), 0)
    average = draw_average(jax.random.fold_in(splits[15], 71), 0)
    stats = draw_stats(jax.random.fold_in(splits[15], 71), 0)
    bases = draw_bases(jax.random.fold_in(splits[15], 71), 0)
    gains = jnp.clip(1.0 + 0.1 * jax.random.normal(splits[11], (GAINS,), jnp.float32), 0.5, 1.5)
    gain_first = bell_draw(splits[12], (GAINS,), (TOKENS ** 0.5 / 9), 128.0, ((0, 8),), jnp.float32)
    gain_second = jnp.clip(jnp.exp(math.log(6881.28) - 1.3843914 * jax.random.uniform(splits[13], (GAINS,), jnp.float32) ** block_scale(splits[13], (GAINS,), ((0, 8),), -0.2, 0.2)), 1723.5968, 6881.28)
    gain_average = jnp.clip(1.0 + 0.1 * jax.random.normal(splits[14], (GAINS,), jnp.float32), 0.5, 1.5)
    return dict(tokens=tokens, cotangent=cotangent, segment_ids=segment_ids, pad_mask=pad_mask, owner_order=owner_order, weights=weights, first_moment=first_moment, second_moment=second_moment, average=average, stats=stats, bases=bases, gains=gains, gain_first=gain_first, gain_second=gain_second, gain_average=gain_average)


beta_one = 0.9
beta_two = 0.95
step_rate = 0.1
gain_rate = 0.75
weight_decay = 0.01
average_keep = 0.5
norm_eps = 1e-05
step_eps = 1e-08
masked_score = -1e+30
highest = lax.Precision.HIGHEST

@jax.custom_vjp
def low(v):
    return lax.optimization_barrier(v.astype(jnp.bfloat16)).astype(jnp.float32)

@jax.custom_vjp
def low_back(v):
    return v

def low_keep(v):
    return (low(v), None)

def low_pass(kept, grad):
    return (grad,)

def back_keep(v):
    return (v, None)

def back_low(kept, grad):
    return (low(grad),)
low.defvjp(low_keep, low_pass)
low_back.defvjp(back_keep, back_low)

def normalize(values):
    center = lax.optimization_barrier(jnp.mean(values, axis=-1, keepdims=True))
    centered = values - center
    variance = lax.optimization_barrier(jnp.mean(centered * centered, axis=-1, keepdims=True))
    return centered * lax.rsqrt(variance + norm_eps)

def assemble(blocks, rows, cols):
    size = blocks.shape[-1]
    count = blocks.shape[0]
    grid = blocks.reshape(count, rows // size, cols // size, size, size)
    return grid.transpose(0, 1, 3, 2, 4).reshape(count, rows, cols)

def unpack(blocks):
    size = blocks.shape[-1]
    first_end = D // size * (3 * HN * HD // size)
    second_end = first_end + HN * HD // size * (D // size)
    third_end = second_end + D // size * (FN // size)
    mixing = assemble(blocks[:, :first_end], D, 3 * HN * HD)
    out_weight = assemble(blocks[:, first_end:second_end], HN * HD, D)
    up_weight = assemble(blocks[:, second_end:third_end], D, FN)
    down_weight = assemble(blocks[:, third_end:], FN, D)
    return (mixing, out_weight, up_weight, down_weight)

def attend(key_rows, value_rows, seg_row, pad_row, block_inputs):
    query_block, query_pos, query_seg = block_inputs
    positions = jnp.arange(TOK_DEV, dtype=jnp.int32)
    scores = low_back(jnp.einsum('qhd,khd->hqk', query_block, key_rows, precision=highest) * HD ** (-0.5))
    allowed = (query_seg[:, None] == seg_row[None, :]) & ((pad_row[None, :] == 1) | (query_pos[:, None] == positions[None, :]))
    masked = jnp.where(allowed[None], scores, masked_score)
    total = jax.nn.logsumexp(masked, axis=-1, keepdims=True)
    probs = low(jnp.exp(masked - total))
    return jnp.einsum('hqk,khd->qhd', probs, value_rows, precision=highest)

def pack_forward(params, pack):
    mixing, out_weight, up_weight, down_weight, gain_one, gain_two = params
    rows_in, seg_row, pad_row = pack
    pad_float = pad_row.astype(jnp.float32)
    normed_one = low(normalize(rows_in) * gain_one)
    copies = low_back(jnp.broadcast_to(normed_one, (N_NARROW, TOK_DEV, D)))
    mixed = low_back(low(jnp.einsum('ntd,ndc->ntc', copies, mixing, precision=highest)))
    grouped = mixed.reshape(N_NARROW, TOK_DEV, 3, HN, HD).transpose(2, 1, 0, 3, 4).reshape(3, TOK_DEV, HEADS, HD)
    block = min(512, TOK_DEV)
    count = TOK_DEV // block
    positions = jnp.arange(TOK_DEV, dtype=jnp.int32)
    attend_fn = jax.checkpoint(partial(attend, grouped[1], grouped[2], seg_row, pad_row))
    attended = lax.map(attend_fn, (grouped[0].reshape(count, block, HEADS, HD), positions.reshape(count, block), seg_row.reshape(count, block)))
    attended = attended.reshape(TOK_DEV, HEADS, HD) * pad_float[:, None, None]
    attended = low_back(low(attended)).reshape(TOK_DEV, N_NARROW, HN * HD)
    branch = low_back(lax.optimization_barrier(jnp.sum(low(jnp.einsum('tnc,ncd->ntd', attended, out_weight, precision=highest)), axis=0)))
    residual = rows_in + branch
    normed_two = low(normalize(residual) * gain_two)
    copies_two = low_back(jnp.broadcast_to(normed_two, (N_NARROW, TOK_DEV, D)))
    up = low_back(jnp.einsum('ntd,ndf->ntf', copies_two, up_weight, precision=highest))
    active = low(jax.nn.gelu(up, approximate=False))
    mlp = low_back(lax.optimization_barrier(jnp.sum(low(jnp.einsum('ntf,nfd->ntd', active, down_weight, precision=highest)), axis=0)))
    return residual + mlp

def orthonormal(matrix):
    gram = jnp.einsum('...ji,...jk->...ik', matrix, matrix, precision=highest)
    lower = jnp.linalg.cholesky(gram)
    solved = jax.scipy.linalg.solve_triangular(lower, jnp.swapaxes(matrix, -1, -2), lower=True)
    return jnp.swapaxes(solved, -1, -2)

def soap_update(grad, weight, first, second, average, stats, bases):
    left = bases[..., 0, :, :]
    right = bases[..., 1, :, :]
    new_first = beta_one * first + (1.0 - beta_one) * grad
    rotated = jnp.einsum('...ji,...jk->...ik', left, jnp.einsum('...jk,...kl->...jl', grad, right, precision=highest), precision=highest)
    new_second = beta_two * second + (1.0 - beta_two) * rotated * rotated
    moment_rot = jnp.einsum('...ji,...jk->...ik', left, jnp.einsum('...jk,...kl->...jl', new_first, right, precision=highest), precision=highest)
    scaled = moment_rot / (jnp.sqrt(new_second) + step_eps)
    direction = jnp.einsum('...ij,...jk->...ik', left, jnp.einsum('...jk,...lk->...jl', scaled, right, precision=highest), precision=highest)
    new_weight = weight - step_rate * (direction + weight_decay * weight)
    new_average = average_keep * average + (1.0 - average_keep) * new_weight
    left_stat = beta_two * stats[..., 0, :, :] + (1.0 - beta_two) * jnp.einsum('...ik,...jk->...ij', grad, grad, precision=highest)
    right_stat = beta_two * stats[..., 1, :, :] + (1.0 - beta_two) * jnp.einsum('...ki,...kj->...ij', grad, grad, precision=highest)
    new_left = orthonormal(jnp.einsum('...ij,...jk->...ik', left_stat, left, precision=highest))
    new_right = orthonormal(jnp.einsum('...ij,...jk->...ik', right_stat, right, precision=highest))
    return (new_weight, new_first, new_second, new_average, jnp.stack([left_stat, right_stat], axis=-3), jnp.stack([new_left, new_right], axis=-3))

def adam_gains(grad, gain, first, second, average):
    new_first = beta_one * first + (1.0 - beta_one) * grad
    new_second = beta_two * second + (1.0 - beta_two) * grad * grad
    new_gain = gain - gain_rate * new_first / (jnp.sqrt(new_second) + step_eps)
    new_average = average_keep * average + (1.0 - average_keep) * new_gain
    return (new_gain, new_first, new_second, new_average)

def reference(tokens, cotangent, segment_ids, pad_mask, owner_order, weights, first_moment, second_moment, average, stats, bases, gains, gain_first, gain_second, gain_average):
    slot_of = jnp.zeros((NB,), jnp.int32).at[owner_order].set(jnp.arange(NB, dtype=jnp.int32))
    blocks = weights[:, slot_of]

    def layer(layer_inputs, block_values, gain_values):
        mixing, out_weight, up_weight, down_weight = unpack(low(block_values))
        gain_low = low(gain_values)
        params = (mixing, out_weight, up_weight, down_weight, gain_low[:D], gain_low[D:])
        step_fn = jax.checkpoint(pack_forward)

        def scan_body(carry, pack):
            return (carry, step_fn(params, pack))
        _, outputs = lax.scan(scan_body, jnp.zeros((), jnp.float32), (layer_inputs.reshape(PACKS, TOK_DEV, D), segment_ids, pad_mask))
        return outputs.reshape(TOKENS, D)
    result, pullback = jax.vjp(layer, tokens.astype(jnp.float32), blocks, gains)
    input_grad, block_grads, gain_grad = pullback(cotangent.astype(jnp.float32))
    slot_grads = block_grads[:, owner_order]
    new_weight, new_first, new_second, new_average, new_stats, new_bases = soap_update(slot_grads, weights, first_moment, second_moment, average, stats, bases)
    new_gains, gain_moment, gain_square, gain_mean = adam_gains(gain_grad, gains, gain_first, gain_second, gain_average)
    return (result.astype(jnp.bfloat16), input_grad, new_weight, new_first, new_second, new_average, new_stats, new_bases, new_gains, gain_moment, gain_square, gain_mean)
```

```python
import functools

import jax
import jax.numpy as jnp
from jax import lax
from jax.experimental import pallas as pl
from jax.experimental.pallas import tpu as pltpu
from jax.sharding import PartitionSpec as P

HEADS = 8
HD = 64
FF = 2048
LANES = 128
SEGS = 4
NEG = -1e30
F32 = jnp.float32
BF = jnp.bfloat16
highest = lax.Precision.HIGHEST

beta_one = 0.9
beta_two = 0.95
step_rate = 0.1
gain_rate = 0.75
weight_decay = 0.01
average_keep = 0.5
norm_eps = 1e-05
step_eps = 1e-08


def nt(a, b):
    return lax.dot_general(a, b, (((1,), (1,)), ((), ())), preferred_element_type=F32)


def nn(a, b):
    return lax.dot_general(a, b, (((1,), (0,)), ((), ())), preferred_element_type=F32)


def tn(a, b):
    return lax.dot_general(a, b, (((0,), (0,)), ((), ())), preferred_element_type=F32)


def split3(x):
    hi = x.astype(BF)
    r = x - hi.astype(F32)
    mid = r.astype(BF)
    lo = (r - mid.astype(F32)).astype(BF)
    return hi, mid, lo


def put3(base, x, lane0):
    lane = lax.broadcasted_iota(jnp.int32, base.shape, 1)
    hi, mid, lo = split3(x)
    out = jnp.where(lane == lane0, hi.astype(F32), base.astype(F32))
    out = jnp.where(lane == lane0 + 1, mid.astype(F32), out)
    out = jnp.where(lane == lane0 + 2, lo.astype(F32), out)
    return out.astype(BF)


VT = 80
QC, AHEAD, QB, BAHEAD = 512, 1, 256, 1


def fwd_kernel(heads, bq, bk, lo_ref, hi_ref, qe_ref, ke_ref, vt_ref, pad_ref, att_ref, qb_ref, m_ref, acc_ref):
    i = pl.program_id(0)
    row0 = pl.multiple_of(i * bq, bq)
    real = pad_ref[...] > 0.5
    for h in range(heads):
        qt = qe_ref[h].astype(F32).T[:HD]
        kt = ke_ref[h, pl.ds(row0, bq), :].astype(F32).T[:HD]
        own = jnp.sum(qt * kt, axis=0, keepdims=True)
        m_ref[h] = jnp.where(real, NEG, own)
        acc_ref[h] = jnp.where(real, 0.0, vt_ref[h, :, pl.ds(row0, bq)].astype(F32))

    def step(j, _):
        col0 = pl.multiple_of(j * bk, bk)
        work = [(h, slice(c, c + QC)) for c in range(0, bq, QC) for h in range(heads)]
        score = lambda h, c: nt(ke_ref[h, pl.ds(col0, bk), :], qe_ref[h, c, :])
        ss = [score(*w) for w in work[:AHEAD]]
        for n, (h, c) in enumerate(work):
            if n + AHEAD < len(work):
                ss.append(score(*work[n + AHEAD]))
            s = ss[n]
            m_old = m_ref[h, :, c]
            m_new = jnp.maximum(m_old, jnp.max(s, axis=0, keepdims=True))
            p = jnp.exp(s - m_new).astype(BF)
            alpha = jnp.exp(m_old - m_new)
            acc_ref[h, :, c] = acc_ref[h, :, c] * alpha + nn(vt_ref[h, :, pl.ds(col0, bk)], p)
            m_ref[h, :, c] = m_new
        return 0

    lax.fori_loop(lo_ref[i], hi_ref[i], step, 0)
    outs = []
    for h in range(heads):
        acc = acc_ref[h]
        total = acc[HD : HD + 1]
        outs.append(jnp.where(real, acc[:HD] / total, 0.0))
        lse = jnp.broadcast_to(m_ref[h] + jnp.log(total), (8, bq)).T[:, :1]
        qb_ref[h] = put3(qe_ref[h], -lse, HD + 4)
    att_ref[...] = (jnp.concatenate(outs, axis=0) if heads > 1 else outs[0]).T.astype(BF)


def attend(qe, ke, vt, padw, lo, hi, bq, bk):
    heads, rows, _ = qe.shape
    full = lambda i, lo, hi: (0, 0, 0)
    return pl.pallas_call(
        functools.partial(fwd_kernel, heads, bq, bk),
        grid_spec=pltpu.PrefetchScalarGridSpec(
            num_scalar_prefetch=2,
            grid=(rows // bq,),
            in_specs=[
                pl.BlockSpec((heads, bq, LANES), lambda i, lo, hi: (0, i, 0)),
                pl.BlockSpec((heads, rows, LANES), full),
                pl.BlockSpec((heads, VT, rows), full),
                pl.BlockSpec((1, bq), lambda i, lo, hi: (0, i)),
            ],
            out_specs=[
                pl.BlockSpec((bq, heads * HD), lambda i, lo, hi: (i, 0)),
                pl.BlockSpec((heads, bq, LANES), lambda i, lo, hi: (0, i, 0)),
            ],
            scratch_shapes=[
                pltpu.VMEM((heads, 1, bq), F32),
                pltpu.VMEM((heads, VT, bq), F32),
            ],
        ),
        out_shape=[
            jax.ShapeDtypeStruct((rows, heads * HD), BF),
            jax.ShapeDtypeStruct((heads, rows, LANES), BF),
        ],
        compiler_params=pltpu.CompilerParams(vmem_limit_bytes=48 << 20),
        name="attend",
    )(lo, hi, qe, ke, vt, padw)


def bwd_kernel(heads, bq, bk, lo_ref, hi_ref, qb_ref, ke_ref, ve_ref, go_ref, att_ref, dq_ref, dk_ref, dv_ref, ge_ref, dqt_ref, kt_ref, qt_ref, got_ref, dkt_ref, dvt_ref):
    j = pl.program_id(0)
    rows = qb_ref.shape[1]

    @pl.when(j == 0)
    def _():
        for h in range(heads):
            dqt_ref[h] = jnp.zeros_like(dqt_ref[h])
            for c in range(rows // 512):
                sl = pl.ds(c * 512, 512)
                go = go_ref[sl, h * HD : (h + 1) * HD]
                at = att_ref[sl, h * HD : (h + 1) * HD]
                delta = jnp.sum(go.astype(F32) * at.astype(F32), axis=1, keepdims=True)
                wide = jnp.concatenate([go, jnp.zeros_like(go)], axis=1)
                ge_ref[h, sl, :] = put3(wide, -delta, HD)
                got_ref[h, :, c * 512 : (c + 1) * 512] = wide.T[:HD]
                qt_ref[h, :, c * 512 : (c + 1) * 512] = qb_ref[h, sl, :].T[:HD]

    for h in range(heads):
        kt_ref[h] = ke_ref[h].T[:HD]

    zero = jnp.zeros((HD, bk), F32)

    def step(i, carry):
        row0 = pl.multiple_of(i * bq, bq)
        work = [(h, pl.ds(row0 + c, QB)) for c in range(0, bq, QB) for h in range(heads)]
        score = lambda h, c: (nt(ke_ref[h], qb_ref[h, c, :]), nt(ve_ref[h], ge_ref[h, c, :]))
        ss = [score(*w) for w in work[:BAHEAD]]
        for n, (h, c) in enumerate(work):
            if n + BAHEAD < len(work):
                ss.append(score(*work[n + BAHEAD]))
            st, dt = ss[n]
            p = jnp.exp(st)
            ds = (p * dt).astype(BF)
            pb = p.astype(BF)
            dvt_ref[h] += nt(got_ref[h, :, c], pb)
            dkt_ref[h] += nt(qt_ref[h, :, c], ds)
            dqt_ref[h, :, c] += nn(kt_ref[h], ds)
        return 0

    for h in range(heads):
        dkt_ref[h] = zero
        dvt_ref[h] = zero
    lax.fori_loop(lo_ref[j], hi_ref[j], step, 0)
    for h in range(heads):
        dk_ref[:, h * HD : (h + 1) * HD] = dkt_ref[h].T.astype(BF)
        dv_ref[:, h * HD : (h + 1) * HD] = dvt_ref[h].T.astype(BF)

    @pl.when(j == pl.num_programs(0) - 1)
    def _():
        for h in range(heads):
            for c in range(rows // 512):
                sl = pl.ds(c * 512, 512)
                dq_ref[sl, h * HD : (h + 1) * HD] = (dqt_ref[h, :, c * 512 : (c + 1) * 512].T * (HD ** -0.5)).astype(BF)


def attend_back(qb, ke, ve, go, att, lo, hi, bq, bk):
    heads, rows, _ = qb.shape
    full3 = lambda i, lo, hi: (0, 0, 0)
    full2 = lambda i, lo, hi: (0, 0)
    blk3 = lambda i, lo, hi: (0, i, 0)
    blk2 = lambda i, lo, hi: (i, 0)
    wide = heads * HD
    return pl.pallas_call(
        functools.partial(bwd_kernel, heads, bq, bk),
        grid_spec=pltpu.PrefetchScalarGridSpec(
            num_scalar_prefetch=2,
            grid=(rows // bk,),
            in_specs=[
                pl.BlockSpec((heads, rows, LANES), full3),
                pl.BlockSpec((heads, bk, LANES), blk3),
                pl.BlockSpec((heads, bk, LANES), blk3),
                pl.BlockSpec((rows, wide), full2),
                pl.BlockSpec((rows, wide), full2),
            ],
            out_specs=[
                pl.BlockSpec((rows, wide), full2),
                pl.BlockSpec((bk, wide), blk2),
                pl.BlockSpec((bk, wide), blk2),
            ],
            scratch_shapes=[
                pltpu.VMEM((heads, rows, LANES), BF),
                pltpu.VMEM((heads, HD, rows), F32),
                pltpu.VMEM((heads, HD, bk), BF),
                pltpu.VMEM((heads, HD, rows), BF),
                pltpu.VMEM((heads, HD, rows), BF),
                pltpu.VMEM((heads, HD, bk), F32),
                pltpu.VMEM((heads, HD, bk), F32),
            ],
        ),
        out_shape=[jax.ShapeDtypeStruct((rows, wide), BF)] * 3,
        compiler_params=pltpu.CompilerParams(vmem_limit_bytes=48 << 20),
        name="attend_back",
    )(lo, hi, qb, ke, ve, go, att)


def dot_f32(a, b, dims):
    return lax.dot_general(a, b, ((dims[:1], dims[1:]), ((), ())), precision=highest, preferred_element_type=F32)


def soap_kernel(group, ga_ref, gb_ref, w_ref, m1_ref, m2_ref, av_ref, st_ref, ba_ref,
                nw_ref, n1_ref, n2_ref, na_ref, ns_ref, nb_ref, aug_ref):
    size = w_ref.shape[-1]
    half = size // 2
    panel = 8
    for s in range(group):
        wire = ga_ref[s * half : (s + 1) * half, :].astype(F32) + gb_ref[s * half : (s + 1) * half, :].astype(F32)
        grad = jnp.concatenate([wire[:, :size], wire[:, size:]], axis=0)
        left, right = ba_ref[0, s, 0], ba_ref[0, s, 1]
        weight = w_ref[0, s]
        first = beta_one * m1_ref[0, s] + (1.0 - beta_one) * grad
        n1_ref[0, s] = first
        both = dot_f32(jnp.concatenate([grad, first], axis=0), right, (1, 0))
        pair = dot_f32(left, jnp.concatenate([both[:size], both[size:]], axis=1), (0, 0))
        rotated, moment = pair[:, :size], pair[:, size:]
        second = beta_two * m2_ref[0, s] + (1.0 - beta_two) * rotated * rotated
        n2_ref[0, s] = second
        scaled = moment / (jnp.sqrt(second) + step_eps)
        direction = dot_f32(left, dot_f32(scaled, right, (1, 1)), (1, 0))
        fresh = weight - step_rate * (direction + weight_decay * weight)
        nw_ref[0, s] = fresh
        na_ref[0, s] = average_keep * av_ref[0, s] + (1.0 - average_keep) * fresh
        for side, base in ((0, left), (1, right)):
            outer = dot_f32(grad, grad, (1, 1) if side == 0 else (0, 0))
            stat = beta_two * st_ref[0, s, side] + (1.0 - beta_two) * outer
            ns_ref[0, s, side] = stat
            mt = dot_f32(base, stat, (0, 1))
            gram = dot_f32(mt, mt, (1, 1))
            aug_ref[2 * s + side] = jnp.concatenate([gram, mt], axis=1)
    count = 2 * group
    row = lax.broadcasted_iota(jnp.int32, (count, panel, LANES), 1)
    for p in range(size // panel):
        top = p * panel
        part = aug_ref[:, top : top + panel, :]
        for r in range(panel):
            pivot = lax.rsqrt(part[:, r : r + 1, top + r : top + r + 1])
            lead = part[:, r : r + 1, :] * pivot
            column = jnp.where(row > r, part[:, :, top + r : top + r + 1] * pivot, 0.0)
            part = jnp.where(row == r, lead, part - column * lead)
        aug_ref[:, top : top + panel, :] = part
        below = top + panel
        if below < size:
            for m in range(count):
                one = part[m]
                aug_ref[m, below:, :] -= dot_f32(one[:, below:size], one, (0, 0))
    for s in range(group):
        for side in range(2):
            nb_ref[0, s, side] = aug_ref[2 * s + side][:, size:].T


def soap(ga, gb, weights, first, second, average, stats, bases, group):
    _, slots, size, _ = weights.shape
    wire = pl.BlockSpec((group * size // 2, LANES), lambda i: (i, 0))
    four = pl.BlockSpec((1, group, size, size), lambda i: (0, i, 0, 0))
    five = pl.BlockSpec((1, group, 2, size, size), lambda i: (0, i, 0, 0, 0))
    like = lambda a: jax.ShapeDtypeStruct(a.shape, a.dtype)
    return pl.pallas_call(
        functools.partial(soap_kernel, group),
        grid=(slots // group,),
        in_specs=[wire, wire, four, four, four, four, five, five],
        out_specs=[four, four, four, four, five, five],
        out_shape=[like(a) for a in (weights, first, second, average, stats, bases)],
        scratch_shapes=[pltpu.VMEM((2 * group, size, LANES), F32)],
        compiler_params=pltpu.CompilerParams(vmem_limit_bytes=48 << 20),
        name="soap",
    )(ga, gb, weights, first, second, average, stats, bases)


def normalize(values):
    center = jnp.mean(values, axis=-1, keepdims=True)
    centered = values - center
    variance = jnp.mean(centered * centered, axis=-1, keepdims=True)
    scale = lax.rsqrt(variance + norm_eps)
    return centered * scale, scale


def norm_back(grad, xhat, scale):
    along = jnp.mean(grad * xhat, axis=-1, keepdims=True)
    return (grad - jnp.mean(grad, axis=-1, keepdims=True) - xhat * along) * scale


TAIL = 0.305
TAIL_FIT = (
    0.1216397411342051,
    0.12246669816059132,
    0.10342157025713879,
    0.1210193967312446,
    -0.037972477455618554,
    0.18571204369074895,
    -0.15298537812807472,
    0.036698452375741396,
)


def gelu_pair(u):
    size = jnp.abs(u)
    bell = jnp.exp(-0.5 * u * u)
    t = 1.0 / (1.0 + TAIL * size)
    poly = jnp.full_like(t, TAIL_FIT[-1])
    for c in TAIL_FIT[-2::-1]:
        poly = poly * t + c
    upper = poly * t * bell
    cdf = jnp.where(u > 0.0, 1.0 - upper, upper)
    return u * cdf, cdf + (0.3989422804014327 * u) * bell


def block_rows(ref, start, half):
    return ref[pl.ds(pl.multiple_of(start, 16), half), :]


def project_kernel(heads, rows_dev, gains_at, row_ref, wire_ref, tok_ref, seg_ref, pad_ref, gain_ref,
                   norm_ref, qe_ref, ke_ref, ve_ref, vt_ref, mix_ref, wide_ref):
    width = tok_ref.shape[1]
    half = HD // 2
    cols = 3 * heads

    @pl.when(pl.program_id(0) == 0)
    def _():
        zero = jnp.zeros((half, HD), BF)

        def fill(r, _):
            low = pl.multiple_of(r * HD, HD)
            for c in range(cols):
                t = block_rows(wire_ref, row_ref[r * cols + c], half)
                for part in range(2):
                    piece = t[:, part * HD : (part + 1) * HD]
                    at = pl.ds(low + part * half, half)
                    wide_ref[at, c * LANES : (c + 1) * LANES] = jnp.concatenate([piece, zero], axis=1)
                    mix_ref[at, c * HD : (c + 1) * HD] = piece
            return 0

        lax.fori_loop(0, width // HD, fill, 0)

    xhat, _ = normalize(tok_ref[...].astype(F32))
    normed = (xhat * gain_ref[...]).astype(BF)
    norm_ref[...] = normed
    count = tok_ref.shape[0]
    lane = lax.broadcasted_iota(jnp.int32, (LANES, count), 0)
    seg = seg_ref[...]
    same = lane - HD == seg
    in_segs = (lane >= HD) & (lane < HD + SEGS)
    ones = (lane >= HD + SEGS) & (lane < HD + SEGS + 3)
    ext_q = jnp.where(same, 1.0, 0.0).T
    ext_k = jnp.where(in_segs, jnp.where(same & (pad_ref[...] > 0.5), 0.0, NEG), jnp.where(ones, 1.0, 0.0)).T
    ext_v = jnp.where((lane >= HD) & (lane < HD + 3), 1.0, 0.0).T
    for h in range(heads):
        for ref, part, scale, ext in ((qe_ref, 0, HD ** -0.5, ext_q), (ke_ref, 1, 1.0, ext_k), (ve_ref, 2, 1.0, ext_v)):
            c = part * heads + h
            mixed = nn(normed, wide_ref[:, c * LANES : (c + 1) * LANES]).astype(BF)
            out = (mixed.astype(F32) * scale + ext).astype(BF)
            ref[h] = out
            if part == 2:
                vt_ref[h] = out.T[:VT]


def project(wire, row_own, tokens, seg, pad, gain_one, heads):
    rows, width = tokens.shape
    tb = min(512, rows)
    full = lambda i, r: (0, 0)
    blk = lambda i, r: (i, 0)
    col = lambda i, r: (0, i)
    ext = lambda i, r: (0, i, 0)
    out = lambda *s: jax.ShapeDtypeStruct(s, BF)
    return pl.pallas_call(
        functools.partial(project_kernel, heads, 0, 0),
        grid_spec=pltpu.PrefetchScalarGridSpec(
            num_scalar_prefetch=1,
            grid=(rows // tb,),
            in_specs=[
                pl.BlockSpec(wire.shape, full),
                pl.BlockSpec((tb, width), blk),
                pl.BlockSpec((1, tb), col),
                pl.BlockSpec((1, tb), col),
                pl.BlockSpec((1, width), full),
            ],
            out_specs=[
                pl.BlockSpec((tb, width), blk),
                pl.BlockSpec((heads, tb, LANES), ext),
                pl.BlockSpec((heads, tb, LANES), ext),
                pl.BlockSpec((heads, tb, LANES), ext),
                pl.BlockSpec((heads, VT, tb), lambda i, r: (0, 0, i)),
                pl.BlockSpec((width, 3 * heads * HD), full),
            ],
            scratch_shapes=[pltpu.VMEM((width, 3 * heads * LANES), BF)],
        ),
        out_shape=[
            out(rows, width),
            out(heads, rows, LANES),
            out(heads, rows, LANES),
            out(heads, rows, LANES),
            out(heads, VT, rows),
            out(width, 3 * heads * HD),
        ],
        compiler_params=pltpu.CompilerParams(vmem_limit_bytes=48 << 20),
        name="project",
    )(row_own, wire, tokens, seg, pad, gain_one)


def middle_kernel(shards, span, units, rows_dev, wide, gain_row, gains_dev,
                  here_ref, row_ref, wire_ref, att_ref, tok_ref, cot_ref, pad_ref, gain_ref,
                  out_ref, res_ref, back_ref, grads_ref, mix_ref,
                  wo_ref, wu_ref, wd_ref, go_ref, gu_ref, gd_ref, gg_ref):
    width = tok_ref.shape[1]
    half = HD // 2
    kinds = (
        (mix_ref, None, width, 3 * span),
        (wo_ref, go_ref, span, width),
        (wu_ref, gu_ref, width, units),
        (wd_ref, gd_ref, units, width),
    )

    @pl.when(pl.program_id(0) == 0)
    def _():
        base = 0
        for ref, acc, rows, cols in kinds:
            grid_cols = cols // HD

            def fill(r, _, ref=ref, base=base, grid_cols=grid_cols):
                low = pl.multiple_of(r * HD, HD)
                for n in range(shards):
                    for c in range(grid_cols):
                        t = block_rows(wire_ref, row_ref[base + r * grid_cols + c] + n * rows_dev, half)
                        for part in range(2):
                            ref[n, pl.ds(low + part * half, half), c * HD : (c + 1) * HD] = t[:, part * HD : (part + 1) * HD]
                return 0

            lax.fori_loop(0, rows // HD, fill, 0)
            base += rows // HD * grid_cols
            if acc is not None:
                acc[...] = jnp.zeros_like(acc)
        gg_ref[...] = jnp.zeros_like(gg_ref)

    tokens = tok_ref[...].astype(F32)
    cot = cot_ref[...]
    branch = nn(att_ref[0], wo_ref[0])
    for n in range(1, shards):
        branch += nn(att_ref[n], wo_ref[n])
    residual = tokens + branch
    xhat, scale = normalize(residual)
    gain = gain_ref[...]
    normed = (xhat * gain).astype(BF)
    mlp = jnp.zeros_like(residual)
    back = jnp.zeros_like(residual)
    for n in range(shards):
        value, slope = gelu_pair(nn(normed, wu_ref[n]))
        active = value.astype(BF)
        mlp += nn(active, wd_ref[n])
        gd_ref[n] += tn(active, cot)
        back_up = (slope * nt(cot, wd_ref[n])).astype(BF)
        gu_ref[n] += tn(normed, back_up)
        back += nt(back_up, wu_ref[n])
    out_ref[...] = (residual + mlp).astype(BF)
    gg_ref[...] += jnp.sum(back * xhat, axis=0, keepdims=True)
    back_res = cot.astype(F32) + norm_back(back * gain, xhat, scale)
    res_ref[...] = back_res
    branch_low = back_res.astype(BF)
    pad = jnp.broadcast_to(pad_ref[...], (8, pad_ref.shape[1])).T[:, :1]
    for n in range(shards):
        go_ref[n] += tn(att_ref[n], branch_low)
        back_ref[n] = (nt(branch_low, wo_ref[n]) * pad).astype(BF)

    @pl.when(pl.program_id(0) == pl.num_programs(0) - 1)
    def _():
        grads_ref[...] = jnp.zeros_like(grads_ref)
        base = 0
        for ref, acc, rows, cols in kinds:
            grid_cols = cols // HD
            if acc is not None:

                def scatter(r, _, acc=acc, base=base, grid_cols=grid_cols):
                    low = pl.multiple_of(r * HD, HD)
                    for n in range(shards):
                        for c in range(grid_cols):
                            at = row_ref[base + r * grid_cols + c] + n * rows_dev
                            cut = slice(c * HD, (c + 1) * HD)
                            value = jnp.concatenate([acc[n, pl.ds(low, half), cut], acc[n, pl.ds(low + half, half), cut]], axis=1)
                            grads_ref[pl.ds(pl.multiple_of(at, 16), half), :] = value.astype(BF)
                    return 0

                lax.fori_loop(0, rows // HD, scatter, 0)
            base += rows // HD * grid_cols
        for w in range(wide):
            piece = w * gains_dev // LANES - width // LANES
            if piece >= 0:
                for n in range(shards):
                    at = (w * shards + n) * rows_dev + gain_row
                    grads_ref[at : at + 1, :] = gg_ref[:, piece * LANES : (piece + 1) * LANES].astype(BF)


def middle(here, row_full, wire, att, tokens, cotangent, pad, gain_two, wide, rows_dev, gain_row, gains_dev):
    shards, own, span = att.shape
    width = tokens.shape[1]
    units = FF // shards
    tb = min(256, own)
    steps = own // tb
    full = lambda i, h, r: (0, 0)
    full3 = lambda i, h, r: (0, 0, 0)
    mine = lambda i, h, r: (h[0] * steps + i, 0)
    blk = lambda i, h, r: (i, 0)
    blk3 = lambda i, h, r: (0, i, 0)
    once = pl.Buffered(1)
    return pl.pallas_call(
        functools.partial(middle_kernel, shards, span, units, rows_dev, wide, gain_row, gains_dev),
        grid_spec=pltpu.PrefetchScalarGridSpec(
            num_scalar_prefetch=2,
            grid=(steps,),
            in_specs=[
                pl.BlockSpec(wire.shape, full, pipeline_mode=once),
                pl.BlockSpec((shards, tb, span), blk3),
                pl.BlockSpec((tb, width), mine),
                pl.BlockSpec((tb, width), mine),
                pl.BlockSpec((1, tb), lambda i, h, r: (0, h[0] * steps + i)),
                pl.BlockSpec((1, width), full),
            ],
            out_specs=[
                pl.BlockSpec((tb, width), blk),
                pl.BlockSpec((tb, width), blk),
                pl.BlockSpec((shards, tb, span), blk3),
                pl.BlockSpec(wire.shape, full, pipeline_mode=once),
                pl.BlockSpec((shards, width, 3 * span), full3, pipeline_mode=once),
            ],
            scratch_shapes=[
                pltpu.VMEM((shards, span, width), BF),
                pltpu.VMEM((shards, width, units), BF),
                pltpu.VMEM((shards, units, width), BF),
                pltpu.VMEM((shards, span, width), F32),
                pltpu.VMEM((shards, width, units), F32),
                pltpu.VMEM((shards, units, width), F32),
                pltpu.VMEM((1, width), F32),
            ],
        ),
        out_shape=[
            jax.ShapeDtypeStruct((own, width), BF),
            jax.ShapeDtypeStruct((own, width), F32),
            jax.ShapeDtypeStruct((shards, own, span), BF),
            jax.ShapeDtypeStruct(wire.shape, BF),
            jax.ShapeDtypeStruct((shards, width, 3 * span), BF),
        ],
        compiler_params=pltpu.CompilerParams(vmem_limit_bytes=56 << 20),
        name="middle",
    )(here, row_full, wire, att, tokens, cotangent, pad, gain_two)


def mixgrad_kernel(heads, rows_dev, wide, gain_row, gains_dev, row_ref, norm_ref, dq_ref, dk_ref, dv_ref, mix_ref, gain_ref, grads_ref, acc_ref):
    width = norm_ref.shape[1]
    span = heads * HD
    half = HD // 2
    cols = 3 * heads

    @pl.when(pl.program_id(0) == 0)
    def _():
        acc_ref[...] = jnp.zeros_like(acc_ref)

    normed = norm_ref[...]
    for part, ref in enumerate((dq_ref, dk_ref, dv_ref)):
        acc_ref[:, part * span : (part + 1) * span] += tn(normed, ref[...])

    @pl.when(pl.program_id(0) == pl.num_programs(0) - 1)
    def _():
        grads_ref[...] = jnp.zeros_like(grads_ref)

        def scatter(r, _):
            low = pl.multiple_of(r * HD, HD)
            for c in range(cols):
                cut = slice(c * HD, (c + 1) * HD)
                value = jnp.concatenate([acc_ref[pl.ds(low, half), cut], acc_ref[pl.ds(low + half, half), cut]], axis=1)
                grads_ref[pl.ds(pl.multiple_of(row_ref[r * cols + c], 16), half), :] = value.astype(BF)
            return 0

        lax.fori_loop(0, width // HD, scatter, 0)
        along = jnp.sum(acc_ref[...] * mix_ref[...].astype(F32), axis=1, keepdims=True)
        line = jnp.broadcast_to(along, (width, LANES)).T[:1] / gain_ref[...]
        for w in range(wide):
            piece = w * gains_dev // LANES
            if piece < width // LANES:
                at = w * rows_dev + gain_row
                grads_ref[at : at + 1, :] = line[:, piece * LANES : (piece + 1) * LANES].astype(BF)


def mixgrad(row_own, normed, dq, dk, dv, mix, gain_one, wire_shape, wide, rows_dev, gain_row, gains_dev):
    rows, width = normed.shape
    span = dq.shape[1]
    tb = min(512, rows)
    full = lambda i, r: (0, 0)
    blk = lambda i, r: (i, 0)
    return pl.pallas_call(
        functools.partial(mixgrad_kernel, span // HD, rows_dev, wide, gain_row, gains_dev),
        grid_spec=pltpu.PrefetchScalarGridSpec(
            num_scalar_prefetch=1,
            grid=(rows // tb,),
            in_specs=[
                pl.BlockSpec((tb, width), blk),
                pl.BlockSpec((tb, span), blk),
                pl.BlockSpec((tb, span), blk),
                pl.BlockSpec((tb, span), blk),
                pl.BlockSpec((width, 3 * span), full),
                pl.BlockSpec((1, width), full),
            ],
            out_specs=pl.BlockSpec(wire_shape, full),
            scratch_shapes=[pltpu.VMEM((width, 3 * span), F32)],
        ),
        out_shape=jax.ShapeDtypeStruct(wire_shape, BF),
        compiler_params=pltpu.CompilerParams(vmem_limit_bytes=48 << 20),
        name="mixgrad",
    )(row_own, normed, dq, dk, dv, mix, gain_one)


def tail_kernel(shards, here_ref, bm_ref, mix_ref, tok_ref, res_ref, gain_ref, out_ref):
    back = nt(bm_ref[0], mix_ref[0])
    for n in range(1, shards):
        back += nt(bm_ref[n], mix_ref[n])
    xhat, scale = normalize(tok_ref[...].astype(F32))
    out_ref[...] = (res_ref[...] + norm_back(back * gain_ref[...], xhat, scale)).astype(BF)


def tail(here, bm, mix, tokens, res, gain_one):
    shards, own, cols = bm.shape
    width = tokens.shape[1]
    tb = min(256, own)
    steps = own // tb
    full3 = lambda i, h: (0, 0, 0)
    return pl.pallas_call(
        functools.partial(tail_kernel, shards),
        grid_spec=pltpu.PrefetchScalarGridSpec(
            num_scalar_prefetch=1,
            grid=(steps,),
            in_specs=[
                pl.BlockSpec((shards, tb, cols), lambda i, h: (0, i, 0)),
                pl.BlockSpec(mix.shape, full3),
                pl.BlockSpec((tb, width), lambda i, h: (h[0] * steps + i, 0)),
                pl.BlockSpec((tb, width), lambda i, h: (i, 0)),
                pl.BlockSpec((1, width), lambda i, h: (0, 0)),
            ],
            out_specs=pl.BlockSpec((tb, width), lambda i, h: (i, 0)),
        ),
        out_shape=jax.ShapeDtypeStruct((own, width), BF),
        compiler_params=pltpu.CompilerParams(vmem_limit_bytes=48 << 20),
        name="tail",
    )(here, bm, mix, tokens, res, gain_one)


def adam_gains(grad, gain, first, second, average):
    new_first = beta_one * first + (1.0 - beta_one) * grad
    new_second = beta_two * second + (1.0 - beta_two) * grad * grad
    new_gain = gain - gain_rate * new_first / (jnp.sqrt(new_second) + step_eps)
    new_average = average_keep * average + (1.0 - average_keep) * new_gain
    return (new_gain, new_first, new_second, new_average)


def to_shards(values, shards):
    rows, cols = values.shape
    return lax.all_to_all(values.reshape(shards, rows // shards, cols), "narrow", 0, 0)


def body(
    tokens,
    cotangent,
    segment_ids,
    pad_mask,
    owner_order,
    weights,
    first_moment,
    second_moment,
    average,
    stats,
    bases,
    gains,
    gain_first,
    gain_second,
    gain_average,
):
    narrow = lax.axis_size("narrow")
    wide = lax.axis_size("wide")
    here = lax.axis_index("narrow")
    heads = HEADS // narrow
    rows, width = tokens.shape
    span = heads * HD
    own = rows // narrow
    slots, size = weights.shape[1], weights.shape[2]
    half = size // 2
    block_count = owner_order.shape[0]
    gains_dev = gains.shape[0]
    gain_row = slots * half
    rows_dev = gain_row + 16

    low = weights[0].astype(BF)
    wire = jnp.concatenate([low[:, :half], low[:, half:]], axis=2).reshape(gain_row, 2 * size)
    wire = jnp.concatenate([wire, jnp.pad(gains.astype(BF)[None], ((0, 15), (0, LANES - gains_dev)))], axis=0)
    wire_own = lax.all_gather(wire, "wide", axis=0, tiled=True)
    wire_full = lax.all_gather(lax.all_gather(wire, "narrow", axis=0, tiled=True), "wide", axis=0, tiled=True)

    ids = jnp.arange(block_count, dtype=jnp.int32)
    slot_of = jnp.sum(jnp.where(owner_order[None, :] == ids[:, None], ids[None, :], 0), axis=1)
    device, place = slot_of // slots, slot_of % slots
    row_own = device * rows_dev + place * half
    row_full = device * (narrow * rows_dev) + place * half
    here_of = jnp.full((1,), here, jnp.int32)

    gain_all = wire_own.reshape(wide, rows_dev, LANES)[:, gain_row, :gains_dev].astype(F32).reshape(1, 2 * width)
    gain_one, gain_two = gain_all[:, :width], gain_all[:, width:]
    seg = segment_ids
    seg_row = segment_ids[0]
    pad = pad_mask.astype(F32)
    block = min(512, rows)
    low_seg = seg_row[::block]
    high_seg = seg_row[block - 1 :: block]
    begin = jnp.sum((seg_row[None, :] < low_seg[:, None]).astype(jnp.int32), axis=1) // block
    end = (jnp.sum((seg_row[None, :] <= high_seg[:, None]).astype(jnp.int32), axis=1) + block - 1) // block

    normed, qe, ke, ve, vt, mix = project(wire_own, row_own, tokens, seg, pad, gain_one, heads)
    attended, qb = attend(qe, ke, vt, pad, begin, end, block, block)
    att_own = to_shards(attended, narrow)
    out_own, back_res, back_own, grads, mix_full = middle(
        here_of, row_full, wire_full, att_own, tokens, cotangent, pad, gain_two, wide, rows_dev, gain_row, gains_dev
    )
    output = lax.all_gather(out_own, "narrow", axis=0, tiled=True)
    back_att = lax.all_to_all(back_own, "narrow", 0, 0).reshape(rows, span)
    dq, dk, dv = attend_back(qb, ke, ve, back_att, attended, begin, end, block, block)
    grads_mix = mixgrad(row_own, normed, dq, dk, dv, mix, gain_one, wire_own.shape, wide, rows_dev, gain_row, gains_dev)
    bm = to_shards(jnp.concatenate([dq, dk, dv], axis=1), narrow)
    grad_own = tail(here_of, bm, mix_full, tokens, back_res, gain_one)
    input_grad = lax.all_gather(grad_own, "narrow", axis=0, tiled=True).astype(F32)

    part_a = lax.psum_scatter(grads, "wide", scatter_dimension=0, tiled=True)
    part_a = lax.psum_scatter(part_a, "narrow", scatter_dimension=0, tiled=True)
    part_b = lax.psum_scatter(grads_mix, "wide", scatter_dimension=0, tiled=True)
    group = 8 if slots % 8 == 0 else 1
    new_weight, new_first, new_second, new_average, new_stats, new_bases = soap(
        part_a, part_b, weights, first_moment, second_moment, average, stats, bases, group
    )
    line = part_a[gain_row].astype(F32) + lax.psum(part_b[gain_row].astype(F32), "narrow")
    offset = lax.axis_index("wide") * gains_dev % LANES
    own_gain = lax.dynamic_slice_in_dim(line, offset, gains_dev, 0)
    new_gains, gain_moment, gain_square, gain_mean = adam_gains(own_gain, gains, gain_first, gain_second, gain_average)
    return (
        output,
        input_grad,
        new_weight,
        new_first,
        new_second,
        new_average,
        new_stats,
        new_bases,
        new_gains,
        gain_moment,
        gain_square,
        gain_mean,
    )


def solution(mesh):
    block = P("narrow", "wide", None, None)
    pair = P("narrow", "wide", None, None, None)
    rows = P("wide", None)
    line = P("wide")
    return jax.shard_map(
        body,
        mesh=mesh,
        in_specs=(rows, rows, rows, rows, P(), block, block, block, block, pair, pair, line, line, line, line),
        out_specs=(rows, rows, block, block, block, block, pair, pair, line, line, line, line),
        check_vma=False,
    )
```

```python
import functools

import jax
import jax.numpy as jnp
from jax import lax
from jax.experimental import pallas as pl
from jax.experimental.pallas import tpu as pltpu
from jax.sharding import PartitionSpec as P

HEADS = 8
HD = 64
FF = 2048
LANES = 128
SEGS = 4
NEG = -1e30
F32 = jnp.float32
BF = jnp.bfloat16
highest = lax.Precision.HIGHEST

beta_one = 0.9
beta_two = 0.95
step_rate = 0.1
gain_rate = 0.75
weight_decay = 0.01
average_keep = 0.5
norm_eps = 1e-05
step_eps = 1e-08


def nt(a, b):
    return lax.dot_general(a, b, (((1,), (1,)), ((), ())), preferred_element_type=F32)


def nn(a, b):
    return lax.dot_general(a, b, (((1,), (0,)), ((), ())), preferred_element_type=F32)


def tn(a, b):
    return lax.dot_general(a, b, (((0,), (0,)), ((), ())), preferred_element_type=F32)


def split3(x):
    hi = x.astype(BF)
    r = x - hi.astype(F32)
    mid = r.astype(BF)
    lo = (r - mid.astype(F32)).astype(BF)
    return hi, mid, lo


def put3(base, x, lane0):
    lane = lax.broadcasted_iota(jnp.int32, base.shape, 1)
    hi, mid, lo = split3(x)
    out = jnp.where(lane == lane0, hi.astype(F32), base.astype(F32))
    out = jnp.where(lane == lane0 + 1, mid.astype(F32), out)
    out = jnp.where(lane == lane0 + 2, lo.astype(F32), out)
    return out.astype(BF)


VT = 80
QC, AHEAD, QB, BAHEAD = 512, 1, 256, 1


def fwd_kernel(heads, bq, bk, lo_ref, hi_ref, qe_ref, ke_ref, vt_ref, pad_ref, att_ref, qb_ref, m_ref, acc_ref):
    i = pl.program_id(0)
    row0 = pl.multiple_of(i * bq, bq)
    real = pad_ref[...] > 0.5
    for h in range(heads):
        qt = qe_ref[h].astype(F32).T[:HD]
        kt = ke_ref[h, pl.ds(row0, bq), :].astype(F32).T[:HD]
        own = jnp.sum(qt * kt, axis=0, keepdims=True)
        m_ref[h] = jnp.where(real, NEG, own)
        acc_ref[h] = jnp.where(real, 0.0, vt_ref[h, :, pl.ds(row0, bq)].astype(F32))

    def step(j, _):
        col0 = pl.multiple_of(j * bk, bk)
        work = [(h, slice(c, c + QC)) for c in range(0, bq, QC) for h in range(heads)]
        score = lambda h, c: nt(ke_ref[h, pl.ds(col0, bk), :], qe_ref[h, c, :])
        ss = [score(*w) for w in work[:AHEAD]]
        for n, (h, c) in enumerate(work):
            if n + AHEAD < len(work):
                ss.append(score(*work[n + AHEAD]))
            s = ss[n]
            m_old = m_ref[h, :, c]
            m_new = jnp.maximum(m_old, jnp.max(s, axis=0, keepdims=True))
            p = jnp.exp(s - m_new).astype(BF)
            alpha = jnp.exp(m_old - m_new)
            acc_ref[h, :, c] = acc_ref[h, :, c] * alpha + nn(vt_ref[h, :, pl.ds(col0, bk)], p)
            m_ref[h, :, c] = m_new
        return 0

    lax.fori_loop(lo_ref[i], hi_ref[i], step, 0)
    outs = []
    for h in range(heads):
        acc = acc_ref[h]
        total = acc[HD : HD + 1]
        outs.append(jnp.where(real, acc[:HD] / total, 0.0))
        lse = jnp.broadcast_to(m_ref[h] + jnp.log(total), (8, bq)).T[:, :1]
        qb_ref[h] = put3(qe_ref[h], -lse, HD + 4)
    att_ref[...] = (jnp.concatenate(outs, axis=0) if heads > 1 else outs[0]).T.astype(BF)


def attend(qe, ke, vt, padw, lo, hi, bq, bk):
    heads, rows, _ = qe.shape
    full = lambda i, lo, hi: (0, 0, 0)
    return pl.pallas_call(
        functools.partial(fwd_kernel, heads, bq, bk),
        grid_spec=pltpu.PrefetchScalarGridSpec(
            num_scalar_prefetch=2,
            grid=(rows // bq,),
            in_specs=[
                pl.BlockSpec((heads, bq, LANES), lambda i, lo, hi: (0, i, 0)),
                pl.BlockSpec((heads, rows, LANES), full),
                pl.BlockSpec((heads, VT, rows), full),
                pl.BlockSpec((1, bq), lambda i, lo, hi: (0, i)),
            ],
            out_specs=[
                pl.BlockSpec((bq, heads * HD), lambda i, lo, hi: (i, 0)),
                pl.BlockSpec((heads, bq, LANES), lambda i, lo, hi: (0, i, 0)),
            ],
            scratch_shapes=[
                pltpu.VMEM((heads, 1, bq), F32),
                pltpu.VMEM((heads, VT, bq), F32),
            ],
        ),
        out_shape=[
            jax.ShapeDtypeStruct((rows, heads * HD), BF),
            jax.ShapeDtypeStruct((heads, rows, LANES), BF),
        ],
        compiler_params=pltpu.CompilerParams(vmem_limit_bytes=60 << 20),
        name="attend",
    )(lo, hi, qe, ke, vt, padw)


def bwd_kernel(heads, bq, bk, lo_ref, hi_ref, qb_ref, ke_ref, ve_ref, go_ref, att_ref, out_ref, ge_ref, dqt_ref, kt_ref, qt_ref, got_ref, dkt_ref, dvt_ref):
    j = pl.program_id(0)
    rows = qb_ref.shape[1]

    @pl.when(j == 0)
    def _():
        for h in range(heads):
            dqt_ref[h] = jnp.zeros_like(dqt_ref[h])
            for c in range(rows // 512):
                sl = pl.ds(c * 512, 512)
                go = go_ref[sl, h * HD : (h + 1) * HD]
                at = att_ref[sl, h * HD : (h + 1) * HD]
                delta = jnp.sum(go.astype(F32) * at.astype(F32), axis=1, keepdims=True)
                wide = jnp.concatenate([go, jnp.zeros_like(go)], axis=1)
                ge_ref[h, sl, :] = put3(wide, -delta, HD)
                got_ref[h, :, c * 512 : (c + 1) * 512] = wide.T[:HD]
                qt_ref[h, :, c * 512 : (c + 1) * 512] = qb_ref[h, sl, :].T[:HD]

    for h in range(heads):
        kt_ref[h] = ke_ref[h].T[:HD]

    zero = jnp.zeros((HD, bk), F32)

    def step(i, carry):
        row0 = pl.multiple_of(i * bq, bq)
        work = [(h, pl.ds(row0 + c, QB)) for c in range(0, bq, QB) for h in range(heads)]
        score = lambda h, c: (nt(ke_ref[h], qb_ref[h, c, :]), nt(ve_ref[h], ge_ref[h, c, :]))
        ss = [score(*w) for w in work[:BAHEAD]]
        for n, (h, c) in enumerate(work):
            if n + BAHEAD < len(work):
                ss.append(score(*work[n + BAHEAD]))
            st, dt = ss[n]
            p = jnp.exp(st)
            ds = (p * dt).astype(BF)
            pb = p.astype(BF)
            dvt_ref[h] += nt(got_ref[h, :, c], pb)
            dkt_ref[h] += nt(qt_ref[h, :, c], ds)
            dqt_ref[h, :, c] += nn(kt_ref[h], ds)
        return 0

    for h in range(heads):
        dkt_ref[h] = zero
        dvt_ref[h] = zero
    lax.fori_loop(lo_ref[j], hi_ref[j], step, 0)
    for h in range(heads):
        for part, ref in ((1, dkt_ref), (2, dvt_ref)):
            at = (part * heads + h) * HD
            out_ref[pl.ds(pl.multiple_of(j * bk, bk), bk), at : at + HD] = ref[h].T.astype(BF)

    @pl.when(j == pl.num_programs(0) - 1)
    def _():
        for h in range(heads):
            for c in range(rows // 512):
                sl = pl.ds(c * 512, 512)
                out_ref[sl, h * HD : (h + 1) * HD] = (dqt_ref[h, :, c * 512 : (c + 1) * 512].T * (HD ** -0.5)).astype(BF)


def attend_back(qb, ke, ve, go, att, lo, hi, bq, bk):
    heads, rows, _ = qb.shape
    full3 = lambda i, lo, hi: (0, 0, 0)
    full2 = lambda i, lo, hi: (0, 0)
    blk3 = lambda i, lo, hi: (0, i, 0)
    wide = heads * HD
    return pl.pallas_call(
        functools.partial(bwd_kernel, heads, bq, bk),
        grid_spec=pltpu.PrefetchScalarGridSpec(
            num_scalar_prefetch=2,
            grid=(rows // bk,),
            in_specs=[
                pl.BlockSpec((heads, rows, LANES), full3),
                pl.BlockSpec((heads, bk, LANES), blk3),
                pl.BlockSpec((heads, bk, LANES), blk3),
                pl.BlockSpec((rows, wide), full2),
                pl.BlockSpec((rows, wide), full2),
            ],
            out_specs=pl.BlockSpec((rows, 3 * wide), full2),
            scratch_shapes=[
                pltpu.VMEM((heads, rows, LANES), BF),
                pltpu.VMEM((heads, HD, rows), F32),
                pltpu.VMEM((heads, HD, bk), BF),
                pltpu.VMEM((heads, HD, rows), BF),
                pltpu.VMEM((heads, HD, rows), BF),
                pltpu.VMEM((heads, HD, bk), F32),
                pltpu.VMEM((heads, HD, bk), F32),
            ],
        ),
        out_shape=jax.ShapeDtypeStruct((rows, 3 * wide), BF),
        compiler_params=pltpu.CompilerParams(vmem_limit_bytes=60 << 20),
        name="attend_back",
    )(lo, hi, qb, ke, ve, go, att)


def dot_f32(a, b, dims):
    return lax.dot_general(a, b, ((dims[:1], dims[1:]), ((), ())), precision=highest, preferred_element_type=F32)


def soap_kernel(group, ga_ref, gb_ref, w_ref, m1_ref, m2_ref, av_ref, st_ref, ba_ref,
                nw_ref, n1_ref, n2_ref, na_ref, ns_ref, nb_ref, aug_ref):
    size = w_ref.shape[-1]
    half = size // 2
    panel = 8
    for s in range(group):
        wire = ga_ref[s * half : (s + 1) * half, :].astype(F32) + gb_ref[s * half : (s + 1) * half, :].astype(F32)
        grad = jnp.concatenate([wire[:, :size], wire[:, size:]], axis=0)
        left, right = ba_ref[0, s, 0], ba_ref[0, s, 1]
        weight = w_ref[0, s]
        first = beta_one * m1_ref[0, s] + (1.0 - beta_one) * grad
        n1_ref[0, s] = first
        both = dot_f32(jnp.concatenate([grad, first], axis=0), right, (1, 0))
        pair = dot_f32(left, jnp.concatenate([both[:size], both[size:]], axis=1), (0, 0))
        rotated, moment = pair[:, :size], pair[:, size:]
        second = beta_two * m2_ref[0, s] + (1.0 - beta_two) * rotated * rotated
        n2_ref[0, s] = second
        scaled = moment / (jnp.sqrt(second) + step_eps)
        direction = dot_f32(left, dot_f32(scaled, right, (1, 1)), (1, 0))
        fresh = weight - step_rate * (direction + weight_decay * weight)
        nw_ref[0, s] = fresh
        na_ref[0, s] = average_keep * av_ref[0, s] + (1.0 - average_keep) * fresh
        for side, base in ((0, left), (1, right)):
            outer = dot_f32(grad, grad, (1, 1) if side == 0 else (0, 0))
            stat = beta_two * st_ref[0, s, side] + (1.0 - beta_two) * outer
            ns_ref[0, s, side] = stat
            mt = dot_f32(base, stat, (0, 1))
            gram = dot_f32(mt, mt, (1, 1))
            aug_ref[2 * s + side] = jnp.concatenate([gram, mt], axis=1)
    count = 2 * group
    row = lax.broadcasted_iota(jnp.int32, (count, panel, LANES), 1)
    for p in range(size // panel):
        top = p * panel
        part = aug_ref[:, top : top + panel, :]
        for r in range(panel):
            pivot = lax.rsqrt(part[:, r : r + 1, top + r : top + r + 1])
            lead = part[:, r : r + 1, :] * pivot
            column = jnp.where(row > r, part[:, :, top + r : top + r + 1] * pivot, 0.0)
            part = jnp.where(row == r, lead, part - column * lead)
        aug_ref[:, top : top + panel, :] = part
        below = top + panel
        if below < size:
            for m in range(count):
                one = part[m]
                aug_ref[m, below:, :] -= dot_f32(one[:, below:size], one, (0, 0))
    for s in range(group):
        for side in range(2):
            nb_ref[0, s, side] = aug_ref[2 * s + side][:, size:].T


def soap(ga, gb, weights, first, second, average, stats, bases, group):
    _, slots, size, _ = weights.shape
    wire = pl.BlockSpec((group * size // 2, LANES), lambda i: (i, 0))
    four = pl.BlockSpec((1, group, size, size), lambda i: (0, i, 0, 0))
    five = pl.BlockSpec((1, group, 2, size, size), lambda i: (0, i, 0, 0, 0))
    like = lambda a: jax.ShapeDtypeStruct(a.shape, a.dtype)
    return pl.pallas_call(
        functools.partial(soap_kernel, group),
        grid=(slots // group,),
        in_specs=[wire, wire, four, four, four, four, five, five],
        out_specs=[four, four, four, four, five, five],
        out_shape=[like(a) for a in (weights, first, second, average, stats, bases)],
        scratch_shapes=[pltpu.VMEM((2 * group, size, LANES), F32)],
        compiler_params=pltpu.CompilerParams(vmem_limit_bytes=60 << 20),
        name="soap",
    )(ga, gb, weights, first, second, average, stats, bases)


def normalize(values):
    center = jnp.mean(values, axis=-1, keepdims=True)
    centered = values - center
    variance = jnp.mean(centered * centered, axis=-1, keepdims=True)
    scale = lax.rsqrt(variance + norm_eps)
    return centered * scale, scale


def norm_back(grad, xhat, scale):
    along = jnp.mean(grad * xhat, axis=-1, keepdims=True)
    return (grad - jnp.mean(grad, axis=-1, keepdims=True) - xhat * along) * scale


TAIL = 0.305
TAIL_FIT = (
    0.1216397411342051,
    0.12246669816059132,
    0.10342157025713879,
    0.1210193967312446,
    -0.037972477455618554,
    0.18571204369074895,
    -0.15298537812807472,
    0.036698452375741396,
)


def gelu_pair(u):
    size = jnp.abs(u)
    bell = jnp.exp(-0.5 * u * u)
    t = 1.0 / (1.0 + TAIL * size)
    poly = jnp.full_like(t, TAIL_FIT[-1])
    for c in TAIL_FIT[-2::-1]:
        poly = poly * t + c
    upper = poly * t * bell
    cdf = jnp.where(u > 0.0, 1.0 - upper, upper)
    return u * cdf, cdf + (0.3989422804014327 * u) * bell


def block_rows(ref, start, half):
    return ref[pl.ds(pl.multiple_of(start, 16), half), :]


def project_kernel(heads, rows_dev, gains_at, row_ref, wire_ref, tok_ref, seg_ref, pad_ref, gain_ref,
                   norm_ref, qe_ref, ke_ref, ve_ref, vt_ref, mix_ref, wide_ref):
    width = tok_ref.shape[1]
    half = HD // 2
    cols = 3 * heads

    @pl.when(pl.program_id(0) == 0)
    def _():
        zero = jnp.zeros((half, HD), BF)

        def fill(r, _):
            low = pl.multiple_of(r * HD, HD)
            for c in range(cols):
                t = block_rows(wire_ref, row_ref[r * cols + c], half)
                for part in range(2):
                    piece = t[:, part * HD : (part + 1) * HD]
                    at = pl.ds(low + part * half, half)
                    wide_ref[at, c * LANES : (c + 1) * LANES] = jnp.concatenate([piece, zero], axis=1)
                    mix_ref[at, c * HD : (c + 1) * HD] = piece
            return 0

        lax.fori_loop(0, width // HD, fill, 0)

    xhat, _ = normalize(tok_ref[...].astype(F32))
    normed = (xhat * gain_ref[...]).astype(BF)
    norm_ref[...] = normed
    count = tok_ref.shape[0]
    lane = lax.broadcasted_iota(jnp.int32, (LANES, count), 0)
    seg = seg_ref[...]
    same = lane - HD == seg
    in_segs = (lane >= HD) & (lane < HD + SEGS)
    ones = (lane >= HD + SEGS) & (lane < HD + SEGS + 3)
    ext_q = jnp.where(same, 1.0, 0.0).T
    ext_k = jnp.where(in_segs, jnp.where(same & (pad_ref[...] > 0.5), 0.0, NEG), jnp.where(ones, 1.0, 0.0)).T
    ext_v = jnp.where((lane >= HD) & (lane < HD + 3), 1.0, 0.0).T
    for h in range(heads):
        for ref, part, scale, ext in ((qe_ref, 0, HD ** -0.5, ext_q), (ke_ref, 1, 1.0, ext_k), (ve_ref, 2, 1.0, ext_v)):
            c = part * heads + h
            mixed = nn(normed, wide_ref[:, c * LANES : (c + 1) * LANES]).astype(BF)
            out = (mixed.astype(F32) * scale + ext).astype(BF)
            ref[h] = out
            if part == 2:
                vt_ref[h] = out.T[:VT]


def project(wire, row_own, tokens, seg, pad, gain_one, heads):
    rows, width = tokens.shape
    tb = min(512, rows)
    full = lambda i, r: (0, 0)
    blk = lambda i, r: (i, 0)
    col = lambda i, r: (0, i)
    ext = lambda i, r: (0, i, 0)
    out = lambda *s: jax.ShapeDtypeStruct(s, BF)
    return pl.pallas_call(
        functools.partial(project_kernel, heads, 0, 0),
        grid_spec=pltpu.PrefetchScalarGridSpec(
            num_scalar_prefetch=1,
            grid=(rows // tb,),
            in_specs=[
                pl.BlockSpec(wire.shape, full),
                pl.BlockSpec((tb, width), blk),
                pl.BlockSpec((1, tb), col),
                pl.BlockSpec((1, tb), col),
                pl.BlockSpec((1, width), full),
            ],
            out_specs=[
                pl.BlockSpec((tb, width), blk),
                pl.BlockSpec((heads, tb, LANES), ext),
                pl.BlockSpec((heads, tb, LANES), ext),
                pl.BlockSpec((heads, tb, LANES), ext),
                pl.BlockSpec((heads, VT, tb), lambda i, r: (0, 0, i)),
                pl.BlockSpec((width, 3 * heads * HD), full),
            ],
            scratch_shapes=[pltpu.VMEM((width, 3 * heads * LANES), BF)],
        ),
        out_shape=[
            out(rows, width),
            out(heads, rows, LANES),
            out(heads, rows, LANES),
            out(heads, rows, LANES),
            out(heads, VT, rows),
            out(width, 3 * heads * HD),
        ],
        compiler_params=pltpu.CompilerParams(vmem_limit_bytes=60 << 20),
        name="project",
    )(row_own, wire, tokens, seg, pad, gain_one)


def middle_kernel(shards, span, units, rows_dev, wide, gain_row, gains_dev,
                  here_ref, row_ref, wire_ref, att_ref, tok_ref, cot_ref, pad_ref, gain_ref,
                  out_ref, res_ref, back_ref, grads_ref, mix_ref,
                  wo_ref, wu_ref, wd_ref, go_ref, gu_ref, gd_ref, gg_ref):
    width = tok_ref.shape[1]
    half = HD // 2
    kinds = (
        (mix_ref, None, width, 3 * span),
        (wo_ref, go_ref, span, width),
        (wu_ref, gu_ref, width, units),
        (wd_ref, gd_ref, units, width),
    )

    @pl.when(pl.program_id(0) == 0)
    def _():
        base = 0
        for ref, acc, rows, cols in kinds:
            grid_cols = cols // HD

            def fill(r, _, ref=ref, base=base, grid_cols=grid_cols):
                low = pl.multiple_of(r * HD, HD)
                for n in range(shards):
                    for c in range(grid_cols):
                        t = block_rows(wire_ref, row_ref[base + r * grid_cols + c] + n * rows_dev, half)
                        for part in range(2):
                            ref[n, pl.ds(low + part * half, half), c * HD : (c + 1) * HD] = t[:, part * HD : (part + 1) * HD]
                return 0

            lax.fori_loop(0, rows // HD, fill, 0)
            base += rows // HD * grid_cols
            if acc is not None:
                acc[...] = jnp.zeros_like(acc)
        gg_ref[...] = jnp.zeros_like(gg_ref)

    tokens = tok_ref[...].astype(F32)
    cot = cot_ref[...]
    branch = nn(att_ref[0], wo_ref[0])
    for n in range(1, shards):
        branch += nn(att_ref[n], wo_ref[n])
    residual = tokens + branch
    xhat, scale = normalize(residual)
    gain = gain_ref[...]
    normed = (xhat * gain).astype(BF)
    mlp = jnp.zeros_like(residual)
    back = jnp.zeros_like(residual)
    for n in range(shards):
        value, slope = gelu_pair(nn(normed, wu_ref[n]))
        active = value.astype(BF)
        mlp += nn(active, wd_ref[n])
        gd_ref[n] += tn(active, cot)
        back_up = (slope * nt(cot, wd_ref[n])).astype(BF)
        gu_ref[n] += tn(normed, back_up)
        back += nt(back_up, wu_ref[n])
    out_ref[...] = (residual + mlp).astype(BF)
    gg_ref[...] += jnp.sum(back * xhat, axis=0, keepdims=True)
    back_res = cot.astype(F32) + norm_back(back * gain, xhat, scale)
    res_ref[...] = back_res
    branch_low = back_res.astype(BF)
    pad = jnp.broadcast_to(pad_ref[...], (8, pad_ref.shape[1])).T[:, :1]
    for n in range(shards):
        go_ref[n] += tn(att_ref[n], branch_low)
        back_ref[n] = (nt(branch_low, wo_ref[n]) * pad).astype(BF)

    @pl.when(pl.program_id(0) == pl.num_programs(0) - 1)
    def _():
        grads_ref[...] = jnp.zeros_like(grads_ref)
        base = 0
        for ref, acc, rows, cols in kinds:
            grid_cols = cols // HD
            if acc is not None:

                def scatter(r, _, acc=acc, base=base, grid_cols=grid_cols):
                    low = pl.multiple_of(r * HD, HD)
                    for n in range(shards):
                        for c in range(grid_cols):
                            at = row_ref[base + r * grid_cols + c] + n * rows_dev
                            cut = slice(c * HD, (c + 1) * HD)
                            value = jnp.concatenate([acc[n, pl.ds(low, half), cut], acc[n, pl.ds(low + half, half), cut]], axis=1)
                            grads_ref[pl.ds(pl.multiple_of(at, 16), half), :] = value.astype(BF)
                    return 0

                lax.fori_loop(0, rows // HD, scatter, 0)
            base += rows // HD * grid_cols
        for w in range(wide):
            piece = w * gains_dev // LANES - width // LANES
            if piece >= 0:
                for n in range(shards):
                    at = (w * shards + n) * rows_dev + gain_row
                    grads_ref[at : at + 1, :] = gg_ref[:, piece * LANES : (piece + 1) * LANES].astype(BF)


def middle(here, row_full, wire, att, tokens, cotangent, pad, gain_two, wide, rows_dev, gain_row, gains_dev):
    shards, own, span = att.shape
    width = tokens.shape[1]
    units = FF // shards
    tb = min(256, own)
    steps = own // tb
    full = lambda i, h, r: (0, 0)
    full3 = lambda i, h, r: (0, 0, 0)
    mine = lambda i, h, r: (h[0] * steps + i, 0)
    blk = lambda i, h, r: (i, 0)
    blk3 = lambda i, h, r: (0, i, 0)
    once = pl.Buffered(1)
    return pl.pallas_call(
        functools.partial(middle_kernel, shards, span, units, rows_dev, wide, gain_row, gains_dev),
        grid_spec=pltpu.PrefetchScalarGridSpec(
            num_scalar_prefetch=2,
            grid=(steps,),
            in_specs=[
                pl.BlockSpec(wire.shape, full, pipeline_mode=once),
                pl.BlockSpec((shards, tb, span), blk3),
                pl.BlockSpec((tb, width), mine),
                pl.BlockSpec((tb, width), mine),
                pl.BlockSpec((1, tb), lambda i, h, r: (0, h[0] * steps + i)),
                pl.BlockSpec((1, width), full),
            ],
            out_specs=[
                pl.BlockSpec((tb, width), blk),
                pl.BlockSpec((tb, width), blk),
                pl.BlockSpec((shards, tb, span), blk3),
                pl.BlockSpec(wire.shape, full, pipeline_mode=once),
                pl.BlockSpec((shards, width, 3 * span), full3, pipeline_mode=once),
            ],
            scratch_shapes=[
                pltpu.VMEM((shards, span, width), BF),
                pltpu.VMEM((shards, width, units), BF),
                pltpu.VMEM((shards, units, width), BF),
                pltpu.VMEM((shards, span, width), F32),
                pltpu.VMEM((shards, width, units), F32),
                pltpu.VMEM((shards, units, width), F32),
                pltpu.VMEM((1, width), F32),
            ],
        ),
        out_shape=[
            jax.ShapeDtypeStruct((own, width), BF),
            jax.ShapeDtypeStruct((own, width), F32),
            jax.ShapeDtypeStruct((shards, own, span), BF),
            jax.ShapeDtypeStruct(wire.shape, BF),
            jax.ShapeDtypeStruct((shards, width, 3 * span), BF),
        ],
        compiler_params=pltpu.CompilerParams(vmem_limit_bytes=60 << 20),
        name="middle",
    )(here, row_full, wire, att, tokens, cotangent, pad, gain_two)


def mixgrad_kernel(heads, rows_dev, wide, gain_row, gains_dev, row_ref, norm_ref, bm_ref, mix_ref, gain_ref, grads_ref, acc_ref):
    width = norm_ref.shape[1]
    half = HD // 2
    cols = 3 * heads

    @pl.when(pl.program_id(0) == 0)
    def _():
        acc_ref[...] = jnp.zeros_like(acc_ref)

    acc_ref[...] += tn(norm_ref[...], bm_ref[...])

    @pl.when(pl.program_id(0) == pl.num_programs(0) - 1)
    def _():
        grads_ref[...] = jnp.zeros_like(grads_ref)

        def scatter(r, _):
            low = pl.multiple_of(r * HD, HD)
            for c in range(cols):
                cut = slice(c * HD, (c + 1) * HD)
                value = jnp.concatenate([acc_ref[pl.ds(low, half), cut], acc_ref[pl.ds(low + half, half), cut]], axis=1)
                grads_ref[pl.ds(pl.multiple_of(row_ref[r * cols + c], 16), half), :] = value.astype(BF)
            return 0

        lax.fori_loop(0, width // HD, scatter, 0)
        along = jnp.sum(acc_ref[...] * mix_ref[...].astype(F32), axis=1, keepdims=True)
        line = jnp.broadcast_to(along, (width, LANES)).T[:1] / gain_ref[...]
        for w in range(wide):
            piece = w * gains_dev // LANES
            if piece < width // LANES:
                at = w * rows_dev + gain_row
                grads_ref[at : at + 1, :] = line[:, piece * LANES : (piece + 1) * LANES].astype(BF)


def mixgrad(row_own, normed, bm, mix, gain_one, wire_shape, wide, rows_dev, gain_row, gains_dev):
    rows, width = normed.shape
    span = bm.shape[1] // 3
    tb = min(512, rows)
    full = lambda i, r: (0, 0)
    blk = lambda i, r: (i, 0)
    return pl.pallas_call(
        functools.partial(mixgrad_kernel, span // HD, rows_dev, wide, gain_row, gains_dev),
        grid_spec=pltpu.PrefetchScalarGridSpec(
            num_scalar_prefetch=1,
            grid=(rows // tb,),
            in_specs=[
                pl.BlockSpec((tb, width), blk),
                pl.BlockSpec((tb, 3 * span), blk),
                pl.BlockSpec((width, 3 * span), full),
                pl.BlockSpec((1, width), full),
            ],
            out_specs=pl.BlockSpec(wire_shape, full),
            scratch_shapes=[pltpu.VMEM((width, 3 * span), F32)],
        ),
        out_shape=jax.ShapeDtypeStruct(wire_shape, BF),
        compiler_params=pltpu.CompilerParams(vmem_limit_bytes=60 << 20),
        name="mixgrad",
    )(row_own, normed, bm, mix, gain_one)


def tail_kernel(shards, tb, gain_row, here_ref, bm_ref, mix_ref, tok_ref, res_ref, gain_ref, part_ref, out_ref):
    back = nt(bm_ref[0], mix_ref[0])
    for n in range(1, shards):
        back += nt(bm_ref[n], mix_ref[n])
    xhat, scale = normalize(tok_ref[...].astype(F32))
    grad = res_ref[...] + norm_back(back * gain_ref[...], xhat, scale)
    at = pl.multiple_of(pl.program_id(0) * tb, tb)
    out_ref[pl.ds(at, tb), :] = grad.astype(BF)

    @pl.when(pl.program_id(0) == pl.num_programs(0) - 1)
    def _():
        out_ref[-16:, :] = jnp.zeros((16, out_ref.shape[1]), BF)
        out_ref[-16:, :LANES] = part_ref[gain_row : gain_row + 16, :]


def tail(here, bm, mix, tokens, res, gain_one, part, gain_row):
    shards, own, cols = bm.shape
    width = tokens.shape[1]
    tb = min(256, own)
    steps = own // tb
    full3 = lambda i, h: (0, 0, 0)
    return pl.pallas_call(
        functools.partial(tail_kernel, shards, tb, gain_row),
        grid_spec=pltpu.PrefetchScalarGridSpec(
            num_scalar_prefetch=1,
            grid=(steps,),
            in_specs=[
                pl.BlockSpec((shards, tb, cols), lambda i, h: (0, i, 0)),
                pl.BlockSpec(mix.shape, full3),
                pl.BlockSpec((tb, width), lambda i, h: (h[0] * steps + i, 0)),
                pl.BlockSpec((tb, width), lambda i, h: (i, 0)),
                pl.BlockSpec((1, width), lambda i, h: (0, 0)),
                pl.BlockSpec(part.shape, lambda i, h: (0, 0)),
            ],
            out_specs=pl.BlockSpec((own + 16, width), lambda i, h: (0, 0)),
        ),
        out_shape=jax.ShapeDtypeStruct((own + 16, width), BF),
        compiler_params=pltpu.CompilerParams(vmem_limit_bytes=60 << 20),
        name="tail",
    )(here, bm, mix, tokens, res, gain_one, part)


def adam_gains(grad, gain, first, second, average):
    new_first = beta_one * first + (1.0 - beta_one) * grad
    new_second = beta_two * second + (1.0 - beta_two) * grad * grad
    new_gain = gain - gain_rate * new_first / (jnp.sqrt(new_second) + step_eps)
    new_average = average_keep * average + (1.0 - average_keep) * new_gain
    return (new_gain, new_first, new_second, new_average)


def to_shards(values, shards):
    rows, cols = values.shape
    return lax.all_to_all(values.reshape(shards, rows // shards, cols), "narrow", 0, 0)


def body(
    tokens,
    cotangent,
    segment_ids,
    pad_mask,
    owner_order,
    weights,
    first_moment,
    second_moment,
    average,
    stats,
    bases,
    gains,
    gain_first,
    gain_second,
    gain_average,
):
    narrow = lax.axis_size("narrow")
    wide = lax.axis_size("wide")
    here = lax.axis_index("narrow")
    heads = HEADS // narrow
    rows, width = tokens.shape
    span = heads * HD
    own = rows // narrow
    slots, size = weights.shape[1], weights.shape[2]
    half = size // 2
    block_count = owner_order.shape[0]
    gains_dev = gains.shape[0]
    gain_row = slots * half
    rows_dev = gain_row + 16

    low = weights[0].astype(BF)
    wire = jnp.concatenate([low[:, :half], low[:, half:]], axis=2).reshape(gain_row, 2 * size)
    wire = jnp.concatenate([wire, jnp.pad(gains.astype(BF)[None], ((0, 15), (0, LANES - gains_dev)))], axis=0)
    wire_own = lax.all_gather(wire, "wide", axis=0, tiled=True)
    wire_full = lax.all_gather(lax.all_gather(wire, "narrow", axis=0, tiled=True), "wide", axis=0, tiled=True)

    ids = jnp.arange(block_count, dtype=jnp.int32)
    slot_of = jnp.sum(jnp.where(owner_order[None, :] == ids[:, None], ids[None, :], 0), axis=1)
    device, place = slot_of // slots, slot_of % slots
    row_own = device * rows_dev + place * half
    row_full = device * (narrow * rows_dev) + place * half
    here_of = jnp.full((1,), here, jnp.int32)

    gain_all = wire_own.reshape(wide, rows_dev, LANES)[:, gain_row, :gains_dev].astype(F32).reshape(1, 2 * width)
    gain_one, gain_two = gain_all[:, :width], gain_all[:, width:]
    seg = segment_ids
    seg_row = segment_ids[0]
    pad = pad_mask.astype(F32)
    block = min(512, rows)
    low_seg = seg_row[::block]
    high_seg = seg_row[block - 1 :: block]
    begin = jnp.sum((seg_row[None, :] < low_seg[:, None]).astype(jnp.int32), axis=1) // block
    end = (jnp.sum((seg_row[None, :] <= high_seg[:, None]).astype(jnp.int32), axis=1) + block - 1) // block

    normed, qe, ke, ve, vt, mix = project(wire_own, row_own, tokens, seg, pad, gain_one, heads)
    attended, qb = attend(qe, ke, vt, pad, begin, end, block, block)
    att_own = to_shards(attended, narrow)
    out_own, back_res, back_own, grads, mix_full = middle(
        here_of, row_full, wire_full, att_own, tokens, cotangent, pad, gain_two, wide, rows_dev, gain_row, gains_dev
    )
    part_a = lax.psum_scatter(grads, "wide", scatter_dimension=0, tiled=True)
    back_att = lax.all_to_all(back_own, "narrow", 0, 0).reshape(rows, span)
    out_own, back_att = lax.optimization_barrier((out_own, back_att))
    output = lax.all_to_all(jnp.broadcast_to(out_own, (narrow, own, width)), "narrow", 0, 0).reshape(rows, width)
    bm = attend_back(qb, ke, ve, back_att, attended, begin, end, block, block)
    bm_own = to_shards(bm, narrow)
    bm, part_a, output = lax.optimization_barrier((bm, part_a, output))
    part_a = lax.psum_scatter(part_a, "narrow", scatter_dimension=0, tiled=True)
    grads_mix = mixgrad(row_own, normed, bm, mix, gain_one, wire_own.shape, wide, rows_dev, gain_row, gains_dev)
    part_b = lax.psum_scatter(grads_mix, "wide", scatter_dimension=0, tiled=True)
    grad_own = tail(here_of, bm_own, mix_full, tokens, back_res, gain_one, part_b, gain_row)
    grad_all = lax.all_gather(grad_own, "narrow", axis=0, tiled=False)
    input_grad = grad_all[:, :own].reshape(rows, width).astype(F32)
    part_a, part_b, _ = lax.optimization_barrier((part_a, part_b, grad_own))
    group = 8 if slots % 8 == 0 else 1
    new_weight, new_first, new_second, new_average, new_stats, new_bases = soap(
        part_a, part_b, weights, first_moment, second_moment, average, stats, bases, group
    )
    line = part_a[gain_row].astype(F32) + jnp.sum(grad_all[:, own, :LANES].astype(F32), axis=0)
    offset = lax.axis_index("wide") * gains_dev % LANES
    own_gain = lax.dynamic_slice_in_dim(line, offset, gains_dev, 0)
    new_gains, gain_moment, gain_square, gain_mean = adam_gains(own_gain, gains, gain_first, gain_second, gain_average)
    return (
        output,
        input_grad,
        new_weight,
        new_first,
        new_second,
        new_average,
        new_stats,
        new_bases,
        new_gains,
        gain_moment,
        gain_square,
        gain_mean,
    )


def solution(mesh):
    block = P("narrow", "wide", None, None)
    pair = P("narrow", "wide", None, None, None)
    rows = P("wide", None)
    line = P("wide")
    return jax.shard_map(
        body,
        mesh=mesh,
        in_specs=(rows, rows, rows, rows, P(), block, block, block, block, pair, pair, line, line, line, line),
        out_specs=(rows, rows, block, block, block, block, pair, pair, line, line, line, line),
        check_vma=False,
    )
```

```python
import functools

import jax
import jax.numpy as jnp
from jax import lax
from jax.experimental import pallas as pl
from jax.experimental.pallas import tpu as pltpu
from jax.sharding import PartitionSpec as P

HEADS = 8
HD = 64
FF = 2048
LANES = 128
SEGS = 4
NEG = -1e30
F32 = jnp.float32
BF = jnp.bfloat16
highest = lax.Precision.HIGHEST

beta_one = 0.9
beta_two = 0.95
step_rate = 0.1
gain_rate = 0.75
weight_decay = 0.01
average_keep = 0.5
norm_eps = 1e-05
step_eps = 1e-08


def nt(a, b):
    return lax.dot_general(a, b, (((1,), (1,)), ((), ())), preferred_element_type=F32)


def nn(a, b):
    return lax.dot_general(a, b, (((1,), (0,)), ((), ())), preferred_element_type=F32)


def tn(a, b):
    return lax.dot_general(a, b, (((0,), (0,)), ((), ())), preferred_element_type=F32)


def split3(x):
    hi = x.astype(BF)
    r = x - hi.astype(F32)
    mid = r.astype(BF)
    lo = (r - mid.astype(F32)).astype(BF)
    return hi, mid, lo


def put3(base, x, lane0):
    lane = lax.broadcasted_iota(jnp.int32, base.shape, 1)
    hi, mid, lo = split3(x)
    out = jnp.where(lane == lane0, hi.astype(F32), base.astype(F32))
    out = jnp.where(lane == lane0 + 1, mid.astype(F32), out)
    out = jnp.where(lane == lane0 + 2, lo.astype(F32), out)
    return out.astype(BF)


VT = 80
QC, AHEAD, QB, BAHEAD = 512, 1, 256, 1


def fwd_kernel(heads, bq, bk, lo_ref, hi_ref, qe_ref, ke_ref, vt_ref, pad_ref, att_ref, qb_ref, m_ref, acc_ref):
    i = pl.program_id(0)
    row0 = pl.multiple_of(i * bq, bq)
    real = pad_ref[...] > 0.5
    for h in range(heads):
        qt = qe_ref[h].astype(F32).T[:HD]
        kt = ke_ref[h, pl.ds(row0, bq), :].astype(F32).T[:HD]
        own = jnp.sum(qt * kt, axis=0, keepdims=True)
        m_ref[h] = jnp.where(real, NEG, own)
        acc_ref[h] = jnp.where(real, 0.0, vt_ref[h, :, pl.ds(row0, bq)].astype(F32))

    def step(j, _):
        col0 = pl.multiple_of(j * bk, bk)
        work = [(h, slice(c, c + QC)) for c in range(0, bq, QC) for h in range(heads)]
        score = lambda h, c: nt(ke_ref[h, pl.ds(col0, bk), :], qe_ref[h, c, :])
        ss = [score(*w) for w in work[:AHEAD]]
        for n, (h, c) in enumerate(work):
            if n + AHEAD < len(work):
                ss.append(score(*work[n + AHEAD]))
            s = ss[n]
            m_old = m_ref[h, :, c]
            m_new = jnp.maximum(m_old, jnp.max(s, axis=0, keepdims=True))
            p = jnp.exp(s - m_new).astype(BF)
            alpha = jnp.exp(m_old - m_new)
            acc_ref[h, :, c] = acc_ref[h, :, c] * alpha + nn(vt_ref[h, :, pl.ds(col0, bk)], p)
            m_ref[h, :, c] = m_new
        return 0

    lax.fori_loop(lo_ref[i], hi_ref[i], step, 0)
    outs = []
    for h in range(heads):
        acc = acc_ref[h]
        total = acc[HD : HD + 1]
        outs.append(jnp.where(real, acc[:HD] / total, 0.0))
        lse = jnp.broadcast_to(m_ref[h] + jnp.log(total), (8, bq)).T[:, :1]
        qb_ref[h] = put3(qe_ref[h], -lse, HD + 4)
    att_ref[...] = (jnp.concatenate(outs, axis=0) if heads > 1 else outs[0]).T.astype(BF)


def attend(qe, ke, vt, padw, lo, hi, bq, bk):
    heads, rows, _ = qe.shape
    full = lambda i, lo, hi: (0, 0, 0)
    return pl.pallas_call(
        functools.partial(fwd_kernel, heads, bq, bk),
        grid_spec=pltpu.PrefetchScalarGridSpec(
            num_scalar_prefetch=2,
            grid=(rows // bq,),
            in_specs=[
                pl.BlockSpec((heads, bq, LANES), lambda i, lo, hi: (0, i, 0)),
                pl.BlockSpec((heads, rows, LANES), full),
                pl.BlockSpec((heads, VT, rows), full),
                pl.BlockSpec((1, bq), lambda i, lo, hi: (0, i)),
            ],
            out_specs=[
                pl.BlockSpec((bq, heads * HD), lambda i, lo, hi: (i, 0)),
                pl.BlockSpec((heads, bq, LANES), lambda i, lo, hi: (0, i, 0)),
            ],
            scratch_shapes=[
                pltpu.VMEM((heads, 1, bq), F32),
                pltpu.VMEM((heads, VT, bq), F32),
            ],
        ),
        out_shape=[
            jax.ShapeDtypeStruct((rows, heads * HD), BF),
            jax.ShapeDtypeStruct((heads, rows, LANES), BF),
        ],
        compiler_params=pltpu.CompilerParams(vmem_limit_bytes=60 << 20),
        name="attend",
    )(lo, hi, qe, ke, vt, padw)


def bwd_kernel(heads, bq, bk, lo_ref, hi_ref, qb_ref, ke_ref, ve_ref, go_ref, att_ref, out_ref, ge_ref, dqt_ref, kt_ref, qt_ref, got_ref, dkt_ref, dvt_ref):
    j = pl.program_id(0)
    rows = qb_ref.shape[1]

    @pl.when(j == 0)
    def _():
        for h in range(heads):
            dqt_ref[h] = jnp.zeros_like(dqt_ref[h])
            for c in range(rows // 512):
                sl = pl.ds(c * 512, 512)
                go = go_ref[sl, h * HD : (h + 1) * HD]
                at = att_ref[sl, h * HD : (h + 1) * HD]
                delta = jnp.sum(go.astype(F32) * at.astype(F32), axis=1, keepdims=True)
                wide = jnp.concatenate([go, jnp.zeros_like(go)], axis=1)
                ge_ref[h, sl, :] = put3(wide, -delta, HD)
                got_ref[h, :, c * 512 : (c + 1) * 512] = wide.T[:HD]
                qt_ref[h, :, c * 512 : (c + 1) * 512] = qb_ref[h, sl, :].T[:HD]

    for h in range(heads):
        kt_ref[h] = ke_ref[h].T[:HD]

    zero = jnp.zeros((HD, bk), F32)

    def step(i, carry):
        row0 = pl.multiple_of(i * bq, bq)
        work = [(h, pl.ds(row0 + c, QB)) for c in range(0, bq, QB) for h in range(heads)]
        score = lambda h, c: (nt(ke_ref[h], qb_ref[h, c, :]), nt(ve_ref[h], ge_ref[h, c, :]))
        ss = [score(*w) for w in work[:BAHEAD]]
        for n, (h, c) in enumerate(work):
            if n + BAHEAD < len(work):
                ss.append(score(*work[n + BAHEAD]))
            st, dt = ss[n]
            p = jnp.exp(st)
            ds = (p * dt).astype(BF)
            pb = p.astype(BF)
            dvt_ref[h] += nt(got_ref[h, :, c], pb)
            dkt_ref[h] += nt(qt_ref[h, :, c], ds)
            dqt_ref[h, :, c] += nn(kt_ref[h], ds)
        return 0

    for h in range(heads):
        dkt_ref[h] = zero
        dvt_ref[h] = zero
    lax.fori_loop(lo_ref[j], hi_ref[j], step, 0)
    for h in range(heads):
        for part, ref in ((1, dkt_ref), (2, dvt_ref)):
            at = (part * heads + h) * HD
            out_ref[pl.ds(pl.multiple_of(j * bk, bk), bk), at : at + HD] = ref[h].T.astype(BF)

    @pl.when(j == pl.num_programs(0) - 1)
    def _():
        for h in range(heads):
            for c in range(rows // 512):
                sl = pl.ds(c * 512, 512)
                out_ref[sl, h * HD : (h + 1) * HD] = (dqt_ref[h, :, c * 512 : (c + 1) * 512].T * (HD ** -0.5)).astype(BF)


def attend_back(qb, ke, ve, go, att, lo, hi, bq, bk):
    heads, rows, _ = qb.shape
    full3 = lambda i, lo, hi: (0, 0, 0)
    full2 = lambda i, lo, hi: (0, 0)
    blk3 = lambda i, lo, hi: (0, i, 0)
    wide = heads * HD
    return pl.pallas_call(
        functools.partial(bwd_kernel, heads, bq, bk),
        grid_spec=pltpu.PrefetchScalarGridSpec(
            num_scalar_prefetch=2,
            grid=(rows // bk,),
            in_specs=[
                pl.BlockSpec((heads, rows, LANES), full3),
                pl.BlockSpec((heads, bk, LANES), blk3),
                pl.BlockSpec((heads, bk, LANES), blk3),
                pl.BlockSpec((rows, wide), full2),
                pl.BlockSpec((rows, wide), full2),
            ],
            out_specs=pl.BlockSpec((rows, 3 * wide), full2),
            scratch_shapes=[
                pltpu.VMEM((heads, rows, LANES), BF),
                pltpu.VMEM((heads, HD, rows), F32),
                pltpu.VMEM((heads, HD, bk), BF),
                pltpu.VMEM((heads, HD, rows), BF),
                pltpu.VMEM((heads, HD, rows), BF),
                pltpu.VMEM((heads, HD, bk), F32),
                pltpu.VMEM((heads, HD, bk), F32),
            ],
        ),
        out_shape=jax.ShapeDtypeStruct((rows, 3 * wide), BF),
        compiler_params=pltpu.CompilerParams(vmem_limit_bytes=60 << 20),
        name="attend_back",
    )(lo, hi, qb, ke, ve, go, att)


def dot_f32(a, b, dims):
    return lax.dot_general(a, b, ((dims[:1], dims[1:]), ((), ())), precision=highest, preferred_element_type=F32)


def soap_kernel(group, ga_ref, gb_ref, w_ref, m1_ref, m2_ref, av_ref, st_ref, ba_ref,
                nw_ref, n1_ref, n2_ref, na_ref, ns_ref, nb_ref, aug_ref):
    size = w_ref.shape[-1]
    half = size // 2
    panel = 8
    every = range(group)
    grads, firsts = [], []
    for s in every:
        wire = ga_ref[s * half : (s + 1) * half, :].astype(F32) + gb_ref[s * half : (s + 1) * half, :].astype(F32)
        grads.append(jnp.concatenate([wire[:, :size], wire[:, size:]], axis=0))
        firsts.append(beta_one * m1_ref[0, s] + (1.0 - beta_one) * grads[s])
        n1_ref[0, s] = firsts[s]
    sides = [(s, side) for s in every for side in range(2)]
    outers = [dot_f32(grads[s], grads[s], (1, 1) if side == 0 else (0, 0)) for s, side in sides]
    both = [dot_f32(jnp.concatenate([grads[s], firsts[s]], axis=0), ba_ref[0, s, 1], (1, 0)) for s in every]
    stats = []
    for (s, side), outer in zip(sides, outers):
        stats.append(beta_two * st_ref[0, s, side] + (1.0 - beta_two) * outer)
        ns_ref[0, s, side] = stats[-1]
    pairs = [dot_f32(ba_ref[0, s, 0], jnp.concatenate([both[s][:size], both[s][size:]], axis=1), (0, 0)) for s in every]
    mts = [dot_f32(ba_ref[0, s, side], stat, (0, 1)) for (s, side), stat in zip(sides, stats)]
    scaled = []
    for s in every:
        rotated, moment = pairs[s][:, :size], pairs[s][:, size:]
        second = beta_two * m2_ref[0, s] + (1.0 - beta_two) * rotated * rotated
        n2_ref[0, s] = second
        scaled.append(moment / (jnp.sqrt(second) + step_eps))
    grams = [dot_f32(mt, mt, (1, 1)) for mt in mts]
    inner = [dot_f32(scaled[s], ba_ref[0, s, 1], (1, 1)) for s in every]
    for m, (gram, mt) in enumerate(zip(grams, mts)):
        aug_ref[m] = jnp.concatenate([gram, mt], axis=1)
    directions = [dot_f32(ba_ref[0, s, 0], inner[s], (1, 0)) for s in every]
    for s in every:
        weight = w_ref[0, s]
        fresh = weight - step_rate * (directions[s] + weight_decay * weight)
        nw_ref[0, s] = fresh
        na_ref[0, s] = average_keep * av_ref[0, s] + (1.0 - average_keep) * fresh
    count = 2 * group
    row = lax.broadcasted_iota(jnp.int32, (count, panel, LANES), 1)
    for p in range(size // panel):
        top = p * panel
        part = aug_ref[:, top : top + panel, :]
        for r in range(panel):
            pivot = lax.rsqrt(part[:, r : r + 1, top + r : top + r + 1])
            lead = part[:, r : r + 1, :] * pivot
            column = jnp.where(row > r, part[:, :, top + r : top + r + 1] * pivot, 0.0)
            part = jnp.where(row == r, lead, part - column * lead)
        aug_ref[:, top : top + panel, :] = part
        below = top + panel
        if below < size:
            high = part.astype(BF).astype(F32)
            rest = part - high
            mid = rest.astype(BF).astype(F32)
            low = rest - mid
            first = jnp.concatenate([high, high, mid, high, mid, low], axis=1).astype(BF)
            other = jnp.concatenate([high, mid, high, low, mid, high], axis=1).astype(BF)
            for m in range(count):
                aug_ref[m, below:, :] -= lax.dot_general(
                    first[m][:, below:size], other[m], (((0,), (0,)), ((), ())), preferred_element_type=F32
                )
    for s in range(group):
        for side in range(2):
            nb_ref[0, s, side] = aug_ref[2 * s + side][:, size:].T


def soap(ga, gb, weights, first, second, average, stats, bases, group):
    _, slots, size, _ = weights.shape
    wire = pl.BlockSpec((group * size // 2, LANES), lambda i: (i, 0))
    four = pl.BlockSpec((1, group, size, size), lambda i: (0, i, 0, 0))
    five = pl.BlockSpec((1, group, 2, size, size), lambda i: (0, i, 0, 0, 0))
    like = lambda a: jax.ShapeDtypeStruct(a.shape, a.dtype)
    return pl.pallas_call(
        functools.partial(soap_kernel, group),
        grid=(slots // group,),
        in_specs=[wire, wire, four, four, four, four, five, five],
        out_specs=[four, four, four, four, five, five],
        out_shape=[like(a) for a in (weights, first, second, average, stats, bases)],
        scratch_shapes=[pltpu.VMEM((2 * group, size, LANES), F32)],
        compiler_params=pltpu.CompilerParams(vmem_limit_bytes=60 << 20),
        name="soap",
    )(ga, gb, weights, first, second, average, stats, bases)


def normalize(values):
    center = jnp.mean(values, axis=-1, keepdims=True)
    centered = values - center
    variance = jnp.mean(centered * centered, axis=-1, keepdims=True)
    scale = lax.rsqrt(variance + norm_eps)
    return centered * scale, scale


def norm_back(grad, xhat, scale):
    along = jnp.mean(grad * xhat, axis=-1, keepdims=True)
    return (grad - jnp.mean(grad, axis=-1, keepdims=True) - xhat * along) * scale


TAIL = 0.305
TAIL_FIT = (
    0.1216397411342051,
    0.12246669816059132,
    0.10342157025713879,
    0.1210193967312446,
    -0.037972477455618554,
    0.18571204369074895,
    -0.15298537812807472,
    0.036698452375741396,
)


def gelu_pair(u):
    size = jnp.abs(u)
    bell = jnp.exp(-0.5 * u * u)
    t = 1.0 / (1.0 + TAIL * size)
    poly = jnp.full_like(t, TAIL_FIT[-1])
    for c in TAIL_FIT[-2::-1]:
        poly = poly * t + c
    upper = poly * t * bell
    cdf = jnp.where(u > 0.0, 1.0 - upper, upper)
    return u * cdf, cdf + (0.3989422804014327 * u) * bell


def block_rows(ref, start, half):
    return ref[pl.ds(pl.multiple_of(start, 16), half), :]


def project_kernel(heads, rows_dev, gains_at, row_ref, wire_ref, tok_ref, seg_ref, pad_ref, gain_ref,
                   norm_ref, qe_ref, ke_ref, ve_ref, vt_ref, mix_ref, wide_ref):
    width = tok_ref.shape[1]
    half = HD // 2
    cols = 3 * heads

    @pl.when(pl.program_id(0) == 0)
    def _():
        zero = jnp.zeros((half, HD), BF)

        def fill(r, _):
            low = pl.multiple_of(r * HD, HD)
            for c in range(cols):
                t = block_rows(wire_ref, row_ref[r * cols + c], half)
                for part in range(2):
                    piece = t[:, part * HD : (part + 1) * HD]
                    at = pl.ds(low + part * half, half)
                    wide_ref[at, c * LANES : (c + 1) * LANES] = jnp.concatenate([piece, zero], axis=1)
                    mix_ref[at, c * HD : (c + 1) * HD] = piece
            return 0

        lax.fori_loop(0, width // HD, fill, 0)

    xhat, _ = normalize(tok_ref[...].astype(F32))
    normed = (xhat * gain_ref[...]).astype(BF)
    norm_ref[...] = normed
    count = tok_ref.shape[0]
    lane = lax.broadcasted_iota(jnp.int32, (LANES, count), 0)
    seg = seg_ref[...]
    same = lane - HD == seg
    in_segs = (lane >= HD) & (lane < HD + SEGS)
    ones = (lane >= HD + SEGS) & (lane < HD + SEGS + 3)
    ext_q = jnp.where(same, 1.0, 0.0).T
    ext_k = jnp.where(in_segs, jnp.where(same & (pad_ref[...] > 0.5), 0.0, NEG), jnp.where(ones, 1.0, 0.0)).T
    ext_v = jnp.where((lane >= HD) & (lane < HD + 3), 1.0, 0.0).T
    for h in range(heads):
        for ref, part, scale, ext in ((qe_ref, 0, HD ** -0.5, ext_q), (ke_ref, 1, 1.0, ext_k), (ve_ref, 2, 1.0, ext_v)):
            c = part * heads + h
            mixed = nn(normed, wide_ref[:, c * LANES : (c + 1) * LANES]).astype(BF)
            out = (mixed.astype(F32) * scale + ext).astype(BF)
            ref[h] = out
            if part == 2:
                vt_ref[h] = out.T[:VT]


def project(wire, row_own, tokens, seg, pad, gain_one, heads):
    rows, width = tokens.shape
    tb = min(512, rows)
    full = lambda i, r: (0, 0)
    blk = lambda i, r: (i, 0)
    col = lambda i, r: (0, i)
    ext = lambda i, r: (0, i, 0)
    out = lambda *s: jax.ShapeDtypeStruct(s, BF)
    return pl.pallas_call(
        functools.partial(project_kernel, heads, 0, 0),
        grid_spec=pltpu.PrefetchScalarGridSpec(
            num_scalar_prefetch=1,
            grid=(rows // tb,),
            in_specs=[
                pl.BlockSpec(wire.shape, full),
                pl.BlockSpec((tb, width), blk),
                pl.BlockSpec((1, tb), col),
                pl.BlockSpec((1, tb), col),
                pl.BlockSpec((1, width), full),
            ],
            out_specs=[
                pl.BlockSpec((tb, width), blk),
                pl.BlockSpec((heads, tb, LANES), ext),
                pl.BlockSpec((heads, tb, LANES), ext),
                pl.BlockSpec((heads, tb, LANES), ext),
                pl.BlockSpec((heads, VT, tb), lambda i, r: (0, 0, i)),
                pl.BlockSpec((width, 3 * heads * HD), full),
            ],
            scratch_shapes=[pltpu.VMEM((width, 3 * heads * LANES), BF)],
        ),
        out_shape=[
            out(rows, width),
            out(heads, rows, LANES),
            out(heads, rows, LANES),
            out(heads, rows, LANES),
            out(heads, VT, rows),
            out(width, 3 * heads * HD),
        ],
        compiler_params=pltpu.CompilerParams(vmem_limit_bytes=60 << 20),
        name="project",
    )(row_own, wire, tokens, seg, pad, gain_one)


def middle_kernel(shards, span, units, rows_dev, wide, gain_row, gains_dev,
                  here_ref, row_ref, wire_ref, att_ref, tok_ref, cot_ref, pad_ref, gain_ref,
                  out_ref, res_ref, back_ref, grads_ref, mix_ref,
                  wo_ref, wu_ref, wd_ref, go_ref, gu_ref, gd_ref, gg_ref):
    width = tok_ref.shape[1]
    half = HD // 2
    kinds = (
        (mix_ref, None, width, 3 * span),
        (wo_ref, go_ref, span, width),
        (wu_ref, gu_ref, width, units),
        (wd_ref, gd_ref, units, width),
    )

    @pl.when(pl.program_id(0) == 0)
    def _():
        base = 0
        for ref, acc, rows, cols in kinds:
            grid_cols = cols // HD

            def fill(r, _, ref=ref, base=base, grid_cols=grid_cols):
                low = pl.multiple_of(r * HD, HD)
                for n in range(shards):
                    for c in range(grid_cols):
                        t = block_rows(wire_ref, row_ref[base + r * grid_cols + c] + n * rows_dev, half)
                        for part in range(2):
                            ref[n, pl.ds(low + part * half, half), c * HD : (c + 1) * HD] = t[:, part * HD : (part + 1) * HD]
                return 0

            lax.fori_loop(0, rows // HD, fill, 0)
            base += rows // HD * grid_cols
            if acc is not None:
                acc[...] = jnp.zeros_like(acc)
        gg_ref[...] = jnp.zeros_like(gg_ref)

    tokens = tok_ref[...].astype(F32)
    cot = cot_ref[...]
    branch = nn(att_ref[0], wo_ref[0])
    for n in range(1, shards):
        branch += nn(att_ref[n], wo_ref[n])
    residual = tokens + branch
    xhat, scale = normalize(residual)
    gain = gain_ref[...]
    normed = (xhat * gain).astype(BF)
    mlp = jnp.zeros_like(residual)
    back = jnp.zeros_like(residual)
    for n in range(shards):
        value, slope = gelu_pair(nn(normed, wu_ref[n]))
        active = value.astype(BF)
        mlp += nn(active, wd_ref[n])
        gd_ref[n] += tn(active, cot)
        back_up = (slope * nt(cot, wd_ref[n])).astype(BF)
        gu_ref[n] += tn(normed, back_up)
        back += nt(back_up, wu_ref[n])
    out_ref[...] = (residual + mlp).astype(BF)
    gg_ref[...] += jnp.sum(back * xhat, axis=0, keepdims=True)
    back_res = cot.astype(F32) + norm_back(back * gain, xhat, scale)
    res_ref[...] = back_res
    branch_low = back_res.astype(BF)
    pad = jnp.broadcast_to(pad_ref[...], (8, pad_ref.shape[1])).T[:, :1]
    for n in range(shards):
        go_ref[n] += tn(att_ref[n], branch_low)
        back_ref[n] = (nt(branch_low, wo_ref[n]) * pad).astype(BF)

    @pl.when(pl.program_id(0) == pl.num_programs(0) - 1)
    def _():
        grads_ref[...] = jnp.zeros_like(grads_ref)
        base = 0
        for ref, acc, rows, cols in kinds:
            grid_cols = cols // HD
            if acc is not None:

                def scatter(r, _, acc=acc, base=base, grid_cols=grid_cols):
                    low = pl.multiple_of(r * HD, HD)
                    for n in range(shards):
                        for c in range(grid_cols):
                            at = row_ref[base + r * grid_cols + c] + n * rows_dev
                            cut = slice(c * HD, (c + 1) * HD)
                            value = jnp.concatenate([acc[n, pl.ds(low, half), cut], acc[n, pl.ds(low + half, half), cut]], axis=1)
                            grads_ref[pl.ds(pl.multiple_of(at, 16), half), :] = value.astype(BF)
                    return 0

                lax.fori_loop(0, rows // HD, scatter, 0)
            base += rows // HD * grid_cols
        for w in range(wide):
            piece = w * gains_dev // LANES - width // LANES
            if piece >= 0:
                for n in range(shards):
                    at = (w * shards + n) * rows_dev + gain_row
                    grads_ref[at : at + 1, :] = gg_ref[:, piece * LANES : (piece + 1) * LANES].astype(BF)


def middle(here, row_full, wire, att, tokens, cotangent, pad, gain_two, wide, rows_dev, gain_row, gains_dev):
    shards, own, span = att.shape
    width = tokens.shape[1]
    units = FF // shards
    tb = min(256, own)
    steps = own // tb
    full = lambda i, h, r: (0, 0)
    full3 = lambda i, h, r: (0, 0, 0)
    mine = lambda i, h, r: (h[0] * steps + i, 0)
    blk = lambda i, h, r: (i, 0)
    blk3 = lambda i, h, r: (0, i, 0)
    once = pl.Buffered(1)
    return pl.pallas_call(
        functools.partial(middle_kernel, shards, span, units, rows_dev, wide, gain_row, gains_dev),
        grid_spec=pltpu.PrefetchScalarGridSpec(
            num_scalar_prefetch=2,
            grid=(steps,),
            in_specs=[
                pl.BlockSpec(wire.shape, full, pipeline_mode=once),
                pl.BlockSpec((shards, tb, span), blk3),
                pl.BlockSpec((tb, width), mine),
                pl.BlockSpec((tb, width), mine),
                pl.BlockSpec((1, tb), lambda i, h, r: (0, h[0] * steps + i)),
                pl.BlockSpec((1, width), full),
            ],
            out_specs=[
                pl.BlockSpec((tb, width), blk),
                pl.BlockSpec((tb, width), blk),
                pl.BlockSpec((shards, tb, span), blk3),
                pl.BlockSpec(wire.shape, full, pipeline_mode=once),
                pl.BlockSpec((shards, width, 3 * span), full3, pipeline_mode=once),
            ],
            scratch_shapes=[
                pltpu.VMEM((shards, span, width), BF),
                pltpu.VMEM((shards, width, units), BF),
                pltpu.VMEM((shards, units, width), BF),
                pltpu.VMEM((shards, span, width), F32),
                pltpu.VMEM((shards, width, units), F32),
                pltpu.VMEM((shards, units, width), F32),
                pltpu.VMEM((1, width), F32),
            ],
        ),
        out_shape=[
            jax.ShapeDtypeStruct((own, width), BF),
            jax.ShapeDtypeStruct((own, width), F32),
            jax.ShapeDtypeStruct((shards, own, span), BF),
            jax.ShapeDtypeStruct(wire.shape, BF),
            jax.ShapeDtypeStruct((shards, width, 3 * span), BF),
        ],
        compiler_params=pltpu.CompilerParams(vmem_limit_bytes=60 << 20),
        name="middle",
    )(here, row_full, wire, att, tokens, cotangent, pad, gain_two)


def mixgrad_kernel(heads, rows_dev, wide, gain_row, gains_dev, row_ref, norm_ref, bm_ref, mix_ref, gain_ref, grads_ref, acc_ref):
    width = norm_ref.shape[1]
    half = HD // 2
    cols = 3 * heads

    @pl.when(pl.program_id(0) == 0)
    def _():
        acc_ref[...] = jnp.zeros_like(acc_ref)

    acc_ref[...] += tn(norm_ref[...], bm_ref[...])

    @pl.when(pl.program_id(0) == pl.num_programs(0) - 1)
    def _():
        grads_ref[...] = jnp.zeros_like(grads_ref)

        def scatter(r, _):
            low = pl.multiple_of(r * HD, HD)
            for c in range(cols):
                cut = slice(c * HD, (c + 1) * HD)
                value = jnp.concatenate([acc_ref[pl.ds(low, half), cut], acc_ref[pl.ds(low + half, half), cut]], axis=1)
                grads_ref[pl.ds(pl.multiple_of(row_ref[r * cols + c], 16), half), :] = value.astype(BF)
            return 0

        lax.fori_loop(0, width // HD, scatter, 0)
        along = jnp.sum(acc_ref[...] * mix_ref[...].astype(F32), axis=1, keepdims=True)
        line = jnp.broadcast_to(along, (width, LANES)).T[:1] / gain_ref[...]
        for w in range(wide):
            piece = w * gains_dev // LANES
            if piece < width // LANES:
                at = w * rows_dev + gain_row
                grads_ref[at : at + 1, :] = line[:, piece * LANES : (piece + 1) * LANES].astype(BF)


def mixgrad(row_own, normed, bm, mix, gain_one, wire_shape, wide, rows_dev, gain_row, gains_dev):
    rows, width = normed.shape
    span = bm.shape[1] // 3
    tb = min(512, rows)
    full = lambda i, r: (0, 0)
    blk = lambda i, r: (i, 0)
    return pl.pallas_call(
        functools.partial(mixgrad_kernel, span // HD, rows_dev, wide, gain_row, gains_dev),
        grid_spec=pltpu.PrefetchScalarGridSpec(
            num_scalar_prefetch=1,
            grid=(rows // tb,),
            in_specs=[
                pl.BlockSpec((tb, width), blk),
                pl.BlockSpec((tb, 3 * span), blk),
                pl.BlockSpec((width, 3 * span), full),
                pl.BlockSpec((1, width), full),
            ],
            out_specs=pl.BlockSpec(wire_shape, full),
            scratch_shapes=[pltpu.VMEM((width, 3 * span), F32)],
        ),
        out_shape=jax.ShapeDtypeStruct(wire_shape, BF),
        compiler_params=pltpu.CompilerParams(vmem_limit_bytes=60 << 20),
        name="mixgrad",
    )(row_own, normed, bm, mix, gain_one)


def tail_kernel(shards, tb, gain_row, here_ref, bm_ref, mix_ref, tok_ref, res_ref, gain_ref, part_ref, out_ref):
    back = nt(bm_ref[0], mix_ref[0])
    for n in range(1, shards):
        back += nt(bm_ref[n], mix_ref[n])
    xhat, scale = normalize(tok_ref[...].astype(F32))
    grad = res_ref[...] + norm_back(back * gain_ref[...], xhat, scale)
    at = pl.multiple_of(pl.program_id(0) * tb, tb)
    out_ref[pl.ds(at, tb), :] = grad.astype(BF)

    @pl.when(pl.program_id(0) == pl.num_programs(0) - 1)
    def _():
        out_ref[-16:, :] = jnp.zeros((16, out_ref.shape[1]), BF)
        out_ref[-16:, :LANES] = part_ref[gain_row : gain_row + 16, :]


def tail(here, bm, mix, tokens, res, gain_one, part, gain_row):
    shards, own, cols = bm.shape
    width = tokens.shape[1]
    tb = min(256, own)
    steps = own // tb
    full3 = lambda i, h: (0, 0, 0)
    return pl.pallas_call(
        functools.partial(tail_kernel, shards, tb, gain_row),
        grid_spec=pltpu.PrefetchScalarGridSpec(
            num_scalar_prefetch=1,
            grid=(steps,),
            in_specs=[
                pl.BlockSpec((shards, tb, cols), lambda i, h: (0, i, 0)),
                pl.BlockSpec(mix.shape, full3),
                pl.BlockSpec((tb, width), lambda i, h: (h[0] * steps + i, 0)),
                pl.BlockSpec((tb, width), lambda i, h: (i, 0)),
                pl.BlockSpec((1, width), lambda i, h: (0, 0)),
                pl.BlockSpec(part.shape, lambda i, h: (0, 0)),
            ],
            out_specs=pl.BlockSpec((own + 16, width), lambda i, h: (0, 0)),
        ),
        out_shape=jax.ShapeDtypeStruct((own + 16, width), BF),
        compiler_params=pltpu.CompilerParams(vmem_limit_bytes=60 << 20),
        name="tail",
    )(here, bm, mix, tokens, res, gain_one, part)


def adam_gains(grad, gain, first, second, average):
    new_first = beta_one * first + (1.0 - beta_one) * grad
    new_second = beta_two * second + (1.0 - beta_two) * grad * grad
    new_gain = gain - gain_rate * new_first / (jnp.sqrt(new_second) + step_eps)
    new_average = average_keep * average + (1.0 - average_keep) * new_gain
    return (new_gain, new_first, new_second, new_average)


def to_shards(values, shards):
    rows, cols = values.shape
    return lax.all_to_all(values.reshape(shards, rows // shards, cols), "narrow", 0, 0)


def spread(values, shards, own):
    cut = own // 2
    first = lax.all_gather(jnp.concatenate([values[:cut], values[own:]], axis=0), "narrow", axis=0, tiled=False)
    rest = lax.all_to_all(jnp.broadcast_to(values[cut:own], (shards, own - cut, values.shape[1])), "narrow", 0, 0)
    return jnp.concatenate([first[:, :cut], rest, first[:, cut:]], axis=1)


def body(
    tokens,
    cotangent,
    segment_ids,
    pad_mask,
    owner_order,
    weights,
    first_moment,
    second_moment,
    average,
    stats,
    bases,
    gains,
    gain_first,
    gain_second,
    gain_average,
):
    narrow = lax.axis_size("narrow")
    wide = lax.axis_size("wide")
    here = lax.axis_index("narrow")
    heads = HEADS // narrow
    rows, width = tokens.shape
    span = heads * HD
    own = rows // narrow
    slots, size = weights.shape[1], weights.shape[2]
    half = size // 2
    block_count = owner_order.shape[0]
    gains_dev = gains.shape[0]
    gain_row = slots * half
    rows_dev = gain_row + 16

    low = weights[0].astype(BF)
    wire = jnp.concatenate([low[:, :half], low[:, half:]], axis=2).reshape(gain_row, 2 * size)
    wire = jnp.concatenate([wire, jnp.pad(gains.astype(BF)[None], ((0, 15), (0, LANES - gains_dev)))], axis=0)
    wire_own = lax.all_gather(wire, "wide", axis=0, tiled=True)
    wire_full = lax.all_gather(lax.all_gather(wire, "narrow", axis=0, tiled=True), "wide", axis=0, tiled=True)

    ids = jnp.arange(block_count, dtype=jnp.int32)
    slot_of = jnp.sum(jnp.where(owner_order[None, :] == ids[:, None], ids[None, :], 0), axis=1)
    device, place = slot_of // slots, slot_of % slots
    row_own = device * rows_dev + place * half
    row_full = device * (narrow * rows_dev) + place * half
    here_of = jnp.full((1,), here, jnp.int32)

    gain_all = wire_own.reshape(wide, rows_dev, LANES)[:, gain_row, :gains_dev].astype(F32).reshape(1, 2 * width)
    gain_one, gain_two = gain_all[:, :width], gain_all[:, width:]
    seg = segment_ids
    seg_row = segment_ids[0]
    pad = pad_mask.astype(F32)
    block = min(512, rows)
    low_seg = seg_row[::block]
    high_seg = seg_row[block - 1 :: block]
    begin = jnp.sum((seg_row[None, :] < low_seg[:, None]).astype(jnp.int32), axis=1) // block
    end = (jnp.sum((seg_row[None, :] <= high_seg[:, None]).astype(jnp.int32), axis=1) + block - 1) // block

    normed, qe, ke, ve, vt, mix = project(wire_own, row_own, tokens, seg, pad, gain_one, heads)
    attended, qb = attend(qe, ke, vt, pad, begin, end, block, block)
    att_own = to_shards(attended, narrow)
    out_own, back_res, back_own, grads, mix_full = middle(
        here_of, row_full, wire_full, att_own, tokens, cotangent, pad, gain_two, wide, rows_dev, gain_row, gains_dev
    )
    part_a = lax.psum_scatter(grads, "wide", scatter_dimension=0, tiled=True)
    back_att = lax.all_to_all(back_own, "narrow", 0, 0).reshape(rows, span)
    out_own, back_att = lax.optimization_barrier((out_own, back_att))
    output = spread(out_own, narrow, own).reshape(rows, width)
    bm = attend_back(qb, ke, ve, back_att, attended, begin, end, block, block)
    bm_own = to_shards(bm, narrow)
    bm, part_a, output = lax.optimization_barrier((bm, part_a, output))
    part_a = lax.psum_scatter(part_a, "narrow", scatter_dimension=0, tiled=True)
    grads_mix = mixgrad(row_own, normed, bm, mix, gain_one, wire_own.shape, wide, rows_dev, gain_row, gains_dev)
    part_b = lax.psum_scatter(grads_mix, "wide", scatter_dimension=0, tiled=True)
    grad_own = tail(here_of, bm_own, mix_full, tokens, back_res, gain_one, part_b, gain_row)
    grad_all = spread(grad_own, narrow, own)
    input_grad = grad_all[:, :own].reshape(rows, width).astype(F32)
    part_a, part_b, _ = lax.optimization_barrier((part_a, part_b, grad_own))
    group = next(g for g in range(min(12, slots), 0, -1) if slots % g == 0)
    new_weight, new_first, new_second, new_average, new_stats, new_bases = soap(
        part_a, part_b, weights, first_moment, second_moment, average, stats, bases, group
    )
    line = part_a[gain_row].astype(F32) + jnp.sum(grad_all[:, own, :LANES].astype(F32), axis=0)
    offset = lax.axis_index("wide") * gains_dev % LANES
    own_gain = lax.dynamic_slice_in_dim(line, offset, gains_dev, 0)
    new_gains, gain_moment, gain_square, gain_mean = adam_gains(own_gain, gains, gain_first, gain_second, gain_average)
    return (
        output,
        input_grad,
        new_weight,
        new_first,
        new_second,
        new_average,
        new_stats,
        new_bases,
        new_gains,
        gain_moment,
        gain_square,
        gain_mean,
    )


def solution(mesh):
    block = P("narrow", "wide", None, None)
    pair = P("narrow", "wide", None, None, None)
    rows = P("wide", None)
    line = P("wide")
    return jax.shard_map(
        body,
        mesh=mesh,
        in_specs=(rows, rows, rows, rows, P(), block, block, block, block, pair, pair, line, line, line, line),
        out_specs=(rows, rows, block, block, block, block, pair, pair, line, line, line, line),
        check_vma=False,
    )
```

```python
import functools

import jax
import jax.numpy as jnp
from jax import lax
from jax.experimental import pallas as pl
from jax.experimental.pallas import tpu as pltpu
from jax.sharding import PartitionSpec as P

HEADS = 8
HD = 64
FF = 2048
LANES = 128
SEGS = 4
NEG = -1e30
F32 = jnp.float32
BF = jnp.bfloat16
highest = lax.Precision.HIGHEST

beta_one = 0.9
beta_two = 0.95
step_rate = 0.1
gain_rate = 0.75
weight_decay = 0.01
average_keep = 0.5
norm_eps = 1e-05
step_eps = 1e-08


def nt(a, b):
    return lax.dot_general(a, b, (((1,), (1,)), ((), ())), preferred_element_type=F32)


def nn(a, b):
    return lax.dot_general(a, b, (((1,), (0,)), ((), ())), preferred_element_type=F32)


def tn(a, b):
    return lax.dot_general(a, b, (((0,), (0,)), ((), ())), preferred_element_type=F32)


def split3(x):
    hi = x.astype(BF)
    r = x - hi.astype(F32)
    mid = r.astype(BF)
    lo = (r - mid.astype(F32)).astype(BF)
    return hi, mid, lo


def put3(base, x, lane0):
    lane = lax.broadcasted_iota(jnp.int32, base.shape, 1)
    hi, mid, lo = split3(x)
    out = jnp.where(lane == lane0, hi.astype(F32), base.astype(F32))
    out = jnp.where(lane == lane0 + 1, mid.astype(F32), out)
    out = jnp.where(lane == lane0 + 2, lo.astype(F32), out)
    return out.astype(BF)


VT = 80
QC, AHEAD, QB, BAHEAD = 512, 1, 256, 1


def fwd_kernel(heads, bq, bk, lo_ref, hi_ref, qe_ref, ke_ref, vt_ref, pad_ref, att_ref, qb_ref, m_ref, acc_ref):
    i = pl.program_id(0)
    row0 = pl.multiple_of(i * bq, bq)
    real = pad_ref[...] > 0.5
    for h in range(heads):
        qt = qe_ref[h].astype(F32).T[:HD]
        kt = ke_ref[h, pl.ds(row0, bq), :].astype(F32).T[:HD]
        own = jnp.sum(qt * kt, axis=0, keepdims=True)
        m_ref[h] = jnp.where(real, NEG, own)
        acc_ref[h] = jnp.where(real, 0.0, vt_ref[h, :, pl.ds(row0, bq)].astype(F32))

    def step(j, _):
        col0 = pl.multiple_of(j * bk, bk)
        work = [(h, slice(c, c + QC)) for c in range(0, bq, QC) for h in range(heads)]
        score = lambda h, c: nt(ke_ref[h, pl.ds(col0, bk), :], qe_ref[h, c, :])
        ss = [score(*w) for w in work[:AHEAD]]
        for n, (h, c) in enumerate(work):
            if n + AHEAD < len(work):
                ss.append(score(*work[n + AHEAD]))
            s = ss[n]
            m_old = m_ref[h, :, c]
            m_new = jnp.maximum(m_old, jnp.max(s, axis=0, keepdims=True))
            p = jnp.exp(s - m_new).astype(BF)
            alpha = jnp.exp(m_old - m_new)
            acc_ref[h, :, c] = acc_ref[h, :, c] * alpha + nn(vt_ref[h, :, pl.ds(col0, bk)], p)
            m_ref[h, :, c] = m_new
        return 0

    lax.fori_loop(lo_ref[i], hi_ref[i], step, 0)
    outs = []
    for h in range(heads):
        acc = acc_ref[h]
        total = acc[HD : HD + 1]
        outs.append(jnp.where(real, acc[:HD] / total, 0.0))
        lse = jnp.broadcast_to(m_ref[h] + jnp.log(total), (8, bq)).T[:, :1]
        qb_ref[h] = put3(qe_ref[h], -lse, HD + 4)
    att_ref[...] = (jnp.concatenate(outs, axis=0) if heads > 1 else outs[0]).T.astype(BF)


def attend(qe, ke, vt, padw, lo, hi, bq, bk):
    heads, rows, _ = qe.shape
    full = lambda i, lo, hi: (0, 0, 0)
    return pl.pallas_call(
        functools.partial(fwd_kernel, heads, bq, bk),
        grid_spec=pltpu.PrefetchScalarGridSpec(
            num_scalar_prefetch=2,
            grid=(rows // bq,),
            in_specs=[
                pl.BlockSpec((heads, bq, LANES), lambda i, lo, hi: (0, i, 0)),
                pl.BlockSpec((heads, rows, LANES), full),
                pl.BlockSpec((heads, VT, rows), full),
                pl.BlockSpec((1, bq), lambda i, lo, hi: (0, i)),
            ],
            out_specs=[
                pl.BlockSpec((bq, heads * HD), lambda i, lo, hi: (i, 0)),
                pl.BlockSpec((heads, bq, LANES), lambda i, lo, hi: (0, i, 0)),
            ],
            scratch_shapes=[
                pltpu.VMEM((heads, 1, bq), F32),
                pltpu.VMEM((heads, VT, bq), F32),
            ],
        ),
        out_shape=[
            jax.ShapeDtypeStruct((rows, heads * HD), BF),
            jax.ShapeDtypeStruct((heads, rows, LANES), BF),
        ],
        compiler_params=pltpu.CompilerParams(vmem_limit_bytes=60 << 20),
        name="attend",
    )(lo, hi, qe, ke, vt, padw)


def bwd_kernel(heads, bq, bk, lo_ref, hi_ref, qb_ref, ke_ref, ve_ref, go_ref, att_ref, out_ref, ge_ref, dqt_ref, kt_ref, qt_ref, got_ref, dkt_ref, dvt_ref):
    j = pl.program_id(0)
    rows = qb_ref.shape[1]

    @pl.when(j == 0)
    def _():
        for h in range(heads):
            dqt_ref[h] = jnp.zeros_like(dqt_ref[h])
            for c in range(rows // 512):
                sl = pl.ds(c * 512, 512)
                go = go_ref[sl, h * HD : (h + 1) * HD]
                at = att_ref[sl, h * HD : (h + 1) * HD]
                delta = jnp.sum(go.astype(F32) * at.astype(F32), axis=1, keepdims=True)
                wide = jnp.concatenate([go, jnp.zeros_like(go)], axis=1)
                ge_ref[h, sl, :] = put3(wide, -delta, HD)
                got_ref[h, :, c * 512 : (c + 1) * 512] = wide.T[:HD]
                qt_ref[h, :, c * 512 : (c + 1) * 512] = qb_ref[h, sl, :].T[:HD]

    for h in range(heads):
        kt_ref[h] = ke_ref[h].T[:HD]

    zero = jnp.zeros((HD, bk), F32)

    def step(i, carry):
        row0 = pl.multiple_of(i * bq, bq)
        work = [(h, pl.ds(row0 + c, QB)) for c in range(0, bq, QB) for h in range(heads)]
        score = lambda h, c: (nt(ke_ref[h], qb_ref[h, c, :]), nt(ve_ref[h], ge_ref[h, c, :]))
        ss = [score(*w) for w in work[:BAHEAD]]
        for n, (h, c) in enumerate(work):
            if n + BAHEAD < len(work):
                ss.append(score(*work[n + BAHEAD]))
            st, dt = ss[n]
            p = jnp.exp(st)
            ds = (p * dt).astype(BF)
            pb = p.astype(BF)
            dvt_ref[h] += nt(got_ref[h, :, c], pb)
            dkt_ref[h] += nt(qt_ref[h, :, c], ds)
            dqt_ref[h, :, c] += nn(kt_ref[h], ds)
        return 0

    for h in range(heads):
        dkt_ref[h] = zero
        dvt_ref[h] = zero
    lax.fori_loop(lo_ref[j], hi_ref[j], step, 0)
    for h in range(heads):
        for part, ref in ((1, dkt_ref), (2, dvt_ref)):
            at = (part * heads + h) * HD
            out_ref[pl.ds(pl.multiple_of(j * bk, bk), bk), at : at + HD] = ref[h].T.astype(BF)

    @pl.when(j == pl.num_programs(0) - 1)
    def _():
        for h in range(heads):
            for c in range(rows // 512):
                sl = pl.ds(c * 512, 512)
                out_ref[sl, h * HD : (h + 1) * HD] = (dqt_ref[h, :, c * 512 : (c + 1) * 512].T * (HD ** -0.5)).astype(BF)


def attend_back(qb, ke, ve, go, att, lo, hi, bq, bk):
    heads, rows, _ = qb.shape
    full3 = lambda i, lo, hi: (0, 0, 0)
    full2 = lambda i, lo, hi: (0, 0)
    blk3 = lambda i, lo, hi: (0, i, 0)
    wide = heads * HD
    return pl.pallas_call(
        functools.partial(bwd_kernel, heads, bq, bk),
        grid_spec=pltpu.PrefetchScalarGridSpec(
            num_scalar_prefetch=2,
            grid=(rows // bk,),
            in_specs=[
                pl.BlockSpec((heads, rows, LANES), full3),
                pl.BlockSpec((heads, bk, LANES), blk3),
                pl.BlockSpec((heads, bk, LANES), blk3),
                pl.BlockSpec((rows, wide), full2),
                pl.BlockSpec((rows, wide), full2),
            ],
            out_specs=pl.BlockSpec((rows, 3 * wide), full2),
            scratch_shapes=[
                pltpu.VMEM((heads, rows, LANES), BF),
                pltpu.VMEM((heads, HD, rows), F32),
                pltpu.VMEM((heads, HD, bk), BF),
                pltpu.VMEM((heads, HD, rows), BF),
                pltpu.VMEM((heads, HD, rows), BF),
                pltpu.VMEM((heads, HD, bk), F32),
                pltpu.VMEM((heads, HD, bk), F32),
            ],
        ),
        out_shape=jax.ShapeDtypeStruct((rows, 3 * wide), BF),
        compiler_params=pltpu.CompilerParams(vmem_limit_bytes=60 << 20),
        name="attend_back",
    )(lo, hi, qb, ke, ve, go, att)


def dot_f32(a, b, dims):
    return lax.dot_general(a, b, ((dims[:1], dims[1:]), ((), ())), precision=highest, preferred_element_type=F32)


def soap_kernel(group, ga_ref, gb_ref, w_ref, m1_ref, m2_ref, av_ref, st_ref, ba_ref,
                nw_ref, n1_ref, n2_ref, na_ref, ns_ref, nb_ref, aug_ref):
    size = w_ref.shape[-1]
    half = size // 2
    panel = 8
    every = range(group)
    grads, firsts = [], []
    for s in every:
        wire = ga_ref[s * half : (s + 1) * half, :].astype(F32) + gb_ref[s * half : (s + 1) * half, :].astype(F32)
        grads.append(jnp.concatenate([wire[:, :size], wire[:, size:]], axis=0))
        firsts.append(beta_one * m1_ref[0, s] + (1.0 - beta_one) * grads[s])
        n1_ref[0, s] = firsts[s]
    sides = [(s, side) for s in every for side in range(2)]
    outers = [dot_f32(grads[s], grads[s], (1, 1) if side == 0 else (0, 0)) for s, side in sides]
    both = [dot_f32(jnp.concatenate([grads[s], firsts[s]], axis=0), ba_ref[0, s, 1], (1, 0)) for s in every]
    stats = []
    for (s, side), outer in zip(sides, outers):
        stats.append(beta_two * st_ref[0, s, side] + (1.0 - beta_two) * outer)
        ns_ref[0, s, side] = stats[-1]
    pairs = [dot_f32(ba_ref[0, s, 0], jnp.concatenate([both[s][:size], both[s][size:]], axis=1), (0, 0)) for s in every]
    mts = [dot_f32(ba_ref[0, s, side], stat, (0, 1)) for (s, side), stat in zip(sides, stats)]
    scaled = []
    for s in every:
        rotated, moment = pairs[s][:, :size], pairs[s][:, size:]
        second = beta_two * m2_ref[0, s] + (1.0 - beta_two) * rotated * rotated
        n2_ref[0, s] = second
        scaled.append(moment / (jnp.sqrt(second) + step_eps))
    grams = [dot_f32(mt, mt, (1, 1)) for mt in mts]
    inner = [dot_f32(scaled[s], ba_ref[0, s, 1], (1, 1)) for s in every]
    for m, (gram, mt) in enumerate(zip(grams, mts)):
        aug_ref[m] = jnp.concatenate([gram, mt], axis=1)
    directions = [dot_f32(ba_ref[0, s, 0], inner[s], (1, 0)) for s in every]
    for s in every:
        weight = w_ref[0, s]
        fresh = weight - step_rate * (directions[s] + weight_decay * weight)
        nw_ref[0, s] = fresh
        na_ref[0, s] = average_keep * av_ref[0, s] + (1.0 - average_keep) * fresh
    count = 2 * group
    row = lax.broadcasted_iota(jnp.int32, (count, panel, LANES), 1)
    for p in range(size // panel):
        top = p * panel
        part = aug_ref[:, top : top + panel, :]
        for r in range(panel):
            pivot = lax.rsqrt(part[:, r : r + 1, top + r : top + r + 1])
            lead = part[:, r : r + 1, :] * pivot
            column = jnp.where(row > r, part[:, :, top + r : top + r + 1] * pivot, 0.0)
            part = jnp.where(row == r, lead, part - column * lead)
        aug_ref[:, top : top + panel, :] = part
        below = top + panel
        if below < size:
            high = part.astype(BF).astype(F32)
            rest = part - high
            mid = rest.astype(BF).astype(F32)
            low = rest - mid
            first = jnp.concatenate([high, high, mid, high, mid, low], axis=1).astype(BF)
            other = jnp.concatenate([high, mid, high, low, mid, high], axis=1).astype(BF)
            for m in range(count):
                aug_ref[m, below:, :] -= lax.dot_general(
                    first[m][:, below:size], other[m], (((0,), (0,)), ((), ())), preferred_element_type=F32
                )
    for s in range(group):
        for side in range(2):
            nb_ref[0, s, side] = aug_ref[2 * s + side][:, size:].T


def soap(ga, gb, weights, first, second, average, stats, bases, group):
    _, slots, size, _ = weights.shape
    wire = pl.BlockSpec((group * size // 2, LANES), lambda i: (i, 0))
    four = pl.BlockSpec((1, group, size, size), lambda i: (0, i, 0, 0))
    five = pl.BlockSpec((1, group, 2, size, size), lambda i: (0, i, 0, 0, 0))
    like = lambda a: jax.ShapeDtypeStruct(a.shape, a.dtype)
    return pl.pallas_call(
        functools.partial(soap_kernel, group),
        grid=(slots // group,),
        in_specs=[wire, wire, four, four, four, four, five, five],
        out_specs=[four, four, four, four, five, five],
        out_shape=[like(a) for a in (weights, first, second, average, stats, bases)],
        scratch_shapes=[pltpu.VMEM((2 * group, size, LANES), F32)],
        compiler_params=pltpu.CompilerParams(vmem_limit_bytes=60 << 20),
        name="soap",
    )(ga, gb, weights, first, second, average, stats, bases)


MESH = pl.DeviceIdType.MESH


def normalize(values):
    center = jnp.mean(values, axis=-1, keepdims=True)
    centered = values - center
    variance = jnp.mean(centered * centered, axis=-1, keepdims=True)
    scale = lax.rsqrt(variance + norm_eps)
    return centered * scale, scale


def norm_back(grad, xhat, scale):
    along = jnp.mean(grad * xhat, axis=-1, keepdims=True)
    return (grad - jnp.mean(grad, axis=-1, keepdims=True) - xhat * along) * scale


TAIL = 0.305
TAIL_FIT = (
    0.1216397411342051,
    0.12246669816059132,
    0.10342157025713879,
    0.1210193967312446,
    -0.037972477455618554,
    0.18571204369074895,
    -0.15298537812807472,
    0.036698452375741396,
)


def gelu_pair(u):
    size = jnp.abs(u)
    bell = jnp.exp(-0.5 * u * u)
    t = 1.0 / (1.0 + TAIL * size)
    poly = jnp.full_like(t, TAIL_FIT[-1])
    for c in TAIL_FIT[-2::-1]:
        poly = poly * t + c
    upper = poly * t * bell
    cdf = jnp.where(u > 0.0, 1.0 - upper, upper)
    return u * cdf, cdf + (0.3989422804014327 * u) * bell


def block_rows(ref, start, half):
    return ref[pl.ds(pl.multiple_of(start, 16), half), :]


def project_kernel(heads, rows_dev, gains_at, row_ref, wire_ref, tok_ref, seg_ref, pad_ref, gain_ref,
                   norm_ref, qe_ref, ke_ref, ve_ref, vt_ref, mix_ref, wide_ref):
    width = tok_ref.shape[1]
    half = HD // 2
    cols = 3 * heads

    @pl.when(pl.program_id(0) == 0)
    def _():
        zero = jnp.zeros((half, HD), BF)

        def fill(r, _):
            low = pl.multiple_of(r * HD, HD)
            for c in range(cols):
                t = block_rows(wire_ref, row_ref[r * cols + c], half)
                for part in range(2):
                    piece = t[:, part * HD : (part + 1) * HD]
                    at = pl.ds(low + part * half, half)
                    wide_ref[at, c * LANES : (c + 1) * LANES] = jnp.concatenate([piece, zero], axis=1)
                    mix_ref[at, c * HD : (c + 1) * HD] = piece
            return 0

        lax.fori_loop(0, width // HD, fill, 0)

    xhat, _ = normalize(tok_ref[...].astype(F32))
    normed = (xhat * gain_ref[...]).astype(BF)
    norm_ref[...] = normed
    count = tok_ref.shape[0]
    lane = lax.broadcasted_iota(jnp.int32, (LANES, count), 0)
    seg = seg_ref[...]
    same = lane - HD == seg
    in_segs = (lane >= HD) & (lane < HD + SEGS)
    ones = (lane >= HD + SEGS) & (lane < HD + SEGS + 3)
    ext_q = jnp.where(same, 1.0, 0.0).T
    ext_k = jnp.where(in_segs, jnp.where(same & (pad_ref[...] > 0.5), 0.0, NEG), jnp.where(ones, 1.0, 0.0)).T
    ext_v = jnp.where((lane >= HD) & (lane < HD + 3), 1.0, 0.0).T
    for h in range(heads):
        for ref, part, scale, ext in ((qe_ref, 0, HD ** -0.5, ext_q), (ke_ref, 1, 1.0, ext_k), (ve_ref, 2, 1.0, ext_v)):
            c = part * heads + h
            mixed = nn(normed, wide_ref[:, c * LANES : (c + 1) * LANES]).astype(BF)
            out = (mixed.astype(F32) * scale + ext).astype(BF)
            ref[h] = out
            if part == 2:
                vt_ref[h] = out.T[:VT]


def project(wire, row_own, tokens, seg, pad, gain_one, heads):
    rows, width = tokens.shape
    tb = min(512, rows)
    full = lambda i, r: (0, 0)
    blk = lambda i, r: (i, 0)
    col = lambda i, r: (0, i)
    ext = lambda i, r: (0, i, 0)
    out = lambda *s: jax.ShapeDtypeStruct(s, BF)
    return pl.pallas_call(
        functools.partial(project_kernel, heads, 0, 0),
        grid_spec=pltpu.PrefetchScalarGridSpec(
            num_scalar_prefetch=1,
            grid=(rows // tb,),
            in_specs=[
                pl.BlockSpec(wire.shape, full),
                pl.BlockSpec((tb, width), blk),
                pl.BlockSpec((1, tb), col),
                pl.BlockSpec((1, tb), col),
                pl.BlockSpec((1, width), full),
            ],
            out_specs=[
                pl.BlockSpec((tb, width), blk),
                pl.BlockSpec((heads, tb, LANES), ext),
                pl.BlockSpec((heads, tb, LANES), ext),
                pl.BlockSpec((heads, tb, LANES), ext),
                pl.BlockSpec((heads, VT, tb), lambda i, r: (0, 0, i)),
                pl.BlockSpec((width, 3 * heads * HD), full),
            ],
            scratch_shapes=[pltpu.VMEM((width, 3 * heads * LANES), BF)],
        ),
        out_shape=[
            out(rows, width),
            out(heads, rows, LANES),
            out(heads, rows, LANES),
            out(heads, rows, LANES),
            out(heads, VT, rows),
            out(width, 3 * heads * HD),
        ],
        compiler_params=pltpu.CompilerParams(vmem_limit_bytes=60 << 20),
        name="project",
    )(row_own, wire, tokens, seg, pad, gain_one)


def middle_kernel(shards, span, units, rows_dev, wide, gain_row, gains_dev,
                  here_ref, row_ref, wire_ref, att_ref, tok_ref, cot_ref, pad_ref, gain_ref,
                  out_ref, res_ref, back_ref, grads_ref, mix_ref,
                  wo_ref, wu_ref, wd_ref, go_ref, gu_ref, gd_ref, gg_ref):
    width = tok_ref.shape[1]
    half = HD // 2
    kinds = (
        (mix_ref, None, width, 3 * span),
        (wo_ref, go_ref, span, width),
        (wu_ref, gu_ref, width, units),
        (wd_ref, gd_ref, units, width),
    )

    @pl.when(pl.program_id(0) == 0)
    def _():
        base = 0
        for ref, acc, rows, cols in kinds:
            grid_cols = cols // HD

            def fill(r, _, ref=ref, base=base, grid_cols=grid_cols):
                low = pl.multiple_of(r * HD, HD)
                for n in range(shards):
                    for c in range(grid_cols):
                        t = block_rows(wire_ref, row_ref[base + r * grid_cols + c] + n * rows_dev, half)
                        for part in range(2):
                            ref[n, pl.ds(low + part * half, half), c * HD : (c + 1) * HD] = t[:, part * HD : (part + 1) * HD]
                return 0

            lax.fori_loop(0, rows // HD, fill, 0)
            base += rows // HD * grid_cols
            if acc is not None:
                acc[...] = jnp.zeros_like(acc)
        gg_ref[...] = jnp.zeros_like(gg_ref)

    tokens = tok_ref[...].astype(F32)
    cot = cot_ref[...]
    branch = nn(att_ref[0], wo_ref[0])
    for n in range(1, shards):
        branch += nn(att_ref[n], wo_ref[n])
    residual = tokens + branch
    xhat, scale = normalize(residual)
    gain = gain_ref[...]
    normed = (xhat * gain).astype(BF)
    mlp = jnp.zeros_like(residual)
    back = jnp.zeros_like(residual)
    for n in range(shards):
        value, slope = gelu_pair(nn(normed, wu_ref[n]))
        active = value.astype(BF)
        mlp += nn(active, wd_ref[n])
        gd_ref[n] += tn(active, cot)
        back_up = (slope * nt(cot, wd_ref[n])).astype(BF)
        gu_ref[n] += tn(normed, back_up)
        back += nt(back_up, wu_ref[n])
    out_ref[...] = (residual + mlp).astype(BF)
    gg_ref[...] += jnp.sum(back * xhat, axis=0, keepdims=True)
    back_res = cot.astype(F32) + norm_back(back * gain, xhat, scale)
    res_ref[...] = back_res
    branch_low = back_res.astype(BF)
    pad = jnp.broadcast_to(pad_ref[...], (8, pad_ref.shape[1])).T[:, :1]
    for n in range(shards):
        go_ref[n] += tn(att_ref[n], branch_low)
        back_ref[n] = (nt(branch_low, wo_ref[n]) * pad).astype(BF)

    @pl.when(pl.program_id(0) == pl.num_programs(0) - 1)
    def _():
        grads_ref[...] = jnp.zeros_like(grads_ref)
        base = 0
        for ref, acc, rows, cols in kinds:
            grid_cols = cols // HD
            if acc is not None:

                def scatter(r, _, acc=acc, base=base, grid_cols=grid_cols):
                    low = pl.multiple_of(r * HD, HD)
                    for n in range(shards):
                        for c in range(grid_cols):
                            at = row_ref[base + r * grid_cols + c] + n * rows_dev
                            cut = slice(c * HD, (c + 1) * HD)
                            value = jnp.concatenate([acc[n, pl.ds(low, half), cut], acc[n, pl.ds(low + half, half), cut]], axis=1)
                            grads_ref[pl.ds(pl.multiple_of(at, 16), half), :] = value.astype(BF)
                    return 0

                lax.fori_loop(0, rows // HD, scatter, 0)
            base += rows // HD * grid_cols
        for w in range(wide):
            piece = w * gains_dev // LANES - width // LANES
            if piece >= 0:
                for n in range(shards):
                    at = (w * shards + n) * rows_dev + gain_row
                    grads_ref[at : at + 1, :] = gg_ref[:, piece * LANES : (piece + 1) * LANES].astype(BF)


def middle(here, row_full, wire, att, tokens, cotangent, pad, gain_two, wide, rows_dev, gain_row, gains_dev):
    shards, own, span = att.shape
    width = tokens.shape[1]
    units = FF // shards
    tb = min(256, own)
    steps = own // tb
    full = lambda i, h, r: (0, 0)
    full3 = lambda i, h, r: (0, 0, 0)
    mine = lambda i, h, r: (h[0] * steps + i, 0)
    blk = lambda i, h, r: (i, 0)
    blk3 = lambda i, h, r: (0, i, 0)
    once = pl.Buffered(1)
    return pl.pallas_call(
        functools.partial(middle_kernel, shards, span, units, rows_dev, wide, gain_row, gains_dev),
        grid_spec=pltpu.PrefetchScalarGridSpec(
            num_scalar_prefetch=2,
            grid=(steps,),
            in_specs=[
                pl.BlockSpec(wire.shape, full, pipeline_mode=once),
                pl.BlockSpec((shards, tb, span), blk3),
                pl.BlockSpec((tb, width), mine),
                pl.BlockSpec((tb, width), mine),
                pl.BlockSpec((1, tb), lambda i, h, r: (0, h[0] * steps + i)),
                pl.BlockSpec((1, width), full),
            ],
            out_specs=[
                pl.BlockSpec((tb, width), blk),
                pl.BlockSpec((tb, width), blk),
                pl.BlockSpec((shards, tb, span), blk3),
                pl.BlockSpec(wire.shape, full, pipeline_mode=once),
                pl.BlockSpec((shards, width, 3 * span), full3, pipeline_mode=once),
            ],
            scratch_shapes=[
                pltpu.VMEM((shards, span, width), BF),
                pltpu.VMEM((shards, width, units), BF),
                pltpu.VMEM((shards, units, width), BF),
                pltpu.VMEM((shards, span, width), F32),
                pltpu.VMEM((shards, width, units), F32),
                pltpu.VMEM((shards, units, width), F32),
                pltpu.VMEM((1, width), F32),
            ],
        ),
        out_shape=[
            jax.ShapeDtypeStruct((own, width), BF),
            jax.ShapeDtypeStruct((own, width), F32),
            jax.ShapeDtypeStruct((shards, own, span), BF),
            jax.ShapeDtypeStruct(wire.shape, BF),
            jax.ShapeDtypeStruct((shards, width, 3 * span), BF),
        ],
        compiler_params=pltpu.CompilerParams(vmem_limit_bytes=60 << 20),
        name="middle",
    )(here, row_full, wire, att, tokens, cotangent, pad, gain_two)


def finish_kernel(shards, wide, gain_row, gains_dev, sel_ref, mix_ref, full_ref, gain_ref, res_ref, bm_ref, norm_ref, tok_ref,
                  out_ref, part_ref, own_ref, normed_ref, tokens_ref, got_ref, acc_ref, blk_ref, grads_ref, sums_ref,
                  local_sem, send_z, recv_z, send_w, recv_w):
    width = norm_ref.shape[1]
    rows, cols = bm_ref.shape
    own = rows // shards
    hold = own // 2
    half = HD // 2
    grid_cols = cols // HD
    blocks = width // HD * grid_cols
    slots = gain_row // half
    z = lax.axis_index("narrow")
    w = lax.axis_index("wide")

    barrier = pltpu.get_barrier_semaphore()
    for d in range(1, shards):
        pl.semaphore_signal(barrier, inc=1, device_id={"narrow": lax.rem(z + d, shards)}, device_id_type=MESH)
    for d in range(1, wide):
        pl.semaphore_signal(barrier, inc=1, device_id={"wide": lax.rem(w + d, wide)}, device_id_type=MESH)
    pl.semaphore_wait(barrier, shards + wide - 2)

    def to_peer(d, part, mine):
        peer = lax.rem(z + d, shards)
        slot = z if mine else peer
        at = pl.multiple_of(peer * own + part * hold, hold)
        return pltpu.make_async_remote_copy(
            src_ref=bm_ref.at[pl.ds(at, hold), :],
            dst_ref=got_ref.at[slot, pl.ds(part * hold, hold), :],
            send_sem=send_z.at[d - 1, part],
            recv_sem=recv_z.at[slot, part],
            device_id={"narrow": peer},
            device_id_type=MESH,
        )

    def to_owner(d, mine):
        peer = lax.rem(w + d, wide)
        slot = w if mine else peer
        return pltpu.make_async_remote_copy(
            src_ref=grads_ref.at[peer],
            dst_ref=sums_ref.at[slot],
            send_sem=send_w.at[d - 1],
            recv_sem=recv_w.at[slot],
            device_id={"wide": peer},
            device_id_type=MESH,
        )

    for part in range(2):
        for d in range(1, shards):
            to_peer(d, part, True).start()
    mine = pl.ds(pl.multiple_of(z * own, own), own)
    copies = [
        pltpu.make_async_copy(bm_ref, own_ref, local_sem.at[0]),
        pltpu.make_async_copy(norm_ref, normed_ref, local_sem.at[1]),
        pltpu.make_async_copy(tok_ref.at[mine, :], tokens_ref, local_sem.at[2]),
        pltpu.make_async_copy(bm_ref.at[mine, :], got_ref.at[z], local_sem.at[3]),
    ]
    for copy in copies:
        copy.start()
    for copy in copies:
        copy.wait()

    acc_ref[...] = jnp.zeros_like(acc_ref)
    tb = min(512, rows)

    def add(i, _):
        at = pl.ds(pl.multiple_of(i * tb, tb), tb)
        acc_ref[...] += tn(normed_ref[at, :], own_ref[at, :])
        return 0

    lax.fori_loop(0, rows // tb, add, 0)
    blk_ref[blocks] = jnp.zeros((half, LANES), BF)

    def cut(r, _):
        low = pl.multiple_of(r * HD, HD)
        for c in range(grid_cols):
            lanes = slice(c * HD, (c + 1) * HD)
            value = jnp.concatenate([acc_ref[pl.ds(low, half), lanes], acc_ref[pl.ds(low + half, half), lanes]], axis=1)
            blk_ref[r * grid_cols + c] = value.astype(BF)
        return 0

    lax.fori_loop(0, width // HD, cut, 0)
    along = jnp.sum(acc_ref[...] * mix_ref[...].astype(F32), axis=1, keepdims=True)
    line = jnp.broadcast_to(along, (width, LANES)).T[:16] / gain_ref[...]
    top = lax.broadcasted_iota(jnp.int32, (16, LANES), 0) == 0
    for v in range(wide):

        def place(i, _, v=v):
            grads_ref[v, pl.ds(pl.multiple_of(i * half, half), half), :] = blk_ref[sel_ref[v * slots + i]]
            return 0

        lax.fori_loop(0, slots, place, 0)
        piece = v * gains_dev // LANES
        if piece < width // LANES:
            value = jnp.where(top, line[:, piece * LANES : (piece + 1) * LANES], 0.0).astype(BF)
        else:
            value = jnp.zeros((16, LANES), BF)
        grads_ref[v, gain_row : gain_row + 16, :] = value
    for d in range(1, wide):
        to_owner(d, True).start()
    part_ref[...] = grads_ref[w].astype(F32)

    tile = min(256, hold)

    def norm_rows(i, _):
        at = pl.ds(pl.multiple_of(i * tile, tile), tile)
        back = nt(got_ref[0, at, :], full_ref[0])
        for n in range(1, shards):
            back += nt(got_ref[n, at, :], full_ref[n])
        xhat, scale = normalize(tokens_ref[at, :].astype(F32))
        out_ref[at, :] = (res_ref[at, :] + norm_back(back * gain_ref[...], xhat, scale)).astype(BF)
        return 0

    for part in range(2):
        for d in range(1, shards):
            to_peer(d, part, False).wait_recv()
        lax.fori_loop(part * hold // tile, (part + 1) * hold // tile, norm_rows, 0)
    for d in range(1, wide):
        to_owner(d, False).wait_recv()
    for d in range(1, wide):
        part_ref[...] += sums_ref[lax.rem(w + d, wide)].astype(F32)
    out_ref[own:, :] = jnp.zeros((16, width), BF)
    out_ref[own:, :LANES] = part_ref[gain_row : gain_row + 16, :].astype(BF)
    for part in range(2):
        for d in range(1, shards):
            to_peer(d, part, True).wait_send()
    for d in range(1, wide):
        to_owner(d, True).wait_send()


def finish(sel, mix, mix_full, gain_one, res, bm, normed, tokens, wide, rows_dev, gain_row, gains_dev):
    shards = mix_full.shape[0]
    rows, cols = bm.shape
    width = normed.shape[1]
    own = rows // shards
    half = HD // 2
    blocks = width // HD * (cols // HD)
    vmem = pl.BlockSpec(memory_space=pltpu.VMEM)
    smem = pl.BlockSpec(memory_space=pltpu.SMEM)
    hbm = pl.BlockSpec(memory_space=pl.ANY)
    dma = pltpu.SemaphoreType.DMA
    return pl.pallas_call(
        functools.partial(finish_kernel, shards, wide, gain_row, gains_dev),
        in_specs=[smem, vmem, vmem, vmem, vmem, hbm, hbm, hbm],
        out_specs=[vmem, vmem],
        out_shape=[jax.ShapeDtypeStruct((own + 16, width), BF), jax.ShapeDtypeStruct((rows_dev, LANES), F32)],
        scratch_shapes=[
            pltpu.VMEM((rows, cols), BF),
            pltpu.VMEM((rows, width), BF),
            pltpu.VMEM((own, width), BF),
            pltpu.VMEM((shards, own, cols), BF),
            pltpu.VMEM((width, cols), F32),
            pltpu.VMEM((blocks + 1, half, LANES), BF),
            pltpu.VMEM((wide, rows_dev, LANES), BF),
            pltpu.VMEM((wide, rows_dev, LANES), BF),
            dma((4,)),
            dma((shards - 1, 2)),
            dma((shards, 2)),
            dma((wide - 1,)),
            dma((wide,)),
        ],
        compiler_params=pltpu.CompilerParams(vmem_limit_bytes=60 << 20, collective_id=1, has_side_effects=True),
        name="finish",
    )(sel, mix, mix_full, gain_one, res, bm, normed, tokens)


def adam_gains(grad, gain, first, second, average):
    new_first = beta_one * first + (1.0 - beta_one) * grad
    new_second = beta_two * second + (1.0 - beta_two) * grad * grad
    new_gain = gain - gain_rate * new_first / (jnp.sqrt(new_second) + step_eps)
    new_average = average_keep * average + (1.0 - average_keep) * new_gain
    return (new_gain, new_first, new_second, new_average)


def to_shards(values, shards):
    rows, cols = values.shape
    return lax.all_to_all(values.reshape(shards, rows // shards, cols), "narrow", 0, 0)


def spread(values, shards, own):
    cut = own // 2
    first = lax.all_gather(jnp.concatenate([values[:cut], values[own:]], axis=0), "narrow", axis=0, tiled=False)
    rest = lax.all_to_all(jnp.broadcast_to(values[cut:own], (shards, own - cut, values.shape[1])), "narrow", 0, 0)
    return jnp.concatenate([first[:, :cut], rest, first[:, cut:]], axis=1)


def body(
    tokens,
    cotangent,
    segment_ids,
    pad_mask,
    owner_order,
    weights,
    first_moment,
    second_moment,
    average,
    stats,
    bases,
    gains,
    gain_first,
    gain_second,
    gain_average,
):
    narrow = lax.axis_size("narrow")
    wide = lax.axis_size("wide")
    here = lax.axis_index("narrow")
    heads = HEADS // narrow
    rows, width = tokens.shape
    span = heads * HD
    own = rows // narrow
    slots, size = weights.shape[1], weights.shape[2]
    half = size // 2
    block_count = owner_order.shape[0]
    gains_dev = gains.shape[0]
    gain_row = slots * half
    rows_dev = gain_row + 16

    low = weights[0].astype(BF)
    wire = jnp.concatenate([low[:, :half], low[:, half:]], axis=2).reshape(gain_row, 2 * size)
    wire = jnp.concatenate([wire, jnp.pad(gains.astype(BF)[None], ((0, 15), (0, LANES - gains_dev)))], axis=0)
    wire_own = lax.all_gather(wire, "wide", axis=0, tiled=True)
    wire_full = lax.all_gather(lax.all_gather(wire, "narrow", axis=0, tiled=True), "wide", axis=0, tiled=True)

    ids = jnp.arange(block_count, dtype=jnp.int32)
    slot_of = jnp.sum(jnp.where(owner_order[None, :] == ids[:, None], ids[None, :], 0), axis=1)
    device, place = slot_of // slots, slot_of % slots
    row_own = device * rows_dev + place * half
    row_full = device * (narrow * rows_dev) + place * half
    here_of = jnp.full((1,), here, jnp.int32)

    gain_all = wire_own.reshape(wide, rows_dev, LANES)[:, gain_row, :gains_dev].astype(F32).reshape(1, 2 * width)
    gain_one, gain_two = gain_all[:, :width], gain_all[:, width:]
    seg = segment_ids
    seg_row = segment_ids[0]
    pad = pad_mask.astype(F32)
    block = min(512, rows)
    low_seg = seg_row[::block]
    high_seg = seg_row[block - 1 :: block]
    begin = jnp.sum((seg_row[None, :] < low_seg[:, None]).astype(jnp.int32), axis=1) // block
    end = (jnp.sum((seg_row[None, :] <= high_seg[:, None]).astype(jnp.int32), axis=1) + block - 1) // block

    normed, qe, ke, ve, vt, mix = project(wire_own, row_own, tokens, seg, pad, gain_one, heads)
    attended, qb = attend(qe, ke, vt, pad, begin, end, block, block)
    att_own = to_shards(attended, narrow)
    out_own, back_res, back_own, grads, mix_full = middle(
        here_of, row_full, wire_full, att_own, tokens, cotangent, pad, gain_two, wide, rows_dev, gain_row, gains_dev
    )
    part_a = lax.psum_scatter(grads, "wide", scatter_dimension=0, tiled=True)
    back_att = lax.all_to_all(back_own, "narrow", 0, 0).reshape(rows, span)
    out_own, back_att = lax.optimization_barrier((out_own, back_att))
    output = lax.all_to_all(jnp.broadcast_to(out_own, (narrow, own, width)), "narrow", 0, 0).reshape(rows, width)
    bm = attend_back(qb, ke, ve, back_att, attended, begin, end, block, block)
    bm, part_a, output = lax.optimization_barrier((bm, part_a, output))
    part_a = lax.psum_scatter(part_a, "narrow", scatter_dimension=0, tiled=True)
    sel = jnp.minimum(owner_order, width // size * 3 * heads)
    grad_own, part_b = finish(
        sel, mix, mix_full, gain_one, back_res, bm, normed, tokens, wide, rows_dev, gain_row, gains_dev
    )
    grad_all = spread(grad_own, narrow, own)
    input_grad = grad_all[:, :own].reshape(rows, width).astype(F32)
    group = next(g for g in range(min(12, slots), 0, -1) if slots % g == 0)
    new_weight, new_first, new_second, new_average, new_stats, new_bases = soap(
        part_a, part_b, weights, first_moment, second_moment, average, stats, bases, group
    )
    line = part_a[gain_row].astype(F32) + jnp.sum(grad_all[:, own, :LANES].astype(F32), axis=0)
    offset = lax.axis_index("wide") * gains_dev % LANES
    own_gain = lax.dynamic_slice_in_dim(line, offset, gains_dev, 0)
    new_gains, gain_moment, gain_square, gain_mean = adam_gains(own_gain, gains, gain_first, gain_second, gain_average)
    return (
        output,
        input_grad,
        new_weight,
        new_first,
        new_second,
        new_average,
        new_stats,
        new_bases,
        new_gains,
        gain_moment,
        gain_square,
        gain_mean,
    )


def solution(mesh):
    block = P("narrow", "wide", None, None)
    pair = P("narrow", "wide", None, None, None)
    rows = P("wide", None)
    line = P("wide")
    return jax.shard_map(
        body,
        mesh=mesh,
        in_specs=(rows, rows, rows, rows, P(), block, block, block, block, pair, pair, line, line, line, line),
        out_specs=(rows, rows, block, block, block, block, pair, pair, line, line, line, line),
        check_vma=False,
    )
```

```python
import functools

import jax
import jax.numpy as jnp
from jax import lax
from jax.experimental import pallas as pl
from jax.experimental.pallas import tpu as pltpu
from jax.sharding import PartitionSpec as P

HEADS = 8
HD = 64
FF = 2048
LANES = 128
SEGS = 4
NEG = -1e30
F32 = jnp.float32
BF = jnp.bfloat16
highest = lax.Precision.HIGHEST

beta_one = 0.9
beta_two = 0.95
step_rate = 0.1
gain_rate = 0.75
weight_decay = 0.01
average_keep = 0.5
norm_eps = 1e-05
step_eps = 1e-08


def nt(a, b):
    return lax.dot_general(a, b, (((1,), (1,)), ((), ())), preferred_element_type=F32)


def nn(a, b):
    return lax.dot_general(a, b, (((1,), (0,)), ((), ())), preferred_element_type=F32)


def tn(a, b):
    return lax.dot_general(a, b, (((0,), (0,)), ((), ())), preferred_element_type=F32)


def split3(x):
    hi = x.astype(BF)
    r = x - hi.astype(F32)
    mid = r.astype(BF)
    lo = (r - mid.astype(F32)).astype(BF)
    return hi, mid, lo


def put3(base, x, lane0):
    lane = lax.broadcasted_iota(jnp.int32, base.shape, 1)
    hi, mid, lo = split3(x)
    out = jnp.where(lane == lane0, hi.astype(F32), base.astype(F32))
    out = jnp.where(lane == lane0 + 1, mid.astype(F32), out)
    out = jnp.where(lane == lane0 + 2, lo.astype(F32), out)
    return out.astype(BF)


VT = 80
QC, AHEAD, QB, BAHEAD = 512, 1, 256, 1


def fwd_kernel(heads, bq, bk, lo_ref, hi_ref, qe_ref, ke_ref, vt_ref, pad_ref, att_ref, qb_ref, m_ref, acc_ref):
    i = pl.program_id(0)
    row0 = pl.multiple_of(i * bq, bq)
    real = pad_ref[...] > 0.5
    for h in range(heads):
        qt = qe_ref[h].astype(F32).T[:HD]
        kt = ke_ref[h, pl.ds(row0, bq), :].astype(F32).T[:HD]
        own = jnp.sum(qt * kt, axis=0, keepdims=True)
        m_ref[h] = jnp.where(real, NEG, own)
        acc_ref[h] = jnp.where(real, 0.0, vt_ref[h, :, pl.ds(row0, bq)].astype(F32))

    def step(j, _):
        col0 = pl.multiple_of(j * bk, bk)
        work = [(h, slice(c, c + QC)) for c in range(0, bq, QC) for h in range(heads)]
        score = lambda h, c: nt(ke_ref[h, pl.ds(col0, bk), :], qe_ref[h, c, :])
        ss = [score(*w) for w in work[:AHEAD]]
        for n, (h, c) in enumerate(work):
            if n + AHEAD < len(work):
                ss.append(score(*work[n + AHEAD]))
            s = ss[n]
            m_old = m_ref[h, :, c]
            m_new = jnp.maximum(m_old, jnp.max(s, axis=0, keepdims=True))
            p = jnp.exp(s - m_new).astype(BF)
            alpha = jnp.exp(m_old - m_new)
            acc_ref[h, :, c] = acc_ref[h, :, c] * alpha + nn(vt_ref[h, :, pl.ds(col0, bk)], p)
            m_ref[h, :, c] = m_new
        return 0

    lax.fori_loop(lo_ref[i], hi_ref[i], step, 0)
    outs = []
    for h in range(heads):
        acc = acc_ref[h]
        total = acc[HD : HD + 1]
        outs.append(jnp.where(real, acc[:HD] / total, 0.0))
        lse = jnp.broadcast_to(m_ref[h] + jnp.log(total), (8, bq)).T[:, :1]
        qb_ref[h] = put3(qe_ref[h], -lse, HD + 4)
    att_ref[...] = (jnp.concatenate(outs, axis=0) if heads > 1 else outs[0]).T.astype(BF)


def attend(qe, ke, vt, padw, lo, hi, bq, bk):
    heads, rows, _ = qe.shape
    full = lambda i, lo, hi: (0, 0, 0)
    return pl.pallas_call(
        functools.partial(fwd_kernel, heads, bq, bk),
        grid_spec=pltpu.PrefetchScalarGridSpec(
            num_scalar_prefetch=2,
            grid=(rows // bq,),
            in_specs=[
                pl.BlockSpec((heads, bq, LANES), lambda i, lo, hi: (0, i, 0)),
                pl.BlockSpec((heads, rows, LANES), full),
                pl.BlockSpec((heads, VT, rows), full),
                pl.BlockSpec((1, bq), lambda i, lo, hi: (0, i)),
            ],
            out_specs=[
                pl.BlockSpec((bq, heads * HD), lambda i, lo, hi: (i, 0)),
                pl.BlockSpec((heads, bq, LANES), lambda i, lo, hi: (0, i, 0)),
            ],
            scratch_shapes=[
                pltpu.VMEM((heads, 1, bq), F32),
                pltpu.VMEM((heads, VT, bq), F32),
            ],
        ),
        out_shape=[
            jax.ShapeDtypeStruct((rows, heads * HD), BF),
            jax.ShapeDtypeStruct((heads, rows, LANES), BF),
        ],
        compiler_params=pltpu.CompilerParams(vmem_limit_bytes=60 << 20),
        name="attend",
    )(lo, hi, qe, ke, vt, padw)


def bwd_kernel(heads, bq, bk, lo_ref, hi_ref, qb_ref, ke_ref, ve_ref, go_ref, att_ref, out_ref, ge_ref, dqt_ref, kt_ref, qt_ref, got_ref, dkt_ref, dvt_ref):
    j = pl.program_id(0)
    rows = qb_ref.shape[1]

    @pl.when(j == 0)
    def _():
        for h in range(heads):
            dqt_ref[h] = jnp.zeros_like(dqt_ref[h])
            for c in range(rows // 512):
                sl = pl.ds(c * 512, 512)
                go = go_ref[sl, h * HD : (h + 1) * HD]
                at = att_ref[sl, h * HD : (h + 1) * HD]
                delta = jnp.sum(go.astype(F32) * at.astype(F32), axis=1, keepdims=True)
                wide = jnp.concatenate([go, jnp.zeros_like(go)], axis=1)
                ge_ref[h, sl, :] = put3(wide, -delta, HD)
                got_ref[h, :, c * 512 : (c + 1) * 512] = wide.T[:HD]
                qt_ref[h, :, c * 512 : (c + 1) * 512] = qb_ref[h, sl, :].T[:HD]

    for h in range(heads):
        kt_ref[h] = ke_ref[h].T[:HD]

    zero = jnp.zeros((HD, bk), F32)

    def step(i, carry):
        row0 = pl.multiple_of(i * bq, bq)
        work = [(h, pl.ds(row0 + c, QB)) for c in range(0, bq, QB) for h in range(heads)]
        score = lambda h, c: (nt(ke_ref[h], qb_ref[h, c, :]), nt(ve_ref[h], ge_ref[h, c, :]))
        ss = [score(*w) for w in work[:BAHEAD]]
        for n, (h, c) in enumerate(work):
            if n + BAHEAD < len(work):
                ss.append(score(*work[n + BAHEAD]))
            st, dt = ss[n]
            p = jnp.exp(st)
            ds = (p * dt).astype(BF)
            pb = p.astype(BF)
            dvt_ref[h] += nt(got_ref[h, :, c], pb)
            dkt_ref[h] += nt(qt_ref[h, :, c], ds)
            dqt_ref[h, :, c] += nn(kt_ref[h], ds)
        return 0

    for h in range(heads):
        dkt_ref[h] = zero
        dvt_ref[h] = zero
    lax.fori_loop(lo_ref[j], hi_ref[j], step, 0)
    for h in range(heads):
        for part, ref in ((1, dkt_ref), (2, dvt_ref)):
            at = (part * heads + h) * HD
            out_ref[pl.ds(pl.multiple_of(j * bk, bk), bk), at : at + HD] = ref[h].T.astype(BF)

    @pl.when(j == pl.num_programs(0) - 1)
    def _():
        for h in range(heads):
            for c in range(rows // 512):
                sl = pl.ds(c * 512, 512)
                out_ref[sl, h * HD : (h + 1) * HD] = (dqt_ref[h, :, c * 512 : (c + 1) * 512].T * (HD ** -0.5)).astype(BF)


def attend_back(qb, ke, ve, go, att, lo, hi, bq, bk):
    heads, rows, _ = qb.shape
    full3 = lambda i, lo, hi: (0, 0, 0)
    full2 = lambda i, lo, hi: (0, 0)
    blk3 = lambda i, lo, hi: (0, i, 0)
    wide = heads * HD
    return pl.pallas_call(
        functools.partial(bwd_kernel, heads, bq, bk),
        grid_spec=pltpu.PrefetchScalarGridSpec(
            num_scalar_prefetch=2,
            grid=(rows // bk,),
            in_specs=[
                pl.BlockSpec((heads, rows, LANES), full3),
                pl.BlockSpec((heads, bk, LANES), blk3),
                pl.BlockSpec((heads, bk, LANES), blk3),
                pl.BlockSpec((rows, wide), full2),
                pl.BlockSpec((rows, wide), full2),
            ],
            out_specs=pl.BlockSpec((rows, 3 * wide), full2),
            scratch_shapes=[
                pltpu.VMEM((heads, rows, LANES), BF),
                pltpu.VMEM((heads, HD, rows), F32),
                pltpu.VMEM((heads, HD, bk), BF),
                pltpu.VMEM((heads, HD, rows), BF),
                pltpu.VMEM((heads, HD, rows), BF),
                pltpu.VMEM((heads, HD, bk), F32),
                pltpu.VMEM((heads, HD, bk), F32),
            ],
        ),
        out_shape=jax.ShapeDtypeStruct((rows, 3 * wide), BF),
        compiler_params=pltpu.CompilerParams(vmem_limit_bytes=60 << 20),
        name="attend_back",
    )(lo, hi, qb, ke, ve, go, att)


def dot_f32(a, b, dims):
    return lax.dot_general(a, b, ((dims[:1], dims[1:]), ((), ())), precision=highest, preferred_element_type=F32)


def soap_group(base, group, ga_ref, gb_ref, w_ref, m1_ref, m2_ref, av_ref, st_ref, ba_ref,
               nw_ref, n1_ref, n2_ref, na_ref, ns_ref, nb_ref, aug_ref):
    size = w_ref.shape[-1]
    half = size // 2
    panel = 8
    every = range(group)
    grads, firsts = [], []
    for s in every:
        rows = slice((base + s) * half, (base + s + 1) * half)
        wire = ga_ref[rows, :].astype(F32) + gb_ref[rows, :]
        grads.append(jnp.concatenate([wire[:, :size], wire[:, size:]], axis=0))
        firsts.append(beta_one * m1_ref[0, base + s] + (1.0 - beta_one) * grads[s])
        n1_ref[0, base + s] = firsts[s]
    sides = [(s, side) for s in every for side in range(2)]
    outers = [dot_f32(grads[s], grads[s], (1, 1) if side == 0 else (0, 0)) for s, side in sides]
    both = [dot_f32(jnp.concatenate([grads[s], firsts[s]], axis=0), ba_ref[0, base + s, 1], (1, 0)) for s in every]
    stats = []
    for (s, side), outer in zip(sides, outers):
        stats.append(beta_two * st_ref[0, base + s, side] + (1.0 - beta_two) * outer)
        ns_ref[0, base + s, side] = stats[-1]
    pairs = [dot_f32(ba_ref[0, base + s, 0], jnp.concatenate([both[s][:size], both[s][size:]], axis=1), (0, 0)) for s in every]
    mts = [dot_f32(ba_ref[0, base + s, side], stat, (0, 1)) for (s, side), stat in zip(sides, stats)]
    scaled = []
    for s in every:
        rotated, moment = pairs[s][:, :size], pairs[s][:, size:]
        second = beta_two * m2_ref[0, base + s] + (1.0 - beta_two) * rotated * rotated
        n2_ref[0, base + s] = second
        scaled.append(moment / (jnp.sqrt(second) + step_eps))
    grams = [dot_f32(mt, mt, (1, 1)) for mt in mts]
    inner = [dot_f32(scaled[s], ba_ref[0, base + s, 1], (1, 1)) for s in every]
    for m, (gram, mt) in enumerate(zip(grams, mts)):
        aug_ref[m] = jnp.concatenate([gram, mt], axis=1)
    directions = [dot_f32(ba_ref[0, base + s, 0], inner[s], (1, 0)) for s in every]
    for s in every:
        weight = w_ref[0, base + s]
        fresh = weight - step_rate * (directions[s] + weight_decay * weight)
        nw_ref[0, base + s] = fresh
        na_ref[0, base + s] = average_keep * av_ref[0, base + s] + (1.0 - average_keep) * fresh
    count = 2 * group
    row = lax.broadcasted_iota(jnp.int32, (count, panel, LANES), 1)
    for p in range(size // panel):
        top = p * panel
        part = aug_ref[:, top : top + panel, :]
        for r in range(panel):
            pivot = lax.rsqrt(part[:, r : r + 1, top + r : top + r + 1])
            lead = part[:, r : r + 1, :] * pivot
            column = jnp.where(row > r, part[:, :, top + r : top + r + 1] * pivot, 0.0)
            part = jnp.where(row == r, lead, part - column * lead)
        aug_ref[:, top : top + panel, :] = part
        below = top + panel
        if below < size:
            high = part.astype(BF).astype(F32)
            rest = part - high
            mid = rest.astype(BF).astype(F32)
            low = rest - mid
            first = jnp.concatenate([high, high, mid, high, mid, low], axis=1).astype(BF)
            other = jnp.concatenate([high, mid, high, low, mid, high], axis=1).astype(BF)
            for m in range(count):
                aug_ref[m, below:, :] -= lax.dot_general(
                    first[m][:, below:size], other[m], (((0,), (0,)), ((), ())), preferred_element_type=F32
                )
    for s in range(group):
        for side in range(2):
            nb_ref[0, base + s, side] = aug_ref[2 * s + side][:, size:].T


MESH = pl.DeviceIdType.MESH


def normalize(values):
    center = jnp.mean(values, axis=-1, keepdims=True)
    centered = values - center
    variance = jnp.mean(centered * centered, axis=-1, keepdims=True)
    scale = lax.rsqrt(variance + norm_eps)
    return centered * scale, scale


def norm_back(grad, xhat, scale):
    along = jnp.mean(grad * xhat, axis=-1, keepdims=True)
    return (grad - jnp.mean(grad, axis=-1, keepdims=True) - xhat * along) * scale


TAIL = 0.305
TAIL_FIT = (
    0.1216397411342051,
    0.12246669816059132,
    0.10342157025713879,
    0.1210193967312446,
    -0.037972477455618554,
    0.18571204369074895,
    -0.15298537812807472,
    0.036698452375741396,
)


def gelu_pair(u):
    size = jnp.abs(u)
    bell = jnp.exp(-0.5 * u * u)
    t = 1.0 / (1.0 + TAIL * size)
    poly = jnp.full_like(t, TAIL_FIT[-1])
    for c in TAIL_FIT[-2::-1]:
        poly = poly * t + c
    upper = poly * t * bell
    cdf = jnp.where(u > 0.0, 1.0 - upper, upper)
    return u * cdf, cdf + (0.3989422804014327 * u) * bell


def block_rows(ref, start, half):
    return ref[pl.ds(pl.multiple_of(start, 16), half), :]


def project_kernel(heads, rows_dev, gains_at, row_ref, wire_ref, tok_ref, seg_ref, pad_ref, gain_ref,
                   norm_ref, qe_ref, ke_ref, ve_ref, vt_ref, mix_ref, wide_ref):
    width = tok_ref.shape[1]
    half = HD // 2
    cols = 3 * heads

    @pl.when(pl.program_id(0) == 0)
    def _():
        zero = jnp.zeros((half, HD), BF)

        def fill(r, _):
            low = pl.multiple_of(r * HD, HD)
            for c in range(cols):
                t = block_rows(wire_ref, row_ref[r * cols + c], half)
                for part in range(2):
                    piece = t[:, part * HD : (part + 1) * HD]
                    at = pl.ds(low + part * half, half)
                    wide_ref[at, c * LANES : (c + 1) * LANES] = jnp.concatenate([piece, zero], axis=1)
                    mix_ref[at, c * HD : (c + 1) * HD] = piece
            return 0

        lax.fori_loop(0, width // HD, fill, 0)

    xhat, _ = normalize(tok_ref[...].astype(F32))
    normed = (xhat * gain_ref[...]).astype(BF)
    norm_ref[...] = normed
    count = tok_ref.shape[0]
    lane = lax.broadcasted_iota(jnp.int32, (LANES, count), 0)
    seg = seg_ref[...]
    same = lane - HD == seg
    in_segs = (lane >= HD) & (lane < HD + SEGS)
    ones = (lane >= HD + SEGS) & (lane < HD + SEGS + 3)
    ext_q = jnp.where(same, 1.0, 0.0).T
    ext_k = jnp.where(in_segs, jnp.where(same & (pad_ref[...] > 0.5), 0.0, NEG), jnp.where(ones, 1.0, 0.0)).T
    ext_v = jnp.where((lane >= HD) & (lane < HD + 3), 1.0, 0.0).T
    for h in range(heads):
        for ref, part, scale, ext in ((qe_ref, 0, HD ** -0.5, ext_q), (ke_ref, 1, 1.0, ext_k), (ve_ref, 2, 1.0, ext_v)):
            c = part * heads + h
            mixed = nn(normed, wide_ref[:, c * LANES : (c + 1) * LANES]).astype(BF)
            out = (mixed.astype(F32) * scale + ext).astype(BF)
            ref[h] = out
            if part == 2:
                vt_ref[h] = out.T[:VT]


def project(wire, row_own, tokens, seg, pad, gain_one, heads):
    rows, width = tokens.shape
    tb = min(512, rows)
    full = lambda i, r: (0, 0)
    blk = lambda i, r: (i, 0)
    col = lambda i, r: (0, i)
    ext = lambda i, r: (0, i, 0)
    out = lambda *s: jax.ShapeDtypeStruct(s, BF)
    return pl.pallas_call(
        functools.partial(project_kernel, heads, 0, 0),
        grid_spec=pltpu.PrefetchScalarGridSpec(
            num_scalar_prefetch=1,
            grid=(rows // tb,),
            in_specs=[
                pl.BlockSpec(wire.shape, full),
                pl.BlockSpec((tb, width), blk),
                pl.BlockSpec((1, tb), col),
                pl.BlockSpec((1, tb), col),
                pl.BlockSpec((1, width), full),
            ],
            out_specs=[
                pl.BlockSpec((tb, width), blk),
                pl.BlockSpec((heads, tb, LANES), ext),
                pl.BlockSpec((heads, tb, LANES), ext),
                pl.BlockSpec((heads, tb, LANES), ext),
                pl.BlockSpec((heads, VT, tb), lambda i, r: (0, 0, i)),
                pl.BlockSpec((width, 3 * heads * HD), full),
            ],
            scratch_shapes=[pltpu.VMEM((width, 3 * heads * LANES), BF)],
        ),
        out_shape=[
            out(rows, width),
            out(heads, rows, LANES),
            out(heads, rows, LANES),
            out(heads, rows, LANES),
            out(heads, VT, rows),
            out(width, 3 * heads * HD),
        ],
        compiler_params=pltpu.CompilerParams(vmem_limit_bytes=60 << 20),
        name="project",
    )(row_own, wire, tokens, seg, pad, gain_one)


def middle_kernel(shards, span, units, rows_dev, wide, gain_row, gains_dev,
                  here_ref, row_ref, wire_ref, att_ref, tok_ref, cot_ref, pad_ref, gain_ref,
                  out_ref, res_ref, back_ref, grads_ref, mix_ref,
                  wo_ref, wu_ref, wd_ref, go_ref, gu_ref, gd_ref, gg_ref):
    width = tok_ref.shape[1]
    half = HD // 2
    kinds = (
        (mix_ref, None, width, 3 * span),
        (wo_ref, go_ref, span, width),
        (wu_ref, gu_ref, width, units),
        (wd_ref, gd_ref, units, width),
    )

    @pl.when(pl.program_id(0) == 0)
    def _():
        base = 0
        for ref, acc, rows, cols in kinds:
            grid_cols = cols // HD

            def fill(r, _, ref=ref, base=base, grid_cols=grid_cols):
                low = pl.multiple_of(r * HD, HD)
                for n in range(shards):
                    for c in range(grid_cols):
                        t = block_rows(wire_ref, row_ref[base + r * grid_cols + c] + n * rows_dev, half)
                        for part in range(2):
                            ref[n, pl.ds(low + part * half, half), c * HD : (c + 1) * HD] = t[:, part * HD : (part + 1) * HD]
                return 0

            lax.fori_loop(0, rows // HD, fill, 0)
            base += rows // HD * grid_cols
            if acc is not None:
                acc[...] = jnp.zeros_like(acc)
        gg_ref[...] = jnp.zeros_like(gg_ref)

    tokens = tok_ref[...].astype(F32)
    cot = cot_ref[...]
    branch = nn(att_ref[0], wo_ref[0])
    for n in range(1, shards):
        branch += nn(att_ref[n], wo_ref[n])
    residual = tokens + branch
    xhat, scale = normalize(residual)
    gain = gain_ref[...]
    normed = (xhat * gain).astype(BF)
    mlp = jnp.zeros_like(residual)
    back = jnp.zeros_like(residual)
    for n in range(shards):
        value, slope = gelu_pair(nn(normed, wu_ref[n]))
        active = value.astype(BF)
        mlp += nn(active, wd_ref[n])
        gd_ref[n] += tn(active, cot)
        back_up = (slope * nt(cot, wd_ref[n])).astype(BF)
        gu_ref[n] += tn(normed, back_up)
        back += nt(back_up, wu_ref[n])
    out_ref[...] = (residual + mlp).astype(BF)
    gg_ref[...] += jnp.sum(back * xhat, axis=0, keepdims=True)
    back_res = cot.astype(F32) + norm_back(back * gain, xhat, scale)
    res_ref[...] = back_res
    branch_low = back_res.astype(BF)
    pad = jnp.broadcast_to(pad_ref[...], (8, pad_ref.shape[1])).T[:, :1]
    for n in range(shards):
        go_ref[n] += tn(att_ref[n], branch_low)
        back_ref[n] = (nt(branch_low, wo_ref[n]) * pad).astype(BF)

    @pl.when(pl.program_id(0) == pl.num_programs(0) - 1)
    def _():
        grads_ref[...] = jnp.zeros_like(grads_ref)
        base = 0
        for ref, acc, rows, cols in kinds:
            grid_cols = cols // HD
            if acc is not None:

                def scatter(r, _, acc=acc, base=base, grid_cols=grid_cols):
                    low = pl.multiple_of(r * HD, HD)
                    for n in range(shards):
                        for c in range(grid_cols):
                            at = row_ref[base + r * grid_cols + c] + n * rows_dev
                            cut = slice(c * HD, (c + 1) * HD)
                            value = jnp.concatenate([acc[n, pl.ds(low, half), cut], acc[n, pl.ds(low + half, half), cut]], axis=1)
                            grads_ref[pl.ds(pl.multiple_of(at, 16), half), :] = value.astype(BF)
                    return 0

                lax.fori_loop(0, rows // HD, scatter, 0)
            base += rows // HD * grid_cols
        for w in range(wide):
            piece = w * gains_dev // LANES - width // LANES
            if piece >= 0:
                for n in range(shards):
                    at = (w * shards + n) * rows_dev + gain_row
                    grads_ref[at : at + 1, :] = gg_ref[:, piece * LANES : (piece + 1) * LANES].astype(BF)


def middle(here, row_full, wire, att, tokens, cotangent, pad, gain_two, wide, rows_dev, gain_row, gains_dev):
    shards, own, span = att.shape
    width = tokens.shape[1]
    units = FF // shards
    tb = min(256, own)
    steps = own // tb
    full = lambda i, h, r: (0, 0)
    full3 = lambda i, h, r: (0, 0, 0)
    mine = lambda i, h, r: (h[0] * steps + i, 0)
    blk = lambda i, h, r: (i, 0)
    blk3 = lambda i, h, r: (0, i, 0)
    once = pl.Buffered(1)
    return pl.pallas_call(
        functools.partial(middle_kernel, shards, span, units, rows_dev, wide, gain_row, gains_dev),
        grid_spec=pltpu.PrefetchScalarGridSpec(
            num_scalar_prefetch=2,
            grid=(steps,),
            in_specs=[
                pl.BlockSpec(wire.shape, full, pipeline_mode=once),
                pl.BlockSpec((shards, tb, span), blk3),
                pl.BlockSpec((tb, width), mine),
                pl.BlockSpec((tb, width), mine),
                pl.BlockSpec((1, tb), lambda i, h, r: (0, h[0] * steps + i)),
                pl.BlockSpec((1, width), full),
            ],
            out_specs=[
                pl.BlockSpec((tb, width), blk),
                pl.BlockSpec((tb, width), blk),
                pl.BlockSpec((shards, tb, span), blk3),
                pl.BlockSpec(wire.shape, full, pipeline_mode=once),
                pl.BlockSpec((shards, width, 3 * span), full3, pipeline_mode=once),
            ],
            scratch_shapes=[
                pltpu.VMEM((shards, span, width), BF),
                pltpu.VMEM((shards, width, units), BF),
                pltpu.VMEM((shards, units, width), BF),
                pltpu.VMEM((shards, span, width), F32),
                pltpu.VMEM((shards, width, units), F32),
                pltpu.VMEM((shards, units, width), F32),
                pltpu.VMEM((1, width), F32),
            ],
        ),
        out_shape=[
            jax.ShapeDtypeStruct((own, width), BF),
            jax.ShapeDtypeStruct((own, width), F32),
            jax.ShapeDtypeStruct((shards, own, span), BF),
            jax.ShapeDtypeStruct(wire.shape, BF),
            jax.ShapeDtypeStruct((shards, width, 3 * span), BF),
        ],
        compiler_params=pltpu.CompilerParams(vmem_limit_bytes=60 << 20),
        name="middle",
    )(here, row_full, wire, att, tokens, cotangent, pad, gain_two)


PARTS = 4


def finish_kernel(shards, wide, gain_row, gains_dev, group, sel_ref, mix_ref, full_ref, gain_ref, res_ref, bm_ref, norm_ref, tok_ref, *refs):
    states, outs = refs[:7], refs[9:15]
    grad_ref, line_ref = refs[7:9]
    (own_ref, normed_ref, tokens_ref, got_ref, acc_ref, blk_ref, grads_ref, sums_ref, part_ref, aug_ref,
     local_sem, send_z, recv_z, send_w, recv_w, send_a, recv_a, send_g, recv_g) = refs[15:]
    width = norm_ref.shape[1]
    rows, cols = bm_ref.shape
    own = rows // shards
    hold = own // PARTS
    half = HD // 2
    grid_cols = cols // HD
    blocks = width // HD * grid_cols
    slots = gain_row // half
    z = lax.axis_index("narrow")
    w = lax.axis_index("wide")

    barrier = pltpu.get_barrier_semaphore()
    for d in range(1, shards):
        pl.semaphore_signal(barrier, inc=1, device_id={"narrow": lax.rem(z + d, shards)}, device_id_type=MESH)
    for d in range(1, wide):
        pl.semaphore_signal(barrier, inc=1, device_id={"wide": lax.rem(w + d, wide)}, device_id_type=MESH)
    pl.semaphore_wait(barrier, shards + wide - 2)

    def to_peer(d, part, mine):
        peer = lax.rem(z + d, shards)
        slot = z if mine else peer
        at = pl.multiple_of(peer * own + part * hold, hold)
        return pltpu.make_async_remote_copy(
            src_ref=bm_ref.at[pl.ds(at, hold), :],
            dst_ref=got_ref.at[slot, pl.ds(part * hold, hold), :],
            send_sem=send_z.at[d - 1, part],
            recv_sem=recv_z.at[slot, part],
            device_id={"narrow": peer},
            device_id_type=MESH,
        )

    def to_owner(d, mine):
        peer = lax.rem(w + d, wide)
        slot = w if mine else peer
        return pltpu.make_async_remote_copy(
            src_ref=grads_ref.at[peer],
            dst_ref=sums_ref.at[slot],
            send_sem=send_w.at[d - 1],
            recv_sem=recv_w.at[slot],
            device_id={"wide": peer},
            device_id_type=MESH,
        )

    def hop_copy(c, part, step):
        at = pl.ds(pl.multiple_of(c * own + part * hold, hold), hold)
        return pltpu.make_async_remote_copy(
            src_ref=grad_ref.at[at, :],
            dst_ref=grad_ref.at[at, :],
            send_sem=send_a.at[step, c, part],
            recv_sem=recv_a.at[c, part],
            device_id={"narrow": lax.rem(z + (1 if step == 0 else shards - 1), shards)},
            device_id_type=MESH,
        )

    def pass_on(c, part, act):
        for step, there in ((0, z < shards - 1), (1, z > 0)):
            if c is None or step == c[0]:
                chunk = z if c is None else c[1]
                ok = there if c is None else there & c[2]

                @pl.when(ok)
                def _(chunk=chunk, step=step):
                    act(hop_copy(chunk, part, step))

    def line_to(d, mine):
        peer = lax.rem(z + d, shards)
        slot = z if mine else peer
        return pltpu.make_async_remote_copy(
            src_ref=line_ref.at[z],
            dst_ref=line_ref.at[slot],
            send_sem=send_g.at[d - 1],
            recv_sem=recv_g.at[slot],
            device_id={"narrow": peer},
            device_id_type=MESH,
        )

    for part in range(PARTS):
        for d in range(1, shards):
            to_peer(d, part, True).start()
    mine = pl.ds(pl.multiple_of(z * own, own), own)
    copies = [
        pltpu.make_async_copy(bm_ref, own_ref, local_sem.at[0]),
        pltpu.make_async_copy(norm_ref, normed_ref, local_sem.at[1]),
        pltpu.make_async_copy(tok_ref.at[mine, :], tokens_ref, local_sem.at[2]),
        pltpu.make_async_copy(bm_ref.at[mine, :], got_ref.at[z], local_sem.at[3]),
    ]
    for copy in copies:
        copy.start()
    for copy in copies:
        copy.wait()

    acc_ref[...] = jnp.zeros_like(acc_ref)
    tb = min(512, rows)

    def add(i, _):
        at = pl.ds(pl.multiple_of(i * tb, tb), tb)
        acc_ref[...] += tn(normed_ref[at, :], own_ref[at, :])
        return 0

    lax.fori_loop(0, rows // tb, add, 0)
    blk_ref[blocks] = jnp.zeros((half, LANES), BF)

    def cut(r, _):
        low = pl.multiple_of(r * HD, HD)
        for c in range(grid_cols):
            lanes = slice(c * HD, (c + 1) * HD)
            value = jnp.concatenate([acc_ref[pl.ds(low, half), lanes], acc_ref[pl.ds(low + half, half), lanes]], axis=1)
            blk_ref[r * grid_cols + c] = value.astype(BF)
        return 0

    lax.fori_loop(0, width // HD, cut, 0)
    along = jnp.sum(acc_ref[...] * mix_ref[...].astype(F32), axis=1, keepdims=True)
    line = jnp.broadcast_to(along, (width, LANES)).T[:16] / gain_ref[...]
    top = lax.broadcasted_iota(jnp.int32, (16, LANES), 0) == 0
    for v in range(wide):

        def place(i, _, v=v):
            grads_ref[v, pl.ds(pl.multiple_of(i * half, half), half), :] = blk_ref[sel_ref[v * slots + i]]
            return 0

        lax.fori_loop(0, slots, place, 0)
        piece = v * gains_dev // LANES
        if piece < width // LANES:
            value = jnp.where(top, line[:, piece * LANES : (piece + 1) * LANES], 0.0).astype(BF)
        else:
            value = jnp.zeros((16, LANES), BF)
        grads_ref[v, gain_row : gain_row + 16, :] = value
    for d in range(1, wide):
        to_owner(d, True).start()
    part_ref[...] = grads_ref[w].astype(F32)

    tile = min(256, hold)

    def norm_rows(i, _):
        at = pl.ds(pl.multiple_of(i * tile, tile), tile)
        back = nt(got_ref[0, at, :], full_ref[0])
        for n in range(1, shards):
            back += nt(got_ref[n, at, :], full_ref[n])
        xhat, scale = normalize(tokens_ref[at, :].astype(F32))
        grad = res_ref[at, :] + norm_back(back * gain_ref[...], xhat, scale)
        grad_ref[pl.ds(pl.multiple_of(z * own + i * tile, tile), tile), :] = grad.astype(BF)
        return 0

    def norm_part(part):
        for d in range(1, shards):
            to_peer(d, part, False).wait_recv()
        lax.fori_loop(part * hold // tile, (part + 1) * hold // tile, norm_rows, 0)
        pass_on(None, part, lambda copy: copy.start())

    for d in range(1, wide):
        to_owner(d, False).wait_recv()
    for d in range(1, wide):
        part_ref[...] += sums_ref[lax.rem(w + d, wide)].astype(F32)
    line_ref[z] = part_ref[gain_row : gain_row + 16, :]
    for d in range(1, shards):
        line_to(d, True).start()
    ready = 0
    rounds = slots // group
    for g in range(rounds):
        soap_group(g * group, group, states[0], part_ref, *states[1:], *outs, aug_ref)
        upto = PARTS * (g + 1) // rounds
        while ready < upto:
            norm_part(ready)
            ready += 1
    hops = [(s, part, step) for s in range(1, shards) for part in range(PARTS) for step in range(2)]
    for s, part, step in hops:
        chunk = z - s if step == 0 else z + s
        there = chunk >= 0 if step == 0 else chunk < shards

        @pl.when(there)
        def _(chunk=chunk, part=part, step=step):
            hop_copy(chunk, part, step).wait_recv()

        pass_on((step, chunk, there), part, lambda copy: copy.start())
    for d in range(1, shards):
        line_to(d, False).wait_recv()
    for part in range(PARTS):
        pass_on(None, part, lambda copy: copy.wait_send())
    for s, part, step in hops:
        chunk = z - s if step == 0 else z + s
        there = chunk >= 0 if step == 0 else chunk < shards
        pass_on((step, chunk, there), part, lambda copy: copy.wait_send())
    for d in range(1, shards):
        line_to(d, True).wait_send()
    for part in range(PARTS):
        for d in range(1, shards):
            to_peer(d, part, True).wait_send()
    for d in range(1, wide):
        to_owner(d, True).wait_send()


def finish(sel, mix, mix_full, gain_one, res, bm, normed, tokens, states, group, wide, rows_dev, gain_row, gains_dev):
    shards = mix_full.shape[0]
    rows, cols = bm.shape
    width = normed.shape[1]
    own = rows // shards
    half = HD // 2
    blocks = width // HD * (cols // HD)
    vmem = pl.BlockSpec(memory_space=pltpu.VMEM)
    smem = pl.BlockSpec(memory_space=pltpu.SMEM)
    hbm = pl.BlockSpec(memory_space=pl.ANY)
    dma = pltpu.SemaphoreType.DMA
    return pl.pallas_call(
        functools.partial(finish_kernel, shards, wide, gain_row, gains_dev, group),
        in_specs=[smem, vmem, vmem, vmem, vmem, hbm, hbm, hbm] + [vmem] * 7,
        out_specs=[vmem] * 8,
        out_shape=[jax.ShapeDtypeStruct((rows, width), BF), jax.ShapeDtypeStruct((shards, 16, LANES), F32)]
        + [jax.ShapeDtypeStruct(a.shape, a.dtype) for a in states[1:]],
        scratch_shapes=[
            pltpu.VMEM((rows, cols), BF),
            pltpu.VMEM((rows, width), BF),
            pltpu.VMEM((own, width), BF),
            pltpu.VMEM((shards, own, cols), BF),
            pltpu.VMEM((width, cols), F32),
            pltpu.VMEM((blocks + 1, half, LANES), BF),
            pltpu.VMEM((wide, rows_dev, LANES), BF),
            pltpu.VMEM((wide, rows_dev, LANES), BF),
            pltpu.VMEM((rows_dev, LANES), F32),
            pltpu.VMEM((2 * group, HD, LANES), F32),
            dma((4,)),
            dma((shards - 1, PARTS)),
            dma((shards, PARTS)),
            dma((wide - 1,)),
            dma((wide,)),
            dma((2, shards, PARTS)),
            dma((shards, PARTS)),
            dma((shards - 1,)),
            dma((shards,)),
        ],
        compiler_params=pltpu.CompilerParams(vmem_limit_bytes=62 << 20, collective_id=1, has_side_effects=True),
        name="finish",
    )(sel, mix, mix_full, gain_one, res, bm, normed, tokens, *states)


def adam_gains(grad, gain, first, second, average):
    new_first = beta_one * first + (1.0 - beta_one) * grad
    new_second = beta_two * second + (1.0 - beta_two) * grad * grad
    new_gain = gain - gain_rate * new_first / (jnp.sqrt(new_second) + step_eps)
    new_average = average_keep * average + (1.0 - average_keep) * new_gain
    return (new_gain, new_first, new_second, new_average)


def to_shards(values, shards):
    rows, cols = values.shape
    return lax.all_to_all(values.reshape(shards, rows // shards, cols), "narrow", 0, 0)


def body(
    tokens,
    cotangent,
    segment_ids,
    pad_mask,
    owner_order,
    weights,
    first_moment,
    second_moment,
    average,
    stats,
    bases,
    gains,
    gain_first,
    gain_second,
    gain_average,
):
    narrow = lax.axis_size("narrow")
    wide = lax.axis_size("wide")
    here = lax.axis_index("narrow")
    heads = HEADS // narrow
    rows, width = tokens.shape
    span = heads * HD
    own = rows // narrow
    slots, size = weights.shape[1], weights.shape[2]
    half = size // 2
    block_count = owner_order.shape[0]
    gains_dev = gains.shape[0]
    gain_row = slots * half
    rows_dev = gain_row + 16

    low = weights[0].astype(BF)
    wire = jnp.concatenate([low[:, :half], low[:, half:]], axis=2).reshape(gain_row, 2 * size)
    wire = jnp.concatenate([wire, jnp.pad(gains.astype(BF)[None], ((0, 15), (0, LANES - gains_dev)))], axis=0)
    wire_own = lax.all_gather(wire, "wide", axis=0, tiled=True)
    wire_full = lax.all_gather(lax.all_gather(wire, "narrow", axis=0, tiled=True), "wide", axis=0, tiled=True)

    ids = jnp.arange(block_count, dtype=jnp.int32)
    slot_of = jnp.sum(jnp.where(owner_order[None, :] == ids[:, None], ids[None, :], 0), axis=1)
    device, place = slot_of // slots, slot_of % slots
    row_own = device * rows_dev + place * half
    row_full = device * (narrow * rows_dev) + place * half
    here_of = jnp.full((1,), here, jnp.int32)

    gain_all = wire_own.reshape(wide, rows_dev, LANES)[:, gain_row, :gains_dev].astype(F32).reshape(1, 2 * width)
    gain_one, gain_two = gain_all[:, :width], gain_all[:, width:]
    seg = segment_ids
    seg_row = segment_ids[0]
    pad = pad_mask.astype(F32)
    block = min(512, rows)
    low_seg = seg_row[::block]
    high_seg = seg_row[block - 1 :: block]
    begin = jnp.sum((seg_row[None, :] < low_seg[:, None]).astype(jnp.int32), axis=1) // block
    end = (jnp.sum((seg_row[None, :] <= high_seg[:, None]).astype(jnp.int32), axis=1) + block - 1) // block

    normed, qe, ke, ve, vt, mix = project(wire_own, row_own, tokens, seg, pad, gain_one, heads)
    attended, qb = attend(qe, ke, vt, pad, begin, end, block, block)
    att_own = to_shards(attended, narrow)
    out_own, back_res, back_own, grads, mix_full = middle(
        here_of, row_full, wire_full, att_own, tokens, cotangent, pad, gain_two, wide, rows_dev, gain_row, gains_dev
    )
    part_a = lax.psum_scatter(grads, ("wide", "narrow"), scatter_dimension=0, tiled=True)
    back_att = lax.all_to_all(back_own, "narrow", 0, 0).reshape(rows, span)
    out_own, back_att = lax.optimization_barrier((out_own, back_att))
    output = lax.all_to_all(jnp.broadcast_to(out_own, (narrow, own, width)), "narrow", 0, 0).reshape(rows, width)
    bm = attend_back(qb, ke, ve, back_att, attended, begin, end, block, block)
    bm, part_a, output = lax.optimization_barrier((bm, part_a, output))
    sel = jnp.minimum(owner_order, width // size * 3 * heads)
    group = next(g for g in range(min(12, slots), 0, -1) if slots % g == 0)
    states = (part_a, weights, first_moment, second_moment, average, stats, bases)
    grad_all, lines, new_weight, new_first, new_second, new_average, new_stats, new_bases = finish(
        sel, mix, mix_full, gain_one, back_res, bm, normed, tokens, states, group, wide, rows_dev, gain_row, gains_dev
    )
    input_grad = grad_all.astype(F32)
    line = part_a[gain_row].astype(F32) + jnp.sum(lines[:, 0], axis=0)
    offset = lax.axis_index("wide") * gains_dev % LANES
    own_gain = lax.dynamic_slice_in_dim(line, offset, gains_dev, 0)
    new_gains, gain_moment, gain_square, gain_mean = adam_gains(own_gain, gains, gain_first, gain_second, gain_average)
    return (
        output,
        input_grad,
        new_weight,
        new_first,
        new_second,
        new_average,
        new_stats,
        new_bases,
        new_gains,
        gain_moment,
        gain_square,
        gain_mean,
    )


def solution(mesh):
    block = P("narrow", "wide", None, None)
    pair = P("narrow", "wide", None, None, None)
    rows = P("wide", None)
    line = P("wide")
    return jax.shard_map(
        body,
        mesh=mesh,
        in_specs=(rows, rows, rows, rows, P(), block, block, block, block, pair, pair, line, line, line, line),
        out_specs=(rows, rows, block, block, block, block, pair, pair, line, line, line, line),
        check_vma=False,
    )
```

```python
import functools

import jax
import jax.numpy as jnp
from jax import lax
from jax.experimental import pallas as pl
from jax.experimental.pallas import tpu as pltpu
from jax.sharding import PartitionSpec as P

HEADS = 8
HD = 64
FF = 2048
LANES = 128
SEGS = 4
NEG = -1e30
F32 = jnp.float32
BF = jnp.bfloat16
highest = lax.Precision.HIGHEST

beta_one = 0.9
beta_two = 0.95
step_rate = 0.1
gain_rate = 0.75
weight_decay = 0.01
average_keep = 0.5
norm_eps = 1e-05
step_eps = 1e-08


def nt(a, b):
    return lax.dot_general(a, b, (((1,), (1,)), ((), ())), preferred_element_type=F32)


def nn(a, b):
    return lax.dot_general(a, b, (((1,), (0,)), ((), ())), preferred_element_type=F32)


def tn(a, b):
    return lax.dot_general(a, b, (((0,), (0,)), ((), ())), preferred_element_type=F32)


def split3(x):
    hi = x.astype(BF)
    r = x - hi.astype(F32)
    mid = r.astype(BF)
    lo = (r - mid.astype(F32)).astype(BF)
    return hi, mid, lo


def put3(base, x, lane0):
    lane = lax.broadcasted_iota(jnp.int32, base.shape, 1)
    hi, mid, lo = split3(x)
    out = jnp.where(lane == lane0, hi.astype(F32), base.astype(F32))
    out = jnp.where(lane == lane0 + 1, mid.astype(F32), out)
    out = jnp.where(lane == lane0 + 2, lo.astype(F32), out)
    return out.astype(BF)


VT = 80
QC, AHEAD, QB, BAHEAD = 512, 1, 256, 1


def fwd_kernel(heads, bq, bk, lo_ref, hi_ref, qe_ref, ke_ref, vt_ref, pad_ref, att_ref, qb_ref, m_ref, acc_ref):
    i = pl.program_id(0)
    row0 = pl.multiple_of(i * bq, bq)
    real = pad_ref[...] > 0.5
    for h in range(heads):
        qt = qe_ref[h].astype(F32).T[:HD]
        kt = ke_ref[h, pl.ds(row0, bq), :].astype(F32).T[:HD]
        own = jnp.sum(qt * kt, axis=0, keepdims=True)
        m_ref[h] = jnp.where(real, NEG, own)
        acc_ref[h] = jnp.where(real, 0.0, vt_ref[h, :, pl.ds(row0, bq)].astype(F32))

    def step(j, _):
        col0 = pl.multiple_of(j * bk, bk)
        work = [(h, slice(c, c + QC)) for c in range(0, bq, QC) for h in range(heads)]
        score = lambda h, c: nt(ke_ref[h, pl.ds(col0, bk), :], qe_ref[h, c, :])
        ss = [score(*w) for w in work[:AHEAD]]
        for n, (h, c) in enumerate(work):
            if n + AHEAD < len(work):
                ss.append(score(*work[n + AHEAD]))
            s = ss[n]
            m_old = m_ref[h, :, c]
            m_new = jnp.maximum(m_old, jnp.max(s, axis=0, keepdims=True))
            p = jnp.exp(s - m_new).astype(BF)
            alpha = jnp.exp(m_old - m_new)
            acc_ref[h, :, c] = acc_ref[h, :, c] * alpha + nn(vt_ref[h, :, pl.ds(col0, bk)], p)
            m_ref[h, :, c] = m_new
        return 0

    lax.fori_loop(lo_ref[i], hi_ref[i], step, 0)
    outs = []
    for h in range(heads):
        acc = acc_ref[h]
        total = acc[HD : HD + 1]
        outs.append(jnp.where(real, acc[:HD] / total, 0.0))
        lse = jnp.broadcast_to(m_ref[h] + jnp.log(total), (8, bq)).T[:, :1]
        qb_ref[h] = put3(qe_ref[h], -lse, HD + 4)
    att_ref[...] = (jnp.concatenate(outs, axis=0) if heads > 1 else outs[0]).T.astype(BF)


def attend(qe, ke, vt, padw, lo, hi, bq, bk):
    heads, rows, _ = qe.shape
    full = lambda i, lo, hi: (0, 0, 0)
    return pl.pallas_call(
        functools.partial(fwd_kernel, heads, bq, bk),
        grid_spec=pltpu.PrefetchScalarGridSpec(
            num_scalar_prefetch=2,
            grid=(rows // bq,),
            in_specs=[
                pl.BlockSpec((heads, bq, LANES), lambda i, lo, hi: (0, i, 0)),
                pl.BlockSpec((heads, rows, LANES), full),
                pl.BlockSpec((heads, VT, rows), full),
                pl.BlockSpec((1, bq), lambda i, lo, hi: (0, i)),
            ],
            out_specs=[
                pl.BlockSpec((bq, heads * HD), lambda i, lo, hi: (i, 0)),
                pl.BlockSpec((heads, bq, LANES), lambda i, lo, hi: (0, i, 0)),
            ],
            scratch_shapes=[
                pltpu.VMEM((heads, 1, bq), F32),
                pltpu.VMEM((heads, VT, bq), F32),
            ],
        ),
        out_shape=[
            jax.ShapeDtypeStruct((rows, heads * HD), BF),
            jax.ShapeDtypeStruct((heads, rows, LANES), BF),
        ],
        compiler_params=pltpu.CompilerParams(vmem_limit_bytes=60 << 20),
        name="attend",
    )(lo, hi, qe, ke, vt, padw)


def bwd_kernel(heads, bq, bk, lo_ref, hi_ref, qb_ref, ke_ref, ve_ref, go_ref, att_ref, out_ref, ge_ref, dqt_ref, kt_ref, qt_ref, got_ref, dkt_ref, dvt_ref):
    j = pl.program_id(0)
    rows = qb_ref.shape[1]

    @pl.when(j == 0)
    def _():
        for h in range(heads):
            dqt_ref[h] = jnp.zeros_like(dqt_ref[h])
            for c in range(rows // 512):
                sl = pl.ds(c * 512, 512)
                go = go_ref[sl, h * HD : (h + 1) * HD]
                at = att_ref[sl, h * HD : (h + 1) * HD]
                delta = jnp.sum(go.astype(F32) * at.astype(F32), axis=1, keepdims=True)
                wide = jnp.concatenate([go, jnp.zeros_like(go)], axis=1)
                ge_ref[h, sl, :] = put3(wide, -delta, HD)
                got_ref[h, :, c * 512 : (c + 1) * 512] = wide.T[:HD]
                qt_ref[h, :, c * 512 : (c + 1) * 512] = qb_ref[h, sl, :].T[:HD]

    for h in range(heads):
        kt_ref[h] = ke_ref[h].T[:HD]

    zero = jnp.zeros((HD, bk), F32)

    def step(i, carry):
        row0 = pl.multiple_of(i * bq, bq)
        work = [(h, pl.ds(row0 + c, QB)) for c in range(0, bq, QB) for h in range(heads)]
        score = lambda h, c: (nt(ke_ref[h], qb_ref[h, c, :]), nt(ve_ref[h], ge_ref[h, c, :]))
        ss = [score(*w) for w in work[:BAHEAD]]
        for n, (h, c) in enumerate(work):
            if n + BAHEAD < len(work):
                ss.append(score(*work[n + BAHEAD]))
            st, dt = ss[n]
            p = jnp.exp(st)
            ds = (p * dt).astype(BF)
            pb = p.astype(BF)
            dvt_ref[h] += nt(got_ref[h, :, c], pb)
            dkt_ref[h] += nt(qt_ref[h, :, c], ds)
            dqt_ref[h, :, c] += nn(kt_ref[h], ds)
        return 0

    for h in range(heads):
        dkt_ref[h] = zero
        dvt_ref[h] = zero
    lax.fori_loop(lo_ref[j], hi_ref[j], step, 0)
    for h in range(heads):
        for part, ref in ((1, dkt_ref), (2, dvt_ref)):
            at = (part * heads + h) * HD
            out_ref[pl.ds(pl.multiple_of(j * bk, bk), bk), at : at + HD] = ref[h].T.astype(BF)

    @pl.when(j == pl.num_programs(0) - 1)
    def _():
        for h in range(heads):
            for c in range(rows // 512):
                sl = pl.ds(c * 512, 512)
                out_ref[sl, h * HD : (h + 1) * HD] = (dqt_ref[h, :, c * 512 : (c + 1) * 512].T * (HD ** -0.5)).astype(BF)


def attend_back(qb, ke, ve, go, att, lo, hi, bq, bk):
    heads, rows, _ = qb.shape
    full3 = lambda i, lo, hi: (0, 0, 0)
    full2 = lambda i, lo, hi: (0, 0)
    blk3 = lambda i, lo, hi: (0, i, 0)
    wide = heads * HD
    return pl.pallas_call(
        functools.partial(bwd_kernel, heads, bq, bk),
        grid_spec=pltpu.PrefetchScalarGridSpec(
            num_scalar_prefetch=2,
            grid=(rows // bk,),
            in_specs=[
                pl.BlockSpec((heads, rows, LANES), full3),
                pl.BlockSpec((heads, bk, LANES), blk3),
                pl.BlockSpec((heads, bk, LANES), blk3),
                pl.BlockSpec((rows, wide), full2),
                pl.BlockSpec((rows, wide), full2),
            ],
            out_specs=pl.BlockSpec((rows, 3 * wide), full2),
            scratch_shapes=[
                pltpu.VMEM((heads, rows, LANES), BF),
                pltpu.VMEM((heads, HD, rows), F32),
                pltpu.VMEM((heads, HD, bk), BF),
                pltpu.VMEM((heads, HD, rows), BF),
                pltpu.VMEM((heads, HD, rows), BF),
                pltpu.VMEM((heads, HD, bk), F32),
                pltpu.VMEM((heads, HD, bk), F32),
            ],
        ),
        out_shape=jax.ShapeDtypeStruct((rows, 3 * wide), BF),
        compiler_params=pltpu.CompilerParams(vmem_limit_bytes=60 << 20),
        name="attend_back",
    )(lo, hi, qb, ke, ve, go, att)


def dot_f32(a, b, dims):
    return lax.dot_general(a, b, ((dims[:1], dims[1:]), ((), ())), precision=highest, preferred_element_type=F32)


def soap_group(base, group, gr_ref, w_ref, m1_ref, m2_ref, av_ref, st_ref, ba_ref,
               nw_ref, n1_ref, n2_ref, na_ref, ns_ref, nb_ref, aug_ref):
    size = w_ref.shape[-1]
    half = size // 2
    panel = 8
    every = range(group)
    grads, firsts = [], []
    for s in every:
        rows = slice((base + s) * half, (base + s + 1) * half)
        wire = gr_ref[rows, :]
        grads.append(jnp.concatenate([wire[:, :size], wire[:, size:]], axis=0))
        firsts.append(beta_one * m1_ref[0, base + s] + (1.0 - beta_one) * grads[s])
        n1_ref[0, base + s] = firsts[s]
    sides = [(s, side) for s in every for side in range(2)]
    outers = [dot_f32(grads[s], grads[s], (1, 1) if side == 0 else (0, 0)) for s, side in sides]
    both = [dot_f32(jnp.concatenate([grads[s], firsts[s]], axis=0), ba_ref[0, base + s, 1], (1, 0)) for s in every]
    stats = []
    for (s, side), outer in zip(sides, outers):
        stats.append(beta_two * st_ref[0, base + s, side] + (1.0 - beta_two) * outer)
        ns_ref[0, base + s, side] = stats[-1]
    pairs = [dot_f32(ba_ref[0, base + s, 0], jnp.concatenate([both[s][:size], both[s][size:]], axis=1), (0, 0)) for s in every]
    mts = [dot_f32(ba_ref[0, base + s, side], stat, (0, 1)) for (s, side), stat in zip(sides, stats)]
    scaled = []
    for s in every:
        rotated, moment = pairs[s][:, :size], pairs[s][:, size:]
        second = beta_two * m2_ref[0, base + s] + (1.0 - beta_two) * rotated * rotated
        n2_ref[0, base + s] = second
        scaled.append(moment / (jnp.sqrt(second) + step_eps))
    grams = [dot_f32(mt, mt, (1, 1)) for mt in mts]
    inner = [dot_f32(scaled[s], ba_ref[0, base + s, 1], (1, 1)) for s in every]
    for m, (gram, mt) in enumerate(zip(grams, mts)):
        aug_ref[m] = jnp.concatenate([gram, mt], axis=1)
    directions = [dot_f32(ba_ref[0, base + s, 0], inner[s], (1, 0)) for s in every]
    for s in every:
        weight = w_ref[0, base + s]
        fresh = weight - step_rate * (directions[s] + weight_decay * weight)
        nw_ref[0, base + s] = fresh
        na_ref[0, base + s] = average_keep * av_ref[0, base + s] + (1.0 - average_keep) * fresh
    count = 2 * group
    row = lax.broadcasted_iota(jnp.int32, (count, panel, LANES), 1)
    for p in range(size // panel):
        top = p * panel
        part = aug_ref[:, top : top + panel, :]
        for r in range(panel):
            pivot = lax.rsqrt(part[:, r : r + 1, top + r : top + r + 1])
            lead = part[:, r : r + 1, :] * pivot
            column = jnp.where(row > r, part[:, :, top + r : top + r + 1] * pivot, 0.0)
            part = jnp.where(row == r, lead, part - column * lead)
        aug_ref[:, top : top + panel, :] = part
        below = top + panel
        if below < size:
            high = part.astype(BF).astype(F32)
            rest = part - high
            mid = rest.astype(BF).astype(F32)
            low = rest - mid
            first = jnp.concatenate([high, high, mid, high, mid, low], axis=1).astype(BF)
            other = jnp.concatenate([high, mid, high, low, mid, high], axis=1).astype(BF)
            for m in range(count):
                aug_ref[m, below:, :] -= lax.dot_general(
                    first[m][:, below:size], other[m], (((0,), (0,)), ((), ())), preferred_element_type=F32
                )
    for s in range(group):
        for side in range(2):
            nb_ref[0, base + s, side] = aug_ref[2 * s + side][:, size:].T


MESH = pl.DeviceIdType.MESH


def normalize(values):
    center = jnp.mean(values, axis=-1, keepdims=True)
    centered = values - center
    variance = jnp.mean(centered * centered, axis=-1, keepdims=True)
    scale = lax.rsqrt(variance + norm_eps)
    return centered * scale, scale


def norm_back(grad, xhat, scale):
    along = jnp.mean(grad * xhat, axis=-1, keepdims=True)
    return (grad - jnp.mean(grad, axis=-1, keepdims=True) - xhat * along) * scale


TAIL = 0.305
TAIL_FIT = (
    0.1216397411342051,
    0.12246669816059132,
    0.10342157025713879,
    0.1210193967312446,
    -0.037972477455618554,
    0.18571204369074895,
    -0.15298537812807472,
    0.036698452375741396,
)


def gelu_pair(u):
    size = jnp.abs(u)
    bell = jnp.exp(-0.5 * u * u)
    t = 1.0 / (1.0 + TAIL * size)
    poly = jnp.full_like(t, TAIL_FIT[-1])
    for c in TAIL_FIT[-2::-1]:
        poly = poly * t + c
    upper = poly * t * bell
    cdf = jnp.where(u > 0.0, 1.0 - upper, upper)
    return u * cdf, cdf + (0.3989422804014327 * u) * bell


def block_rows(ref, start, half):
    return ref[pl.ds(pl.multiple_of(start, 16), half), :]


def project_kernel(heads, rows_dev, gains_at, row_ref, wire_ref, tok_ref, seg_ref, pad_ref, gain_ref,
                   norm_ref, qe_ref, ke_ref, ve_ref, vt_ref, mix_ref, wide_ref):
    width = tok_ref.shape[1]
    half = HD // 2
    cols = 3 * heads

    @pl.when(pl.program_id(0) == 0)
    def _():
        zero = jnp.zeros((half, HD), BF)

        def fill(r, _):
            low = pl.multiple_of(r * HD, HD)
            for c in range(cols):
                t = block_rows(wire_ref, row_ref[r * cols + c], half)
                for part in range(2):
                    piece = t[:, part * HD : (part + 1) * HD]
                    at = pl.ds(low + part * half, half)
                    wide_ref[at, c * LANES : (c + 1) * LANES] = jnp.concatenate([piece, zero], axis=1)
                    mix_ref[at, c * HD : (c + 1) * HD] = piece
            return 0

        lax.fori_loop(0, width // HD, fill, 0)

    xhat, _ = normalize(tok_ref[...].astype(F32))
    normed = (xhat * gain_ref[...]).astype(BF)
    norm_ref[...] = normed
    count = tok_ref.shape[0]
    lane = lax.broadcasted_iota(jnp.int32, (LANES, count), 0)
    seg = seg_ref[...]
    same = lane - HD == seg
    in_segs = (lane >= HD) & (lane < HD + SEGS)
    ones = (lane >= HD + SEGS) & (lane < HD + SEGS + 3)
    ext_q = jnp.where(same, 1.0, 0.0).T
    ext_k = jnp.where(in_segs, jnp.where(same & (pad_ref[...] > 0.5), 0.0, NEG), jnp.where(ones, 1.0, 0.0)).T
    ext_v = jnp.where((lane >= HD) & (lane < HD + 3), 1.0, 0.0).T
    for h in range(heads):
        for ref, part, scale, ext in ((qe_ref, 0, HD ** -0.5, ext_q), (ke_ref, 1, 1.0, ext_k), (ve_ref, 2, 1.0, ext_v)):
            c = part * heads + h
            mixed = nn(normed, wide_ref[:, c * LANES : (c + 1) * LANES]).astype(BF)
            out = (mixed.astype(F32) * scale + ext).astype(BF)
            ref[h] = out
            if part == 2:
                vt_ref[h] = out.T[:VT]


def project(wire, row_own, tokens, seg, pad, gain_one, heads):
    rows, width = tokens.shape
    tb = min(512, rows)
    full = lambda i, r: (0, 0)
    blk = lambda i, r: (i, 0)
    col = lambda i, r: (0, i)
    ext = lambda i, r: (0, i, 0)
    out = lambda *s: jax.ShapeDtypeStruct(s, BF)
    return pl.pallas_call(
        functools.partial(project_kernel, heads, 0, 0),
        grid_spec=pltpu.PrefetchScalarGridSpec(
            num_scalar_prefetch=1,
            grid=(rows // tb,),
            in_specs=[
                pl.BlockSpec(wire.shape, full),
                pl.BlockSpec((tb, width), blk),
                pl.BlockSpec((1, tb), col),
                pl.BlockSpec((1, tb), col),
                pl.BlockSpec((1, width), full),
            ],
            out_specs=[
                pl.BlockSpec((tb, width), blk),
                pl.BlockSpec((heads, tb, LANES), ext),
                pl.BlockSpec((heads, tb, LANES), ext),
                pl.BlockSpec((heads, tb, LANES), ext),
                pl.BlockSpec((heads, VT, tb), lambda i, r: (0, 0, i)),
                pl.BlockSpec((width, 3 * heads * HD), full),
            ],
            scratch_shapes=[pltpu.VMEM((width, 3 * heads * LANES), BF)],
        ),
        out_shape=[
            out(rows, width),
            out(heads, rows, LANES),
            out(heads, rows, LANES),
            out(heads, rows, LANES),
            out(heads, VT, rows),
            out(width, 3 * heads * HD),
        ],
        compiler_params=pltpu.CompilerParams(vmem_limit_bytes=60 << 20),
        name="project",
    )(row_own, wire, tokens, seg, pad, gain_one)


def middle_kernel(shards, span, units, rows_dev, wide, gain_row, gains_dev,
                  here_ref, row_ref, wire_ref, att_ref, tok_ref, cot_ref, pad_ref, gain_ref,
                  out_ref, res_ref, back_ref, grads_ref, mix_ref,
                  wo_ref, wu_ref, wd_ref, go_ref, gu_ref, gd_ref, gg_ref):
    width = tok_ref.shape[1]
    half = HD // 2
    kinds = (
        (mix_ref, None, width, 3 * span),
        (wo_ref, go_ref, span, width),
        (wu_ref, gu_ref, width, units),
        (wd_ref, gd_ref, units, width),
    )

    @pl.when(pl.program_id(0) == 0)
    def _():
        base = 0
        for ref, acc, rows, cols in kinds:
            grid_cols = cols // HD

            def fill(r, _, ref=ref, base=base, grid_cols=grid_cols):
                low = pl.multiple_of(r * HD, HD)
                for n in range(shards):
                    for c in range(grid_cols):
                        t = block_rows(wire_ref, row_ref[base + r * grid_cols + c] + n * rows_dev, half)
                        for part in range(2):
                            ref[n, pl.ds(low + part * half, half), c * HD : (c + 1) * HD] = t[:, part * HD : (part + 1) * HD]
                return 0

            lax.fori_loop(0, rows // HD, fill, 0)
            base += rows // HD * grid_cols
            if acc is not None:
                acc[...] = jnp.zeros_like(acc)
        gg_ref[...] = jnp.zeros_like(gg_ref)

    tokens = tok_ref[...].astype(F32)
    cot = cot_ref[...]
    branch = nn(att_ref[0], wo_ref[0])
    for n in range(1, shards):
        branch += nn(att_ref[n], wo_ref[n])
    residual = tokens + branch
    xhat, scale = normalize(residual)
    gain = gain_ref[...]
    normed = (xhat * gain).astype(BF)
    mlp = jnp.zeros_like(residual)
    back = jnp.zeros_like(residual)
    for n in range(shards):
        value, slope = gelu_pair(nn(normed, wu_ref[n]))
        active = value.astype(BF)
        mlp += nn(active, wd_ref[n])
        gd_ref[n] += tn(active, cot)
        back_up = (slope * nt(cot, wd_ref[n])).astype(BF)
        gu_ref[n] += tn(normed, back_up)
        back += nt(back_up, wu_ref[n])
    out_ref[...] = (residual + mlp).astype(BF)
    gg_ref[...] += jnp.sum(back * xhat, axis=0, keepdims=True)
    back_res = cot.astype(F32) + norm_back(back * gain, xhat, scale)
    res_ref[...] = back_res
    branch_low = back_res.astype(BF)
    pad = jnp.broadcast_to(pad_ref[...], (8, pad_ref.shape[1])).T[:, :1]
    for n in range(shards):
        go_ref[n] += tn(att_ref[n], branch_low)
        back_ref[n] = (nt(branch_low, wo_ref[n]) * pad).astype(BF)

    @pl.when(pl.program_id(0) == pl.num_programs(0) - 1)
    def _():
        grads_ref[...] = jnp.zeros_like(grads_ref)
        base = 0
        for ref, acc, rows, cols in kinds:
            grid_cols = cols // HD
            if acc is not None:

                def scatter(r, _, acc=acc, base=base, grid_cols=grid_cols):
                    low = pl.multiple_of(r * HD, HD)
                    for n in range(shards):
                        for c in range(grid_cols):
                            at = row_ref[base + r * grid_cols + c] + n * rows_dev
                            cut = slice(c * HD, (c + 1) * HD)
                            value = jnp.concatenate([acc[n, pl.ds(low, half), cut], acc[n, pl.ds(low + half, half), cut]], axis=1)
                            grads_ref[pl.ds(pl.multiple_of(at, 16), half), :] = value.astype(BF)
                    return 0

                lax.fori_loop(0, rows // HD, scatter, 0)
            base += rows // HD * grid_cols
        for w in range(wide):
            piece = w * gains_dev // LANES - width // LANES
            if piece >= 0:
                for n in range(shards):
                    at = (w * shards + n) * rows_dev + gain_row
                    grads_ref[at : at + 1, :] = gg_ref[:, piece * LANES : (piece + 1) * LANES].astype(BF)


def middle(here, row_full, wire, att, tokens, cotangent, pad, gain_two, wide, rows_dev, gain_row, gains_dev):
    shards, own, span = att.shape
    width = tokens.shape[1]
    units = FF // shards
    tb = min(256, own)
    steps = own // tb
    full = lambda i, h, r: (0, 0)
    full3 = lambda i, h, r: (0, 0, 0)
    mine = lambda i, h, r: (h[0] * steps + i, 0)
    blk = lambda i, h, r: (i, 0)
    blk3 = lambda i, h, r: (0, i, 0)
    once = pl.Buffered(1)
    return pl.pallas_call(
        functools.partial(middle_kernel, shards, span, units, rows_dev, wide, gain_row, gains_dev),
        grid_spec=pltpu.PrefetchScalarGridSpec(
            num_scalar_prefetch=2,
            grid=(steps,),
            in_specs=[
                pl.BlockSpec(wire.shape, full, pipeline_mode=once),
                pl.BlockSpec((shards, tb, span), blk3),
                pl.BlockSpec((tb, width), mine),
                pl.BlockSpec((tb, width), mine),
                pl.BlockSpec((1, tb), lambda i, h, r: (0, h[0] * steps + i)),
                pl.BlockSpec((1, width), full),
            ],
            out_specs=[
                pl.BlockSpec((tb, width), blk),
                pl.BlockSpec((tb, width), blk),
                pl.BlockSpec((shards, tb, span), blk3),
                pl.BlockSpec(wire.shape, full, pipeline_mode=once),
                pl.BlockSpec((shards, width, 3 * span), full3, pipeline_mode=once),
            ],
            scratch_shapes=[
                pltpu.VMEM((shards, span, width), BF),
                pltpu.VMEM((shards, width, units), BF),
                pltpu.VMEM((shards, units, width), BF),
                pltpu.VMEM((shards, span, width), F32),
                pltpu.VMEM((shards, width, units), F32),
                pltpu.VMEM((shards, units, width), F32),
                pltpu.VMEM((1, width), F32),
            ],
        ),
        out_shape=[
            jax.ShapeDtypeStruct((own, width), BF),
            jax.ShapeDtypeStruct((own, width), F32),
            jax.ShapeDtypeStruct((shards, own, span), BF),
            jax.ShapeDtypeStruct(wire.shape, BF),
            jax.ShapeDtypeStruct((shards, width, 3 * span), BF),
        ],
        compiler_params=pltpu.CompilerParams(vmem_limit_bytes=60 << 20),
        name="middle",
    )(here, row_full, wire, att, tokens, cotangent, pad, gain_two)


PARTS = 4


def finish_kernel(shards, wide, gain_row, gains_dev, group, sel_ref, mix_ref, full_ref, gain_ref, res_ref, bm_ref, norm_ref, tok_ref, *refs):
    states, outs = refs[1:7], refs[9:15]
    first_ref, grad_ref, line_ref = refs[0], refs[7], refs[8]
    (own_ref, normed_ref, tokens_ref, got_ref, acc_ref, blk_ref, grads_ref, sums_ref, firsts_ref, part_ref, aug_ref,
     local_sem, send_z, recv_z, send_w, recv_w, send_a, recv_a, send_g, recv_g, send_f, recv_f) = refs[15:]
    width = norm_ref.shape[1]
    rows, cols = bm_ref.shape
    own = rows // shards
    hold = own // PARTS
    half = HD // 2
    grid_cols = cols // HD
    blocks = width // HD * grid_cols
    slots = gain_row // half
    z = lax.axis_index("narrow")
    w = lax.axis_index("wide")

    barrier = pltpu.get_barrier_semaphore()
    for d in range(1, shards):
        pl.semaphore_signal(barrier, inc=1, device_id={"narrow": lax.rem(z + d, shards)}, device_id_type=MESH)
    for d in range(1, wide):
        pl.semaphore_signal(barrier, inc=1, device_id={"wide": lax.rem(w + d, wide)}, device_id_type=MESH)
    pl.semaphore_wait(barrier, shards + wide - 2)

    def to_peer(d, part, mine):
        peer = lax.rem(z + d, shards)
        slot = z if mine else peer
        at = pl.multiple_of(peer * own + part * hold, hold)
        return pltpu.make_async_remote_copy(
            src_ref=bm_ref.at[pl.ds(at, hold), :],
            dst_ref=got_ref.at[slot, pl.ds(part * hold, hold), :],
            send_sem=send_z.at[d - 1, part],
            recv_sem=recv_z.at[slot, part],
            device_id={"narrow": peer},
            device_id_type=MESH,
        )

    def to_owner(d, mine):
        peer = lax.rem(w + d, wide)
        slot = w if mine else peer
        return pltpu.make_async_remote_copy(
            src_ref=grads_ref.at[peer],
            dst_ref=sums_ref.at[slot],
            send_sem=send_w.at[d - 1],
            recv_sem=recv_w.at[slot],
            device_id={"wide": peer},
            device_id_type=MESH,
        )

    def hop_copy(c, part, step):
        at = pl.ds(pl.multiple_of(c * own + part * hold, hold), hold)
        return pltpu.make_async_remote_copy(
            src_ref=grad_ref.at[at, :],
            dst_ref=grad_ref.at[at, :],
            send_sem=send_a.at[step, c, part],
            recv_sem=recv_a.at[c, part],
            device_id={"narrow": lax.rem(z + (1 if step == 0 else shards - 1), shards)},
            device_id_type=MESH,
        )

    def pass_on(c, part, act):
        for step, there in ((0, z < shards - 1), (1, z > 0)):
            if c is None or step == c[0]:
                chunk = z if c is None else c[1]
                ok = there if c is None else there & c[2]

                @pl.when(ok)
                def _(chunk=chunk, step=step):
                    act(hop_copy(chunk, part, step))

    def line_to(d, mine):
        peer = lax.rem(z + d, shards)
        slot = z if mine else peer
        return pltpu.make_async_remote_copy(
            src_ref=line_ref.at[z],
            dst_ref=line_ref.at[slot],
            send_sem=send_g.at[d - 1],
            recv_sem=recv_g.at[slot],
            device_id={"narrow": peer},
            device_id_type=MESH,
        )

    rows_dev = part_ref.shape[0]

    def first_to(d, mine):
        peer = lax.rem(z + d, shards)
        slot = z if mine else peer
        return pltpu.make_async_remote_copy(
            src_ref=first_ref.at[pl.ds(pl.multiple_of(peer * rows_dev, 16), rows_dev), :],
            dst_ref=firsts_ref.at[slot],
            send_sem=send_f.at[d - 1],
            recv_sem=recv_f.at[slot],
            device_id={"narrow": peer},
            device_id_type=MESH,
        )

    for d in range(1, shards):
        first_to(d, True).start()
    for part in range(PARTS):
        for d in range(1, shards):
            to_peer(d, part, True).start()
    mine = pl.ds(pl.multiple_of(z * own, own), own)
    copies = [
        pltpu.make_async_copy(bm_ref, own_ref, local_sem.at[0]),
        pltpu.make_async_copy(norm_ref, normed_ref, local_sem.at[1]),
        pltpu.make_async_copy(tok_ref.at[mine, :], tokens_ref, local_sem.at[2]),
        pltpu.make_async_copy(bm_ref.at[mine, :], got_ref.at[z], local_sem.at[3]),
        pltpu.make_async_copy(
            first_ref.at[pl.ds(pl.multiple_of(z * rows_dev, 16), rows_dev), :], firsts_ref.at[z], local_sem.at[4]
        ),
    ]
    for copy in copies:
        copy.start()
    for copy in copies:
        copy.wait()

    acc_ref[...] = jnp.zeros_like(acc_ref)
    tb = min(512, rows)

    def add(i, _):
        at = pl.ds(pl.multiple_of(i * tb, tb), tb)
        acc_ref[...] += tn(normed_ref[at, :], own_ref[at, :])
        return 0

    lax.fori_loop(0, rows // tb, add, 0)
    blk_ref[blocks] = jnp.zeros((half, LANES), BF)

    def cut(r, _):
        low = pl.multiple_of(r * HD, HD)
        for c in range(grid_cols):
            lanes = slice(c * HD, (c + 1) * HD)
            value = jnp.concatenate([acc_ref[pl.ds(low, half), lanes], acc_ref[pl.ds(low + half, half), lanes]], axis=1)
            blk_ref[r * grid_cols + c] = value.astype(BF)
        return 0

    lax.fori_loop(0, width // HD, cut, 0)
    along = jnp.sum(acc_ref[...] * mix_ref[...].astype(F32), axis=1, keepdims=True)
    line = jnp.broadcast_to(along, (width, LANES)).T[:16] / gain_ref[...]
    top = lax.broadcasted_iota(jnp.int32, (16, LANES), 0) == 0
    for v in range(wide):

        def place(i, _, v=v):
            grads_ref[v, pl.ds(pl.multiple_of(i * half, half), half), :] = blk_ref[sel_ref[v * slots + i]]
            return 0

        lax.fori_loop(0, slots, place, 0)
        piece = v * gains_dev // LANES
        if piece < width // LANES:
            value = jnp.where(top, line[:, piece * LANES : (piece + 1) * LANES], 0.0).astype(BF)
        else:
            value = jnp.zeros((16, LANES), BF)
        grads_ref[v, gain_row : gain_row + 16, :] = value
    for d in range(1, wide):
        to_owner(d, True).start()
    part_ref[...] = grads_ref[w].astype(F32)

    tile = min(256, hold)

    def norm_rows(i, _):
        at = pl.ds(pl.multiple_of(i * tile, tile), tile)
        back = nt(got_ref[0, at, :], full_ref[0])
        for n in range(1, shards):
            back += nt(got_ref[n, at, :], full_ref[n])
        xhat, scale = normalize(tokens_ref[at, :].astype(F32))
        grad = res_ref[at, :] + norm_back(back * gain_ref[...], xhat, scale)
        grad_ref[pl.ds(pl.multiple_of(z * own + i * tile, tile), tile), :] = grad.astype(BF)
        return 0

    def norm_part(part):
        for d in range(1, shards):
            to_peer(d, part, False).wait_recv()
        lax.fori_loop(part * hold // tile, (part + 1) * hold // tile, norm_rows, 0)
        pass_on(None, part, lambda copy: copy.start())

    for d in range(1, wide):
        to_owner(d, False).wait_recv()
    for d in range(1, wide):
        part_ref[...] += sums_ref[lax.rem(w + d, wide)].astype(F32)
    line_ref[z] = part_ref[gain_row : gain_row + 16, :]
    for d in range(1, shards):
        line_to(d, True).start()
    for d in range(1, shards):
        first_to(d, False).wait_recv()
    total = firsts_ref[0].astype(F32)
    for n in range(1, shards):
        total += firsts_ref[n].astype(F32)
    line_ref[shards] = total[gain_row : gain_row + 16, :]
    part_ref[...] += total
    ready = 0
    rounds = slots // group
    for g in range(rounds):
        soap_group(g * group, group, part_ref, *states, *outs, aug_ref)
        upto = PARTS * (g + 1) // rounds
        while ready < upto:
            norm_part(ready)
            ready += 1
    hops = [(s, part, step) for s in range(1, shards) for part in range(PARTS) for step in range(2)]
    for s, part, step in hops:
        chunk = z - s if step == 0 else z + s
        there = chunk >= 0 if step == 0 else chunk < shards

        @pl.when(there)
        def _(chunk=chunk, part=part, step=step):
            hop_copy(chunk, part, step).wait_recv()

        pass_on((step, chunk, there), part, lambda copy: copy.start())
    for d in range(1, shards):
        line_to(d, False).wait_recv()
    for part in range(PARTS):
        pass_on(None, part, lambda copy: copy.wait_send())
    for s, part, step in hops:
        chunk = z - s if step == 0 else z + s
        there = chunk >= 0 if step == 0 else chunk < shards
        pass_on((step, chunk, there), part, lambda copy: copy.wait_send())
    for d in range(1, shards):
        line_to(d, True).wait_send()
        first_to(d, True).wait_send()
    for part in range(PARTS):
        for d in range(1, shards):
            to_peer(d, part, True).wait_send()
    for d in range(1, wide):
        to_owner(d, True).wait_send()


def finish(sel, mix, mix_full, gain_one, res, bm, normed, tokens, states, group, wide, rows_dev, gain_row, gains_dev):
    shards = mix_full.shape[0]
    rows, cols = bm.shape
    width = normed.shape[1]
    own = rows // shards
    half = HD // 2
    blocks = width // HD * (cols // HD)
    vmem = pl.BlockSpec(memory_space=pltpu.VMEM)
    smem = pl.BlockSpec(memory_space=pltpu.SMEM)
    hbm = pl.BlockSpec(memory_space=pl.ANY)
    dma = pltpu.SemaphoreType.DMA
    return pl.pallas_call(
        functools.partial(finish_kernel, shards, wide, gain_row, gains_dev, group),
        in_specs=[smem, vmem, vmem, vmem, vmem, hbm, hbm, hbm, hbm] + [vmem] * 6,
        out_specs=[vmem] * 8,
        out_shape=[jax.ShapeDtypeStruct((rows, width), BF), jax.ShapeDtypeStruct((shards + 1, 16, LANES), F32)]
        + [jax.ShapeDtypeStruct(a.shape, a.dtype) for a in states[1:]],
        scratch_shapes=[
            pltpu.VMEM((rows, cols), BF),
            pltpu.VMEM((rows, width), BF),
            pltpu.VMEM((own, width), BF),
            pltpu.VMEM((shards, own, cols), BF),
            pltpu.VMEM((width, cols), F32),
            pltpu.VMEM((blocks + 1, half, LANES), BF),
            pltpu.VMEM((wide, rows_dev, LANES), BF),
            pltpu.VMEM((wide, rows_dev, LANES), BF),
            pltpu.VMEM((shards, rows_dev, LANES), BF),
            pltpu.VMEM((rows_dev, LANES), F32),
            pltpu.VMEM((2 * group, HD, LANES), F32),
            dma((5,)),
            dma((shards - 1, PARTS)),
            dma((shards, PARTS)),
            dma((wide - 1,)),
            dma((wide,)),
            dma((2, shards, PARTS)),
            dma((shards, PARTS)),
            dma((shards - 1,)),
            dma((shards,)),
            dma((shards - 1,)),
            dma((shards,)),
        ],
        compiler_params=pltpu.CompilerParams(vmem_limit_bytes=62 << 20, collective_id=1, has_side_effects=True),
        name="finish",
    )(sel, mix, mix_full, gain_one, res, bm, normed, tokens, *states)


def adam_gains(grad, gain, first, second, average):
    new_first = beta_one * first + (1.0 - beta_one) * grad
    new_second = beta_two * second + (1.0 - beta_two) * grad * grad
    new_gain = gain - gain_rate * new_first / (jnp.sqrt(new_second) + step_eps)
    new_average = average_keep * average + (1.0 - average_keep) * new_gain
    return (new_gain, new_first, new_second, new_average)


def to_shards(values, shards):
    rows, cols = values.shape
    return lax.all_to_all(values.reshape(shards, rows // shards, cols), "narrow", 0, 0)


def body(
    tokens,
    cotangent,
    segment_ids,
    pad_mask,
    owner_order,
    weights,
    first_moment,
    second_moment,
    average,
    stats,
    bases,
    gains,
    gain_first,
    gain_second,
    gain_average,
):
    narrow = lax.axis_size("narrow")
    wide = lax.axis_size("wide")
    here = lax.axis_index("narrow")
    heads = HEADS // narrow
    rows, width = tokens.shape
    span = heads * HD
    own = rows // narrow
    slots, size = weights.shape[1], weights.shape[2]
    half = size // 2
    block_count = owner_order.shape[0]
    gains_dev = gains.shape[0]
    gain_row = slots * half
    rows_dev = gain_row + 16

    low = weights[0].astype(BF)
    wire = jnp.concatenate([low[:, :half], low[:, half:]], axis=2).reshape(gain_row, 2 * size)
    wire = jnp.concatenate([wire, jnp.pad(gains.astype(BF)[None], ((0, 15), (0, LANES - gains_dev)))], axis=0)
    wire_own = lax.all_gather(wire, "wide", axis=0, tiled=True)
    wire_full = lax.all_gather(lax.all_gather(wire, "narrow", axis=0, tiled=True), "wide", axis=0, tiled=True)

    ids = jnp.arange(block_count, dtype=jnp.int32)
    slot_of = jnp.sum(jnp.where(owner_order[None, :] == ids[:, None], ids[None, :], 0), axis=1)
    device, place = slot_of // slots, slot_of % slots
    row_own = device * rows_dev + place * half
    row_full = device * (narrow * rows_dev) + place * half
    here_of = jnp.full((1,), here, jnp.int32)

    gain_all = wire_own.reshape(wide, rows_dev, LANES)[:, gain_row, :gains_dev].astype(F32).reshape(1, 2 * width)
    gain_one, gain_two = gain_all[:, :width], gain_all[:, width:]
    seg = segment_ids
    seg_row = segment_ids[0]
    pad = pad_mask.astype(F32)
    block = min(512, rows)
    low_seg = seg_row[::block]
    high_seg = seg_row[block - 1 :: block]
    begin = jnp.sum((seg_row[None, :] < low_seg[:, None]).astype(jnp.int32), axis=1) // block
    end = (jnp.sum((seg_row[None, :] <= high_seg[:, None]).astype(jnp.int32), axis=1) + block - 1) // block

    normed, qe, ke, ve, vt, mix = project(wire_own, row_own, tokens, seg, pad, gain_one, heads)
    attended, qb = attend(qe, ke, vt, pad, begin, end, block, block)
    att_own = to_shards(attended, narrow)
    out_own, back_res, back_own, grads, mix_full = middle(
        here_of, row_full, wire_full, att_own, tokens, cotangent, pad, gain_two, wide, rows_dev, gain_row, gains_dev
    )
    part_a = lax.psum_scatter(grads, "wide", scatter_dimension=0, tiled=True)
    back_att = lax.all_to_all(back_own, "narrow", 0, 0).reshape(rows, span)
    out_own, back_att = lax.optimization_barrier((out_own, back_att))
    output = lax.all_to_all(jnp.broadcast_to(out_own, (narrow, own, width)), "narrow", 0, 0).reshape(rows, width)
    bm = attend_back(qb, ke, ve, back_att, attended, begin, end, block, block)
    bm, part_a, output = lax.optimization_barrier((bm, part_a, output))
    sel = jnp.minimum(owner_order, width // size * 3 * heads)
    group = next(g for g in range(min(12, slots), 0, -1) if slots % g == 0)
    states = (part_a, weights, first_moment, second_moment, average, stats, bases)
    grad_all, lines, new_weight, new_first, new_second, new_average, new_stats, new_bases = finish(
        sel, mix, mix_full, gain_one, back_res, bm, normed, tokens, states, group, wide, rows_dev, gain_row, gains_dev
    )
    input_grad = grad_all.astype(F32)
    line = jnp.sum(lines[:, 0], axis=0)
    offset = lax.axis_index("wide") * gains_dev % LANES
    own_gain = lax.dynamic_slice_in_dim(line, offset, gains_dev, 0)
    new_gains, gain_moment, gain_square, gain_mean = adam_gains(own_gain, gains, gain_first, gain_second, gain_average)
    return (
        output,
        input_grad,
        new_weight,
        new_first,
        new_second,
        new_average,
        new_stats,
        new_bases,
        new_gains,
        gain_moment,
        gain_square,
        gain_mean,
    )


def solution(mesh):
    block = P("narrow", "wide", None, None)
    pair = P("narrow", "wide", None, None, None)
    rows = P("wide", None)
    line = P("wide")
    return jax.shard_map(
        body,
        mesh=mesh,
        in_specs=(rows, rows, rows, rows, P(), block, block, block, block, pair, pair, line, line, line, line),
        out_specs=(rows, rows, block, block, block, block, pair, pair, line, line, line, line),
        check_vma=False,
    )
```

```python
import functools

import jax
import jax.numpy as jnp
from jax import lax
from jax.experimental import pallas as pl
from jax.experimental.pallas import tpu as pltpu
from jax.sharding import PartitionSpec as P

HEADS = 8
HD = 64
FF = 2048
LANES = 128
SEGS = 4
NEG = -1e30
F32 = jnp.float32
BF = jnp.bfloat16
highest = lax.Precision.HIGHEST

beta_one = 0.9
beta_two = 0.95
step_rate = 0.1
gain_rate = 0.75
weight_decay = 0.01
average_keep = 0.5
norm_eps = 1e-05
step_eps = 1e-08


def nt(a, b):
    return lax.dot_general(a, b, (((1,), (1,)), ((), ())), preferred_element_type=F32)


def nn(a, b):
    return lax.dot_general(a, b, (((1,), (0,)), ((), ())), preferred_element_type=F32)


def tn(a, b):
    return lax.dot_general(a, b, (((0,), (0,)), ((), ())), preferred_element_type=F32)


def split3(x):
    hi = x.astype(BF)
    r = x - hi.astype(F32)
    mid = r.astype(BF)
    lo = (r - mid.astype(F32)).astype(BF)
    return hi, mid, lo


def put3(base, x, lane0):
    lane = lax.broadcasted_iota(jnp.int32, base.shape, 1)
    hi, mid, lo = split3(x)
    out = jnp.where(lane == lane0, hi.astype(F32), base.astype(F32))
    out = jnp.where(lane == lane0 + 1, mid.astype(F32), out)
    out = jnp.where(lane == lane0 + 2, lo.astype(F32), out)
    return out.astype(BF)


VT = 80
QC, AHEAD, QB, BAHEAD = 512, 1, 256, 1


def fwd_kernel(heads, bq, bk, lo_ref, hi_ref, qe_ref, ke_ref, vt_ref, pad_ref, att_ref, qb_ref, m_ref, acc_ref):
    i = pl.program_id(0)
    row0 = pl.multiple_of(i * bq, bq)
    real = pad_ref[...] > 0.5
    for h in range(heads):
        qt = qe_ref[h].astype(F32).T[:HD]
        kt = ke_ref[h, pl.ds(row0, bq), :].astype(F32).T[:HD]
        own = jnp.sum(qt * kt, axis=0, keepdims=True)
        m_ref[h] = jnp.where(real, NEG, own)
        acc_ref[h] = jnp.where(real, 0.0, vt_ref[h, :, pl.ds(row0, bq)].astype(F32))

    def step(j, _):
        col0 = pl.multiple_of(j * bk, bk)
        work = [(h, slice(c, c + QC)) for c in range(0, bq, QC) for h in range(heads)]
        score = lambda h, c: nt(ke_ref[h, pl.ds(col0, bk), :], qe_ref[h, c, :])
        ss = [score(*w) for w in work[:AHEAD]]
        for n, (h, c) in enumerate(work):
            if n + AHEAD < len(work):
                ss.append(score(*work[n + AHEAD]))
            s = ss[n]
            m_old = m_ref[h, :, c]
            m_new = jnp.maximum(m_old, jnp.max(s, axis=0, keepdims=True))
            p = jnp.exp(s - m_new).astype(BF)
            alpha = jnp.exp(m_old - m_new)
            acc_ref[h, :, c] = acc_ref[h, :, c] * alpha + nn(vt_ref[h, :, pl.ds(col0, bk)], p)
            m_ref[h, :, c] = m_new
        return 0

    lax.fori_loop(lo_ref[i], hi_ref[i], step, 0)
    outs = []
    for h in range(heads):
        acc = acc_ref[h]
        total = acc[HD : HD + 1]
        outs.append(jnp.where(real, acc[:HD] / total, 0.0))
        lse = jnp.broadcast_to(m_ref[h] + jnp.log(total), (8, bq)).T[:, :1]
        qb_ref[h] = put3(qe_ref[h], -lse, HD + 4)
    att_ref[...] = (jnp.concatenate(outs, axis=0) if heads > 1 else outs[0]).T.astype(BF)


def attend(qe, ke, vt, padw, lo, hi, bq, bk):
    heads, rows, _ = qe.shape
    full = lambda i, lo, hi: (0, 0, 0)
    return pl.pallas_call(
        functools.partial(fwd_kernel, heads, bq, bk),
        grid_spec=pltpu.PrefetchScalarGridSpec(
            num_scalar_prefetch=2,
            grid=(rows // bq,),
            in_specs=[
                pl.BlockSpec((heads, bq, LANES), lambda i, lo, hi: (0, i, 0)),
                pl.BlockSpec((heads, rows, LANES), full),
                pl.BlockSpec((heads, VT, rows), full),
                pl.BlockSpec((1, bq), lambda i, lo, hi: (0, i)),
            ],
            out_specs=[
                pl.BlockSpec((bq, heads * HD), lambda i, lo, hi: (i, 0)),
                pl.BlockSpec((heads, bq, LANES), lambda i, lo, hi: (0, i, 0)),
            ],
            scratch_shapes=[
                pltpu.VMEM((heads, 1, bq), F32),
                pltpu.VMEM((heads, VT, bq), F32),
            ],
        ),
        out_shape=[
            jax.ShapeDtypeStruct((rows, heads * HD), BF),
            jax.ShapeDtypeStruct((heads, rows, LANES), BF),
        ],
        compiler_params=pltpu.CompilerParams(vmem_limit_bytes=60 << 20),
        name="attend",
    )(lo, hi, qe, ke, vt, padw)


def bwd_kernel(heads, bq, bk, lo_ref, hi_ref, qb_ref, ke_ref, ve_ref, go_ref, att_ref, out_ref, ge_ref, dqt_ref, kt_ref, qt_ref, got_ref, dkt_ref, dvt_ref):
    j = pl.program_id(0)
    rows = qb_ref.shape[1]

    @pl.when(j == 0)
    def _():
        for h in range(heads):
            dqt_ref[h] = jnp.zeros_like(dqt_ref[h])
            for c in range(rows // 512):
                sl = pl.ds(c * 512, 512)
                go = go_ref[sl, h * HD : (h + 1) * HD]
                at = att_ref[sl, h * HD : (h + 1) * HD]
                delta = jnp.sum(go.astype(F32) * at.astype(F32), axis=1, keepdims=True)
                wide = jnp.concatenate([go, jnp.zeros_like(go)], axis=1)
                ge_ref[h, sl, :] = put3(wide, -delta, HD)
                got_ref[h, :, c * 512 : (c + 1) * 512] = wide.T[:HD]
                qt_ref[h, :, c * 512 : (c + 1) * 512] = qb_ref[h, sl, :].T[:HD]

    for h in range(heads):
        kt_ref[h] = ke_ref[h].T[:HD]

    zero = jnp.zeros((HD, bk), F32)

    def step(i, carry):
        row0 = pl.multiple_of(i * bq, bq)
        work = [(h, pl.ds(row0 + c, QB)) for c in range(0, bq, QB) for h in range(heads)]
        score = lambda h, c: (nt(ke_ref[h], qb_ref[h, c, :]), nt(ve_ref[h], ge_ref[h, c, :]))
        ss = [score(*w) for w in work[:BAHEAD]]
        for n, (h, c) in enumerate(work):
            if n + BAHEAD < len(work):
                ss.append(score(*work[n + BAHEAD]))
            st, dt = ss[n]
            p = jnp.exp(st)
            ds = (p * dt).astype(BF)
            pb = p.astype(BF)
            dvt_ref[h] += nt(got_ref[h, :, c], pb)
            dkt_ref[h] += nt(qt_ref[h, :, c], ds)
            dqt_ref[h, :, c] += nn(kt_ref[h], ds)
        return 0

    for h in range(heads):
        dkt_ref[h] = zero
        dvt_ref[h] = zero
    lax.fori_loop(lo_ref[j], hi_ref[j], step, 0)
    for h in range(heads):
        for part, ref in ((1, dkt_ref), (2, dvt_ref)):
            at = (part * heads + h) * HD
            out_ref[pl.ds(pl.multiple_of(j * bk, bk), bk), at : at + HD] = ref[h].T.astype(BF)

    @pl.when(j == pl.num_programs(0) - 1)
    def _():
        for h in range(heads):
            for c in range(rows // 512):
                sl = pl.ds(c * 512, 512)
                out_ref[sl, h * HD : (h + 1) * HD] = (dqt_ref[h, :, c * 512 : (c + 1) * 512].T * (HD ** -0.5)).astype(BF)


def attend_back(qb, ke, ve, go, att, lo, hi, bq, bk):
    heads, rows, _ = qb.shape
    full3 = lambda i, lo, hi: (0, 0, 0)
    full2 = lambda i, lo, hi: (0, 0)
    blk3 = lambda i, lo, hi: (0, i, 0)
    wide = heads * HD
    return pl.pallas_call(
        functools.partial(bwd_kernel, heads, bq, bk),
        grid_spec=pltpu.PrefetchScalarGridSpec(
            num_scalar_prefetch=2,
            grid=(rows // bk,),
            in_specs=[
                pl.BlockSpec((heads, rows, LANES), full3),
                pl.BlockSpec((heads, bk, LANES), blk3),
                pl.BlockSpec((heads, bk, LANES), blk3),
                pl.BlockSpec((rows, wide), full2),
                pl.BlockSpec((rows, wide), full2),
            ],
            out_specs=pl.BlockSpec((rows, 3 * wide), full2),
            scratch_shapes=[
                pltpu.VMEM((heads, rows, LANES), BF),
                pltpu.VMEM((heads, HD, rows), F32),
                pltpu.VMEM((heads, HD, bk), BF),
                pltpu.VMEM((heads, HD, rows), BF),
                pltpu.VMEM((heads, HD, rows), BF),
                pltpu.VMEM((heads, HD, bk), F32),
                pltpu.VMEM((heads, HD, bk), F32),
            ],
        ),
        out_shape=jax.ShapeDtypeStruct((rows, 3 * wide), BF),
        compiler_params=pltpu.CompilerParams(vmem_limit_bytes=60 << 20),
        name="attend_back",
    )(lo, hi, qb, ke, ve, go, att)


def dot_f32(a, b, dims):
    return lax.dot_general(a, b, ((dims[:1], dims[1:]), ((), ())), precision=highest, preferred_element_type=F32)


def soap_group(base, group, gr_ref, w_ref, m1_ref, m2_ref, av_ref, st_ref, ba_ref,
               nw_ref, n1_ref, n2_ref, na_ref, ns_ref, nb_ref, aug_ref):
    size = w_ref.shape[-1]
    half = size // 2
    panel = 8
    every = range(group)
    grads, firsts = [], []
    for s in every:
        rows = slice((base + s) * half, (base + s + 1) * half)
        wire = gr_ref[rows, :]
        grads.append(jnp.concatenate([wire[:, :size], wire[:, size:]], axis=0))
        firsts.append(beta_one * m1_ref[0, base + s] + (1.0 - beta_one) * grads[s])
        n1_ref[0, base + s] = firsts[s]
    sides = [(s, side) for s in every for side in range(2)]
    outers = [dot_f32(grads[s], grads[s], (1, 1) if side == 0 else (0, 0)) for s, side in sides]
    both = [dot_f32(jnp.concatenate([grads[s], firsts[s]], axis=0), ba_ref[0, base + s, 1], (1, 0)) for s in every]
    stats = []
    for (s, side), outer in zip(sides, outers):
        stats.append(beta_two * st_ref[0, base + s, side] + (1.0 - beta_two) * outer)
        ns_ref[0, base + s, side] = stats[-1]
    pairs = [dot_f32(ba_ref[0, base + s, 0], jnp.concatenate([both[s][:size], both[s][size:]], axis=1), (0, 0)) for s in every]
    mts = [dot_f32(ba_ref[0, base + s, side], stat, (0, 1)) for (s, side), stat in zip(sides, stats)]
    scaled = []
    for s in every:
        rotated, moment = pairs[s][:, :size], pairs[s][:, size:]
        second = beta_two * m2_ref[0, base + s] + (1.0 - beta_two) * rotated * rotated
        n2_ref[0, base + s] = second
        scaled.append(moment / (jnp.sqrt(second) + step_eps))
    grams = [dot_f32(mt, mt, (1, 1)) for mt in mts]
    inner = [dot_f32(scaled[s], ba_ref[0, base + s, 1], (1, 1)) for s in every]
    for m, (gram, mt) in enumerate(zip(grams, mts)):
        aug_ref[m] = jnp.concatenate([gram, mt], axis=1)
    directions = [dot_f32(ba_ref[0, base + s, 0], inner[s], (1, 0)) for s in every]
    for s in every:
        weight = w_ref[0, base + s]
        fresh = weight - step_rate * (directions[s] + weight_decay * weight)
        nw_ref[0, base + s] = fresh
        na_ref[0, base + s] = average_keep * av_ref[0, base + s] + (1.0 - average_keep) * fresh
    count = 2 * group
    row = lax.broadcasted_iota(jnp.int32, (count, panel, LANES), 1)
    for p in range(size // panel):
        top = p * panel
        part = aug_ref[:, top : top + panel, :]
        for r in range(panel):
            pivot = lax.rsqrt(part[:, r : r + 1, top + r : top + r + 1])
            lead = part[:, r : r + 1, :] * pivot
            column = jnp.where(row > r, part[:, :, top + r : top + r + 1] * pivot, 0.0)
            part = jnp.where(row == r, lead, part - column * lead)
        aug_ref[:, top : top + panel, :] = part
        below = top + panel
        if below < size:
            high = part.astype(BF).astype(F32)
            rest = part - high
            mid = rest.astype(BF).astype(F32)
            low = rest - mid
            first = jnp.concatenate([high, high, mid, high, mid, low], axis=1).astype(BF)
            other = jnp.concatenate([high, mid, high, low, mid, high], axis=1).astype(BF)
            for m in range(count):
                aug_ref[m, below:, :] -= lax.dot_general(
                    first[m][:, below:size], other[m], (((0,), (0,)), ((), ())), preferred_element_type=F32
                )
    for s in range(group):
        for side in range(2):
            nb_ref[0, base + s, side] = aug_ref[2 * s + side][:, size:].T


MESH = pl.DeviceIdType.MESH


def normalize(values):
    center = jnp.mean(values, axis=-1, keepdims=True)
    centered = values - center
    variance = jnp.mean(centered * centered, axis=-1, keepdims=True)
    scale = lax.rsqrt(variance + norm_eps)
    return centered * scale, scale


def norm_back(grad, xhat, scale):
    along = jnp.mean(grad * xhat, axis=-1, keepdims=True)
    return (grad - jnp.mean(grad, axis=-1, keepdims=True) - xhat * along) * scale


TAIL = 0.305
TAIL_FIT = (
    0.1216397411342051,
    0.12246669816059132,
    0.10342157025713879,
    0.1210193967312446,
    -0.037972477455618554,
    0.18571204369074895,
    -0.15298537812807472,
    0.036698452375741396,
)


def gelu_pair(u):
    size = jnp.abs(u)
    bell = jnp.exp(-0.5 * u * u)
    t = 1.0 / (1.0 + TAIL * size)
    poly = jnp.full_like(t, TAIL_FIT[-1])
    for c in TAIL_FIT[-2::-1]:
        poly = poly * t + c
    upper = poly * t * bell
    cdf = jnp.where(u > 0.0, 1.0 - upper, upper)
    return u * cdf, cdf + (0.3989422804014327 * u) * bell


def block_rows(ref, start, half):
    return ref[pl.ds(pl.multiple_of(start, 16), half), :]


def project_kernel(heads, rows_dev, gains_at, row_ref, wire_ref, tok_ref, seg_ref, pad_ref, gain_ref,
                   norm_ref, qe_ref, ke_ref, ve_ref, vt_ref, mix_ref, wide_ref):
    width = tok_ref.shape[1]
    half = HD // 2
    cols = 3 * heads

    @pl.when(pl.program_id(0) == 0)
    def _():
        zero = jnp.zeros((half, HD), BF)

        def fill(r, _):
            low = pl.multiple_of(r * HD, HD)
            for c in range(cols):
                t = block_rows(wire_ref, row_ref[r * cols + c], half)
                for part in range(2):
                    piece = t[:, part * HD : (part + 1) * HD]
                    at = pl.ds(low + part * half, half)
                    wide_ref[at, c * LANES : (c + 1) * LANES] = jnp.concatenate([piece, zero], axis=1)
                    mix_ref[at, c * HD : (c + 1) * HD] = piece
            return 0

        lax.fori_loop(0, width // HD, fill, 0)

    xhat, _ = normalize(tok_ref[...].astype(F32))
    normed = (xhat * gain_ref[...]).astype(BF)
    norm_ref[...] = normed
    count = tok_ref.shape[0]
    lane = lax.broadcasted_iota(jnp.int32, (LANES, count), 0)
    seg = seg_ref[...]
    same = lane - HD == seg
    in_segs = (lane >= HD) & (lane < HD + SEGS)
    ones = (lane >= HD + SEGS) & (lane < HD + SEGS + 3)
    ext_q = jnp.where(same, 1.0, 0.0).T
    ext_k = jnp.where(in_segs, jnp.where(same & (pad_ref[...] > 0.5), 0.0, NEG), jnp.where(ones, 1.0, 0.0)).T
    ext_v = jnp.where((lane >= HD) & (lane < HD + 3), 1.0, 0.0).T
    for h in range(heads):
        for ref, part, scale, ext in ((qe_ref, 0, HD ** -0.5, ext_q), (ke_ref, 1, 1.0, ext_k), (ve_ref, 2, 1.0, ext_v)):
            c = part * heads + h
            mixed = nn(normed, wide_ref[:, c * LANES : (c + 1) * LANES]).astype(BF)
            out = (mixed.astype(F32) * scale + ext).astype(BF)
            ref[h] = out
            if part == 2:
                vt_ref[h] = out.T[:VT]


def project(wire, row_own, tokens, seg, pad, gain_one, heads):
    rows, width = tokens.shape
    tb = min(512, rows)
    full = lambda i, r: (0, 0)
    blk = lambda i, r: (i, 0)
    col = lambda i, r: (0, i)
    ext = lambda i, r: (0, i, 0)
    out = lambda *s: jax.ShapeDtypeStruct(s, BF)
    return pl.pallas_call(
        functools.partial(project_kernel, heads, 0, 0),
        grid_spec=pltpu.PrefetchScalarGridSpec(
            num_scalar_prefetch=1,
            grid=(rows // tb,),
            in_specs=[
                pl.BlockSpec(wire.shape, full),
                pl.BlockSpec((tb, width), blk),
                pl.BlockSpec((1, tb), col),
                pl.BlockSpec((1, tb), col),
                pl.BlockSpec((1, width), full),
            ],
            out_specs=[
                pl.BlockSpec((tb, width), blk),
                pl.BlockSpec((heads, tb, LANES), ext),
                pl.BlockSpec((heads, tb, LANES), ext),
                pl.BlockSpec((heads, tb, LANES), ext),
                pl.BlockSpec((heads, VT, tb), lambda i, r: (0, 0, i)),
                pl.BlockSpec((width, 3 * heads * HD), full),
            ],
            scratch_shapes=[pltpu.VMEM((width, 3 * heads * LANES), BF)],
        ),
        out_shape=[
            out(rows, width),
            out(heads, rows, LANES),
            out(heads, rows, LANES),
            out(heads, rows, LANES),
            out(heads, VT, rows),
            out(width, 3 * heads * HD),
        ],
        compiler_params=pltpu.CompilerParams(vmem_limit_bytes=60 << 20),
        name="project",
    )(row_own, wire, tokens, seg, pad, gain_one)


def middle_kernel(shards, span, units, wide, gain_row, gains_dev, inside,
                  unit_ref, sel_ref, wire_ref, gain_ref, pad_ref, att_ref, tok_ref, cot_ref,
                  outa_ref, outb_ref, res_ref, back_ref, grads_ref, mix_ref,
                  tokens_ref, cots_ref, got_ref, give_ref, wo_ref, wu_ref, wd_ref, go_ref, gu_ref, gd_ref, gg_ref, blk_ref,
                  local_sem, send_i, recv_i, send_b, recv_b, send_a, recv_a):
    own, width = tokens_ref.shape
    parts = recv_i.shape[1]
    tb = own // parts
    half = HD // 2
    rows_dev = grads_ref.shape[1]
    z = lax.axis_index("narrow")
    kinds = (
        (mix_ref, None, width, 3 * span),
        (wo_ref, go_ref, span, width),
        (wu_ref, gu_ref, width, units),
        (wd_ref, gd_ref, units, width),
    )
    mix_blocks = width // HD * (3 * span // HD)
    per = blk_ref.shape[0] // shards

    barrier = pltpu.get_barrier_semaphore()
    for d in range(1, shards):
        pl.semaphore_signal(barrier, inc=1, device_id={"narrow": lax.rem(z + d, shards)}, device_id_type=MESH)
    pl.semaphore_wait(barrier, shards - 1)

    def bring(d, t, mine):
        peer = lax.rem(z + d, shards)
        slot = z if mine else peer
        return pltpu.make_async_remote_copy(
            src_ref=att_ref.at[pl.ds(pl.multiple_of(peer * own + t * tb, tb), tb), :],
            dst_ref=got_ref.at[slot, pl.ds(pl.multiple_of(t * tb, tb), tb), :],
            send_sem=send_i.at[d - 1, t],
            recv_sem=recv_i.at[slot, t],
            device_id={"narrow": peer},
            device_id_type=MESH,
        )

    def give(d, t, mine):
        peer = lax.rem(z + d, shards)
        slot = z if mine else peer
        return pltpu.make_async_remote_copy(
            src_ref=give_ref.at[peer, pl.ds(pl.multiple_of(t * tb, tb), tb), :],
            dst_ref=back_ref.at[pl.ds(pl.multiple_of(slot * own + t * tb, tb), tb), :],
            send_sem=send_b.at[d - 1, t],
            recv_sem=recv_b.at[slot, t],
            device_id={"narrow": peer},
            device_id_type=MESH,
        )

    def hop_copy(c, t, step):
        at = pl.ds(pl.multiple_of(t * tb, tb), tb)
        return pltpu.make_async_remote_copy(
            src_ref=outa_ref.at[c, at, :],
            dst_ref=outa_ref.at[c, at, :],
            send_sem=send_a.at[step, c, t],
            recv_sem=recv_a.at[c, t],
            device_id={"narrow": lax.rem(z + (1 if step == 0 else shards - 1), shards)},
            device_id_type=MESH,
        )

    room = (z < shards - 1, z > 0)
    for t in range(parts):
        for d in range(1, shards):
            bring(d, t, True).start()
    mine = pl.ds(pl.multiple_of(z * own, own), own)
    copies = [
        pltpu.make_async_copy(att_ref.at[mine, :], got_ref.at[z], local_sem.at[0]),
        pltpu.make_async_copy(tok_ref.at[mine, :], tokens_ref, local_sem.at[1]),
        pltpu.make_async_copy(cot_ref.at[mine, :], cots_ref, local_sem.at[2]),
    ]
    for copy in copies:
        copy.start()

    base = 0
    for ref, acc, rows, cols in kinds:
        grid_cols = cols // HD

        def fill(r, _, ref=ref, base=base, grid_cols=grid_cols):
            low = pl.multiple_of(r * HD, HD)
            for n in range(shards):
                for c in range(grid_cols):
                    unit = unit_ref[base + r * grid_cols + c] + n * (rows_dev // 16)
                    t = jnp.concatenate([wire_ref[unit], wire_ref[unit + 1]], axis=0)
                    for part in range(2):
                        ref[n, pl.ds(low + part * half, half), c * HD : (c + 1) * HD] = t[:, part * HD : (part + 1) * HD]
            return 0

        lax.fori_loop(0, rows // HD, fill, 0)
        base += rows // HD * grid_cols
        if acc is not None:
            acc[...] = jnp.zeros_like(acc)
    gg_ref[...] = jnp.zeros_like(gg_ref)
    for copy in copies:
        copy.wait()

    def block(t, _):
        at = pl.ds(pl.multiple_of(t * tb, tb), tb)
        for d in range(1, shards):
            bring(d, t, False).wait_recv()
        tokens = tokens_ref[at, :].astype(F32)
        cot = cots_ref[at, :]
        branch = nn(got_ref[0, at, :], wo_ref[0])
        for n in range(1, shards):
            branch += nn(got_ref[n, at, :], wo_ref[n])
        residual = tokens + branch
        xhat, scale = normalize(residual)
        gain = gain_ref[...]
        normed = (xhat * gain).astype(BF)
        ups = [nn(normed, wu_ref[n]) for n in range(shards)]
        downs = [nt(cot, wd_ref[n]) for n in range(shards)]
        actives, back_ups = [], []
        for n in range(shards):
            value, slope = gelu_pair(ups[n])
            actives.append(value.astype(BF))
            back_ups.append((slope * downs[n]).astype(BF))
        mlp = nn(actives[0], wd_ref[0])
        back = nt(back_ups[0], wu_ref[0])
        for n in range(1, shards):
            mlp += nn(actives[n], wd_ref[n])
            back += nt(back_ups[n], wu_ref[n])
        out = (residual + mlp).astype(BF)

        @pl.when(t < inside)
        def _():
            outa_ref[z, at, :] = out
            for step in range(2):

                @pl.when(room[step])
                def _(step=step):
                    hop_copy(z, t, step).start()

        @pl.when(t >= inside)
        def _():
            outb_ref[pl.ds(pl.multiple_of((t - inside) * tb, tb), tb), :] = out

        gg_ref[...] += jnp.sum(back * xhat, axis=0, keepdims=True)
        back_res = cot.astype(F32) + norm_back(back * gain, xhat, scale)
        res_ref[at, :] = back_res
        branch_low = back_res.astype(BF)
        line = pad_ref[:, pl.ds(pl.multiple_of(z * own + t * tb, LANES), tb)]
        pad = jnp.broadcast_to(line, (8, tb)).T[:, :1]
        for n in range(shards):
            give_ref[n, at, :] = (nt(branch_low, wo_ref[n]) * pad).astype(BF)
        for d in range(1, shards):
            give(d, t, True).start()
        for n in range(shards):
            gd_ref[n] += tn(actives[n], cot)
            gu_ref[n] += tn(normed, back_ups[n])
            go_ref[n] += tn(got_ref[n, at, :], branch_low)
        return 0

    lax.fori_loop(0, parts, block, 0)
    back_ref[mine, :] = give_ref[z]
    base = 0
    for ref, acc, rows, cols in kinds:
        grid_cols = cols // HD
        if acc is not None:

            def cut(r, _, acc=acc, base=base, grid_cols=grid_cols):
                low = pl.multiple_of(r * HD, HD)
                for n in range(shards):
                    for c in range(grid_cols):
                        lanes = slice(c * HD, (c + 1) * HD)
                        value = jnp.concatenate([acc[n, pl.ds(low, half), lanes], acc[n, pl.ds(low + half, half), lanes]], axis=1)
                        blk_ref[n * per + base - mix_blocks + r * grid_cols + c] = value.astype(BF)
                return 0

            lax.fori_loop(0, rows // HD, cut, 0)
        base += rows // HD * grid_cols
    for n in range(shards):
        blk_ref[(n + 1) * per - 1] = jnp.zeros((half, LANES), BF)
    slots = gain_row // half
    top = lax.broadcasted_iota(jnp.int32, (16, LANES), 0) == 0

    def place(v, _):
        for n in range(shards):
            for i in range(slots):
                grads_ref[v * shards + n, i * half : (i + 1) * half, :] = blk_ref[sel_ref[v * slots + i] + n * per]
        return 0

    lax.fori_loop(0, wide, place, 0)
    for v in range(wide):
        piece = v * gains_dev // LANES - width // LANES
        for n in range(shards):
            if piece >= 0:
                value = jnp.where(top, gg_ref[:, piece * LANES : (piece + 1) * LANES], 0.0).astype(BF)
            else:
                value = jnp.zeros((16, LANES), BF)
            grads_ref[v * shards + n, gain_row:, :] = value

    hops = [(s, t, step) for s in range(1, shards) for t in range(inside) for step in range(2)]
    for s, t, step in hops:
        chunk = z - s if step == 0 else z + s
        there = chunk >= 0 if step == 0 else chunk < shards

        @pl.when(there)
        def _(chunk=chunk, t=t, step=step):
            hop_copy(chunk, t, step).wait_recv()

        @pl.when(there & room[step])
        def _(chunk=chunk, t=t, step=step):
            hop_copy(chunk, t, step).start()

    for t in range(parts):
        for d in range(1, shards):
            give(d, t, False).wait_recv()
    for t in range(parts):
        for d in range(1, shards):
            bring(d, t, True).wait_send()
            give(d, t, True).wait_send()
    for t in range(inside):
        for step in range(2):

            @pl.when(room[step])
            def _(t=t, step=step):
                hop_copy(z, t, step).wait_send()

    for s, t, step in hops:
        chunk = z - s if step == 0 else z + s
        there = chunk >= 0 if step == 0 else chunk < shards

        @pl.when(there & room[step])
        def _(chunk=chunk, t=t, step=step):
            hop_copy(chunk, t, step).wait_send()


def middle(unit, sel, wire, gain_two, pad, att, tokens, cotangent, shards, wide, rows_dev, gain_row, gains_dev):
    rows, span = att.shape
    width = tokens.shape[1]
    units = FF // shards
    own = rows // shards
    tb = min(256, own)
    parts = own // tb
    inside = parts // 2
    blocks = unit.shape[0] - width // HD * (3 * span // HD)
    vmem = pl.BlockSpec(memory_space=pltpu.VMEM)
    smem = pl.BlockSpec(memory_space=pltpu.SMEM)
    hbm = pl.BlockSpec(memory_space=pl.ANY)
    dma = pltpu.SemaphoreType.DMA
    return pl.pallas_call(
        functools.partial(middle_kernel, shards, span, units, wide, gain_row, gains_dev, inside),
        in_specs=[smem, smem, vmem, vmem, vmem, hbm, hbm, hbm],
        out_specs=[vmem] * 6,
        out_shape=[
            jax.ShapeDtypeStruct((shards, inside * tb, width), BF),
            jax.ShapeDtypeStruct((own - inside * tb, width), BF),
            jax.ShapeDtypeStruct((own, width), F32),
            jax.ShapeDtypeStruct((rows, span), BF),
            jax.ShapeDtypeStruct((wide * shards, rows_dev, LANES), BF),
            jax.ShapeDtypeStruct((shards, width, 3 * span), BF),
        ],
        scratch_shapes=[
            pltpu.VMEM((own, width), BF),
            pltpu.VMEM((own, width), BF),
            pltpu.VMEM((shards, own, span), BF),
            pltpu.VMEM((shards, own, span), BF),
            pltpu.VMEM((shards, span, width), BF),
            pltpu.VMEM((shards, width, units), BF),
            pltpu.VMEM((shards, units, width), BF),
            pltpu.VMEM((shards, span, width), F32),
            pltpu.VMEM((shards, width, units), F32),
            pltpu.VMEM((shards, units, width), F32),
            pltpu.VMEM((1, width), F32),
            pltpu.VMEM((shards * (blocks + 1), HD // 2, LANES), BF),
            dma((3,)),
            dma((shards - 1, parts)),
            dma((shards, parts)),
            dma((shards - 1, parts)),
            dma((shards, parts)),
            dma((2, shards, inside)),
            dma((shards, inside)),
        ],
        compiler_params=pltpu.CompilerParams(vmem_limit_bytes=63 << 20, collective_id=2, has_side_effects=True),
        name="middle",
    )(unit, sel, wire, gain_two, pad, att, tokens, cotangent)


PARTS = 4


def finish_kernel(shards, wide, gain_row, gains_dev, group, sel_ref, mix_ref, full_ref, gain_ref, res_ref, bm_ref, norm_ref, tok_ref, *refs):
    states, outs = refs[1:7], refs[9:15]
    first_ref, grad_ref, line_ref = refs[0], refs[7], refs[8]
    (own_ref, normed_ref, tokens_ref, got_ref, acc_ref, blk_ref, grads_ref, sums_ref, firsts_ref, part_ref, aug_ref,
     local_sem, send_z, recv_z, send_w, recv_w, send_a, recv_a, send_g, recv_g, send_f, recv_f) = refs[15:]
    width = norm_ref.shape[1]
    rows, cols = bm_ref.shape
    own = rows // shards
    hold = own // PARTS
    half = HD // 2
    grid_cols = cols // HD
    blocks = width // HD * grid_cols
    slots = gain_row // half
    z = lax.axis_index("narrow")
    w = lax.axis_index("wide")

    barrier = pltpu.get_barrier_semaphore()
    for d in range(1, shards):
        pl.semaphore_signal(barrier, inc=1, device_id={"narrow": lax.rem(z + d, shards)}, device_id_type=MESH)
    for d in range(1, wide):
        pl.semaphore_signal(barrier, inc=1, device_id={"wide": lax.rem(w + d, wide)}, device_id_type=MESH)
    pl.semaphore_wait(barrier, shards + wide - 2)

    def to_peer(d, part, mine):
        peer = lax.rem(z + d, shards)
        slot = z if mine else peer
        at = pl.multiple_of(peer * own + part * hold, hold)
        return pltpu.make_async_remote_copy(
            src_ref=bm_ref.at[pl.ds(at, hold), :],
            dst_ref=got_ref.at[slot, pl.ds(part * hold, hold), :],
            send_sem=send_z.at[d - 1, part],
            recv_sem=recv_z.at[slot, part],
            device_id={"narrow": peer},
            device_id_type=MESH,
        )

    def to_owner(d, mine):
        peer = lax.rem(w + d, wide)
        slot = w if mine else peer
        return pltpu.make_async_remote_copy(
            src_ref=grads_ref.at[peer],
            dst_ref=sums_ref.at[slot],
            send_sem=send_w.at[d - 1],
            recv_sem=recv_w.at[slot],
            device_id={"wide": peer},
            device_id_type=MESH,
        )

    def hop_copy(c, part, step):
        at = pl.ds(pl.multiple_of(c * own + part * hold, hold), hold)
        return pltpu.make_async_remote_copy(
            src_ref=grad_ref.at[at, :],
            dst_ref=grad_ref.at[at, :],
            send_sem=send_a.at[step, c, part],
            recv_sem=recv_a.at[c, part],
            device_id={"narrow": lax.rem(z + (1 if step == 0 else shards - 1), shards)},
            device_id_type=MESH,
        )

    def pass_on(c, part, act):
        for step, there in ((0, z < shards - 1), (1, z > 0)):
            if c is None or step == c[0]:
                chunk = z if c is None else c[1]
                ok = there if c is None else there & c[2]

                @pl.when(ok)
                def _(chunk=chunk, step=step):
                    act(hop_copy(chunk, part, step))

    def line_to(d, mine):
        peer = lax.rem(z + d, shards)
        slot = z if mine else peer
        return pltpu.make_async_remote_copy(
            src_ref=line_ref.at[z],
            dst_ref=line_ref.at[slot],
            send_sem=send_g.at[d - 1],
            recv_sem=recv_g.at[slot],
            device_id={"narrow": peer},
            device_id_type=MESH,
        )

    rows_dev = part_ref.shape[0]

    def first_to(d, mine):
        peer = lax.rem(z + d, shards)
        slot = z if mine else peer
        return pltpu.make_async_remote_copy(
            src_ref=first_ref.at[pl.ds(pl.multiple_of(peer * rows_dev, 16), rows_dev), :],
            dst_ref=firsts_ref.at[slot],
            send_sem=send_f.at[d - 1],
            recv_sem=recv_f.at[slot],
            device_id={"narrow": peer},
            device_id_type=MESH,
        )

    for d in range(1, shards):
        first_to(d, True).start()
    for part in range(PARTS):
        for d in range(1, shards):
            to_peer(d, part, True).start()
    mine = pl.ds(pl.multiple_of(z * own, own), own)
    copies = [
        pltpu.make_async_copy(bm_ref, own_ref, local_sem.at[0]),
        pltpu.make_async_copy(norm_ref, normed_ref, local_sem.at[1]),
        pltpu.make_async_copy(tok_ref.at[mine, :], tokens_ref, local_sem.at[2]),
        pltpu.make_async_copy(bm_ref.at[mine, :], got_ref.at[z], local_sem.at[3]),
        pltpu.make_async_copy(
            first_ref.at[pl.ds(pl.multiple_of(z * rows_dev, 16), rows_dev), :], firsts_ref.at[z], local_sem.at[4]
        ),
    ]
    for copy in copies:
        copy.start()
    for copy in copies:
        copy.wait()

    acc_ref[...] = jnp.zeros_like(acc_ref)
    tb = min(512, rows)

    def add(i, _):
        at = pl.ds(pl.multiple_of(i * tb, tb), tb)
        acc_ref[...] += tn(normed_ref[at, :], own_ref[at, :])
        return 0

    lax.fori_loop(0, rows // tb, add, 0)
    blk_ref[blocks] = jnp.zeros((half, LANES), BF)

    def cut(r, _):
        low = pl.multiple_of(r * HD, HD)
        for c in range(grid_cols):
            lanes = slice(c * HD, (c + 1) * HD)
            value = jnp.concatenate([acc_ref[pl.ds(low, half), lanes], acc_ref[pl.ds(low + half, half), lanes]], axis=1)
            blk_ref[r * grid_cols + c] = value.astype(BF)
        return 0

    lax.fori_loop(0, width // HD, cut, 0)
    along = jnp.sum(acc_ref[...] * mix_ref[...].astype(F32), axis=1, keepdims=True)
    line = jnp.broadcast_to(along, (width, LANES)).T[:16] / gain_ref[...]
    top = lax.broadcasted_iota(jnp.int32, (16, LANES), 0) == 0
    for v in range(wide):

        def place(i, _, v=v):
            grads_ref[v, pl.ds(pl.multiple_of(i * half, half), half), :] = blk_ref[sel_ref[v * slots + i]]
            return 0

        lax.fori_loop(0, slots, place, 0)
        piece = v * gains_dev // LANES
        if piece < width // LANES:
            value = jnp.where(top, line[:, piece * LANES : (piece + 1) * LANES], 0.0).astype(BF)
        else:
            value = jnp.zeros((16, LANES), BF)
        grads_ref[v, gain_row : gain_row + 16, :] = value
    for d in range(1, wide):
        to_owner(d, True).start()
    part_ref[...] = grads_ref[w].astype(F32)

    tile = min(256, hold)

    def norm_rows(i, _):
        at = pl.ds(pl.multiple_of(i * tile, tile), tile)
        back = nt(got_ref[0, at, :], full_ref[0])
        for n in range(1, shards):
            back += nt(got_ref[n, at, :], full_ref[n])
        xhat, scale = normalize(tokens_ref[at, :].astype(F32))
        grad = res_ref[at, :] + norm_back(back * gain_ref[...], xhat, scale)
        grad_ref[pl.ds(pl.multiple_of(z * own + i * tile, tile), tile), :] = grad.astype(BF)
        return 0

    def norm_part(part):
        for d in range(1, shards):
            to_peer(d, part, False).wait_recv()
        lax.fori_loop(part * hold // tile, (part + 1) * hold // tile, norm_rows, 0)
        pass_on(None, part, lambda copy: copy.start())

    for d in range(1, wide):
        to_owner(d, False).wait_recv()
    for d in range(1, wide):
        part_ref[...] += sums_ref[lax.rem(w + d, wide)].astype(F32)
    line_ref[z] = part_ref[gain_row : gain_row + 16, :]
    for d in range(1, shards):
        line_to(d, True).start()
    for d in range(1, shards):
        first_to(d, False).wait_recv()
    total = firsts_ref[0].astype(F32)
    for n in range(1, shards):
        total += firsts_ref[n].astype(F32)
    line_ref[shards] = total[gain_row : gain_row + 16, :]
    part_ref[...] += total
    ready = 0
    rounds = slots // group
    for g in range(rounds):
        soap_group(g * group, group, part_ref, *states, *outs, aug_ref)
        upto = PARTS * (g + 1) // rounds
        while ready < upto:
            norm_part(ready)
            ready += 1
    hops = [(s, part, step) for s in range(1, shards) for part in range(PARTS) for step in range(2)]
    for s, part, step in hops:
        chunk = z - s if step == 0 else z + s
        there = chunk >= 0 if step == 0 else chunk < shards

        @pl.when(there)
        def _(chunk=chunk, part=part, step=step):
            hop_copy(chunk, part, step).wait_recv()

        pass_on((step, chunk, there), part, lambda copy: copy.start())
    for d in range(1, shards):
        line_to(d, False).wait_recv()
    for part in range(PARTS):
        pass_on(None, part, lambda copy: copy.wait_send())
    for s, part, step in hops:
        chunk = z - s if step == 0 else z + s
        there = chunk >= 0 if step == 0 else chunk < shards
        pass_on((step, chunk, there), part, lambda copy: copy.wait_send())
    for d in range(1, shards):
        line_to(d, True).wait_send()
        first_to(d, True).wait_send()
    for part in range(PARTS):
        for d in range(1, shards):
            to_peer(d, part, True).wait_send()
    for d in range(1, wide):
        to_owner(d, True).wait_send()


def finish(sel, mix, mix_full, gain_one, res, bm, normed, tokens, states, group, wide, rows_dev, gain_row, gains_dev):
    shards = mix_full.shape[0]
    rows, cols = bm.shape
    width = normed.shape[1]
    own = rows // shards
    half = HD // 2
    blocks = width // HD * (cols // HD)
    vmem = pl.BlockSpec(memory_space=pltpu.VMEM)
    smem = pl.BlockSpec(memory_space=pltpu.SMEM)
    hbm = pl.BlockSpec(memory_space=pl.ANY)
    dma = pltpu.SemaphoreType.DMA
    return pl.pallas_call(
        functools.partial(finish_kernel, shards, wide, gain_row, gains_dev, group),
        in_specs=[smem, vmem, vmem, vmem, vmem, hbm, hbm, hbm, hbm] + [vmem] * 6,
        out_specs=[vmem] * 8,
        out_shape=[jax.ShapeDtypeStruct((rows, width), BF), jax.ShapeDtypeStruct((shards + 1, 16, LANES), F32)]
        + [jax.ShapeDtypeStruct(a.shape, a.dtype) for a in states[1:]],
        scratch_shapes=[
            pltpu.VMEM((rows, cols), BF),
            pltpu.VMEM((rows, width), BF),
            pltpu.VMEM((own, width), BF),
            pltpu.VMEM((shards, own, cols), BF),
            pltpu.VMEM((width, cols), F32),
            pltpu.VMEM((blocks + 1, half, LANES), BF),
            pltpu.VMEM((wide, rows_dev, LANES), BF),
            pltpu.VMEM((wide, rows_dev, LANES), BF),
            pltpu.VMEM((shards, rows_dev, LANES), BF),
            pltpu.VMEM((rows_dev, LANES), F32),
            pltpu.VMEM((2 * group, HD, LANES), F32),
            dma((5,)),
            dma((shards - 1, PARTS)),
            dma((shards, PARTS)),
            dma((wide - 1,)),
            dma((wide,)),
            dma((2, shards, PARTS)),
            dma((shards, PARTS)),
            dma((shards - 1,)),
            dma((shards,)),
            dma((shards - 1,)),
            dma((shards,)),
        ],
        compiler_params=pltpu.CompilerParams(vmem_limit_bytes=62 << 20, collective_id=1, has_side_effects=True),
        name="finish",
    )(sel, mix, mix_full, gain_one, res, bm, normed, tokens, *states)


def adam_gains(grad, gain, first, second, average):
    new_first = beta_one * first + (1.0 - beta_one) * grad
    new_second = beta_two * second + (1.0 - beta_two) * grad * grad
    new_gain = gain - gain_rate * new_first / (jnp.sqrt(new_second) + step_eps)
    new_average = average_keep * average + (1.0 - average_keep) * new_gain
    return (new_gain, new_first, new_second, new_average)


def body(
    tokens,
    cotangent,
    segment_ids,
    pad_mask,
    owner_order,
    weights,
    first_moment,
    second_moment,
    average,
    stats,
    bases,
    gains,
    gain_first,
    gain_second,
    gain_average,
):
    narrow = lax.axis_size("narrow")
    wide = lax.axis_size("wide")
    heads = HEADS // narrow
    rows, width = tokens.shape
    span = heads * HD
    own = rows // narrow
    slots, size = weights.shape[1], weights.shape[2]
    half = size // 2
    block_count = owner_order.shape[0]
    gains_dev = gains.shape[0]
    gain_row = slots * half
    rows_dev = gain_row + 16

    low = weights[0].astype(BF)
    wire = jnp.concatenate([low[:, :half], low[:, half:]], axis=2).reshape(gain_row, 2 * size)
    wire = jnp.concatenate([wire, jnp.pad(gains.astype(BF)[None], ((0, 15), (0, LANES - gains_dev)))], axis=0)
    wire_own = lax.all_gather(wire, "wide", axis=0, tiled=True)
    wire_full = lax.all_gather(lax.all_gather(wire, "narrow", axis=0, tiled=True), "wide", axis=0, tiled=True)

    ids = jnp.arange(block_count, dtype=jnp.int32)
    slot_of = jnp.sum(jnp.where(owner_order[None, :] == ids[:, None], ids[None, :], 0), axis=1)
    device, place = slot_of // slots, slot_of % slots
    row_own = device * rows_dev + place * half
    row_full = device * (narrow * rows_dev) + place * half

    gain_all = wire_own.reshape(wide, rows_dev, LANES)[:, gain_row, :gains_dev].astype(F32).reshape(1, 2 * width)
    gain_one, gain_two = gain_all[:, :width], gain_all[:, width:]
    seg = segment_ids
    seg_row = segment_ids[0]
    pad = pad_mask.astype(F32)
    block = min(512, rows)
    low_seg = seg_row[::block]
    high_seg = seg_row[block - 1 :: block]
    begin = jnp.sum((seg_row[None, :] < low_seg[:, None]).astype(jnp.int32), axis=1) // block
    end = (jnp.sum((seg_row[None, :] <= high_seg[:, None]).astype(jnp.int32), axis=1) + block - 1) // block

    normed, qe, ke, ve, vt, mix = project(wire_own, row_own, tokens, seg, pad, gain_one, heads)
    attended, qb = attend(qe, ke, vt, pad, begin, end, block, block)
    unit = row_full // 16
    mix_blocks = width // size * 3 * heads
    sel_rest = jnp.where(owner_order >= mix_blocks, owner_order - mix_blocks, block_count - mix_blocks)
    out_a, out_b, back_res, back_att, grads, mix_full = middle(
        unit, sel_rest, wire_full.reshape(-1, 16, LANES), gain_two, pad, attended, tokens, cotangent,
        narrow, wide, rows_dev, gain_row, gains_dev,
    )
    part_a = lax.psum_scatter(grads.reshape(-1, LANES), "wide", scatter_dimension=0, tiled=True)
    out_b = lax.all_to_all(jnp.broadcast_to(out_b, (narrow, *out_b.shape)), "narrow", 0, 0)
    bm = attend_back(qb, ke, ve, back_att, attended, begin, end, block, block)
    bm, part_a, out_b = lax.optimization_barrier((bm, part_a, out_b))
    output = jnp.concatenate([out_a, out_b], axis=1).reshape(rows, width)
    sel = jnp.minimum(owner_order, mix_blocks)
    group = next(g for g in range(min(12, slots), 0, -1) if slots % g == 0)
    states = (part_a, weights, first_moment, second_moment, average, stats, bases)
    grad_all, lines, new_weight, new_first, new_second, new_average, new_stats, new_bases = finish(
        sel, mix, mix_full, gain_one, back_res, bm, normed, tokens, states, group, wide, rows_dev, gain_row, gains_dev
    )
    input_grad = grad_all.astype(F32)
    line = jnp.sum(lines[:, 0], axis=0)
    offset = lax.axis_index("wide") * gains_dev % LANES
    own_gain = lax.dynamic_slice_in_dim(line, offset, gains_dev, 0)
    new_gains, gain_moment, gain_square, gain_mean = adam_gains(own_gain, gains, gain_first, gain_second, gain_average)
    return (
        output,
        input_grad,
        new_weight,
        new_first,
        new_second,
        new_average,
        new_stats,
        new_bases,
        new_gains,
        gain_moment,
        gain_square,
        gain_mean,
    )


def solution(mesh):
    block = P("narrow", "wide", None, None)
    pair = P("narrow", "wide", None, None, None)
    rows = P("wide", None)
    line = P("wide")
    return jax.shard_map(
        body,
        mesh=mesh,
        in_specs=(rows, rows, rows, rows, P(), block, block, block, block, pair, pair, line, line, line, line),
        out_specs=(rows, rows, block, block, block, block, pair, pair, line, line, line, line),
        check_vma=False,
    )
```

```python
import functools

import jax
import jax.numpy as jnp
from jax import lax
from jax.experimental import pallas as pl
from jax.experimental.pallas import tpu as pltpu
from jax.sharding import PartitionSpec as P

HEADS = 8
HD = 64
FF = 2048
LANES = 128
SEGS = 4
NEG = -1e30
F32 = jnp.float32
BF = jnp.bfloat16
highest = lax.Precision.HIGHEST

beta_one = 0.9
beta_two = 0.95
step_rate = 0.1
gain_rate = 0.75
weight_decay = 0.01
average_keep = 0.5
norm_eps = 1e-05
step_eps = 1e-08


def nt(a, b):
    return lax.dot_general(a, b, (((1,), (1,)), ((), ())), preferred_element_type=F32)


def nn(a, b):
    return lax.dot_general(a, b, (((1,), (0,)), ((), ())), preferred_element_type=F32)


def tn(a, b):
    return lax.dot_general(a, b, (((0,), (0,)), ((), ())), preferred_element_type=F32)


def split3(x):
    hi = x.astype(BF)
    r = x - hi.astype(F32)
    mid = r.astype(BF)
    lo = (r - mid.astype(F32)).astype(BF)
    return hi, mid, lo


def put3(base, x, lane0):
    lane = lax.broadcasted_iota(jnp.int32, base.shape, 1)
    hi, mid, lo = split3(x)
    out = jnp.where(lane == lane0, hi.astype(F32), base.astype(F32))
    out = jnp.where(lane == lane0 + 1, mid.astype(F32), out)
    out = jnp.where(lane == lane0 + 2, lo.astype(F32), out)
    return out.astype(BF)


VT = 80
UNIT = 256


def in_steps(begin, end, block, step):
    per = block // UNIT
    count = end - begin
    whole = count // per

    def long(i, _):
        step((begin + i * per) * UNIT, block)
        return 0

    def short(i, _):
        step((begin + whole * per + i) * UNIT, UNIT)
        return 0

    lax.fori_loop(0, whole, long, 0)
    lax.fori_loop(0, count - whole * per, short, 0)


QC, AHEAD, QB, BAHEAD = 512, 1, 256, 1


def fwd_kernel(heads, bq, bk, lo_ref, hi_ref, qe_ref, ke_ref, vt_ref, pad_ref, att_ref, qb_ref, m_ref, acc_ref):
    i = pl.program_id(0)
    row0 = pl.multiple_of(i * bq, bq)
    real = pad_ref[...] > 0.5
    for h in range(heads):
        qt = qe_ref[h].astype(F32).T[:HD]
        kt = ke_ref[h, pl.ds(row0, bq), :].astype(F32).T[:HD]
        own = jnp.sum(qt * kt, axis=0, keepdims=True)
        m_ref[h] = jnp.where(real, NEG, own)
        acc_ref[h] = jnp.where(real, 0.0, vt_ref[h, :, pl.ds(row0, bq)].astype(F32))

    def step(at, bk):
        col0 = pl.multiple_of(at, UNIT)
        work = [(h, slice(c, c + QC)) for c in range(0, bq, QC) for h in range(heads)]
        score = lambda h, c: nt(ke_ref[h, pl.ds(col0, bk), :], qe_ref[h, c, :])
        ss = [score(*w) for w in work[:AHEAD]]
        for n, (h, c) in enumerate(work):
            if n + AHEAD < len(work):
                ss.append(score(*work[n + AHEAD]))
            s = ss[n]
            m_old = m_ref[h, :, c]
            m_new = jnp.maximum(m_old, jnp.max(s, axis=0, keepdims=True))
            p = jnp.exp(s - m_new).astype(BF)
            alpha = jnp.exp(m_old - m_new)
            acc_ref[h, :, c] = acc_ref[h, :, c] * alpha + nn(vt_ref[h, :, pl.ds(col0, bk)], p)
            m_ref[h, :, c] = m_new

    in_steps(lo_ref[i], hi_ref[i], bk, step)
    outs = []
    for h in range(heads):
        acc = acc_ref[h]
        total = acc[HD : HD + 1]
        outs.append(jnp.where(real, acc[:HD] / total, 0.0))
        lse = jnp.broadcast_to(m_ref[h] + jnp.log(total), (8, bq)).T[:, :1]
        qb_ref[h] = put3(qe_ref[h], -lse, HD + 4)
    att_ref[...] = (jnp.concatenate(outs, axis=0) if heads > 1 else outs[0]).T.astype(BF)


def attend(qe, ke, vt, padw, lo, hi, bq, bk):
    heads, rows, _ = qe.shape
    full = lambda i, lo, hi: (0, 0, 0)
    return pl.pallas_call(
        functools.partial(fwd_kernel, heads, bq, bk),
        grid_spec=pltpu.PrefetchScalarGridSpec(
            num_scalar_prefetch=2,
            grid=(rows // bq,),
            in_specs=[
                pl.BlockSpec((heads, bq, LANES), lambda i, lo, hi: (0, i, 0)),
                pl.BlockSpec((heads, rows, LANES), full),
                pl.BlockSpec((heads, VT, rows), full),
                pl.BlockSpec((1, bq), lambda i, lo, hi: (0, i)),
            ],
            out_specs=[
                pl.BlockSpec((bq, heads * HD), lambda i, lo, hi: (i, 0)),
                pl.BlockSpec((heads, bq, LANES), lambda i, lo, hi: (0, i, 0)),
            ],
            scratch_shapes=[
                pltpu.VMEM((heads, 1, bq), F32),
                pltpu.VMEM((heads, VT, bq), F32),
            ],
        ),
        out_shape=[
            jax.ShapeDtypeStruct((rows, heads * HD), BF),
            jax.ShapeDtypeStruct((heads, rows, LANES), BF),
        ],
        compiler_params=pltpu.CompilerParams(vmem_limit_bytes=60 << 20),
        name="attend",
    )(lo, hi, qe, ke, vt, padw)


def bwd_kernel(heads, bq, bk, lo_ref, hi_ref, qb_ref, ke_ref, ve_ref, go_ref, att_ref, out_ref, ge_ref, dqt_ref, kt_ref, qt_ref, got_ref, dkt_ref, dvt_ref):
    j = pl.program_id(0)
    rows = qb_ref.shape[1]

    @pl.when(j == 0)
    def _():
        for h in range(heads):
            dqt_ref[h] = jnp.zeros_like(dqt_ref[h])
            for c in range(rows // 512):
                sl = pl.ds(c * 512, 512)
                go = go_ref[sl, h * HD : (h + 1) * HD]
                at = att_ref[sl, h * HD : (h + 1) * HD]
                delta = jnp.sum(go.astype(F32) * at.astype(F32), axis=1, keepdims=True)
                wide = jnp.concatenate([go, jnp.zeros_like(go)], axis=1)
                ge_ref[h, sl, :] = put3(wide, -delta, HD)
                got_ref[h, :, c * 512 : (c + 1) * 512] = wide.T[:HD]
                qt_ref[h, :, c * 512 : (c + 1) * 512] = qb_ref[h, sl, :].T[:HD]

    for h in range(heads):
        kt_ref[h] = ke_ref[h].T[:HD]

    zero = jnp.zeros((HD, bk), F32)

    def step(at, bq):
        row0 = pl.multiple_of(at, UNIT)
        work = [(h, pl.ds(row0 + c, QB)) for c in range(0, bq, QB) for h in range(heads)]
        score = lambda h, c: (nt(ke_ref[h], qb_ref[h, c, :]), nt(ve_ref[h], ge_ref[h, c, :]))
        ss = [score(*w) for w in work[:BAHEAD]]
        for n, (h, c) in enumerate(work):
            if n + BAHEAD < len(work):
                ss.append(score(*work[n + BAHEAD]))
            st, dt = ss[n]
            p = jnp.exp(st)
            ds = (p * dt).astype(BF)
            pb = p.astype(BF)
            dvt_ref[h] += nt(got_ref[h, :, c], pb)
            dkt_ref[h] += nt(qt_ref[h, :, c], ds)
            dqt_ref[h, :, c] += nn(kt_ref[h], ds)

    for h in range(heads):
        dkt_ref[h] = zero
        dvt_ref[h] = zero
    in_steps(lo_ref[j], hi_ref[j], bq, step)
    for h in range(heads):
        for part, ref in ((1, dkt_ref), (2, dvt_ref)):
            at = (part * heads + h) * HD
            out_ref[pl.ds(pl.multiple_of(j * bk, bk), bk), at : at + HD] = ref[h].T.astype(BF)

    @pl.when(j == pl.num_programs(0) - 1)
    def _():
        for h in range(heads):
            for c in range(rows // 512):
                sl = pl.ds(c * 512, 512)
                out_ref[sl, h * HD : (h + 1) * HD] = (dqt_ref[h, :, c * 512 : (c + 1) * 512].T * (HD ** -0.5)).astype(BF)


def attend_back(qb, ke, ve, go, att, lo, hi, bq, bk):
    heads, rows, _ = qb.shape
    full3 = lambda i, lo, hi: (0, 0, 0)
    full2 = lambda i, lo, hi: (0, 0)
    blk3 = lambda i, lo, hi: (0, i, 0)
    wide = heads * HD
    return pl.pallas_call(
        functools.partial(bwd_kernel, heads, bq, bk),
        grid_spec=pltpu.PrefetchScalarGridSpec(
            num_scalar_prefetch=2,
            grid=(rows // bk,),
            in_specs=[
                pl.BlockSpec((heads, rows, LANES), full3),
                pl.BlockSpec((heads, bk, LANES), blk3),
                pl.BlockSpec((heads, bk, LANES), blk3),
                pl.BlockSpec((rows, wide), full2),
                pl.BlockSpec((rows, wide), full2),
            ],
            out_specs=pl.BlockSpec((rows, 3 * wide), full2),
            scratch_shapes=[
                pltpu.VMEM((heads, rows, LANES), BF),
                pltpu.VMEM((heads, HD, rows), F32),
                pltpu.VMEM((heads, HD, bk), BF),
                pltpu.VMEM((heads, HD, rows), BF),
                pltpu.VMEM((heads, HD, rows), BF),
                pltpu.VMEM((heads, HD, bk), F32),
                pltpu.VMEM((heads, HD, bk), F32),
            ],
        ),
        out_shape=jax.ShapeDtypeStruct((rows, 3 * wide), BF),
        compiler_params=pltpu.CompilerParams(vmem_limit_bytes=60 << 20),
        name="attend_back",
    )(lo, hi, qb, ke, ve, go, att)


def dot_f32(a, b, dims):
    return lax.dot_general(a, b, ((dims[:1], dims[1:]), ((), ())), precision=highest, preferred_element_type=F32)


def soap_group(base, group, gr_ref, w_ref, m1_ref, m2_ref, av_ref, st_ref, ba_ref,
               nw_ref, n1_ref, n2_ref, na_ref, ns_ref, nb_ref, aug_ref):
    size = w_ref.shape[-1]
    half = size // 2
    panel = 8
    every = range(group)
    grads, firsts = [], []
    for s in every:
        rows = slice((base + s) * half, (base + s + 1) * half)
        wire = gr_ref[rows, :]
        grads.append(jnp.concatenate([wire[:, :size], wire[:, size:]], axis=0))
        firsts.append(beta_one * m1_ref[0, base + s] + (1.0 - beta_one) * grads[s])
        n1_ref[0, base + s] = firsts[s]
    sides = [(s, side) for s in every for side in range(2)]
    outers = [dot_f32(grads[s], grads[s], (1, 1) if side == 0 else (0, 0)) for s, side in sides]
    both = [dot_f32(jnp.concatenate([grads[s], firsts[s]], axis=0), ba_ref[0, base + s, 1], (1, 0)) for s in every]
    stats = []
    for (s, side), outer in zip(sides, outers):
        stats.append(beta_two * st_ref[0, base + s, side] + (1.0 - beta_two) * outer)
        ns_ref[0, base + s, side] = stats[-1]
    pairs = [dot_f32(ba_ref[0, base + s, 0], jnp.concatenate([both[s][:size], both[s][size:]], axis=1), (0, 0)) for s in every]
    mts = [dot_f32(ba_ref[0, base + s, side], stat, (0, 1)) for (s, side), stat in zip(sides, stats)]
    scaled = []
    for s in every:
        rotated, moment = pairs[s][:, :size], pairs[s][:, size:]
        second = beta_two * m2_ref[0, base + s] + (1.0 - beta_two) * rotated * rotated
        n2_ref[0, base + s] = second
        scaled.append(moment / (jnp.sqrt(second) + step_eps))
    grams = [dot_f32(mt, mt, (1, 1)) for mt in mts]
    inner = [dot_f32(scaled[s], ba_ref[0, base + s, 1], (1, 1)) for s in every]
    for m, (gram, mt) in enumerate(zip(grams, mts)):
        aug_ref[m] = jnp.concatenate([gram, mt], axis=1)
    directions = [dot_f32(ba_ref[0, base + s, 0], inner[s], (1, 0)) for s in every]
    for s in every:
        weight = w_ref[0, base + s]
        fresh = weight - step_rate * (directions[s] + weight_decay * weight)
        nw_ref[0, base + s] = fresh
        na_ref[0, base + s] = average_keep * av_ref[0, base + s] + (1.0 - average_keep) * fresh
    count = 2 * group
    row = lax.broadcasted_iota(jnp.int32, (count, panel, LANES), 1)
    for p in range(size // panel):
        top = p * panel
        part = aug_ref[:, top : top + panel, :]
        for r in range(panel):
            pivot = lax.rsqrt(part[:, r : r + 1, top + r : top + r + 1])
            lead = part[:, r : r + 1, :] * pivot
            column = jnp.where(row > r, part[:, :, top + r : top + r + 1] * pivot, 0.0)
            part = jnp.where(row == r, lead, part - column * lead)
        aug_ref[:, top : top + panel, :] = part
        below = top + panel
        if below < size:
            high = part.astype(BF).astype(F32)
            rest = part - high
            mid = rest.astype(BF).astype(F32)
            low = rest - mid
            first = jnp.concatenate([high, high, mid, high, mid, low], axis=1).astype(BF)
            other = jnp.concatenate([high, mid, high, low, mid, high], axis=1).astype(BF)
            for m in range(count):
                aug_ref[m, below:, :] -= lax.dot_general(
                    first[m][:, below:size], other[m], (((0,), (0,)), ((), ())), preferred_element_type=F32
                )
    for s in range(group):
        for side in range(2):
            nb_ref[0, base + s, side] = aug_ref[2 * s + side][:, size:].T


MESH = pl.DeviceIdType.MESH


def normalize(values):
    center = jnp.mean(values, axis=-1, keepdims=True)
    centered = values - center
    variance = jnp.mean(centered * centered, axis=-1, keepdims=True)
    scale = lax.rsqrt(variance + norm_eps)
    return centered * scale, scale


def norm_back(grad, xhat, scale):
    along = jnp.mean(grad * xhat, axis=-1, keepdims=True)
    return (grad - jnp.mean(grad, axis=-1, keepdims=True) - xhat * along) * scale


TAIL = 0.305
TAIL_FIT = (
    0.1216397411342051,
    0.12246669816059132,
    0.10342157025713879,
    0.1210193967312446,
    -0.037972477455618554,
    0.18571204369074895,
    -0.15298537812807472,
    0.036698452375741396,
)


def gelu_pair(u):
    size = jnp.abs(u)
    bell = jnp.exp(-0.5 * u * u)
    t = 1.0 / (1.0 + TAIL * size)
    poly = jnp.full_like(t, TAIL_FIT[-1])
    for c in TAIL_FIT[-2::-1]:
        poly = poly * t + c
    upper = poly * t * bell
    cdf = jnp.where(u > 0.0, 1.0 - upper, upper)
    return u * cdf, cdf + (0.3989422804014327 * u) * bell


def block_rows(ref, start, half):
    return ref[pl.ds(pl.multiple_of(start, 16), half), :]


def project_kernel(heads, rows_dev, gains_at, row_ref, wire_ref, tok_ref, seg_ref, pad_ref, gain_ref,
                   norm_ref, qe_ref, ke_ref, ve_ref, vt_ref, mix_ref, wide_ref):
    width = tok_ref.shape[1]
    half = HD // 2
    cols = 3 * heads

    @pl.when(pl.program_id(0) == 0)
    def _():
        zero = jnp.zeros((half, HD), BF)

        def fill(r, _):
            low = pl.multiple_of(r * HD, HD)
            for c in range(cols):
                t = block_rows(wire_ref, row_ref[r * cols + c], half)
                for part in range(2):
                    piece = t[:, part * HD : (part + 1) * HD]
                    at = pl.ds(low + part * half, half)
                    wide_ref[at, c * LANES : (c + 1) * LANES] = jnp.concatenate([piece, zero], axis=1)
                    mix_ref[at, c * HD : (c + 1) * HD] = piece
            return 0

        lax.fori_loop(0, width // HD, fill, 0)

    xhat, _ = normalize(tok_ref[...].astype(F32))
    normed = (xhat * gain_ref[...]).astype(BF)
    norm_ref[...] = normed
    count = tok_ref.shape[0]
    lane = lax.broadcasted_iota(jnp.int32, (LANES, count), 0)
    seg = seg_ref[...]
    same = lane - HD == seg
    in_segs = (lane >= HD) & (lane < HD + SEGS)
    ones = (lane >= HD + SEGS) & (lane < HD + SEGS + 3)
    ext_q = jnp.where(same, 1.0, 0.0).T
    ext_k = jnp.where(in_segs, jnp.where(same & (pad_ref[...] > 0.5), 0.0, NEG), jnp.where(ones, 1.0, 0.0)).T
    ext_v = jnp.where((lane >= HD) & (lane < HD + 3), 1.0, 0.0).T
    for h in range(heads):
        for ref, part, scale, ext in ((qe_ref, 0, HD ** -0.5, ext_q), (ke_ref, 1, 1.0, ext_k), (ve_ref, 2, 1.0, ext_v)):
            c = part * heads + h
            mixed = nn(normed, wide_ref[:, c * LANES : (c + 1) * LANES]).astype(BF)
            out = (mixed.astype(F32) * scale + ext).astype(BF)
            ref[h] = out
            if part == 2:
                vt_ref[h] = out.T[:VT]


def project(wire, row_own, tokens, seg, pad, gain_one, heads):
    rows, width = tokens.shape
    tb = min(512, rows)
    full = lambda i, r: (0, 0)
    blk = lambda i, r: (i, 0)
    col = lambda i, r: (0, i)
    ext = lambda i, r: (0, i, 0)
    out = lambda *s: jax.ShapeDtypeStruct(s, BF)
    return pl.pallas_call(
        functools.partial(project_kernel, heads, 0, 0),
        grid_spec=pltpu.PrefetchScalarGridSpec(
            num_scalar_prefetch=1,
            grid=(rows // tb,),
            in_specs=[
                pl.BlockSpec(wire.shape, full),
                pl.BlockSpec((tb, width), blk),
                pl.BlockSpec((1, tb), col),
                pl.BlockSpec((1, tb), col),
                pl.BlockSpec((1, width), full),
            ],
            out_specs=[
                pl.BlockSpec((tb, width), blk),
                pl.BlockSpec((heads, tb, LANES), ext),
                pl.BlockSpec((heads, tb, LANES), ext),
                pl.BlockSpec((heads, tb, LANES), ext),
                pl.BlockSpec((heads, VT, tb), lambda i, r: (0, 0, i)),
                pl.BlockSpec((width, 3 * heads * HD), full),
            ],
            scratch_shapes=[pltpu.VMEM((width, 3 * heads * LANES), BF)],
        ),
        out_shape=[
            out(rows, width),
            out(heads, rows, LANES),
            out(heads, rows, LANES),
            out(heads, rows, LANES),
            out(heads, VT, rows),
            out(width, 3 * heads * HD),
        ],
        compiler_params=pltpu.CompilerParams(vmem_limit_bytes=60 << 20),
        name="project",
    )(row_own, wire, tokens, seg, pad, gain_one)


def middle_kernel(shards, span, units, wide, gain_row, gains_dev, inside,
                  unit_ref, sel_ref, wire_ref, gain_ref, pad_ref, att_ref, tok_ref, cot_ref,
                  outa_ref, outb_ref, res_ref, back_ref, grads_ref, mix_ref,
                  tokens_ref, cots_ref, got_ref, give_ref, wo_ref, wu_ref, wd_ref, go_ref, gu_ref, gd_ref, gg_ref, blk_ref,
                  local_sem, send_i, recv_i, send_b, recv_b, send_a, recv_a):
    own, width = tokens_ref.shape
    parts = recv_i.shape[1]
    tb = own // parts
    half = HD // 2
    rows_dev = grads_ref.shape[1]
    z = lax.axis_index("narrow")
    kinds = (
        (mix_ref, None, width, 3 * span),
        (wo_ref, go_ref, span, width),
        (wu_ref, gu_ref, width, units),
        (wd_ref, gd_ref, units, width),
    )
    mix_blocks = width // HD * (3 * span // HD)
    per = blk_ref.shape[0] // shards

    barrier = pltpu.get_barrier_semaphore()
    for d in range(1, shards):
        pl.semaphore_signal(barrier, inc=1, device_id={"narrow": lax.rem(z + d, shards)}, device_id_type=MESH)
    pl.semaphore_wait(barrier, shards - 1)

    def bring(d, t, mine):
        peer = lax.rem(z + d, shards)
        slot = z if mine else peer
        return pltpu.make_async_remote_copy(
            src_ref=att_ref.at[pl.ds(pl.multiple_of(peer * own + t * tb, tb), tb), :],
            dst_ref=got_ref.at[slot, pl.ds(pl.multiple_of(t * tb, tb), tb), :],
            send_sem=send_i.at[d - 1, t],
            recv_sem=recv_i.at[slot, t],
            device_id={"narrow": peer},
            device_id_type=MESH,
        )

    def give(d, t, mine):
        peer = lax.rem(z + d, shards)
        slot = z if mine else peer
        return pltpu.make_async_remote_copy(
            src_ref=give_ref.at[peer, pl.ds(pl.multiple_of(t * tb, tb), tb), :],
            dst_ref=back_ref.at[pl.ds(pl.multiple_of(slot * own + t * tb, tb), tb), :],
            send_sem=send_b.at[d - 1, t],
            recv_sem=recv_b.at[slot, t],
            device_id={"narrow": peer},
            device_id_type=MESH,
        )

    def hop_copy(c, t, step):
        at = pl.ds(pl.multiple_of(t * tb, tb), tb)
        return pltpu.make_async_remote_copy(
            src_ref=outa_ref.at[c, at, :],
            dst_ref=outa_ref.at[c, at, :],
            send_sem=send_a.at[step, c, t],
            recv_sem=recv_a.at[c, t],
            device_id={"narrow": lax.rem(z + (1 if step == 0 else shards - 1), shards)},
            device_id_type=MESH,
        )

    room = (z < shards - 1, z > 0)
    for t in range(parts):
        for d in range(1, shards):
            bring(d, t, True).start()
    mine = pl.ds(pl.multiple_of(z * own, own), own)
    copies = [
        pltpu.make_async_copy(att_ref.at[mine, :], got_ref.at[z], local_sem.at[0]),
        pltpu.make_async_copy(tok_ref.at[mine, :], tokens_ref, local_sem.at[1]),
        pltpu.make_async_copy(cot_ref.at[mine, :], cots_ref, local_sem.at[2]),
    ]
    for copy in copies:
        copy.start()

    base = 0
    for ref, acc, rows, cols in kinds:
        grid_cols = cols // HD

        def fill(r, _, ref=ref, base=base, grid_cols=grid_cols):
            low = pl.multiple_of(r * HD, HD)
            for n in range(shards):
                for c in range(grid_cols):
                    unit = unit_ref[base + r * grid_cols + c] + n * (rows_dev // 16)
                    t = jnp.concatenate([wire_ref[unit], wire_ref[unit + 1]], axis=0)
                    for part in range(2):
                        ref[n, pl.ds(low + part * half, half), c * HD : (c + 1) * HD] = t[:, part * HD : (part + 1) * HD]
            return 0

        lax.fori_loop(0, rows // HD, fill, 0)
        base += rows // HD * grid_cols
        if acc is not None:
            acc[...] = jnp.zeros_like(acc)
    gg_ref[...] = jnp.zeros_like(gg_ref)
    for copy in copies:
        copy.wait()

    def block(t, _):
        at = pl.ds(pl.multiple_of(t * tb, tb), tb)
        for d in range(1, shards):
            bring(d, t, False).wait_recv()
        tokens = tokens_ref[at, :].astype(F32)
        cot = cots_ref[at, :]
        branch = nn(got_ref[0, at, :], wo_ref[0])
        for n in range(1, shards):
            branch += nn(got_ref[n, at, :], wo_ref[n])
        residual = tokens + branch
        xhat, scale = normalize(residual)
        gain = gain_ref[...]
        normed = (xhat * gain).astype(BF)
        ups = [nn(normed, wu_ref[n]) for n in range(shards)]
        downs = [nt(cot, wd_ref[n]) for n in range(shards)]
        actives, back_ups = [], []
        for n in range(shards):
            value, slope = gelu_pair(ups[n])
            actives.append(value.astype(BF))
            back_ups.append((slope * downs[n]).astype(BF))
        mlp = nn(actives[0], wd_ref[0])
        back = nt(back_ups[0], wu_ref[0])
        for n in range(1, shards):
            mlp += nn(actives[n], wd_ref[n])
            back += nt(back_ups[n], wu_ref[n])
        out = (residual + mlp).astype(BF)

        @pl.when(t < inside)
        def _():
            outa_ref[z, at, :] = out
            for step in range(2):

                @pl.when(room[step])
                def _(step=step):
                    hop_copy(z, t, step).start()

        @pl.when(t >= inside)
        def _():
            outb_ref[pl.ds(pl.multiple_of((t - inside) * tb, tb), tb), :] = out

        gg_ref[...] += jnp.sum(back * xhat, axis=0, keepdims=True)
        back_res = cot.astype(F32) + norm_back(back * gain, xhat, scale)
        res_ref[at, :] = back_res
        branch_low = back_res.astype(BF)
        line = pad_ref[:, pl.ds(pl.multiple_of(z * own + t * tb, LANES), tb)]
        pad = jnp.broadcast_to(line, (8, tb)).T[:, :1]
        for n in range(shards):
            give_ref[n, at, :] = (nt(branch_low, wo_ref[n]) * pad).astype(BF)
        for d in range(1, shards):
            give(d, t, True).start()
        for n in range(shards):
            gd_ref[n] += tn(actives[n], cot)
            gu_ref[n] += tn(normed, back_ups[n])
            go_ref[n] += tn(got_ref[n, at, :], branch_low)
        return 0

    lax.fori_loop(0, parts, block, 0)
    back_ref[mine, :] = give_ref[z]
    base = 0
    for ref, acc, rows, cols in kinds:
        grid_cols = cols // HD
        if acc is not None:

            def cut(r, _, acc=acc, base=base, grid_cols=grid_cols):
                low = pl.multiple_of(r * HD, HD)
                for n in range(shards):
                    for c in range(grid_cols):
                        lanes = slice(c * HD, (c + 1) * HD)
                        value = jnp.concatenate([acc[n, pl.ds(low, half), lanes], acc[n, pl.ds(low + half, half), lanes]], axis=1)
                        blk_ref[n * per + base - mix_blocks + r * grid_cols + c] = value.astype(BF)
                return 0

            lax.fori_loop(0, rows // HD, cut, 0)
        base += rows // HD * grid_cols
    for n in range(shards):
        blk_ref[(n + 1) * per - 1] = jnp.zeros((half, LANES), BF)
    slots = gain_row // half
    top = lax.broadcasted_iota(jnp.int32, (16, LANES), 0) == 0

    def place(v, _):
        for n in range(shards):
            for i in range(slots):
                grads_ref[v * shards + n, i * half : (i + 1) * half, :] = blk_ref[sel_ref[v * slots + i] + n * per]
        return 0

    lax.fori_loop(0, wide, place, 0)
    for v in range(wide):
        piece = v * gains_dev // LANES - width // LANES
        for n in range(shards):
            if piece >= 0:
                value = jnp.where(top, gg_ref[:, piece * LANES : (piece + 1) * LANES], 0.0).astype(BF)
            else:
                value = jnp.zeros((16, LANES), BF)
            grads_ref[v * shards + n, gain_row:, :] = value

    hops = [(s, t, step) for s in range(1, shards) for t in range(inside) for step in range(2)]
    for s, t, step in hops:
        chunk = z - s if step == 0 else z + s
        there = chunk >= 0 if step == 0 else chunk < shards

        @pl.when(there)
        def _(chunk=chunk, t=t, step=step):
            hop_copy(chunk, t, step).wait_recv()

        @pl.when(there & room[step])
        def _(chunk=chunk, t=t, step=step):
            hop_copy(chunk, t, step).start()

    for t in range(parts):
        for d in range(1, shards):
            give(d, t, False).wait_recv()
    for t in range(parts):
        for d in range(1, shards):
            bring(d, t, True).wait_send()
            give(d, t, True).wait_send()
    for t in range(inside):
        for step in range(2):

            @pl.when(room[step])
            def _(t=t, step=step):
                hop_copy(z, t, step).wait_send()

    for s, t, step in hops:
        chunk = z - s if step == 0 else z + s
        there = chunk >= 0 if step == 0 else chunk < shards

        @pl.when(there & room[step])
        def _(chunk=chunk, t=t, step=step):
            hop_copy(chunk, t, step).wait_send()


def middle(unit, sel, wire, gain_two, pad, att, tokens, cotangent, shards, wide, rows_dev, gain_row, gains_dev):
    rows, span = att.shape
    width = tokens.shape[1]
    units = FF // shards
    own = rows // shards
    tb = min(256, own)
    parts = own // tb
    inside = max(1, parts // 4)
    blocks = unit.shape[0] - width // HD * (3 * span // HD)
    vmem = pl.BlockSpec(memory_space=pltpu.VMEM)
    smem = pl.BlockSpec(memory_space=pltpu.SMEM)
    hbm = pl.BlockSpec(memory_space=pl.ANY)
    dma = pltpu.SemaphoreType.DMA
    return pl.pallas_call(
        functools.partial(middle_kernel, shards, span, units, wide, gain_row, gains_dev, inside),
        in_specs=[smem, smem, vmem, vmem, vmem, hbm, hbm, hbm],
        out_specs=[vmem] * 6,
        out_shape=[
            jax.ShapeDtypeStruct((shards, inside * tb, width), BF),
            jax.ShapeDtypeStruct((own - inside * tb, width), BF),
            jax.ShapeDtypeStruct((own, width), F32),
            jax.ShapeDtypeStruct((rows, span), BF),
            jax.ShapeDtypeStruct((wide * shards, rows_dev, LANES), BF),
            jax.ShapeDtypeStruct((shards, width, 3 * span), BF),
        ],
        scratch_shapes=[
            pltpu.VMEM((own, width), BF),
            pltpu.VMEM((own, width), BF),
            pltpu.VMEM((shards, own, span), BF),
            pltpu.VMEM((shards, own, span), BF),
            pltpu.VMEM((shards, span, width), BF),
            pltpu.VMEM((shards, width, units), BF),
            pltpu.VMEM((shards, units, width), BF),
            pltpu.VMEM((shards, span, width), F32),
            pltpu.VMEM((shards, width, units), F32),
            pltpu.VMEM((shards, units, width), F32),
            pltpu.VMEM((1, width), F32),
            pltpu.VMEM((shards * (blocks + 1), HD // 2, LANES), BF),
            dma((3,)),
            dma((shards - 1, parts)),
            dma((shards, parts)),
            dma((shards - 1, parts)),
            dma((shards, parts)),
            dma((2, shards, inside)),
            dma((shards, inside)),
        ],
        compiler_params=pltpu.CompilerParams(vmem_limit_bytes=63 << 20, collective_id=2, has_side_effects=True),
        name="middle",
    )(unit, sel, wire, gain_two, pad, att, tokens, cotangent)


PARTS = 4


def finish_kernel(shards, wide, gain_row, gains_dev, group, sel_ref, mix_ref, full_ref, gain_ref, res_ref, bm_ref, norm_ref, tok_ref, *refs):
    states, outs = refs[1:7], refs[9:15]
    first_ref, grad_ref, line_ref = refs[0], refs[7], refs[8]
    (own_ref, normed_ref, tokens_ref, got_ref, acc_ref, blk_ref, grads_ref, sums_ref, firsts_ref, part_ref, aug_ref,
     local_sem, send_z, recv_z, send_w, recv_w, send_a, recv_a, send_g, recv_g, send_f, recv_f) = refs[15:]
    width = norm_ref.shape[1]
    rows, cols = bm_ref.shape
    own = rows // shards
    hold = own // PARTS
    half = HD // 2
    grid_cols = cols // HD
    blocks = width // HD * grid_cols
    slots = gain_row // half
    z = lax.axis_index("narrow")
    w = lax.axis_index("wide")

    barrier = pltpu.get_barrier_semaphore()
    for d in range(1, shards):
        pl.semaphore_signal(barrier, inc=1, device_id={"narrow": lax.rem(z + d, shards)}, device_id_type=MESH)
    for d in range(1, wide):
        pl.semaphore_signal(barrier, inc=1, device_id={"wide": lax.rem(w + d, wide)}, device_id_type=MESH)
    pl.semaphore_wait(barrier, shards + wide - 2)

    def to_peer(d, part, mine):
        peer = lax.rem(z + d, shards)
        slot = z if mine else peer
        at = pl.multiple_of(peer * own + part * hold, hold)
        return pltpu.make_async_remote_copy(
            src_ref=bm_ref.at[pl.ds(at, hold), :],
            dst_ref=got_ref.at[slot, pl.ds(part * hold, hold), :],
            send_sem=send_z.at[d - 1, part],
            recv_sem=recv_z.at[slot, part],
            device_id={"narrow": peer},
            device_id_type=MESH,
        )

    def to_owner(d, mine):
        peer = lax.rem(w + d, wide)
        slot = w if mine else peer
        return pltpu.make_async_remote_copy(
            src_ref=grads_ref.at[peer],
            dst_ref=sums_ref.at[slot],
            send_sem=send_w.at[d - 1],
            recv_sem=recv_w.at[slot],
            device_id={"wide": peer},
            device_id_type=MESH,
        )

    def hop_copy(c, part, step):
        at = pl.ds(pl.multiple_of(c * own + part * hold, hold), hold)
        return pltpu.make_async_remote_copy(
            src_ref=grad_ref.at[at, :],
            dst_ref=grad_ref.at[at, :],
            send_sem=send_a.at[step, c, part],
            recv_sem=recv_a.at[c, part],
            device_id={"narrow": lax.rem(z + (1 if step == 0 else shards - 1), shards)},
            device_id_type=MESH,
        )

    def pass_on(c, part, act):
        for step, there in ((0, z < shards - 1), (1, z > 0)):
            if c is None or step == c[0]:
                chunk = z if c is None else c[1]
                ok = there if c is None else there & c[2]

                @pl.when(ok)
                def _(chunk=chunk, step=step):
                    act(hop_copy(chunk, part, step))

    def line_to(d, mine):
        peer = lax.rem(z + d, shards)
        slot = z if mine else peer
        return pltpu.make_async_remote_copy(
            src_ref=line_ref.at[z],
            dst_ref=line_ref.at[slot],
            send_sem=send_g.at[d - 1],
            recv_sem=recv_g.at[slot],
            device_id={"narrow": peer},
            device_id_type=MESH,
        )

    rows_dev = part_ref.shape[0]

    def first_to(d, mine):
        peer = lax.rem(z + d, shards)
        slot = z if mine else peer
        return pltpu.make_async_remote_copy(
            src_ref=first_ref.at[pl.ds(pl.multiple_of(peer * rows_dev, 16), rows_dev), :],
            dst_ref=firsts_ref.at[slot],
            send_sem=send_f.at[d - 1],
            recv_sem=recv_f.at[slot],
            device_id={"narrow": peer},
            device_id_type=MESH,
        )

    for d in range(1, shards):
        first_to(d, True).start()
    for part in range(PARTS):
        for d in range(1, shards):
            to_peer(d, part, True).start()
    mine = pl.ds(pl.multiple_of(z * own, own), own)
    copies = [
        pltpu.make_async_copy(bm_ref, own_ref, local_sem.at[0]),
        pltpu.make_async_copy(norm_ref, normed_ref, local_sem.at[1]),
        pltpu.make_async_copy(tok_ref.at[mine, :], tokens_ref, local_sem.at[2]),
        pltpu.make_async_copy(bm_ref.at[mine, :], got_ref.at[z], local_sem.at[3]),
        pltpu.make_async_copy(
            first_ref.at[pl.ds(pl.multiple_of(z * rows_dev, 16), rows_dev), :], firsts_ref.at[z], local_sem.at[4]
        ),
    ]
    for copy in copies:
        copy.start()
    for copy in copies:
        copy.wait()

    acc_ref[...] = jnp.zeros_like(acc_ref)
    tb = min(512, rows)

    def add(i, _):
        at = pl.ds(pl.multiple_of(i * tb, tb), tb)
        acc_ref[...] += tn(normed_ref[at, :], own_ref[at, :])
        return 0

    lax.fori_loop(0, rows // tb, add, 0)
    blk_ref[blocks] = jnp.zeros((half, LANES), BF)

    def cut(r, _):
        low = pl.multiple_of(r * HD, HD)
        for c in range(grid_cols):
            lanes = slice(c * HD, (c + 1) * HD)
            value = jnp.concatenate([acc_ref[pl.ds(low, half), lanes], acc_ref[pl.ds(low + half, half), lanes]], axis=1)
            blk_ref[r * grid_cols + c] = value.astype(BF)
        return 0

    lax.fori_loop(0, width // HD, cut, 0)
    along = jnp.sum(acc_ref[...] * mix_ref[...].astype(F32), axis=1, keepdims=True)
    line = jnp.broadcast_to(along, (width, LANES)).T[:16] / gain_ref[...]
    top = lax.broadcasted_iota(jnp.int32, (16, LANES), 0) == 0
    for v in range(wide):

        def place(i, _, v=v):
            grads_ref[v, pl.ds(pl.multiple_of(i * half, half), half), :] = blk_ref[sel_ref[v * slots + i]]
            return 0

        lax.fori_loop(0, slots, place, 0)
        piece = v * gains_dev // LANES
        if piece < width // LANES:
            value = jnp.where(top, line[:, piece * LANES : (piece + 1) * LANES], 0.0).astype(BF)
        else:
            value = jnp.zeros((16, LANES), BF)
        grads_ref[v, gain_row : gain_row + 16, :] = value
    for d in range(1, wide):
        to_owner(d, True).start()
    part_ref[...] = grads_ref[w].astype(F32)

    tile = min(256, hold)

    def norm_rows(i, _):
        at = pl.ds(pl.multiple_of(i * tile, tile), tile)
        back = nt(got_ref[0, at, :], full_ref[0])
        for n in range(1, shards):
            back += nt(got_ref[n, at, :], full_ref[n])
        xhat, scale = normalize(tokens_ref[at, :].astype(F32))
        grad = res_ref[at, :] + norm_back(back * gain_ref[...], xhat, scale)
        grad_ref[pl.ds(pl.multiple_of(z * own + i * tile, tile), tile), :] = grad.astype(BF)
        return 0

    def norm_part(part):
        for d in range(1, shards):
            to_peer(d, part, False).wait_recv()
        lax.fori_loop(part * hold // tile, (part + 1) * hold // tile, norm_rows, 0)
        pass_on(None, part, lambda copy: copy.start())

    for d in range(1, wide):
        to_owner(d, False).wait_recv()
    for d in range(1, wide):
        part_ref[...] += sums_ref[lax.rem(w + d, wide)].astype(F32)
    line_ref[z] = part_ref[gain_row : gain_row + 16, :]
    for d in range(1, shards):
        line_to(d, True).start()
    for d in range(1, shards):
        first_to(d, False).wait_recv()
    total = firsts_ref[0].astype(F32)
    for n in range(1, shards):
        total += firsts_ref[n].astype(F32)
    line_ref[shards] = total[gain_row : gain_row + 16, :]
    part_ref[...] += total
    hops = [(s, part, step) for part in range(PARTS) for s in range(1, shards) for step in range(2)]
    hops.sort(key=lambda hop: hop[0] + hop[1])

    def wave(done, upto):
        for s, part, step in hops:
            if done < s + part <= upto:
                chunk = z - s if step == 0 else z + s
                there = chunk >= 0 if step == 0 else chunk < shards

                @pl.when(there)
                def _(chunk=chunk, part=part, step=step):
                    hop_copy(chunk, part, step).wait_recv()

                pass_on((step, chunk, there), part, lambda copy: copy.start())

    rounds = slots // group
    ready = 0
    for g in range(rounds):
        upto = PARTS * (g + 1) // (2 * rounds)
        while ready < upto:
            norm_part(ready)
            wave(ready - 1, ready)
            ready += 1
        soap_group(g * group, group, part_ref, *states, *outs, aug_ref)
    while ready < PARTS:
        norm_part(ready)
        wave(ready - 1, ready)
        ready += 1
    wave(PARTS - 1, PARTS + shards)
    for d in range(1, shards):
        line_to(d, False).wait_recv()
    for part in range(PARTS):
        pass_on(None, part, lambda copy: copy.wait_send())
    for s, part, step in hops:
        chunk = z - s if step == 0 else z + s
        there = chunk >= 0 if step == 0 else chunk < shards
        pass_on((step, chunk, there), part, lambda copy: copy.wait_send())
    for d in range(1, shards):
        line_to(d, True).wait_send()
        first_to(d, True).wait_send()
    for part in range(PARTS):
        for d in range(1, shards):
            to_peer(d, part, True).wait_send()
    for d in range(1, wide):
        to_owner(d, True).wait_send()


def finish(sel, mix, mix_full, gain_one, res, bm, normed, tokens, states, group, wide, rows_dev, gain_row, gains_dev):
    shards = mix_full.shape[0]
    rows, cols = bm.shape
    width = normed.shape[1]
    own = rows // shards
    half = HD // 2
    blocks = width // HD * (cols // HD)
    vmem = pl.BlockSpec(memory_space=pltpu.VMEM)
    smem = pl.BlockSpec(memory_space=pltpu.SMEM)
    hbm = pl.BlockSpec(memory_space=pl.ANY)
    dma = pltpu.SemaphoreType.DMA
    return pl.pallas_call(
        functools.partial(finish_kernel, shards, wide, gain_row, gains_dev, group),
        in_specs=[smem, vmem, vmem, vmem, vmem, hbm, hbm, hbm, hbm] + [vmem] * 6,
        out_specs=[vmem] * 8,
        out_shape=[jax.ShapeDtypeStruct((rows, width), BF), jax.ShapeDtypeStruct((shards + 1, 16, LANES), F32)]
        + [jax.ShapeDtypeStruct(a.shape, a.dtype) for a in states[1:]],
        scratch_shapes=[
            pltpu.VMEM((rows, cols), BF),
            pltpu.VMEM((rows, width), BF),
            pltpu.VMEM((own, width), BF),
            pltpu.VMEM((shards, own, cols), BF),
            pltpu.VMEM((width, cols), F32),
            pltpu.VMEM((blocks + 1, half, LANES), BF),
            pltpu.VMEM((wide, rows_dev, LANES), BF),
            pltpu.VMEM((wide, rows_dev, LANES), BF),
            pltpu.VMEM((shards, rows_dev, LANES), BF),
            pltpu.VMEM((rows_dev, LANES), F32),
            pltpu.VMEM((2 * group, HD, LANES), F32),
            dma((5,)),
            dma((shards - 1, PARTS)),
            dma((shards, PARTS)),
            dma((wide - 1,)),
            dma((wide,)),
            dma((2, shards, PARTS)),
            dma((shards, PARTS)),
            dma((shards - 1,)),
            dma((shards,)),
            dma((shards - 1,)),
            dma((shards,)),
        ],
        compiler_params=pltpu.CompilerParams(vmem_limit_bytes=62 << 20, collective_id=1, has_side_effects=True),
        name="finish",
    )(sel, mix, mix_full, gain_one, res, bm, normed, tokens, *states)


def wrap_kernel(count, inside, grad_ref, outa_ref, outb_ref, *refs):
    shards = outa_ref.shape[0]
    olds, wide_ref, out_ref, news, sem = refs[:count], refs[count], refs[count + 1], refs[count + 2 : -1], refs[-1]
    copies = [pltpu.make_async_copy(old, new, sem.at[k]) for k, (old, new) in enumerate(zip(olds, news))]
    for n in range(shards):
        copies.append(pltpu.make_async_copy(outa_ref.at[n], out_ref.at[n, :inside], sem.at[count + 2 * n]))
        copies.append(pltpu.make_async_copy(outb_ref.at[n], out_ref.at[n, inside:], sem.at[count + 2 * n + 1]))

    @pl.when(pl.program_id(0) == 0)
    def _():
        for copy in copies:
            copy.start()

    wide_ref[...] = grad_ref[...].astype(F32)

    @pl.when(pl.program_id(0) == pl.num_programs(0) - 1)
    def _():
        for copy in copies:
            copy.wait()


def wrap(grad, out_a, out_b, olds):
    rows, width = grad.shape
    shards, inside, _ = out_a.shape
    own = inside + out_b.shape[1]
    tb = min(512, rows)
    hbm = pl.BlockSpec(memory_space=pl.ANY)
    blk = pl.BlockSpec((tb, width), lambda i: (i, 0))
    return pl.pallas_call(
        functools.partial(wrap_kernel, len(olds), inside),
        grid=(rows // tb,),
        in_specs=[blk, hbm, hbm] + [hbm] * len(olds),
        out_specs=[blk, hbm] + [hbm] * len(olds),
        out_shape=[jax.ShapeDtypeStruct((rows, width), F32), jax.ShapeDtypeStruct((shards, own, width), BF)]
        + [jax.ShapeDtypeStruct(a.shape, a.dtype) for a in olds],
        scratch_shapes=[pltpu.SemaphoreType.DMA((len(olds) + 2 * shards,))],
        compiler_params=pltpu.CompilerParams(vmem_limit_bytes=60 << 20),
        name="wrap",
    )(grad, out_a, out_b, *olds)


def adam_gains(grad, gain, first, second, average):
    new_first = beta_one * first + (1.0 - beta_one) * grad
    new_second = beta_two * second + (1.0 - beta_two) * grad * grad
    new_gain = gain - gain_rate * new_first / (jnp.sqrt(new_second) + step_eps)
    new_average = average_keep * average + (1.0 - average_keep) * new_gain
    return (new_gain, new_first, new_second, new_average)


def body(
    tokens,
    cotangent,
    segment_ids,
    pad_mask,
    owner_order,
    weights,
    first_moment,
    second_moment,
    average,
    stats,
    bases,
    gains,
    gain_first,
    gain_second,
    gain_average,
):
    narrow = lax.axis_size("narrow")
    wide = lax.axis_size("wide")
    heads = HEADS // narrow
    rows, width = tokens.shape
    span = heads * HD
    own = rows // narrow
    slots, size = weights.shape[1], weights.shape[2]
    half = size // 2
    block_count = owner_order.shape[0]
    gains_dev = gains.shape[0]
    gain_row = slots * half
    rows_dev = gain_row + 16

    low = weights[0].astype(BF)
    wire = jnp.concatenate([low[:, :half], low[:, half:]], axis=2).reshape(gain_row, 2 * size)
    wire = jnp.concatenate([wire, jnp.pad(gains.astype(BF)[None], ((0, 15), (0, LANES - gains_dev)))], axis=0)
    wire_own = lax.all_gather(wire, "wide", axis=0, tiled=True)
    wire_full = lax.all_gather(lax.all_gather(wire, "narrow", axis=0, tiled=True), "wide", axis=0, tiled=True)

    ids = jnp.arange(block_count, dtype=jnp.int32)
    slot_of = jnp.sum(jnp.where(owner_order[None, :] == ids[:, None], ids[None, :], 0), axis=1)
    device, place = slot_of // slots, slot_of % slots
    row_own = device * rows_dev + place * half
    row_full = device * (narrow * rows_dev) + place * half

    gain_all = wire_own.reshape(wide, rows_dev, LANES)[:, gain_row, :gains_dev].astype(F32).reshape(1, 2 * width)
    gain_one, gain_two = gain_all[:, :width], gain_all[:, width:]
    seg = segment_ids
    seg_row = segment_ids[0]
    pad = pad_mask.astype(F32)
    block = min(512, rows)
    low_seg = seg_row[::block]
    high_seg = seg_row[block - 1 :: block]
    begin = jnp.sum((seg_row[None, :] < low_seg[:, None]).astype(jnp.int32), axis=1) // UNIT
    end = (jnp.sum((seg_row[None, :] <= high_seg[:, None]).astype(jnp.int32), axis=1) + UNIT - 1) // UNIT

    normed, qe, ke, ve, vt, mix = project(wire_own, row_own, tokens, seg, pad, gain_one, heads)
    attended, qb = attend(qe, ke, vt, pad, begin, end, block, block)
    unit = row_full // 16
    mix_blocks = width // size * 3 * heads
    sel_rest = jnp.where(owner_order >= mix_blocks, owner_order - mix_blocks, block_count - mix_blocks)
    out_a, out_b, back_res, back_att, grads, mix_full = middle(
        unit, sel_rest, wire_full.reshape(-1, 16, LANES), gain_two, pad, attended, tokens, cotangent,
        narrow, wide, rows_dev, gain_row, gains_dev,
    )
    part_a = lax.psum_scatter(grads.reshape(-1, LANES), "wide", scatter_dimension=0, tiled=True)
    out_b = lax.all_to_all(jnp.broadcast_to(out_b, (narrow, *out_b.shape)), "narrow", 0, 0)
    bm = attend_back(qb, ke, ve, back_att, attended, begin, end, block, block)
    bm, part_a, out_b = lax.optimization_barrier((bm, part_a, out_b))
    sel = jnp.minimum(owner_order, mix_blocks)
    group = next(g for g in range(min(12, slots), 0, -1) if slots % g == 0)
    states = (part_a, weights, first_moment, second_moment, average, stats, bases)
    grad_all, lines, *fresh = finish(
        sel, mix, mix_full, gain_one, back_res, bm, normed, tokens, states, group, wide, rows_dev, gain_row, gains_dev
    )
    input_grad, output, new_weight, new_first, new_second, new_average, new_stats, new_bases = wrap(
        grad_all, out_a, out_b, fresh
    )
    output = output.reshape(rows, width)
    line = jnp.sum(lines[:, 0], axis=0)
    offset = lax.axis_index("wide") * gains_dev % LANES
    own_gain = lax.dynamic_slice_in_dim(line, offset, gains_dev, 0)
    new_gains, gain_moment, gain_square, gain_mean = adam_gains(own_gain, gains, gain_first, gain_second, gain_average)
    return (
        output,
        input_grad,
        new_weight,
        new_first,
        new_second,
        new_average,
        new_stats,
        new_bases,
        new_gains,
        gain_moment,
        gain_square,
        gain_mean,
    )


def solution(mesh):
    block = P("narrow", "wide", None, None)
    pair = P("narrow", "wide", None, None, None)
    rows = P("wide", None)
    line = P("wide")
    return jax.shard_map(
        body,
        mesh=mesh,
        in_specs=(rows, rows, rows, rows, P(), block, block, block, block, pair, pair, line, line, line, line),
        out_specs=(rows, rows, block, block, block, block, pair, pair, line, line, line, line),
        check_vma=False,
    )
```

```python
import functools

import jax
import jax.numpy as jnp
from jax import lax
from jax.experimental import pallas as pl
from jax.experimental.pallas import tpu as pltpu
from jax.sharding import PartitionSpec as P

HEADS = 8
HD = 64
FF = 2048
LANES = 128
SEGS = 4
NEG = -1e30
F32 = jnp.float32
BF = jnp.bfloat16
highest = lax.Precision.HIGHEST

beta_one = 0.9
beta_two = 0.95
step_rate = 0.1
gain_rate = 0.75
weight_decay = 0.01
average_keep = 0.5
norm_eps = 1e-05
step_eps = 1e-08


def nt(a, b):
    return lax.dot_general(a, b, (((1,), (1,)), ((), ())), preferred_element_type=F32)


def nn(a, b):
    return lax.dot_general(a, b, (((1,), (0,)), ((), ())), preferred_element_type=F32)


def tn(a, b):
    return lax.dot_general(a, b, (((0,), (0,)), ((), ())), preferred_element_type=F32)


def split3(x):
    hi = x.astype(BF)
    r = x - hi.astype(F32)
    mid = r.astype(BF)
    lo = (r - mid.astype(F32)).astype(BF)
    return hi, mid, lo


def put3(base, x, lane0):
    lane = lax.broadcasted_iota(jnp.int32, base.shape, 1)
    hi, mid, lo = split3(x)
    out = jnp.where(lane == lane0, hi.astype(F32), base.astype(F32))
    out = jnp.where(lane == lane0 + 1, mid.astype(F32), out)
    out = jnp.where(lane == lane0 + 2, lo.astype(F32), out)
    return out.astype(BF)


VT = 80
UNIT = 256


def in_steps(begin, end, block, step):
    per = block // UNIT
    count = end - begin
    whole = count // per

    def long(i, _):
        step((begin + i * per) * UNIT, block)
        return 0

    def short(i, _):
        step((begin + whole * per + i) * UNIT, UNIT)
        return 0

    lax.fori_loop(0, whole, long, 0)
    lax.fori_loop(0, count - whole * per, short, 0)


QC, AHEAD, QB, BAHEAD = 512, 1, 256, 1


def fwd_kernel(heads, bq, bk, lo_ref, hi_ref, qe_ref, ke_ref, vt_ref, pad_ref, att_ref, qb_ref, m_ref, acc_ref):
    i = pl.program_id(0)
    row0 = pl.multiple_of(i * bq, bq)
    real = pad_ref[...] > 0.5
    for h in range(heads):
        qt = qe_ref[h].astype(F32).T[:HD]
        kt = ke_ref[h, pl.ds(row0, bq), :].astype(F32).T[:HD]
        own = jnp.sum(qt * kt, axis=0, keepdims=True)
        m_ref[h] = jnp.where(real, NEG, own)
        acc_ref[h] = jnp.where(real, 0.0, vt_ref[h, :, pl.ds(row0, bq)].astype(F32))

    def step(at, bk):
        col0 = pl.multiple_of(at, UNIT)
        work = [(h, slice(c, c + QC)) for c in range(0, bq, QC) for h in range(heads)]
        score = lambda h, c: nt(ke_ref[h, pl.ds(col0, bk), :], qe_ref[h, c, :])
        ss = [score(*w) for w in work[:AHEAD]]
        for n, (h, c) in enumerate(work):
            if n + AHEAD < len(work):
                ss.append(score(*work[n + AHEAD]))
            s = ss[n]
            m_old = m_ref[h, :, c]
            m_new = jnp.maximum(m_old, jnp.max(s, axis=0, keepdims=True))
            p = jnp.exp(s - m_new).astype(BF)
            alpha = jnp.exp(m_old - m_new)
            acc_ref[h, :, c] = acc_ref[h, :, c] * alpha + nn(vt_ref[h, :, pl.ds(col0, bk)], p)
            m_ref[h, :, c] = m_new

    in_steps(lo_ref[i], hi_ref[i], bk, step)
    outs = []
    for h in range(heads):
        acc = acc_ref[h]
        total = acc[HD : HD + 1]
        outs.append(jnp.where(real, acc[:HD] / total, 0.0))
        lse = jnp.broadcast_to(m_ref[h] + jnp.log(total), (8, bq)).T[:, :1]
        qb_ref[h] = put3(qe_ref[h], -lse, HD + 4)
    att_ref[...] = (jnp.concatenate(outs, axis=0) if heads > 1 else outs[0]).T.astype(BF)


def attend(qe, ke, vt, padw, lo, hi, bq, bk):
    heads, rows, _ = qe.shape
    full = lambda i, lo, hi: (0, 0, 0)
    return pl.pallas_call(
        functools.partial(fwd_kernel, heads, bq, bk),
        grid_spec=pltpu.PrefetchScalarGridSpec(
            num_scalar_prefetch=2,
            grid=(rows // bq,),
            in_specs=[
                pl.BlockSpec((heads, bq, LANES), lambda i, lo, hi: (0, i, 0)),
                pl.BlockSpec((heads, rows, LANES), full),
                pl.BlockSpec((heads, VT, rows), full),
                pl.BlockSpec((1, bq), lambda i, lo, hi: (0, i)),
            ],
            out_specs=[
                pl.BlockSpec((bq, heads * HD), lambda i, lo, hi: (i, 0)),
                pl.BlockSpec((heads, bq, LANES), lambda i, lo, hi: (0, i, 0)),
            ],
            scratch_shapes=[
                pltpu.VMEM((heads, 1, bq), F32),
                pltpu.VMEM((heads, VT, bq), F32),
            ],
        ),
        out_shape=[
            jax.ShapeDtypeStruct((rows, heads * HD), BF),
            jax.ShapeDtypeStruct((heads, rows, LANES), BF),
        ],
        compiler_params=pltpu.CompilerParams(vmem_limit_bytes=60 << 20),
        name="attend",
    )(lo, hi, qe, ke, vt, padw)


def bwd_kernel(heads, bq, bk, lo_ref, hi_ref, qb_ref, ke_ref, ve_ref, go_ref, att_ref, out_ref, ge_ref, dqt_ref, kt_ref, qt_ref, got_ref, dkt_ref, dvt_ref):
    j = pl.program_id(0)
    rows = qb_ref.shape[1]

    @pl.when(j == 0)
    def _():
        for h in range(heads):
            dqt_ref[h] = jnp.zeros_like(dqt_ref[h])
            for c in range(rows // 512):
                sl = pl.ds(c * 512, 512)
                go = go_ref[sl, h * HD : (h + 1) * HD]
                at = att_ref[sl, h * HD : (h + 1) * HD]
                delta = jnp.sum(go.astype(F32) * at.astype(F32), axis=1, keepdims=True)
                wide = jnp.concatenate([go, jnp.zeros_like(go)], axis=1)
                ge_ref[h, sl, :] = put3(wide, -delta, HD)
                got_ref[h, :, c * 512 : (c + 1) * 512] = wide.T[:HD]
                qt_ref[h, :, c * 512 : (c + 1) * 512] = qb_ref[h, sl, :].T[:HD]

    for h in range(heads):
        kt_ref[h] = ke_ref[h].T[:HD]

    zero = jnp.zeros((HD, bk), F32)

    def step(at, bq):
        row0 = pl.multiple_of(at, UNIT)
        work = [(h, pl.ds(row0 + c, QB)) for c in range(0, bq, QB) for h in range(heads)]
        score = lambda h, c: (nt(ke_ref[h], qb_ref[h, c, :]), nt(ve_ref[h], ge_ref[h, c, :]))
        ss = [score(*w) for w in work[:BAHEAD]]
        for n, (h, c) in enumerate(work):
            if n + BAHEAD < len(work):
                ss.append(score(*work[n + BAHEAD]))
            st, dt = ss[n]
            p = jnp.exp(st)
            ds = (p * dt).astype(BF)
            pb = p.astype(BF)
            dvt_ref[h] += nt(got_ref[h, :, c], pb)
            dkt_ref[h] += nt(qt_ref[h, :, c], ds)
            dqt_ref[h, :, c] += nn(kt_ref[h], ds)

    for h in range(heads):
        dkt_ref[h] = zero
        dvt_ref[h] = zero
    in_steps(lo_ref[j], hi_ref[j], bq, step)
    for h in range(heads):
        for part, ref in ((1, dkt_ref), (2, dvt_ref)):
            at = (part * heads + h) * HD
            out_ref[pl.ds(pl.multiple_of(j * bk, bk), bk), at : at + HD] = ref[h].T.astype(BF)

    @pl.when(j == pl.num_programs(0) - 1)
    def _():
        for h in range(heads):
            for c in range(rows // 512):
                sl = pl.ds(c * 512, 512)
                out_ref[sl, h * HD : (h + 1) * HD] = (dqt_ref[h, :, c * 512 : (c + 1) * 512].T * (HD ** -0.5)).astype(BF)


def attend_back(qb, ke, ve, go, att, lo, hi, bq, bk):
    heads, rows, _ = qb.shape
    full3 = lambda i, lo, hi: (0, 0, 0)
    full2 = lambda i, lo, hi: (0, 0)
    blk3 = lambda i, lo, hi: (0, i, 0)
    wide = heads * HD
    return pl.pallas_call(
        functools.partial(bwd_kernel, heads, bq, bk),
        grid_spec=pltpu.PrefetchScalarGridSpec(
            num_scalar_prefetch=2,
            grid=(rows // bk,),
            in_specs=[
                pl.BlockSpec((heads, rows, LANES), full3),
                pl.BlockSpec((heads, bk, LANES), blk3),
                pl.BlockSpec((heads, bk, LANES), blk3),
                pl.BlockSpec((rows, wide), full2),
                pl.BlockSpec((rows, wide), full2),
            ],
            out_specs=pl.BlockSpec((rows, 3 * wide), full2),
            scratch_shapes=[
                pltpu.VMEM((heads, rows, LANES), BF),
                pltpu.VMEM((heads, HD, rows), F32),
                pltpu.VMEM((heads, HD, bk), BF),
                pltpu.VMEM((heads, HD, rows), BF),
                pltpu.VMEM((heads, HD, rows), BF),
                pltpu.VMEM((heads, HD, bk), F32),
                pltpu.VMEM((heads, HD, bk), F32),
            ],
        ),
        out_shape=jax.ShapeDtypeStruct((rows, 3 * wide), BF),
        compiler_params=pltpu.CompilerParams(vmem_limit_bytes=60 << 20),
        name="attend_back",
    )(lo, hi, qb, ke, ve, go, att)


def dot_f32(a, b, dims):
    return lax.dot_general(a, b, ((dims[:1], dims[1:]), ((), ())), precision=highest, preferred_element_type=F32)


def soap_group(base, group, gr_ref, w_ref, m1_ref, m2_ref, av_ref, st_ref, ba_ref,
               nw_ref, n1_ref, n2_ref, na_ref, ns_ref, nb_ref, aug_ref):
    size = w_ref.shape[-1]
    half = size // 2
    panel = 8
    every = range(group)
    grads, firsts = [], []
    for s in every:
        rows = slice((base + s) * half, (base + s + 1) * half)
        wire = gr_ref[rows, :]
        grads.append(jnp.concatenate([wire[:, :size], wire[:, size:]], axis=0))
        firsts.append(beta_one * m1_ref[0, base + s] + (1.0 - beta_one) * grads[s])
        n1_ref[0, base + s] = firsts[s]
    sides = [(s, side) for s in every for side in range(2)]
    outers = [dot_f32(grads[s], grads[s], (1, 1) if side == 0 else (0, 0)) for s, side in sides]
    both = [dot_f32(jnp.concatenate([grads[s], firsts[s]], axis=0), ba_ref[0, base + s, 1], (1, 0)) for s in every]
    stats = []
    for (s, side), outer in zip(sides, outers):
        stats.append(beta_two * st_ref[0, base + s, side] + (1.0 - beta_two) * outer)
        ns_ref[0, base + s, side] = stats[-1]
    pairs = [dot_f32(ba_ref[0, base + s, 0], jnp.concatenate([both[s][:size], both[s][size:]], axis=1), (0, 0)) for s in every]
    mts = [dot_f32(ba_ref[0, base + s, side], stat, (0, 1)) for (s, side), stat in zip(sides, stats)]
    scaled = []
    for s in every:
        rotated, moment = pairs[s][:, :size], pairs[s][:, size:]
        second = beta_two * m2_ref[0, base + s] + (1.0 - beta_two) * rotated * rotated
        n2_ref[0, base + s] = second
        scaled.append(moment / (jnp.sqrt(second) + step_eps))
    grams = [dot_f32(mt, mt, (1, 1)) for mt in mts]
    inner = [dot_f32(scaled[s], ba_ref[0, base + s, 1], (1, 1)) for s in every]
    for m, (gram, mt) in enumerate(zip(grams, mts)):
        aug_ref[m] = jnp.concatenate([gram, mt], axis=1)
    directions = [dot_f32(ba_ref[0, base + s, 0], inner[s], (1, 0)) for s in every]
    for s in every:
        weight = w_ref[0, base + s]
        fresh = weight - step_rate * (directions[s] + weight_decay * weight)
        nw_ref[0, base + s] = fresh
        na_ref[0, base + s] = average_keep * av_ref[0, base + s] + (1.0 - average_keep) * fresh
    count = 2 * group
    row = lax.broadcasted_iota(jnp.int32, (count, panel, LANES), 1)
    for p in range(size // panel):
        top = p * panel
        part = aug_ref[:, top : top + panel, :]
        for r in range(panel):
            pivot = lax.rsqrt(part[:, r : r + 1, top + r : top + r + 1])
            lead = part[:, r : r + 1, :] * pivot
            column = jnp.where(row > r, part[:, :, top + r : top + r + 1] * pivot, 0.0)
            part = jnp.where(row == r, lead, part - column * lead)
        aug_ref[:, top : top + panel, :] = part
        below = top + panel
        if below < size:
            high = part.astype(BF).astype(F32)
            rest = part - high
            mid = rest.astype(BF).astype(F32)
            low = rest - mid
            first = jnp.concatenate([high, high, mid, high, mid, low], axis=1).astype(BF)
            other = jnp.concatenate([high, mid, high, low, mid, high], axis=1).astype(BF)
            for m in range(count):
                aug_ref[m, below:, :] -= lax.dot_general(
                    first[m][:, below:size], other[m], (((0,), (0,)), ((), ())), preferred_element_type=F32
                )
    for s in range(group):
        for side in range(2):
            nb_ref[0, base + s, side] = aug_ref[2 * s + side][:, size:].T


MESH = pl.DeviceIdType.MESH


def normalize(values):
    center = jnp.mean(values, axis=-1, keepdims=True)
    centered = values - center
    variance = jnp.mean(centered * centered, axis=-1, keepdims=True)
    scale = lax.rsqrt(variance + norm_eps)
    return centered * scale, scale


def norm_back(grad, xhat, scale):
    along = jnp.mean(grad * xhat, axis=-1, keepdims=True)
    return (grad - jnp.mean(grad, axis=-1, keepdims=True) - xhat * along) * scale


TAIL = 0.305
TAIL_FIT = (
    0.1216397411342051,
    0.12246669816059132,
    0.10342157025713879,
    0.1210193967312446,
    -0.037972477455618554,
    0.18571204369074895,
    -0.15298537812807472,
    0.036698452375741396,
)


def gelu_pair(u):
    size = jnp.abs(u)
    bell = jnp.exp(-0.5 * u * u)
    t = 1.0 / (1.0 + TAIL * size)
    poly = jnp.full_like(t, TAIL_FIT[-1])
    for c in TAIL_FIT[-2::-1]:
        poly = poly * t + c
    upper = poly * t * bell
    cdf = jnp.where(u > 0.0, 1.0 - upper, upper)
    return u * cdf, cdf + (0.3989422804014327 * u) * bell


def project_kernel(heads, shards, wide, gain_row, gains_dev, unit_ref, wire_ref, tok_ref, seg_ref, pad_ref,
                   norm_ref, qe_ref, ke_ref, ve_ref, vt_ref, mix_ref, line_ref, along_ref,
                   wide_ref, all_ref, near_ref, gain_ref, send_w, recv_w, send_z, recv_z):
    width = tok_ref.shape[1]
    half = HD // 2
    cols = 3 * heads
    units = wire_ref.shape[0]

    @pl.when(pl.program_id(0) == 0)
    def _():
        z = lax.axis_index("narrow")
        w = lax.axis_index("wide")
        twin = w + 1 - 2 * lax.rem(w, 2)
        chips = wide // 2
        barrier = pltpu.get_barrier_semaphore()
        pl.semaphore_signal(barrier, inc=1, device_id={"wide": twin}, device_id_type=MESH)
        for d in range(1, chips):
            pl.semaphore_signal(barrier, inc=1, device_id={"wide": lax.rem(w + 2 * d, wide)}, device_id_type=MESH)
        for d in range(1, shards):
            pl.semaphore_signal(barrier, inc=1, device_id={"narrow": lax.rem(z + d, shards)}, device_id_type=MESH)
        pl.semaphore_wait(barrier, chips + shards - 1)

        def slot(s):
            return all_ref.at[pl.ds(s * units, units)]

        def to_chip(d, mine):
            peer = lax.rem(w + 2 * d, wide)
            return pltpu.make_async_remote_copy(
                src_ref=wire_ref,
                dst_ref=slot(w if mine else peer),
                send_sem=send_w.at[d],
                recv_sem=recv_w.at[w if mine else peer],
                device_id={"wide": peer},
                device_id_type=MESH,
            )

        def to_twin(d, mine):
            owner = lax.rem((w if mine else twin) + 2 * d, wide)
            return pltpu.make_async_remote_copy(
                src_ref=wire_ref if d == 0 else slot(owner),
                dst_ref=slot(owner),
                send_sem=send_w.at[chips + d],
                recv_sem=recv_w.at[owner],
                device_id={"wide": twin},
                device_id_type=MESH,
            )

        def to_shard(d, mine):
            peer = lax.rem(z + d, shards)
            return pltpu.make_async_remote_copy(
                src_ref=wire_ref,
                dst_ref=near_ref.at[z if mine else peer],
                send_sem=send_z.at[d - 1],
                recv_sem=recv_z.at[z if mine else peer],
                device_id={"narrow": peer},
                device_id_type=MESH,
            )

        for d in range(1, chips):
            to_chip(d, True).start()
        to_twin(0, True).start()
        for d in range(1, shards):
            to_shard(d, True).start()
        all_ref[pl.ds(w * units, units)] = wire_ref[...]
        near_ref[z] = wire_ref[...]
        for d in range(1, chips):
            to_chip(d, False).wait_recv()
            to_twin(d, True).start()
        for d in range(chips):
            to_twin(d, False).wait_recv()

        for v in range(wide):
            line_ref[v] = all_ref[v * units + gain_row // 16]
        pieces = [line_ref[v].astype(F32)[:1, :gains_dev] for v in range(wide // 2)]
        gain_ref[...] = jnp.concatenate(pieces, axis=1)
        zero = jnp.zeros((half, HD), BF)

        def fill(r, _):
            low = pl.multiple_of(r * HD, HD)
            for c in range(cols):
                unit = unit_ref[r * cols + c]
                t = jnp.concatenate([all_ref[unit], all_ref[unit + 1]], axis=0)
                for part in range(2):
                    piece = t[:, part * HD : (part + 1) * HD]
                    at = pl.ds(low + part * half, half)
                    wide_ref[at, c * LANES : (c + 1) * LANES] = jnp.concatenate([piece, zero], axis=1)
                    mix_ref[at, c * HD : (c + 1) * HD] = piece
            return 0

        lax.fori_loop(0, width // HD, fill, 0)
        for d in range(1, shards):
            to_shard(d, False).wait_recv()
            to_shard(d, True).wait_send()
        along_ref[...] = near_ref[...]
        for d in range(1, chips):
            to_chip(d, True).wait_send()
        for d in range(chips):
            to_twin(d, True).wait_send()

    xhat, _ = normalize(tok_ref[...].astype(F32))
    normed = (xhat * gain_ref[...]).astype(BF)
    norm_ref[...] = normed
    count = tok_ref.shape[0]
    lane = lax.broadcasted_iota(jnp.int32, (LANES, count), 0)
    seg = seg_ref[...]
    same = lane - HD == seg
    in_segs = (lane >= HD) & (lane < HD + SEGS)
    ones = (lane >= HD + SEGS) & (lane < HD + SEGS + 3)
    ext_q = jnp.where(same, 1.0, 0.0).T
    ext_k = jnp.where(in_segs, jnp.where(same & (pad_ref[...] > 0.5), 0.0, NEG), jnp.where(ones, 1.0, 0.0)).T
    ext_v = jnp.where((lane >= HD) & (lane < HD + 3), 1.0, 0.0).T
    for h in range(heads):
        for ref, part, scale, ext in ((qe_ref, 0, HD ** -0.5, ext_q), (ke_ref, 1, 1.0, ext_k), (ve_ref, 2, 1.0, ext_v)):
            c = part * heads + h
            mixed = nn(normed, wide_ref[:, c * LANES : (c + 1) * LANES]).astype(BF)
            out = (mixed.astype(F32) * scale + ext).astype(BF)
            ref[h] = out
            if part == 2:
                vt_ref[h] = out.T[:VT]


def project(wire, unit, tokens, seg, pad, heads, shards, wide, gain_row, gains_dev):
    rows, width = tokens.shape
    tb = min(512, rows)
    full = lambda i, r: (0, 0)
    full3 = lambda i, r: (0, 0, 0)
    blk = lambda i, r: (i, 0)
    col = lambda i, r: (0, i)
    ext = lambda i, r: (0, i, 0)
    out = lambda *s: jax.ShapeDtypeStruct(s, BF)
    dma = pltpu.SemaphoreType.DMA
    units = wire.shape[0]
    return pl.pallas_call(
        functools.partial(project_kernel, heads, shards, wide, gain_row, gains_dev),
        grid_spec=pltpu.PrefetchScalarGridSpec(
            num_scalar_prefetch=1,
            grid=(rows // tb,),
            in_specs=[
                pl.BlockSpec(wire.shape, full3),
                pl.BlockSpec((tb, width), blk),
                pl.BlockSpec((1, tb), col),
                pl.BlockSpec((1, tb), col),
            ],
            out_specs=[
                pl.BlockSpec((tb, width), blk),
                pl.BlockSpec((heads, tb, LANES), ext),
                pl.BlockSpec((heads, tb, LANES), ext),
                pl.BlockSpec((heads, tb, LANES), ext),
                pl.BlockSpec((heads, VT, tb), lambda i, r: (0, 0, i)),
                pl.BlockSpec((width, 3 * heads * HD), full),
                pl.BlockSpec((wide, 16, LANES), full3),
                pl.BlockSpec((shards, units, 16, LANES), lambda i, r: (0, 0, 0, 0)),
            ],
            scratch_shapes=[
                pltpu.VMEM((width, 3 * heads * LANES), BF),
                pltpu.VMEM((wide * units, 16, LANES), BF),
                pltpu.VMEM((shards, units, 16, LANES), BF),
                pltpu.VMEM((1, width), F32),
                dma((wide,)),
                dma((wide,)),
                dma((shards - 1,)),
                dma((shards,)),
            ],
        ),
        out_shape=[
            out(rows, width),
            out(heads, rows, LANES),
            out(heads, rows, LANES),
            out(heads, rows, LANES),
            out(heads, VT, rows),
            out(width, 3 * heads * HD),
            out(wide, 16, LANES),
            out(shards, units, 16, LANES),
        ],
        compiler_params=pltpu.CompilerParams(vmem_limit_bytes=60 << 20, collective_id=3, has_side_effects=True),
        name="project",
    )(unit, wire, tokens, seg, pad)


def middle_kernel(shards, span, units, wide, gain_row, gains_dev, inside,
                  unit_ref, sel_ref, wire_ref, gain_ref, pad_ref, att_ref, tok_ref, cot_ref,
                  outa_ref, outb_ref, res_ref, back_ref, grads_ref, mix_ref,
                  tokens_ref, cots_ref, got_ref, give_ref, wo_ref, wu_ref, wd_ref, go_ref, gu_ref, gd_ref, gg_ref, blk_ref,
                  local_sem, send_i, recv_i, send_b, recv_b, send_a, recv_a):
    own, width = tokens_ref.shape
    parts = recv_i.shape[1]
    tb = own // parts
    half = HD // 2
    rows_dev = grads_ref.shape[1]
    z = lax.axis_index("narrow")
    kinds = (
        (mix_ref, None, width, 3 * span),
        (wo_ref, go_ref, span, width),
        (wu_ref, gu_ref, width, units),
        (wd_ref, gd_ref, units, width),
    )
    mix_blocks = width // HD * (3 * span // HD)
    per = blk_ref.shape[0] // shards

    barrier = pltpu.get_barrier_semaphore()
    for d in range(1, shards):
        pl.semaphore_signal(barrier, inc=1, device_id={"narrow": lax.rem(z + d, shards)}, device_id_type=MESH)
    pl.semaphore_wait(barrier, shards - 1)

    def bring(d, t, mine):
        peer = lax.rem(z + d, shards)
        slot = z if mine else peer
        return pltpu.make_async_remote_copy(
            src_ref=att_ref.at[pl.ds(pl.multiple_of(peer * own + t * tb, tb), tb), :],
            dst_ref=got_ref.at[slot, pl.ds(pl.multiple_of(t * tb, tb), tb), :],
            send_sem=send_i.at[d - 1, t],
            recv_sem=recv_i.at[slot, t],
            device_id={"narrow": peer},
            device_id_type=MESH,
        )

    def give(d, t, mine):
        peer = lax.rem(z + d, shards)
        slot = z if mine else peer
        return pltpu.make_async_remote_copy(
            src_ref=give_ref.at[peer, pl.ds(pl.multiple_of(t * tb, tb), tb), :],
            dst_ref=back_ref.at[pl.ds(pl.multiple_of(slot * own + t * tb, tb), tb), :],
            send_sem=send_b.at[d - 1, t],
            recv_sem=recv_b.at[slot, t],
            device_id={"narrow": peer},
            device_id_type=MESH,
        )

    def hop_copy(c, t, step):
        at = pl.ds(pl.multiple_of(t * tb, tb), tb)
        return pltpu.make_async_remote_copy(
            src_ref=outa_ref.at[c, at, :],
            dst_ref=outa_ref.at[c, at, :],
            send_sem=send_a.at[step, c, t],
            recv_sem=recv_a.at[c, t],
            device_id={"narrow": lax.rem(z + (1 if step == 0 else shards - 1), shards)},
            device_id_type=MESH,
        )

    room = (z < shards - 1, z > 0)
    for t in range(parts):
        for d in range(1, shards):
            bring(d, t, True).start()
    mine = pl.ds(pl.multiple_of(z * own, own), own)
    copies = [
        pltpu.make_async_copy(att_ref.at[mine, :], got_ref.at[z], local_sem.at[0]),
        pltpu.make_async_copy(tok_ref.at[mine, :], tokens_ref, local_sem.at[1]),
        pltpu.make_async_copy(cot_ref.at[mine, :], cots_ref, local_sem.at[2]),
    ]
    for copy in copies:
        copy.start()

    base = 0
    for ref, acc, rows, cols in kinds:
        grid_cols = cols // HD

        def fill(r, _, ref=ref, base=base, grid_cols=grid_cols):
            low = pl.multiple_of(r * HD, HD)
            for n in range(shards):
                for c in range(grid_cols):
                    unit = unit_ref[base + r * grid_cols + c] + n * (rows_dev // 16)
                    t = jnp.concatenate([wire_ref[unit], wire_ref[unit + 1]], axis=0)
                    for part in range(2):
                        ref[n, pl.ds(low + part * half, half), c * HD : (c + 1) * HD] = t[:, part * HD : (part + 1) * HD]
            return 0

        lax.fori_loop(0, rows // HD, fill, 0)
        base += rows // HD * grid_cols
        if acc is not None:
            acc[...] = jnp.zeros_like(acc)
    gg_ref[...] = jnp.zeros_like(gg_ref)
    for copy in copies:
        copy.wait()

    def block(t, _):
        at = pl.ds(pl.multiple_of(t * tb, tb), tb)
        for d in range(1, shards):
            bring(d, t, False).wait_recv()
        tokens = tokens_ref[at, :].astype(F32)
        cot = cots_ref[at, :]
        branch = nn(got_ref[0, at, :], wo_ref[0])
        for n in range(1, shards):
            branch += nn(got_ref[n, at, :], wo_ref[n])
        residual = tokens + branch
        xhat, scale = normalize(residual)
        gain = gain_ref[...]
        normed = (xhat * gain).astype(BF)
        ups = [nn(normed, wu_ref[n]) for n in range(shards)]
        downs = [nt(cot, wd_ref[n]) for n in range(shards)]
        actives, back_ups = [], []
        for n in range(shards):
            value, slope = gelu_pair(ups[n])
            actives.append(value.astype(BF))
            back_ups.append((slope * downs[n]).astype(BF))
        mlp = nn(actives[0], wd_ref[0])
        back = nt(back_ups[0], wu_ref[0])
        for n in range(1, shards):
            mlp += nn(actives[n], wd_ref[n])
            back += nt(back_ups[n], wu_ref[n])
        out = (residual + mlp).astype(BF)

        @pl.when(t < inside)
        def _():
            outa_ref[z, at, :] = out
            for step in range(2):

                @pl.when(room[step])
                def _(step=step):
                    hop_copy(z, t, step).start()

        @pl.when(t >= inside)
        def _():
            outb_ref[pl.ds(pl.multiple_of((t - inside) * tb, tb), tb), :] = out

        gg_ref[...] += jnp.sum(back * xhat, axis=0, keepdims=True)
        back_res = cot.astype(F32) + norm_back(back * gain, xhat, scale)
        res_ref[at, :] = back_res
        branch_low = back_res.astype(BF)
        line = pad_ref[:, pl.ds(pl.multiple_of(z * own + t * tb, LANES), tb)]
        pad = jnp.broadcast_to(line, (8, tb)).T[:, :1]
        for n in range(shards):
            give_ref[n, at, :] = (nt(branch_low, wo_ref[n]) * pad).astype(BF)
        for d in range(1, shards):
            give(d, t, True).start()
        for n in range(shards):
            gd_ref[n] += tn(actives[n], cot)
            gu_ref[n] += tn(normed, back_ups[n])
            go_ref[n] += tn(got_ref[n, at, :], branch_low)
        return 0

    lax.fori_loop(0, parts, block, 0)
    back_ref[mine, :] = give_ref[z]
    base = 0
    for ref, acc, rows, cols in kinds:
        grid_cols = cols // HD
        if acc is not None:

            def cut(r, _, acc=acc, base=base, grid_cols=grid_cols):
                low = pl.multiple_of(r * HD, HD)
                for n in range(shards):
                    for c in range(grid_cols):
                        lanes = slice(c * HD, (c + 1) * HD)
                        value = jnp.concatenate([acc[n, pl.ds(low, half), lanes], acc[n, pl.ds(low + half, half), lanes]], axis=1)
                        blk_ref[n * per + base - mix_blocks + r * grid_cols + c] = value.astype(BF)
                return 0

            lax.fori_loop(0, rows // HD, cut, 0)
        base += rows // HD * grid_cols
    for n in range(shards):
        blk_ref[(n + 1) * per - 1] = jnp.zeros((half, LANES), BF)
    slots = gain_row // half
    top = lax.broadcasted_iota(jnp.int32, (16, LANES), 0) == 0

    def place(v, _):
        for n in range(shards):
            for i in range(slots):
                grads_ref[v * shards + n, i * half : (i + 1) * half, :] = blk_ref[sel_ref[v * slots + i] + n * per]
        return 0

    lax.fori_loop(0, wide, place, 0)
    for v in range(wide):
        piece = v * gains_dev // LANES - width // LANES
        for n in range(shards):
            if piece >= 0:
                value = jnp.where(top, gg_ref[:, piece * LANES : (piece + 1) * LANES], 0.0).astype(BF)
            else:
                value = jnp.zeros((16, LANES), BF)
            grads_ref[v * shards + n, gain_row:, :] = value

    hops = [(s, t, step) for s in range(1, shards) for t in range(inside) for step in range(2)]
    for s, t, step in hops:
        chunk = z - s if step == 0 else z + s
        there = chunk >= 0 if step == 0 else chunk < shards

        @pl.when(there)
        def _(chunk=chunk, t=t, step=step):
            hop_copy(chunk, t, step).wait_recv()

        @pl.when(there & room[step])
        def _(chunk=chunk, t=t, step=step):
            hop_copy(chunk, t, step).start()

    for t in range(parts):
        for d in range(1, shards):
            give(d, t, False).wait_recv()
    for t in range(parts):
        for d in range(1, shards):
            bring(d, t, True).wait_send()
            give(d, t, True).wait_send()
    for t in range(inside):
        for step in range(2):

            @pl.when(room[step])
            def _(t=t, step=step):
                hop_copy(z, t, step).wait_send()

    for s, t, step in hops:
        chunk = z - s if step == 0 else z + s
        there = chunk >= 0 if step == 0 else chunk < shards

        @pl.when(there & room[step])
        def _(chunk=chunk, t=t, step=step):
            hop_copy(chunk, t, step).wait_send()


def middle(unit, sel, wire, gain_two, pad, att, tokens, cotangent, shards, wide, rows_dev, gain_row, gains_dev):
    rows, span = att.shape
    width = tokens.shape[1]
    units = FF // shards
    own = rows // shards
    tb = min(256, own)
    parts = own // tb
    inside = max(1, parts // 4)
    blocks = unit.shape[0] - width // HD * (3 * span // HD)
    vmem = pl.BlockSpec(memory_space=pltpu.VMEM)
    smem = pl.BlockSpec(memory_space=pltpu.SMEM)
    hbm = pl.BlockSpec(memory_space=pl.ANY)
    dma = pltpu.SemaphoreType.DMA
    return pl.pallas_call(
        functools.partial(middle_kernel, shards, span, units, wide, gain_row, gains_dev, inside),
        in_specs=[smem, smem, vmem, vmem, vmem, hbm, hbm, hbm],
        out_specs=[vmem] * 6,
        out_shape=[
            jax.ShapeDtypeStruct((shards, inside * tb, width), BF),
            jax.ShapeDtypeStruct((own - inside * tb, width), BF),
            jax.ShapeDtypeStruct((own, width), F32),
            jax.ShapeDtypeStruct((rows, span), BF),
            jax.ShapeDtypeStruct((wide * shards, rows_dev, LANES), BF),
            jax.ShapeDtypeStruct((shards, width, 3 * span), BF),
        ],
        scratch_shapes=[
            pltpu.VMEM((own, width), BF),
            pltpu.VMEM((own, width), BF),
            pltpu.VMEM((shards, own, span), BF),
            pltpu.VMEM((shards, own, span), BF),
            pltpu.VMEM((shards, span, width), BF),
            pltpu.VMEM((shards, width, units), BF),
            pltpu.VMEM((shards, units, width), BF),
            pltpu.VMEM((shards, span, width), F32),
            pltpu.VMEM((shards, width, units), F32),
            pltpu.VMEM((shards, units, width), F32),
            pltpu.VMEM((1, width), F32),
            pltpu.VMEM((shards * (blocks + 1), HD // 2, LANES), BF),
            dma((3,)),
            dma((shards - 1, parts)),
            dma((shards, parts)),
            dma((shards - 1, parts)),
            dma((shards, parts)),
            dma((2, shards, inside)),
            dma((shards, inside)),
        ],
        compiler_params=pltpu.CompilerParams(vmem_limit_bytes=63 << 20, collective_id=2, has_side_effects=True),
        name="middle",
    )(unit, sel, wire, gain_two, pad, att, tokens, cotangent)


PARTS = 4


def finish_kernel(shards, wide, gain_row, gains_dev, group, sel_ref, mix_ref, full_ref, gain_ref, res_ref, bm_ref, norm_ref, tok_ref, *refs):
    states, outs = refs[1:7], refs[9:15]
    first_ref, grad_ref, line_ref = refs[0], refs[7], refs[8]
    (own_ref, normed_ref, tokens_ref, got_ref, acc_ref, blk_ref, grads_ref, sums_ref, firsts_ref, part_ref, aug_ref,
     local_sem, send_z, recv_z, send_w, recv_w, send_a, recv_a, send_g, recv_g, send_f, recv_f) = refs[15:]
    width = norm_ref.shape[1]
    rows, cols = bm_ref.shape
    own = rows // shards
    hold = own // PARTS
    half = HD // 2
    grid_cols = cols // HD
    blocks = width // HD * grid_cols
    slots = gain_row // half
    z = lax.axis_index("narrow")
    w = lax.axis_index("wide")

    barrier = pltpu.get_barrier_semaphore()
    for d in range(1, shards):
        pl.semaphore_signal(barrier, inc=1, device_id={"narrow": lax.rem(z + d, shards)}, device_id_type=MESH)
    for d in range(1, wide):
        pl.semaphore_signal(barrier, inc=1, device_id={"wide": lax.rem(w + d, wide)}, device_id_type=MESH)
    pl.semaphore_wait(barrier, shards + wide - 2)

    def to_peer(d, part, mine):
        peer = lax.rem(z + d, shards)
        slot = z if mine else peer
        at = pl.multiple_of(peer * own + part * hold, hold)
        return pltpu.make_async_remote_copy(
            src_ref=bm_ref.at[pl.ds(at, hold), :],
            dst_ref=got_ref.at[slot, pl.ds(part * hold, hold), :],
            send_sem=send_z.at[d - 1, part],
            recv_sem=recv_z.at[slot, part],
            device_id={"narrow": peer},
            device_id_type=MESH,
        )

    def to_owner(d, mine):
        peer = lax.rem(w + d, wide)
        slot = w if mine else peer
        return pltpu.make_async_remote_copy(
            src_ref=grads_ref.at[peer],
            dst_ref=sums_ref.at[slot],
            send_sem=send_w.at[d - 1],
            recv_sem=recv_w.at[slot],
            device_id={"wide": peer},
            device_id_type=MESH,
        )

    def hop_copy(c, part, step):
        at = pl.ds(pl.multiple_of(c * own + part * hold, hold), hold)
        return pltpu.make_async_remote_copy(
            src_ref=grad_ref.at[at, :],
            dst_ref=grad_ref.at[at, :],
            send_sem=send_a.at[step, c, part],
            recv_sem=recv_a.at[c, part],
            device_id={"narrow": lax.rem(z + (1 if step == 0 else shards - 1), shards)},
            device_id_type=MESH,
        )

    def pass_on(c, part, act):
        for step, there in ((0, z < shards - 1), (1, z > 0)):
            if c is None or step == c[0]:
                chunk = z if c is None else c[1]
                ok = there if c is None else there & c[2]

                @pl.when(ok)
                def _(chunk=chunk, step=step):
                    act(hop_copy(chunk, part, step))

    def line_to(d, mine):
        peer = lax.rem(z + d, shards)
        slot = z if mine else peer
        return pltpu.make_async_remote_copy(
            src_ref=line_ref.at[z],
            dst_ref=line_ref.at[slot],
            send_sem=send_g.at[d - 1],
            recv_sem=recv_g.at[slot],
            device_id={"narrow": peer},
            device_id_type=MESH,
        )

    rows_dev = part_ref.shape[0]

    def first_to(d, mine):
        peer = lax.rem(z + d, shards)
        slot = z if mine else peer
        return pltpu.make_async_remote_copy(
            src_ref=first_ref.at[pl.ds(pl.multiple_of(peer * rows_dev, 16), rows_dev), :],
            dst_ref=firsts_ref.at[slot],
            send_sem=send_f.at[d - 1],
            recv_sem=recv_f.at[slot],
            device_id={"narrow": peer},
            device_id_type=MESH,
        )

    for d in range(1, shards):
        first_to(d, True).start()
    for part in range(PARTS):
        for d in range(1, shards):
            to_peer(d, part, True).start()
    mine = pl.ds(pl.multiple_of(z * own, own), own)
    copies = [
        pltpu.make_async_copy(bm_ref, own_ref, local_sem.at[0]),
        pltpu.make_async_copy(norm_ref, normed_ref, local_sem.at[1]),
        pltpu.make_async_copy(tok_ref.at[mine, :], tokens_ref, local_sem.at[2]),
        pltpu.make_async_copy(bm_ref.at[mine, :], got_ref.at[z], local_sem.at[3]),
        pltpu.make_async_copy(
            first_ref.at[pl.ds(pl.multiple_of(z * rows_dev, 16), rows_dev), :], firsts_ref.at[z], local_sem.at[4]
        ),
    ]
    for copy in copies:
        copy.start()
    for copy in copies:
        copy.wait()

    acc_ref[...] = jnp.zeros_like(acc_ref)
    tb = min(512, rows)

    def add(i, _):
        at = pl.ds(pl.multiple_of(i * tb, tb), tb)
        acc_ref[...] += tn(normed_ref[at, :], own_ref[at, :])
        return 0

    lax.fori_loop(0, rows // tb, add, 0)
    blk_ref[blocks] = jnp.zeros((half, LANES), BF)

    def cut(r, _):
        low = pl.multiple_of(r * HD, HD)
        for c in range(grid_cols):
            lanes = slice(c * HD, (c + 1) * HD)
            value = jnp.concatenate([acc_ref[pl.ds(low, half), lanes], acc_ref[pl.ds(low + half, half), lanes]], axis=1)
            blk_ref[r * grid_cols + c] = value.astype(BF)
        return 0

    lax.fori_loop(0, width // HD, cut, 0)
    along = jnp.sum(acc_ref[...] * mix_ref[...].astype(F32), axis=1, keepdims=True)
    line = jnp.broadcast_to(along, (width, LANES)).T[:16] / gain_ref[...]
    top = lax.broadcasted_iota(jnp.int32, (16, LANES), 0) == 0
    for v in range(wide):

        def place(i, _, v=v):
            grads_ref[v, pl.ds(pl.multiple_of(i * half, half), half), :] = blk_ref[sel_ref[v * slots + i]]
            return 0

        lax.fori_loop(0, slots, place, 0)
        piece = v * gains_dev // LANES
        if piece < width // LANES:
            value = jnp.where(top, line[:, piece * LANES : (piece + 1) * LANES], 0.0).astype(BF)
        else:
            value = jnp.zeros((16, LANES), BF)
        grads_ref[v, gain_row : gain_row + 16, :] = value
    for d in range(1, wide):
        to_owner(d, True).start()
    part_ref[...] = grads_ref[w].astype(F32)

    tile = min(256, hold)

    def norm_rows(i, _):
        at = pl.ds(pl.multiple_of(i * tile, tile), tile)
        back = nt(got_ref[0, at, :], full_ref[0])
        for n in range(1, shards):
            back += nt(got_ref[n, at, :], full_ref[n])
        xhat, scale = normalize(tokens_ref[at, :].astype(F32))
        grad = res_ref[at, :] + norm_back(back * gain_ref[...], xhat, scale)
        grad_ref[pl.ds(pl.multiple_of(z * own + i * tile, tile), tile), :] = grad.astype(BF)
        return 0

    def norm_part(part):
        for d in range(1, shards):
            to_peer(d, part, False).wait_recv()
        lax.fori_loop(part * hold // tile, (part + 1) * hold // tile, norm_rows, 0)
        pass_on(None, part, lambda copy: copy.start())

    for d in range(1, wide):
        to_owner(d, False).wait_recv()
    for d in range(1, wide):
        part_ref[...] += sums_ref[lax.rem(w + d, wide)].astype(F32)
    line_ref[z] = part_ref[gain_row : gain_row + 16, :]
    for d in range(1, shards):
        line_to(d, True).start()
    for d in range(1, shards):
        first_to(d, False).wait_recv()
    total = firsts_ref[0].astype(F32)
    for n in range(1, shards):
        total += firsts_ref[n].astype(F32)
    line_ref[shards] = total[gain_row : gain_row + 16, :]
    part_ref[...] += total
    ready = 0
    rounds = slots // group
    for g in range(rounds):
        soap_group(g * group, group, part_ref, *states, *outs, aug_ref)
        upto = PARTS * (g + 1) // rounds
        while ready < upto:
            norm_part(ready)
            ready += 1
    hops = [(s, part, step) for s in range(1, shards) for part in range(PARTS) for step in range(2)]
    for s, part, step in hops:
        chunk = z - s if step == 0 else z + s
        there = chunk >= 0 if step == 0 else chunk < shards

        @pl.when(there)
        def _(chunk=chunk, part=part, step=step):
            hop_copy(chunk, part, step).wait_recv()

        pass_on((step, chunk, there), part, lambda copy: copy.start())
    for d in range(1, shards):
        line_to(d, False).wait_recv()
    for part in range(PARTS):
        pass_on(None, part, lambda copy: copy.wait_send())
    for s, part, step in hops:
        chunk = z - s if step == 0 else z + s
        there = chunk >= 0 if step == 0 else chunk < shards
        pass_on((step, chunk, there), part, lambda copy: copy.wait_send())
    for d in range(1, shards):
        line_to(d, True).wait_send()
        first_to(d, True).wait_send()
    for part in range(PARTS):
        for d in range(1, shards):
            to_peer(d, part, True).wait_send()
    for d in range(1, wide):
        to_owner(d, True).wait_send()


def finish(sel, mix, mix_full, gain_one, res, bm, normed, tokens, states, group, wide, rows_dev, gain_row, gains_dev):
    shards = mix_full.shape[0]
    rows, cols = bm.shape
    width = normed.shape[1]
    own = rows // shards
    half = HD // 2
    blocks = width // HD * (cols // HD)
    vmem = pl.BlockSpec(memory_space=pltpu.VMEM)
    smem = pl.BlockSpec(memory_space=pltpu.SMEM)
    hbm = pl.BlockSpec(memory_space=pl.ANY)
    dma = pltpu.SemaphoreType.DMA
    return pl.pallas_call(
        functools.partial(finish_kernel, shards, wide, gain_row, gains_dev, group),
        in_specs=[smem, vmem, vmem, vmem, vmem, hbm, hbm, hbm, hbm] + [vmem] * 6,
        out_specs=[vmem] * 8,
        out_shape=[jax.ShapeDtypeStruct((rows, width), BF), jax.ShapeDtypeStruct((shards + 1, 16, LANES), F32)]
        + [jax.ShapeDtypeStruct(a.shape, a.dtype) for a in states[1:]],
        scratch_shapes=[
            pltpu.VMEM((rows, cols), BF),
            pltpu.VMEM((rows, width), BF),
            pltpu.VMEM((own, width), BF),
            pltpu.VMEM((shards, own, cols), BF),
            pltpu.VMEM((width, cols), F32),
            pltpu.VMEM((blocks + 1, half, LANES), BF),
            pltpu.VMEM((wide, rows_dev, LANES), BF),
            pltpu.VMEM((wide, rows_dev, LANES), BF),
            pltpu.VMEM((shards, rows_dev, LANES), BF),
            pltpu.VMEM((rows_dev, LANES), F32),
            pltpu.VMEM((2 * group, HD, LANES), F32),
            dma((5,)),
            dma((shards - 1, PARTS)),
            dma((shards, PARTS)),
            dma((wide - 1,)),
            dma((wide,)),
            dma((2, shards, PARTS)),
            dma((shards, PARTS)),
            dma((shards - 1,)),
            dma((shards,)),
            dma((shards - 1,)),
            dma((shards,)),
        ],
        compiler_params=pltpu.CompilerParams(vmem_limit_bytes=62 << 20, collective_id=1, has_side_effects=True),
        name="finish",
    )(sel, mix, mix_full, gain_one, res, bm, normed, tokens, *states)


def wrap_kernel(count, per, grad_ref, outa_ref, outb_ref, *refs):
    olds, wide_ref, out_ref, news = refs[:count], refs[count], refs[count + 1], refs[count + 2 :]
    for old, new in zip(olds, news):
        new[...] = old[...]
    wide_ref[...] = grad_ref[...].astype(F32)
    place = lax.rem(pl.program_id(0), per)

    @pl.when(place == 0)
    def _():
        out_ref[...] = outa_ref[0]

    @pl.when(place > 0)
    def _():
        out_ref[...] = outb_ref[0]


def wrap(grad, out_a, out_b, olds):
    rows, width = grad.shape
    tb = out_a.shape[1]
    per = 1 + out_b.shape[1] // tb
    steps = rows // tb
    slots = olds[0].shape[1]
    group = next(g for g in range(1, slots + 1) if slots % g == 0 and slots // g <= steps)
    last = slots // group - 1
    blk = pl.BlockSpec((tb, width), lambda i: (i, 0))
    part_a = pl.BlockSpec((1, tb, width), lambda i: (i // per, 0, 0))
    part_b = pl.BlockSpec((1, tb, width), lambda i: (i // per, jnp.maximum(i % per - 1, 0), 0))
    states = [
        pl.BlockSpec((1, group, *a.shape[2:]), lambda i, k=a.ndim: (0, jnp.minimum(i, last)) + (0,) * (k - 2)) for a in olds
    ]
    return pl.pallas_call(
        functools.partial(wrap_kernel, len(olds), per),
        grid=(steps,),
        in_specs=[blk, part_a, part_b] + states,
        out_specs=[blk, blk] + states,
        out_shape=[jax.ShapeDtypeStruct((rows, width), F32), jax.ShapeDtypeStruct((rows, width), BF)]
        + [jax.ShapeDtypeStruct(a.shape, a.dtype) for a in olds],
        compiler_params=pltpu.CompilerParams(vmem_limit_bytes=60 << 20),
        name="wrap",
    )(grad, out_a, out_b, *olds)


def adam_gains(grad, gain, first, second, average):
    new_first = beta_one * first + (1.0 - beta_one) * grad
    new_second = beta_two * second + (1.0 - beta_two) * grad * grad
    new_gain = gain - gain_rate * new_first / (jnp.sqrt(new_second) + step_eps)
    new_average = average_keep * average + (1.0 - average_keep) * new_gain
    return (new_gain, new_first, new_second, new_average)


def body(
    tokens,
    cotangent,
    segment_ids,
    pad_mask,
    owner_order,
    weights,
    first_moment,
    second_moment,
    average,
    stats,
    bases,
    gains,
    gain_first,
    gain_second,
    gain_average,
):
    narrow = lax.axis_size("narrow")
    wide = lax.axis_size("wide")
    heads = HEADS // narrow
    rows, width = tokens.shape
    span = heads * HD
    own = rows // narrow
    slots, size = weights.shape[1], weights.shape[2]
    half = size // 2
    block_count = owner_order.shape[0]
    gains_dev = gains.shape[0]
    gain_row = slots * half
    rows_dev = gain_row + 16

    low = weights[0].astype(BF)
    wire = jnp.concatenate([low[:, :half], low[:, half:]], axis=2).reshape(gain_row, 2 * size)
    wire = jnp.concatenate([wire, jnp.pad(gains.astype(BF)[None], ((0, 15), (0, LANES - gains_dev)))], axis=0)

    ids = jnp.arange(block_count, dtype=jnp.int32)
    slot_of = jnp.sum(jnp.where(owner_order[None, :] == ids[:, None], ids[None, :], 0), axis=1)
    device, place = slot_of // slots, slot_of % slots
    row_own = device * rows_dev + place * half
    row_full = device * (narrow * rows_dev) + place * half

    seg = segment_ids
    seg_row = segment_ids[0]
    pad = pad_mask.astype(F32)
    block = min(512, rows)
    low_seg = seg_row[::block]
    high_seg = seg_row[block - 1 :: block]
    begin = jnp.sum((seg_row[None, :] < low_seg[:, None]).astype(jnp.int32), axis=1) // UNIT
    end = (jnp.sum((seg_row[None, :] <= high_seg[:, None]).astype(jnp.int32), axis=1) + UNIT - 1) // UNIT

    normed, qe, ke, ve, vt, mix, lines, along = project(
        wire.reshape(-1, 16, LANES), row_own // 16, tokens, seg, pad, heads, narrow, wide, gain_row, gains_dev
    )
    wire_full = lax.all_gather(along.reshape(-1, LANES), "wide", axis=0, tiled=True)
    gain_all = lines[:, 0, :gains_dev].astype(F32).reshape(1, 2 * width)
    gain_one, gain_two = gain_all[:, :width], gain_all[:, width:]
    attended, qb = attend(qe, ke, vt, pad, begin, end, block, block)
    unit = row_full // 16
    mix_blocks = width // size * 3 * heads
    sel_rest = jnp.where(owner_order >= mix_blocks, owner_order - mix_blocks, block_count - mix_blocks)
    out_a, out_b, back_res, back_att, grads, mix_full = middle(
        unit, sel_rest, wire_full.reshape(-1, 16, LANES), gain_two, pad, attended, tokens, cotangent,
        narrow, wide, rows_dev, gain_row, gains_dev,
    )
    part_a = lax.psum_scatter(grads.reshape(-1, LANES), "wide", scatter_dimension=0, tiled=True)
    out_b = lax.all_to_all(jnp.broadcast_to(out_b, (narrow, *out_b.shape)), "narrow", 0, 0)
    bm = attend_back(qb, ke, ve, back_att, attended, begin, end, block, block)
    bm, part_a, out_b = lax.optimization_barrier((bm, part_a, out_b))
    sel = jnp.minimum(owner_order, mix_blocks)
    group = next(g for g in range(min(12, slots), 0, -1) if slots % g == 0)
    states = (part_a, weights, first_moment, second_moment, average, stats, bases)
    grad_all, lines, *fresh = finish(
        sel, mix, mix_full, gain_one, back_res, bm, normed, tokens, states, group, wide, rows_dev, gain_row, gains_dev
    )
    input_grad, output, new_weight, new_first, new_second, new_average, new_stats, new_bases = wrap(
        grad_all, out_a, out_b, fresh
    )
    line = jnp.sum(lines[:, 0], axis=0)
    offset = lax.axis_index("wide") * gains_dev % LANES
    own_gain = lax.dynamic_slice_in_dim(line, offset, gains_dev, 0)
    new_gains, gain_moment, gain_square, gain_mean = adam_gains(own_gain, gains, gain_first, gain_second, gain_average)
    return (
        output,
        input_grad,
        new_weight,
        new_first,
        new_second,
        new_average,
        new_stats,
        new_bases,
        new_gains,
        gain_moment,
        gain_square,
        gain_mean,
    )


def solution(mesh):
    block = P("narrow", "wide", None, None)
    pair = P("narrow", "wide", None, None, None)
    rows = P("wide", None)
    line = P("wide")
    return jax.shard_map(
        body,
        mesh=mesh,
        in_specs=(rows, rows, rows, rows, P(), block, block, block, block, pair, pair, line, line, line, line),
        out_specs=(rows, rows, block, block, block, block, pair, pair, line, line, line, line),
        check_vma=False,
    )
```

```python
import functools

import jax
import jax.numpy as jnp
from jax import lax
from jax.experimental import pallas as pl
from jax.experimental.pallas import tpu as pltpu
from jax.sharding import PartitionSpec as P

HEADS = 8
HD = 64
FF = 2048
LANES = 128
SEGS = 4
NEG = -1e30
F32 = jnp.float32
BF = jnp.bfloat16
highest = lax.Precision.HIGHEST

beta_one = 0.9
beta_two = 0.95
step_rate = 0.1
gain_rate = 0.75
weight_decay = 0.01
average_keep = 0.5
norm_eps = 1e-05
step_eps = 1e-08


def nt(a, b):
    return lax.dot_general(a, b, (((1,), (1,)), ((), ())), preferred_element_type=F32)


def nn(a, b):
    return lax.dot_general(a, b, (((1,), (0,)), ((), ())), preferred_element_type=F32)


def tn(a, b):
    return lax.dot_general(a, b, (((0,), (0,)), ((), ())), preferred_element_type=F32)


def split3(x):
    hi = x.astype(BF)
    r = x - hi.astype(F32)
    mid = r.astype(BF)
    lo = (r - mid.astype(F32)).astype(BF)
    return hi, mid, lo


def put3(base, x, lane0):
    lane = lax.broadcasted_iota(jnp.int32, base.shape, 1)
    hi, mid, lo = split3(x)
    out = jnp.where(lane == lane0, hi.astype(F32), base.astype(F32))
    out = jnp.where(lane == lane0 + 1, mid.astype(F32), out)
    out = jnp.where(lane == lane0 + 2, lo.astype(F32), out)
    return out.astype(BF)


VT = 80
UNIT = 256


def in_steps(begin, end, block, step):
    per = block // UNIT
    count = end - begin
    whole = count // per

    def long(i, _):
        step((begin + i * per) * UNIT, block)
        return 0

    def short(i, _):
        step((begin + whole * per + i) * UNIT, UNIT)
        return 0

    lax.fori_loop(0, whole, long, 0)
    lax.fori_loop(0, count - whole * per, short, 0)


QC, AHEAD, QB, BAHEAD = 512, 1, 256, 1


def fwd_kernel(heads, bq, bk, lo_ref, hi_ref, qe_ref, ke_ref, vt_ref, pad_ref, att_ref, qb_ref, m_ref, acc_ref):
    i = pl.program_id(0)
    row0 = pl.multiple_of(i * bq, bq)
    real = pad_ref[...] > 0.5
    for h in range(heads):
        qt = qe_ref[h].astype(F32).T[:HD]
        kt = ke_ref[h, pl.ds(row0, bq), :].astype(F32).T[:HD]
        own = jnp.sum(qt * kt, axis=0, keepdims=True)
        m_ref[h] = jnp.where(real, NEG, own)
        acc_ref[h] = jnp.where(real, 0.0, vt_ref[h, :, pl.ds(row0, bq)].astype(F32))

    def step(at, bk):
        col0 = pl.multiple_of(at, UNIT)
        work = [(h, slice(c, c + QC)) for c in range(0, bq, QC) for h in range(heads)]
        score = lambda h, c: nt(ke_ref[h, pl.ds(col0, bk), :], qe_ref[h, c, :])
        ss = [score(*w) for w in work[:AHEAD]]
        for n, (h, c) in enumerate(work):
            if n + AHEAD < len(work):
                ss.append(score(*work[n + AHEAD]))
            s = ss[n]
            m_old = m_ref[h, :, c]
            m_new = jnp.maximum(m_old, jnp.max(s, axis=0, keepdims=True))
            p = jnp.exp(s - m_new).astype(BF)
            alpha = jnp.exp(m_old - m_new)
            acc_ref[h, :, c] = acc_ref[h, :, c] * alpha + nn(vt_ref[h, :, pl.ds(col0, bk)], p)
            m_ref[h, :, c] = m_new

    in_steps(lo_ref[i], hi_ref[i], bk, step)
    outs = []
    for h in range(heads):
        acc = acc_ref[h]
        total = acc[HD : HD + 1]
        outs.append(jnp.where(real, acc[:HD] / total, 0.0))
        lse = jnp.broadcast_to(m_ref[h] + jnp.log(total), (8, bq)).T[:, :1]
        qb_ref[h] = put3(qe_ref[h], -lse, HD + 4)
    att_ref[...] = (jnp.concatenate(outs, axis=0) if heads > 1 else outs[0]).T.astype(BF)


def attend(qe, ke, vt, padw, lo, hi, bq, bk):
    heads, rows, _ = qe.shape
    full = lambda i, lo, hi: (0, 0, 0)
    return pl.pallas_call(
        functools.partial(fwd_kernel, heads, bq, bk),
        grid_spec=pltpu.PrefetchScalarGridSpec(
            num_scalar_prefetch=2,
            grid=(rows // bq,),
            in_specs=[
                pl.BlockSpec((heads, bq, LANES), lambda i, lo, hi: (0, i, 0)),
                pl.BlockSpec((heads, rows, LANES), full),
                pl.BlockSpec((heads, VT, rows), full),
                pl.BlockSpec((1, bq), lambda i, lo, hi: (0, i)),
            ],
            out_specs=[
                pl.BlockSpec((bq, heads * HD), lambda i, lo, hi: (i, 0)),
                pl.BlockSpec((heads, bq, LANES), lambda i, lo, hi: (0, i, 0)),
            ],
            scratch_shapes=[
                pltpu.VMEM((heads, 1, bq), F32),
                pltpu.VMEM((heads, VT, bq), F32),
            ],
        ),
        out_shape=[
            jax.ShapeDtypeStruct((rows, heads * HD), BF),
            jax.ShapeDtypeStruct((heads, rows, LANES), BF),
        ],
        compiler_params=pltpu.CompilerParams(vmem_limit_bytes=60 << 20),
        name="attend",
    )(lo, hi, qe, ke, vt, padw)


def bwd_kernel(heads, bq, bk, lo_ref, hi_ref, qb_ref, ke_ref, ve_ref, go_ref, att_ref, out_ref, ge_ref, dqt_ref, kt_ref, qt_ref, got_ref, dkt_ref, dvt_ref):
    j = pl.program_id(0)
    rows = qb_ref.shape[1]

    @pl.when(j == 0)
    def _():
        for h in range(heads):
            dqt_ref[h] = jnp.zeros_like(dqt_ref[h])
            for c in range(rows // 512):
                sl = pl.ds(c * 512, 512)
                go = go_ref[sl, h * HD : (h + 1) * HD]
                at = att_ref[sl, h * HD : (h + 1) * HD]
                delta = jnp.sum(go.astype(F32) * at.astype(F32), axis=1, keepdims=True)
                wide = jnp.concatenate([go, jnp.zeros_like(go)], axis=1)
                ge_ref[h, sl, :] = put3(wide, -delta, HD)
                got_ref[h, :, c * 512 : (c + 1) * 512] = wide.T[:HD]
                qt_ref[h, :, c * 512 : (c + 1) * 512] = qb_ref[h, sl, :].T[:HD]

    for h in range(heads):
        kt_ref[h] = ke_ref[h].T[:HD]

    zero = jnp.zeros((HD, bk), F32)

    def step(at, bq):
        row0 = pl.multiple_of(at, UNIT)
        work = [(h, pl.ds(row0 + c, QB)) for c in range(0, bq, QB) for h in range(heads)]
        score = lambda h, c: (nt(ke_ref[h], qb_ref[h, c, :]), nt(ve_ref[h], ge_ref[h, c, :]))
        ss = [score(*w) for w in work[:BAHEAD]]
        for n, (h, c) in enumerate(work):
            if n + BAHEAD < len(work):
                ss.append(score(*work[n + BAHEAD]))
            st, dt = ss[n]
            p = jnp.exp(st)
            ds = (p * dt).astype(BF)
            pb = p.astype(BF)
            dvt_ref[h] += nt(got_ref[h, :, c], pb)
            dkt_ref[h] += nt(qt_ref[h, :, c], ds)
            dqt_ref[h, :, c] += nn(kt_ref[h], ds)

    for h in range(heads):
        dkt_ref[h] = zero
        dvt_ref[h] = zero
    in_steps(lo_ref[j], hi_ref[j], bq, step)
    for h in range(heads):
        for part, ref in ((1, dkt_ref), (2, dvt_ref)):
            at = (part * heads + h) * HD
            out_ref[pl.ds(pl.multiple_of(j * bk, bk), bk), at : at + HD] = ref[h].T.astype(BF)

    @pl.when(j == pl.num_programs(0) - 1)
    def _():
        for h in range(heads):
            for c in range(rows // 512):
                sl = pl.ds(c * 512, 512)
                out_ref[sl, h * HD : (h + 1) * HD] = (dqt_ref[h, :, c * 512 : (c + 1) * 512].T * (HD ** -0.5)).astype(BF)


def attend_back(qb, ke, ve, go, att, lo, hi, bq, bk):
    heads, rows, _ = qb.shape
    full3 = lambda i, lo, hi: (0, 0, 0)
    full2 = lambda i, lo, hi: (0, 0)
    blk3 = lambda i, lo, hi: (0, i, 0)
    wide = heads * HD
    return pl.pallas_call(
        functools.partial(bwd_kernel, heads, bq, bk),
        grid_spec=pltpu.PrefetchScalarGridSpec(
            num_scalar_prefetch=2,
            grid=(rows // bk,),
            in_specs=[
                pl.BlockSpec((heads, rows, LANES), full3),
                pl.BlockSpec((heads, bk, LANES), blk3),
                pl.BlockSpec((heads, bk, LANES), blk3),
                pl.BlockSpec((rows, wide), full2),
                pl.BlockSpec((rows, wide), full2),
            ],
            out_specs=pl.BlockSpec((rows, 3 * wide), full2),
            scratch_shapes=[
                pltpu.VMEM((heads, rows, LANES), BF),
                pltpu.VMEM((heads, HD, rows), F32),
                pltpu.VMEM((heads, HD, bk), BF),
                pltpu.VMEM((heads, HD, rows), BF),
                pltpu.VMEM((heads, HD, rows), BF),
                pltpu.VMEM((heads, HD, bk), F32),
                pltpu.VMEM((heads, HD, bk), F32),
            ],
        ),
        out_shape=jax.ShapeDtypeStruct((rows, 3 * wide), BF),
        compiler_params=pltpu.CompilerParams(vmem_limit_bytes=60 << 20),
        name="attend_back",
    )(lo, hi, qb, ke, ve, go, att)


def dot_f32(a, b, dims):
    return lax.dot_general(a, b, ((dims[:1], dims[1:]), ((), ())), precision=highest, preferred_element_type=F32)


def soap_group(base, group, gr_ref, w_ref, m1_ref, m2_ref, av_ref, st_ref, ba_ref,
               nw_ref, n1_ref, n2_ref, na_ref, ns_ref, nb_ref, aug_ref):
    size = w_ref.shape[-1]
    half = size // 2
    panel = 8
    every = range(group)
    grads, firsts = [], []
    for s in every:
        rows = slice((base + s) * half, (base + s + 1) * half)
        wire = gr_ref[rows, :]
        grads.append(jnp.concatenate([wire[:, :size], wire[:, size:]], axis=0))
        firsts.append(beta_one * m1_ref[0, base + s] + (1.0 - beta_one) * grads[s])
        n1_ref[0, base + s] = firsts[s]
    sides = [(s, side) for s in every for side in range(2)]
    outers = [dot_f32(grads[s], grads[s], (1, 1) if side == 0 else (0, 0)) for s, side in sides]
    both = [dot_f32(jnp.concatenate([grads[s], firsts[s]], axis=0), ba_ref[0, base + s, 1], (1, 0)) for s in every]
    stats = []
    for (s, side), outer in zip(sides, outers):
        stats.append(beta_two * st_ref[0, base + s, side] + (1.0 - beta_two) * outer)
        ns_ref[0, base + s, side] = stats[-1]
    pairs = [dot_f32(ba_ref[0, base + s, 0], jnp.concatenate([both[s][:size], both[s][size:]], axis=1), (0, 0)) for s in every]
    mts = [dot_f32(ba_ref[0, base + s, side], stat, (0, 1)) for (s, side), stat in zip(sides, stats)]
    scaled = []
    for s in every:
        rotated, moment = pairs[s][:, :size], pairs[s][:, size:]
        second = beta_two * m2_ref[0, base + s] + (1.0 - beta_two) * rotated * rotated
        n2_ref[0, base + s] = second
        scaled.append(moment / (jnp.sqrt(second) + step_eps))
    grams = [dot_f32(mt, mt, (1, 1)) for mt in mts]
    inner = [dot_f32(scaled[s], ba_ref[0, base + s, 1], (1, 1)) for s in every]
    for m, (gram, mt) in enumerate(zip(grams, mts)):
        aug_ref[m] = jnp.concatenate([gram, mt], axis=1)
    directions = [dot_f32(ba_ref[0, base + s, 0], inner[s], (1, 0)) for s in every]
    for s in every:
        weight = w_ref[0, base + s]
        fresh = weight - step_rate * (directions[s] + weight_decay * weight)
        nw_ref[0, base + s] = fresh
        na_ref[0, base + s] = average_keep * av_ref[0, base + s] + (1.0 - average_keep) * fresh
    count = 2 * group
    row = lax.broadcasted_iota(jnp.int32, (count, panel, LANES), 1)
    for p in range(size // panel):
        top = p * panel
        part = aug_ref[:, top : top + panel, :]
        for r in range(panel):
            pivot = lax.rsqrt(part[:, r : r + 1, top + r : top + r + 1])
            lead = part[:, r : r + 1, :] * pivot
            column = jnp.where(row > r, part[:, :, top + r : top + r + 1] * pivot, 0.0)
            part = jnp.where(row == r, lead, part - column * lead)
        aug_ref[:, top : top + panel, :] = part
        below = top + panel
        if below < size:
            high = part.astype(BF).astype(F32)
            rest = part - high
            mid = rest.astype(BF).astype(F32)
            low = rest - mid
            first = jnp.concatenate([high, high, mid, high, mid, low], axis=1).astype(BF)
            other = jnp.concatenate([high, mid, high, low, mid, high], axis=1).astype(BF)
            for m in range(count):
                aug_ref[m, below:, :] -= lax.dot_general(
                    first[m][:, below:size], other[m], (((0,), (0,)), ((), ())), preferred_element_type=F32
                )
    for s in range(group):
        for side in range(2):
            nb_ref[0, base + s, side] = aug_ref[2 * s + side][:, size:].T


MESH = pl.DeviceIdType.MESH


def normalize(values):
    center = jnp.mean(values, axis=-1, keepdims=True)
    centered = values - center
    variance = jnp.mean(centered * centered, axis=-1, keepdims=True)
    scale = lax.rsqrt(variance + norm_eps)
    return centered * scale, scale


def norm_back(grad, xhat, scale):
    along = jnp.mean(grad * xhat, axis=-1, keepdims=True)
    return (grad - jnp.mean(grad, axis=-1, keepdims=True) - xhat * along) * scale


TAIL = 0.305
TAIL_FIT = (
    0.1216397411342051,
    0.12246669816059132,
    0.10342157025713879,
    0.1210193967312446,
    -0.037972477455618554,
    0.18571204369074895,
    -0.15298537812807472,
    0.036698452375741396,
)


def gelu_pair(u):
    size = jnp.abs(u)
    bell = jnp.exp(-0.5 * u * u)
    t = 1.0 / (1.0 + TAIL * size)
    poly = jnp.full_like(t, TAIL_FIT[-1])
    for c in TAIL_FIT[-2::-1]:
        poly = poly * t + c
    upper = poly * t * bell
    cdf = jnp.where(u > 0.0, 1.0 - upper, upper)
    return u * cdf, cdf + (0.3989422804014327 * u) * bell


def project_kernel(heads, shards, wide, gain_row, gains_dev, unit_ref, wire_ref, tok_ref, seg_ref, pad_ref,
                   norm_ref, qe_ref, ke_ref, ve_ref, vt_ref, mix_ref, line_ref, along_ref,
                   wide_ref, all_ref, near_ref, gain_ref, send_w, recv_w, send_z, recv_z):
    width = tok_ref.shape[1]
    half = HD // 2
    cols = 3 * heads
    units = wire_ref.shape[0]

    @pl.when(pl.program_id(0) == 0)
    def _():
        z = lax.axis_index("narrow")
        w = lax.axis_index("wide")
        twin = w + 1 - 2 * lax.rem(w, 2)
        chips = wide // 2
        barrier = pltpu.get_barrier_semaphore()
        pl.semaphore_signal(barrier, inc=1, device_id={"wide": twin}, device_id_type=MESH)
        for d in range(1, chips):
            pl.semaphore_signal(barrier, inc=1, device_id={"wide": lax.rem(w + 2 * d, wide)}, device_id_type=MESH)
        for d in range(1, shards):
            pl.semaphore_signal(barrier, inc=1, device_id={"narrow": lax.rem(z + d, shards)}, device_id_type=MESH)
        pl.semaphore_wait(barrier, chips + shards - 1)

        def slot(s):
            return all_ref.at[pl.ds(s * units, units)]

        def to_chip(d, mine):
            peer = lax.rem(w + 2 * d, wide)
            return pltpu.make_async_remote_copy(
                src_ref=wire_ref,
                dst_ref=slot(w if mine else peer),
                send_sem=send_w.at[d],
                recv_sem=recv_w.at[w if mine else peer],
                device_id={"wide": peer},
                device_id_type=MESH,
            )

        def to_twin(d, mine):
            owner = lax.rem((w if mine else twin) + 2 * d, wide)
            return pltpu.make_async_remote_copy(
                src_ref=wire_ref if d == 0 else slot(owner),
                dst_ref=slot(owner),
                send_sem=send_w.at[chips + d],
                recv_sem=recv_w.at[owner],
                device_id={"wide": twin},
                device_id_type=MESH,
            )

        def to_shard(d, mine):
            peer = lax.rem(z + d, shards)
            return pltpu.make_async_remote_copy(
                src_ref=wire_ref,
                dst_ref=near_ref.at[z if mine else peer],
                send_sem=send_z.at[d - 1],
                recv_sem=recv_z.at[z if mine else peer],
                device_id={"narrow": peer},
                device_id_type=MESH,
            )

        for d in range(1, chips):
            to_chip(d, True).start()
        to_twin(0, True).start()
        for d in range(1, shards):
            to_shard(d, True).start()
        all_ref[pl.ds(w * units, units)] = wire_ref[...]
        near_ref[z] = wire_ref[...]
        for d in range(1, chips):
            to_chip(d, False).wait_recv()
            to_twin(d, True).start()
        for d in range(chips):
            to_twin(d, False).wait_recv()

        for v in range(wide):
            line_ref[v] = all_ref[v * units + gain_row // 16]
        pieces = [line_ref[v].astype(F32)[:1, :gains_dev] for v in range(wide // 2)]
        gain_ref[...] = jnp.concatenate(pieces, axis=1)
        zero = jnp.zeros((half, HD), BF)

        def fill(r, _):
            low = pl.multiple_of(r * HD, HD)
            for c in range(cols):
                unit = unit_ref[r * cols + c]
                t = jnp.concatenate([all_ref[unit], all_ref[unit + 1]], axis=0)
                for part in range(2):
                    piece = t[:, part * HD : (part + 1) * HD]
                    at = pl.ds(low + part * half, half)
                    wide_ref[at, c * LANES : (c + 1) * LANES] = jnp.concatenate([piece, zero], axis=1)
                    mix_ref[at, c * HD : (c + 1) * HD] = piece
            return 0

        lax.fori_loop(0, width // HD, fill, 0)
        for d in range(1, shards):
            to_shard(d, False).wait_recv()
            to_shard(d, True).wait_send()
        along_ref[...] = near_ref[...]
        for d in range(1, chips):
            to_chip(d, True).wait_send()
        for d in range(chips):
            to_twin(d, True).wait_send()

    xhat, _ = normalize(tok_ref[...].astype(F32))
    normed = (xhat * gain_ref[...]).astype(BF)
    norm_ref[...] = normed
    count = tok_ref.shape[0]
    lane = lax.broadcasted_iota(jnp.int32, (LANES, count), 0)
    seg = seg_ref[...]
    same = lane - HD == seg
    in_segs = (lane >= HD) & (lane < HD + SEGS)
    ones = (lane >= HD + SEGS) & (lane < HD + SEGS + 3)
    ext_q = jnp.where(same, 1.0, 0.0).T
    ext_k = jnp.where(in_segs, jnp.where(same & (pad_ref[...] > 0.5), 0.0, NEG), jnp.where(ones, 1.0, 0.0)).T
    ext_v = jnp.where((lane >= HD) & (lane < HD + 3), 1.0, 0.0).T
    for h in range(heads):
        for ref, part, scale, ext in ((qe_ref, 0, HD ** -0.5, ext_q), (ke_ref, 1, 1.0, ext_k), (ve_ref, 2, 1.0, ext_v)):
            c = part * heads + h
            mixed = nn(normed, wide_ref[:, c * LANES : (c + 1) * LANES]).astype(BF)
            out = (mixed.astype(F32) * scale + ext).astype(BF)
            ref[h] = out
            if part == 2:
                vt_ref[h] = out.T[:VT]


def project(wire, unit, tokens, seg, pad, heads, shards, wide, gain_row, gains_dev):
    rows, width = tokens.shape
    tb = min(512, rows)
    full = lambda i, r: (0, 0)
    full3 = lambda i, r: (0, 0, 0)
    blk = lambda i, r: (i, 0)
    col = lambda i, r: (0, i)
    ext = lambda i, r: (0, i, 0)
    out = lambda *s: jax.ShapeDtypeStruct(s, BF)
    dma = pltpu.SemaphoreType.DMA
    units = wire.shape[0]
    return pl.pallas_call(
        functools.partial(project_kernel, heads, shards, wide, gain_row, gains_dev),
        grid_spec=pltpu.PrefetchScalarGridSpec(
            num_scalar_prefetch=1,
            grid=(rows // tb,),
            in_specs=[
                pl.BlockSpec(wire.shape, full3),
                pl.BlockSpec((tb, width), blk),
                pl.BlockSpec((1, tb), col),
                pl.BlockSpec((1, tb), col),
            ],
            out_specs=[
                pl.BlockSpec((tb, width), blk),
                pl.BlockSpec((heads, tb, LANES), ext),
                pl.BlockSpec((heads, tb, LANES), ext),
                pl.BlockSpec((heads, tb, LANES), ext),
                pl.BlockSpec((heads, VT, tb), lambda i, r: (0, 0, i)),
                pl.BlockSpec((width, 3 * heads * HD), full),
                pl.BlockSpec((wide, 16, LANES), full3),
                pl.BlockSpec((shards, units, 16, LANES), lambda i, r: (0, 0, 0, 0)),
            ],
            scratch_shapes=[
                pltpu.VMEM((width, 3 * heads * LANES), BF),
                pltpu.VMEM((wide * units, 16, LANES), BF),
                pltpu.VMEM((shards, units, 16, LANES), BF),
                pltpu.VMEM((1, width), F32),
                dma((wide,)),
                dma((wide,)),
                dma((shards - 1,)),
                dma((shards,)),
            ],
        ),
        out_shape=[
            out(rows, width),
            out(heads, rows, LANES),
            out(heads, rows, LANES),
            out(heads, rows, LANES),
            out(heads, VT, rows),
            out(width, 3 * heads * HD),
            out(wide, 16, LANES),
            out(shards, units, 16, LANES),
        ],
        compiler_params=pltpu.CompilerParams(vmem_limit_bytes=60 << 20, collective_id=3, has_side_effects=True),
        name="project",
    )(unit, wire, tokens, seg, pad)


def middle_kernel(shards, span, units, wide, gain_row, gains_dev, inside,
                  unit_ref, sel_ref, gain_ref, pad_ref, wire_ref, att_ref, tok_ref, cot_ref,
                  outa_ref, outb_ref, back_ref, res_ref, grads_ref, mix_ref,
                  tokens_ref, cots_ref, got_ref, give_ref, wo_ref, wu_ref, wd_ref, go_ref, gu_ref, gd_ref, gg_ref, blk_ref,
                  hold_ref, resv_ref, mixv_ref, gradv_ref, local_sem, send_i, recv_i, send_b, recv_b, send_a, recv_a):
    own, width = tokens_ref.shape
    parts = recv_i.shape[1]
    tb = own // parts
    half = HD // 2
    rows_dev = gradv_ref.shape[1]
    z = lax.axis_index("narrow")
    kinds = (
        (mixv_ref, None, width, 3 * span),
        (wo_ref, go_ref, span, width),
        (wu_ref, gu_ref, width, units),
        (wd_ref, gd_ref, units, width),
    )
    mix_blocks = width // HD * (3 * span // HD)
    per = blk_ref.shape[0] // shards

    barrier = pltpu.get_barrier_semaphore()
    for d in range(1, shards):
        pl.semaphore_signal(barrier, inc=1, device_id={"narrow": lax.rem(z + d, shards)}, device_id_type=MESH)
    pl.semaphore_wait(barrier, shards - 1)

    def bring(d, t, mine):
        peer = lax.rem(z + d, shards)
        slot = z if mine else peer
        return pltpu.make_async_remote_copy(
            src_ref=att_ref.at[pl.ds(pl.multiple_of(peer * own + t * tb, tb), tb), :],
            dst_ref=got_ref.at[slot, pl.ds(pl.multiple_of(t * tb, tb), tb), :],
            send_sem=send_i.at[d - 1, t],
            recv_sem=recv_i.at[slot, t],
            device_id={"narrow": peer},
            device_id_type=MESH,
        )

    def give(d, t, mine):
        peer = lax.rem(z + d, shards)
        slot = z if mine else peer
        return pltpu.make_async_remote_copy(
            src_ref=give_ref.at[peer, pl.ds(pl.multiple_of(t * tb, tb), tb), :],
            dst_ref=back_ref.at[pl.ds(pl.multiple_of(slot * own + t * tb, tb), tb), :],
            send_sem=send_b.at[d - 1, t],
            recv_sem=recv_b.at[slot, t],
            device_id={"narrow": peer},
            device_id_type=MESH,
        )

    def hop_copy(c, t, step):
        at = pl.ds(pl.multiple_of(t * tb, tb), tb)
        return pltpu.make_async_remote_copy(
            src_ref=outa_ref.at[c, at, :],
            dst_ref=outa_ref.at[c, at, :],
            send_sem=send_a.at[step, c, t],
            recv_sem=recv_a.at[c, t],
            device_id={"narrow": lax.rem(z + (1 if step == 0 else shards - 1), shards)},
            device_id_type=MESH,
        )

    room = (z < shards - 1, z > 0)
    for t in range(parts):
        for d in range(1, shards):
            bring(d, t, True).start()
    mine = pl.ds(pl.multiple_of(z * own, own), own)
    copies = [
        pltpu.make_async_copy(att_ref.at[mine, :], got_ref.at[z], local_sem.at[0]),
        pltpu.make_async_copy(tok_ref.at[mine, :], tokens_ref, local_sem.at[1]),
        pltpu.make_async_copy(cot_ref.at[mine, :], cots_ref, local_sem.at[2]),
    ]
    fetch = pltpu.make_async_copy(wire_ref, hold_ref, local_sem.at[3])
    fetch.start()
    for copy in copies:
        copy.start()
    fetch.wait()

    base = 0
    for ref, acc, rows, cols in kinds:
        grid_cols = cols // HD

        def fill(r, _, ref=ref, base=base, grid_cols=grid_cols):
            low = pl.multiple_of(r * HD, HD)
            for n in range(shards):
                for c in range(grid_cols):
                    unit = unit_ref[base + r * grid_cols + c] + n * (rows_dev // 16)
                    t = jnp.concatenate([hold_ref[unit], hold_ref[unit + 1]], axis=0)
                    for part in range(2):
                        ref[n, pl.ds(low + part * half, half), c * HD : (c + 1) * HD] = t[:, part * HD : (part + 1) * HD]
            return 0

        lax.fori_loop(0, rows // HD, fill, 0)
        base += rows // HD * grid_cols
        if acc is not None:
            acc[...] = jnp.zeros_like(acc)
    gg_ref[...] = jnp.zeros_like(gg_ref)
    stores = [
        pltpu.make_async_copy(mixv_ref, mix_ref, local_sem.at[4]),
        pltpu.make_async_copy(resv_ref, res_ref, local_sem.at[5]),
        pltpu.make_async_copy(gradv_ref, grads_ref, local_sem.at[6]),
    ]
    stores[0].start()
    for copy in copies:
        copy.wait()

    def block(t, _):
        at = pl.ds(pl.multiple_of(t * tb, tb), tb)
        for d in range(1, shards):
            bring(d, t, False).wait_recv()
        tokens = tokens_ref[at, :].astype(F32)
        cot = cots_ref[at, :]
        branch = nn(got_ref[0, at, :], wo_ref[0])
        for n in range(1, shards):
            branch += nn(got_ref[n, at, :], wo_ref[n])
        residual = tokens + branch
        xhat, scale = normalize(residual)
        gain = gain_ref[...]
        normed = (xhat * gain).astype(BF)
        ups = [nn(normed, wu_ref[n]) for n in range(shards)]
        downs = [nt(cot, wd_ref[n]) for n in range(shards)]
        actives, back_ups = [], []
        for n in range(shards):
            value, slope = gelu_pair(ups[n])
            actives.append(value.astype(BF))
            back_ups.append((slope * downs[n]).astype(BF))
        mlp = nn(actives[0], wd_ref[0])
        back = nt(back_ups[0], wu_ref[0])
        for n in range(1, shards):
            mlp += nn(actives[n], wd_ref[n])
            back += nt(back_ups[n], wu_ref[n])
        out = (residual + mlp).astype(BF)

        @pl.when(t < inside)
        def _():
            outa_ref[z, at, :] = out
            for step in range(2):

                @pl.when(room[step])
                def _(step=step):
                    hop_copy(z, t, step).start()

        @pl.when(t >= inside)
        def _():
            outb_ref[pl.ds(pl.multiple_of((t - inside) * tb, tb), tb), :] = out

        gg_ref[...] += jnp.sum(back * xhat, axis=0, keepdims=True)
        back_res = cot.astype(F32) + norm_back(back * gain, xhat, scale)
        resv_ref[at, :] = back_res
        branch_low = back_res.astype(BF)
        line = pad_ref[:, pl.ds(pl.multiple_of(z * own + t * tb, LANES), tb)]
        pad = jnp.broadcast_to(line, (8, tb)).T[:, :1]
        for n in range(shards):
            give_ref[n, at, :] = (nt(branch_low, wo_ref[n]) * pad).astype(BF)
        for d in range(1, shards):
            give(d, t, True).start()
        for n in range(shards):
            gd_ref[n] += tn(actives[n], cot)
            gu_ref[n] += tn(normed, back_ups[n])
            go_ref[n] += tn(got_ref[n, at, :], branch_low)
        return 0

    lax.fori_loop(0, parts, block, 0)
    stores[1].start()
    back_ref[mine, :] = give_ref[z]
    base = 0
    for ref, acc, rows, cols in kinds:
        grid_cols = cols // HD
        if acc is not None:

            def cut(r, _, acc=acc, base=base, grid_cols=grid_cols):
                low = pl.multiple_of(r * HD, HD)
                for n in range(shards):
                    for c in range(grid_cols):
                        lanes = slice(c * HD, (c + 1) * HD)
                        value = jnp.concatenate([acc[n, pl.ds(low, half), lanes], acc[n, pl.ds(low + half, half), lanes]], axis=1)
                        blk_ref[n * per + base - mix_blocks + r * grid_cols + c] = value.astype(BF)
                return 0

            lax.fori_loop(0, rows // HD, cut, 0)
        base += rows // HD * grid_cols
    for n in range(shards):
        blk_ref[(n + 1) * per - 1] = jnp.zeros((half, LANES), BF)
    slots = gain_row // half
    top = lax.broadcasted_iota(jnp.int32, (16, LANES), 0) == 0

    def place(v, _):
        for n in range(shards):
            for i in range(slots):
                gradv_ref[v * shards + n, i * half : (i + 1) * half, :] = blk_ref[sel_ref[v * slots + i] + n * per]
        return 0

    lax.fori_loop(0, wide, place, 0)
    for v in range(wide):
        piece = v * gains_dev // LANES - width // LANES
        for n in range(shards):
            if piece >= 0:
                value = jnp.where(top, gg_ref[:, piece * LANES : (piece + 1) * LANES], 0.0).astype(BF)
            else:
                value = jnp.zeros((16, LANES), BF)
            gradv_ref[v * shards + n, gain_row:, :] = value
    stores[2].start()

    hops = [(s, t, step) for s in range(1, shards) for t in range(inside) for step in range(2)]
    for s, t, step in hops:
        chunk = z - s if step == 0 else z + s
        there = chunk >= 0 if step == 0 else chunk < shards

        @pl.when(there)
        def _(chunk=chunk, t=t, step=step):
            hop_copy(chunk, t, step).wait_recv()

        @pl.when(there & room[step])
        def _(chunk=chunk, t=t, step=step):
            hop_copy(chunk, t, step).start()

    for t in range(parts):
        for d in range(1, shards):
            give(d, t, False).wait_recv()
    for copy in stores:
        copy.wait()
    for t in range(parts):
        for d in range(1, shards):
            bring(d, t, True).wait_send()
            give(d, t, True).wait_send()
    for t in range(inside):
        for step in range(2):

            @pl.when(room[step])
            def _(t=t, step=step):
                hop_copy(z, t, step).wait_send()

    for s, t, step in hops:
        chunk = z - s if step == 0 else z + s
        there = chunk >= 0 if step == 0 else chunk < shards

        @pl.when(there & room[step])
        def _(chunk=chunk, t=t, step=step):
            hop_copy(chunk, t, step).wait_send()


def middle(unit, sel, wire, gain_two, pad, att, tokens, cotangent, shards, wide, rows_dev, gain_row, gains_dev):
    rows, span = att.shape
    width = tokens.shape[1]
    units = FF // shards
    own = rows // shards
    tb = min(256, own)
    parts = own // tb
    inside = max(1, parts // 4)
    blocks = unit.shape[0] - width // HD * (3 * span // HD)
    vmem = pl.BlockSpec(memory_space=pltpu.VMEM)
    smem = pl.BlockSpec(memory_space=pltpu.SMEM)
    hbm = pl.BlockSpec(memory_space=pl.ANY)
    dma = pltpu.SemaphoreType.DMA
    return pl.pallas_call(
        functools.partial(middle_kernel, shards, span, units, wide, gain_row, gains_dev, inside),
        in_specs=[smem, smem, vmem, vmem, hbm, hbm, hbm, hbm],
        out_specs=[vmem] * 3 + [hbm] * 3,
        out_shape=[
            jax.ShapeDtypeStruct((shards, inside * tb, width), BF),
            jax.ShapeDtypeStruct((own - inside * tb, width), BF),
            jax.ShapeDtypeStruct((rows, span), BF),
            jax.ShapeDtypeStruct((own, width), F32),
            jax.ShapeDtypeStruct((wide * shards, rows_dev, LANES), BF),
            jax.ShapeDtypeStruct((shards, width, 3 * span), BF),
        ],
        scratch_shapes=[
            pltpu.VMEM((own, width), BF),
            pltpu.VMEM((own, width), BF),
            pltpu.VMEM((shards, own, span), BF),
            pltpu.VMEM((shards, own, span), BF),
            pltpu.VMEM((shards, span, width), BF),
            pltpu.VMEM((shards, width, units), BF),
            pltpu.VMEM((shards, units, width), BF),
            pltpu.VMEM((shards, span, width), F32),
            pltpu.VMEM((shards, width, units), F32),
            pltpu.VMEM((shards, units, width), F32),
            pltpu.VMEM((1, width), F32),
            pltpu.VMEM((shards * (blocks + 1), HD // 2, LANES), BF),
            pltpu.VMEM(wire.shape, BF),
            pltpu.VMEM((own, width), F32),
            pltpu.VMEM((shards, width, 3 * span), BF),
            pltpu.VMEM((wide * shards, rows_dev, LANES), BF),
            dma((7,)),
            dma((shards - 1, parts)),
            dma((shards, parts)),
            dma((shards - 1, parts)),
            dma((shards, parts)),
            dma((2, shards, inside)),
            dma((shards, inside)),
        ],
        compiler_params=pltpu.CompilerParams(vmem_limit_bytes=63 << 20, collective_id=2, has_side_effects=True),
        name="middle",
    )(unit, sel, gain_two, pad, wire, att, tokens, cotangent)


PARTS = 4


def finish_kernel(shards, wide, gain_row, gains_dev, group, sel_ref, mix_ref, gain_ref, fullh_ref, resh_ref, bm_ref, norm_ref, tok_ref, *refs):
    given, taken = refs[1:7], refs[9:15]
    states, outs, (full_ref, res_ref) = refs[15:21], refs[21:27], refs[27:29]
    first_ref, grad_ref, line_ref = refs[0], refs[7], refs[8]
    (own_ref, normed_ref, tokens_ref, got_ref, acc_ref, blk_ref, grads_ref, sums_ref, firsts_ref, part_ref, aug_ref,
     local_sem, send_z, recv_z, send_w, recv_w, send_a, recv_a, send_g, recv_g, send_f, recv_f) = refs[29:]
    width = norm_ref.shape[1]
    rows, cols = bm_ref.shape
    own = rows // shards
    hold = own // PARTS
    half = HD // 2
    grid_cols = cols // HD
    blocks = width // HD * grid_cols
    slots = gain_row // half
    z = lax.axis_index("narrow")
    w = lax.axis_index("wide")

    barrier = pltpu.get_barrier_semaphore()
    for d in range(1, shards):
        pl.semaphore_signal(barrier, inc=1, device_id={"narrow": lax.rem(z + d, shards)}, device_id_type=MESH)
    for d in range(1, wide):
        pl.semaphore_signal(barrier, inc=1, device_id={"wide": lax.rem(w + d, wide)}, device_id_type=MESH)
    pl.semaphore_wait(barrier, shards + wide - 2)

    def to_peer(d, part, mine):
        peer = lax.rem(z + d, shards)
        slot = z if mine else peer
        at = pl.multiple_of(peer * own + part * hold, hold)
        return pltpu.make_async_remote_copy(
            src_ref=bm_ref.at[pl.ds(at, hold), :],
            dst_ref=got_ref.at[slot, pl.ds(part * hold, hold), :],
            send_sem=send_z.at[d - 1, part],
            recv_sem=recv_z.at[slot, part],
            device_id={"narrow": peer},
            device_id_type=MESH,
        )

    def to_owner(d, mine):
        peer = lax.rem(w + d, wide)
        slot = w if mine else peer
        return pltpu.make_async_remote_copy(
            src_ref=grads_ref.at[peer],
            dst_ref=sums_ref.at[slot],
            send_sem=send_w.at[d - 1],
            recv_sem=recv_w.at[slot],
            device_id={"wide": peer},
            device_id_type=MESH,
        )

    def hop_copy(c, part, step):
        at = pl.ds(pl.multiple_of(c * own + part * hold, hold), hold)
        return pltpu.make_async_remote_copy(
            src_ref=grad_ref.at[at, :],
            dst_ref=grad_ref.at[at, :],
            send_sem=send_a.at[step, c, part],
            recv_sem=recv_a.at[c, part],
            device_id={"narrow": lax.rem(z + (1 if step == 0 else shards - 1), shards)},
            device_id_type=MESH,
        )

    def pass_on(c, part, act):
        for step, there in ((0, z < shards - 1), (1, z > 0)):
            if c is None or step == c[0]:
                chunk = z if c is None else c[1]
                ok = there if c is None else there & c[2]

                @pl.when(ok)
                def _(chunk=chunk, step=step):
                    act(hop_copy(chunk, part, step))

    def line_to(d, mine):
        peer = lax.rem(z + d, shards)
        slot = z if mine else peer
        return pltpu.make_async_remote_copy(
            src_ref=line_ref.at[z],
            dst_ref=line_ref.at[slot],
            send_sem=send_g.at[d - 1],
            recv_sem=recv_g.at[slot],
            device_id={"narrow": peer},
            device_id_type=MESH,
        )

    rows_dev = part_ref.shape[0]

    def first_to(d, mine):
        peer = lax.rem(z + d, shards)
        slot = z if mine else peer
        return pltpu.make_async_remote_copy(
            src_ref=first_ref.at[pl.ds(pl.multiple_of(peer * rows_dev, 16), rows_dev), :],
            dst_ref=firsts_ref.at[slot],
            send_sem=send_f.at[d - 1],
            recv_sem=recv_f.at[slot],
            device_id={"narrow": peer},
            device_id_type=MESH,
        )

    for d in range(1, shards):
        first_to(d, True).start()
    for part in range(PARTS):
        for d in range(1, shards):
            to_peer(d, part, True).start()
    mine = pl.ds(pl.multiple_of(z * own, own), own)
    copies = [
        pltpu.make_async_copy(bm_ref, own_ref, local_sem.at[0]),
        pltpu.make_async_copy(norm_ref, normed_ref, local_sem.at[1]),
        pltpu.make_async_copy(tok_ref.at[mine, :], tokens_ref, local_sem.at[2]),
        pltpu.make_async_copy(bm_ref.at[mine, :], got_ref.at[z], local_sem.at[3]),
        pltpu.make_async_copy(
            first_ref.at[pl.ds(pl.multiple_of(z * rows_dev, 16), rows_dev), :], firsts_ref.at[z], local_sem.at[4]
        ),
    ]
    late = [
        pltpu.make_async_copy(a, b, local_sem.at[5 + k])
        for k, (a, b) in enumerate(zip((fullh_ref, resh_ref, *given), (full_ref, res_ref, *states)))
    ]
    for copy in copies + late:
        copy.start()
    for copy in copies:
        copy.wait()

    acc_ref[...] = jnp.zeros_like(acc_ref)
    tb = min(512, rows)

    def add(i, _):
        at = pl.ds(pl.multiple_of(i * tb, tb), tb)
        acc_ref[...] += tn(normed_ref[at, :], own_ref[at, :])
        return 0

    lax.fori_loop(0, rows // tb, add, 0)
    blk_ref[blocks] = jnp.zeros((half, LANES), BF)

    def cut(r, _):
        low = pl.multiple_of(r * HD, HD)
        for c in range(grid_cols):
            lanes = slice(c * HD, (c + 1) * HD)
            value = jnp.concatenate([acc_ref[pl.ds(low, half), lanes], acc_ref[pl.ds(low + half, half), lanes]], axis=1)
            blk_ref[r * grid_cols + c] = value.astype(BF)
        return 0

    lax.fori_loop(0, width // HD, cut, 0)
    along = jnp.sum(acc_ref[...] * mix_ref[...].astype(F32), axis=1, keepdims=True)
    line = jnp.broadcast_to(along, (width, LANES)).T[:16] / gain_ref[...]
    top = lax.broadcasted_iota(jnp.int32, (16, LANES), 0) == 0
    for v in range(wide):

        def place(i, _, v=v):
            grads_ref[v, pl.ds(pl.multiple_of(i * half, half), half), :] = blk_ref[sel_ref[v * slots + i]]
            return 0

        lax.fori_loop(0, slots, place, 0)
        piece = v * gains_dev // LANES
        if piece < width // LANES:
            value = jnp.where(top, line[:, piece * LANES : (piece + 1) * LANES], 0.0).astype(BF)
        else:
            value = jnp.zeros((16, LANES), BF)
        grads_ref[v, gain_row : gain_row + 16, :] = value
    for d in range(1, wide):
        to_owner(d, True).start()
    part_ref[...] = grads_ref[w].astype(F32)

    tile = min(256, hold)

    def norm_rows(i, _):
        at = pl.ds(pl.multiple_of(i * tile, tile), tile)
        back = nt(got_ref[0, at, :], full_ref[0])
        for n in range(1, shards):
            back += nt(got_ref[n, at, :], full_ref[n])
        xhat, scale = normalize(tokens_ref[at, :].astype(F32))
        grad = res_ref[at, :] + norm_back(back * gain_ref[...], xhat, scale)
        grad_ref[pl.ds(pl.multiple_of(z * own + i * tile, tile), tile), :] = grad.astype(BF)
        return 0

    def norm_part(part):
        for d in range(1, shards):
            to_peer(d, part, False).wait_recv()
        lax.fori_loop(part * hold // tile, (part + 1) * hold // tile, norm_rows, 0)
        pass_on(None, part, lambda copy: copy.start())

    for d in range(1, wide):
        to_owner(d, False).wait_recv()
    for d in range(1, wide):
        part_ref[...] += sums_ref[lax.rem(w + d, wide)].astype(F32)
    line_ref[z] = part_ref[gain_row : gain_row + 16, :]
    for d in range(1, shards):
        line_to(d, True).start()
    for d in range(1, shards):
        first_to(d, False).wait_recv()
    total = firsts_ref[0].astype(F32)
    for n in range(1, shards):
        total += firsts_ref[n].astype(F32)
    line_ref[shards] = total[gain_row : gain_row + 16, :]
    part_ref[...] += total
    for copy in late:
        copy.wait()
    stores = [pltpu.make_async_copy(a, b, local_sem.at[13 + k]) for k, (a, b) in enumerate(zip(outs, taken))]
    ready = 0
    rounds = slots // group
    for g in range(rounds):
        soap_group(g * group, group, part_ref, *states, *outs, aug_ref)
        upto = PARTS * (g + 1) // rounds
        while ready < upto:
            norm_part(ready)
            ready += 1
    for copy in stores:
        copy.start()
    hops = [(s, part, step) for s in range(1, shards) for part in range(PARTS) for step in range(2)]
    for s, part, step in hops:
        chunk = z - s if step == 0 else z + s
        there = chunk >= 0 if step == 0 else chunk < shards

        @pl.when(there)
        def _(chunk=chunk, part=part, step=step):
            hop_copy(chunk, part, step).wait_recv()

        pass_on((step, chunk, there), part, lambda copy: copy.start())
    for copy in stores:
        copy.wait()
    for d in range(1, shards):
        line_to(d, False).wait_recv()
    for part in range(PARTS):
        pass_on(None, part, lambda copy: copy.wait_send())
    for s, part, step in hops:
        chunk = z - s if step == 0 else z + s
        there = chunk >= 0 if step == 0 else chunk < shards
        pass_on((step, chunk, there), part, lambda copy: copy.wait_send())
    for d in range(1, shards):
        line_to(d, True).wait_send()
        first_to(d, True).wait_send()
    for part in range(PARTS):
        for d in range(1, shards):
            to_peer(d, part, True).wait_send()
    for d in range(1, wide):
        to_owner(d, True).wait_send()


def finish(sel, mix, mix_full, gain_one, res, bm, normed, tokens, states, group, wide, rows_dev, gain_row, gains_dev):
    shards = mix_full.shape[0]
    rows, cols = bm.shape
    width = normed.shape[1]
    own = rows // shards
    half = HD // 2
    blocks = width // HD * (cols // HD)
    vmem = pl.BlockSpec(memory_space=pltpu.VMEM)
    smem = pl.BlockSpec(memory_space=pltpu.SMEM)
    hbm = pl.BlockSpec(memory_space=pl.ANY)
    dma = pltpu.SemaphoreType.DMA
    return pl.pallas_call(
        functools.partial(finish_kernel, shards, wide, gain_row, gains_dev, group),
        in_specs=[smem, vmem, vmem, hbm, hbm, hbm, hbm, hbm, hbm] + [hbm] * 6,
        out_specs=[vmem] * 2 + [hbm] * 6,
        out_shape=[jax.ShapeDtypeStruct((rows, width), BF), jax.ShapeDtypeStruct((shards + 1, 16, LANES), F32)]
        + [jax.ShapeDtypeStruct(a.shape, a.dtype) for a in states[1:]],
        scratch_shapes=[pltpu.VMEM(a.shape, a.dtype) for a in states[1:]] * 2
        + [
            pltpu.VMEM(mix_full.shape, BF),
            pltpu.VMEM(res.shape, F32),
            pltpu.VMEM((rows, cols), BF),
            pltpu.VMEM((rows, width), BF),
            pltpu.VMEM((own, width), BF),
            pltpu.VMEM((shards, own, cols), BF),
            pltpu.VMEM((width, cols), F32),
            pltpu.VMEM((blocks + 1, half, LANES), BF),
            pltpu.VMEM((wide, rows_dev, LANES), BF),
            pltpu.VMEM((wide, rows_dev, LANES), BF),
            pltpu.VMEM((shards, rows_dev, LANES), BF),
            pltpu.VMEM((rows_dev, LANES), F32),
            pltpu.VMEM((2 * group, HD, LANES), F32),
            dma((19,)),
            dma((shards - 1, PARTS)),
            dma((shards, PARTS)),
            dma((wide - 1,)),
            dma((wide,)),
            dma((2, shards, PARTS)),
            dma((shards, PARTS)),
            dma((shards - 1,)),
            dma((shards,)),
            dma((shards - 1,)),
            dma((shards,)),
        ],
        compiler_params=pltpu.CompilerParams(vmem_limit_bytes=62 << 20, collective_id=1, has_side_effects=True),
        name="finish",
    )(sel, mix, gain_one, mix_full, res, bm, normed, tokens, *states)


def wrap_kernel(count, per, grad_ref, outa_ref, outb_ref, *refs):
    olds, wide_ref, out_ref, news = refs[:count], refs[count], refs[count + 1], refs[count + 2 :]
    for old, new in zip(olds, news):
        new[...] = old[...]
    wide_ref[...] = grad_ref[...].astype(F32)
    place = lax.rem(pl.program_id(0), per)

    @pl.when(place == 0)
    def _():
        out_ref[...] = outa_ref[0]

    @pl.when(place > 0)
    def _():
        out_ref[...] = outb_ref[0]


def wrap(grad, out_a, out_b, olds):
    rows, width = grad.shape
    tb = out_a.shape[1]
    per = 1 + out_b.shape[1] // tb
    steps = rows // tb
    slots = olds[0].shape[1]
    group = next(g for g in range(1, slots + 1) if slots % g == 0 and slots // g <= steps)
    last = slots // group - 1
    blk = pl.BlockSpec((tb, width), lambda i: (i, 0))
    part_a = pl.BlockSpec((1, tb, width), lambda i: (i // per, 0, 0))
    part_b = pl.BlockSpec((1, tb, width), lambda i: (i // per, jnp.maximum(i % per - 1, 0), 0))
    states = [
        pl.BlockSpec((1, group, *a.shape[2:]), lambda i, k=a.ndim: (0, jnp.minimum(i, last)) + (0,) * (k - 2)) for a in olds
    ]
    return pl.pallas_call(
        functools.partial(wrap_kernel, len(olds), per),
        grid=(steps,),
        in_specs=[blk, part_a, part_b] + states,
        out_specs=[blk, blk] + states,
        out_shape=[jax.ShapeDtypeStruct((rows, width), F32), jax.ShapeDtypeStruct((rows, width), BF)]
        + [jax.ShapeDtypeStruct(a.shape, a.dtype) for a in olds],
        compiler_params=pltpu.CompilerParams(vmem_limit_bytes=60 << 20),
        name="wrap",
    )(grad, out_a, out_b, *olds)


def adam_gains(grad, gain, first, second, average):
    new_first = beta_one * first + (1.0 - beta_one) * grad
    new_second = beta_two * second + (1.0 - beta_two) * grad * grad
    new_gain = gain - gain_rate * new_first / (jnp.sqrt(new_second) + step_eps)
    new_average = average_keep * average + (1.0 - average_keep) * new_gain
    return (new_gain, new_first, new_second, new_average)


def body(
    tokens,
    cotangent,
    segment_ids,
    pad_mask,
    owner_order,
    weights,
    first_moment,
    second_moment,
    average,
    stats,
    bases,
    gains,
    gain_first,
    gain_second,
    gain_average,
):
    narrow = lax.axis_size("narrow")
    wide = lax.axis_size("wide")
    heads = HEADS // narrow
    rows, width = tokens.shape
    span = heads * HD
    own = rows // narrow
    slots, size = weights.shape[1], weights.shape[2]
    half = size // 2
    block_count = owner_order.shape[0]
    gains_dev = gains.shape[0]
    gain_row = slots * half
    rows_dev = gain_row + 16

    low = weights[0].astype(BF)
    wire = jnp.concatenate([low[:, :half], low[:, half:]], axis=2).reshape(gain_row, 2 * size)
    wire = jnp.concatenate([wire, jnp.pad(gains.astype(BF)[None], ((0, 15), (0, LANES - gains_dev)))], axis=0)

    ids = jnp.arange(block_count, dtype=jnp.int32)
    slot_of = jnp.sum(jnp.where(owner_order[None, :] == ids[:, None], ids[None, :], 0), axis=1)
    device, place = slot_of // slots, slot_of % slots
    row_own = device * rows_dev + place * half
    row_full = device * (narrow * rows_dev) + place * half

    seg = segment_ids
    seg_row = segment_ids[0]
    pad = pad_mask.astype(F32)
    block = min(512, rows)
    low_seg = seg_row[::block]
    high_seg = seg_row[block - 1 :: block]
    begin = jnp.sum((seg_row[None, :] < low_seg[:, None]).astype(jnp.int32), axis=1) // UNIT
    end = (jnp.sum((seg_row[None, :] <= high_seg[:, None]).astype(jnp.int32), axis=1) + UNIT - 1) // UNIT

    normed, qe, ke, ve, vt, mix, lines, along = project(
        wire.reshape(-1, 16, LANES), row_own // 16, tokens, seg, pad, heads, narrow, wide, gain_row, gains_dev
    )
    wire_full = lax.all_gather(along.reshape(-1, LANES), "wide", axis=0, tiled=True)
    gain_all = lines[:, 0, :gains_dev].astype(F32).reshape(1, 2 * width)
    gain_one, gain_two = gain_all[:, :width], gain_all[:, width:]
    attended, qb = attend(qe, ke, vt, pad, begin, end, block, block)
    unit = row_full // 16
    mix_blocks = width // size * 3 * heads
    sel_rest = jnp.where(owner_order >= mix_blocks, owner_order - mix_blocks, block_count - mix_blocks)
    out_a, out_b, back_att, back_res, grads, mix_full = middle(
        unit, sel_rest, wire_full.reshape(-1, 16, LANES), gain_two, pad, attended, tokens, cotangent,
        narrow, wide, rows_dev, gain_row, gains_dev,
    )
    part_a = lax.psum_scatter(grads.reshape(-1, LANES), "wide", scatter_dimension=0, tiled=True)
    out_b = lax.all_to_all(jnp.broadcast_to(out_b, (narrow, *out_b.shape)), "narrow", 0, 0)
    bm = attend_back(qb, ke, ve, back_att, attended, begin, end, block, block)
    bm, part_a, out_b = lax.optimization_barrier((bm, part_a, out_b))
    sel = jnp.minimum(owner_order, mix_blocks)
    group = next(g for g in range(min(12, slots), 0, -1) if slots % g == 0)
    states = (part_a, weights, first_moment, second_moment, average, stats, bases)
    grad_all, lines, *fresh = finish(
        sel, mix, mix_full, gain_one, back_res, bm, normed, tokens, states, group, wide, rows_dev, gain_row, gains_dev
    )
    input_grad, output, new_weight, new_first, new_second, new_average, new_stats, new_bases = wrap(
        grad_all, out_a, out_b, fresh
    )
    line = jnp.sum(lines[:, 0], axis=0)
    offset = lax.axis_index("wide") * gains_dev % LANES
    own_gain = lax.dynamic_slice_in_dim(line, offset, gains_dev, 0)
    new_gains, gain_moment, gain_square, gain_mean = adam_gains(own_gain, gains, gain_first, gain_second, gain_average)
    return (
        output,
        input_grad,
        new_weight,
        new_first,
        new_second,
        new_average,
        new_stats,
        new_bases,
        new_gains,
        gain_moment,
        gain_square,
        gain_mean,
    )


def solution(mesh):
    block = P("narrow", "wide", None, None)
    pair = P("narrow", "wide", None, None, None)
    rows = P("wide", None)
    line = P("wide")
    return jax.shard_map(
        body,
        mesh=mesh,
        in_specs=(rows, rows, rows, rows, P(), block, block, block, block, pair, pair, line, line, line, line),
        out_specs=(rows, rows, block, block, block, block, pair, pair, line, line, line, line),
        check_vma=False,
    )
```

```python
import functools

import jax
import jax.numpy as jnp
from jax import lax
from jax.experimental import pallas as pl
from jax.experimental.pallas import tpu as pltpu
from jax.sharding import PartitionSpec as P

HEADS = 8
HD = 64
FF = 2048
LANES = 128
SEGS = 4
NEG = -1e30
F32 = jnp.float32
BF = jnp.bfloat16
highest = lax.Precision.HIGHEST

beta_one = 0.9
beta_two = 0.95
step_rate = 0.1
gain_rate = 0.75
weight_decay = 0.01
average_keep = 0.5
norm_eps = 1e-05
step_eps = 1e-08


def nt(a, b):
    return lax.dot_general(a, b, (((1,), (1,)), ((), ())), preferred_element_type=F32)


def nn(a, b):
    return lax.dot_general(a, b, (((1,), (0,)), ((), ())), preferred_element_type=F32)


def tn(a, b):
    return lax.dot_general(a, b, (((0,), (0,)), ((), ())), preferred_element_type=F32)


def split3(x):
    hi = x.astype(BF)
    r = x - hi.astype(F32)
    mid = r.astype(BF)
    lo = (r - mid.astype(F32)).astype(BF)
    return hi, mid, lo


def put3(base, x, lane0):
    lane = lax.broadcasted_iota(jnp.int32, base.shape, 1)
    hi, mid, lo = split3(x)
    out = jnp.where(lane == lane0, hi.astype(F32), base.astype(F32))
    out = jnp.where(lane == lane0 + 1, mid.astype(F32), out)
    out = jnp.where(lane == lane0 + 2, lo.astype(F32), out)
    return out.astype(BF)


VT = 80
UNIT = 256


def in_steps(begin, end, block, step):
    per = block // UNIT
    count = end - begin
    whole = count // per

    def long(i, _):
        step((begin + i * per) * UNIT, block)
        return 0

    def short(i, _):
        step((begin + whole * per + i) * UNIT, UNIT)
        return 0

    lax.fori_loop(0, whole, long, 0)
    lax.fori_loop(0, count - whole * per, short, 0)


QC, AHEAD, QB, BAHEAD = 512, 1, 256, 1


def fwd_kernel(heads, bq, bk, lo_ref, hi_ref, qe_ref, ke_ref, vt_ref, pad_ref, att_ref, qb_ref, m_ref, acc_ref):
    i = pl.program_id(0)
    row0 = pl.multiple_of(i * bq, bq)
    real = pad_ref[...] > 0
    for h in range(heads):
        qt = qe_ref[h].astype(F32).T[:HD]
        kt = ke_ref[h, pl.ds(row0, bq), :].astype(F32).T[:HD]
        own = jnp.sum(qt * kt, axis=0, keepdims=True)
        m_ref[h] = jnp.where(real, NEG, own)
        acc_ref[h] = jnp.where(real, 0.0, vt_ref[h, :, pl.ds(row0, bq)].astype(F32))

    def step(at, bk):
        col0 = pl.multiple_of(at, UNIT)
        work = [(h, slice(c, c + QC)) for c in range(0, bq, QC) for h in range(heads)]
        score = lambda h, c: nt(ke_ref[h, pl.ds(col0, bk), :], qe_ref[h, c, :])
        ss = [score(*w) for w in work[:AHEAD]]
        for n, (h, c) in enumerate(work):
            if n + AHEAD < len(work):
                ss.append(score(*work[n + AHEAD]))
            s = ss[n]
            m_old = m_ref[h, :, c]
            m_new = jnp.maximum(m_old, jnp.max(s, axis=0, keepdims=True))
            p = jnp.exp(s - m_new).astype(BF)
            alpha = jnp.exp(m_old - m_new)
            acc_ref[h, :, c] = acc_ref[h, :, c] * alpha + nn(vt_ref[h, :, pl.ds(col0, bk)], p)
            m_ref[h, :, c] = m_new

    in_steps(lo_ref[i], hi_ref[i], bk, step)
    outs = []
    for h in range(heads):
        acc = acc_ref[h]
        total = acc[HD : HD + 1]
        outs.append(jnp.where(real, acc[:HD] / total, 0.0))
        lse = jnp.broadcast_to(m_ref[h] + jnp.log(total), (8, bq)).T[:, :1]
        qb_ref[h] = put3(qe_ref[h], -lse, HD + 4)
    att_ref[...] = (jnp.concatenate(outs, axis=0) if heads > 1 else outs[0]).T.astype(BF)


def attend(qe, ke, vt, padw, lo, hi, bq, bk):
    heads, rows, _ = qe.shape
    full = lambda i, lo, hi: (0, 0, 0)
    return pl.pallas_call(
        functools.partial(fwd_kernel, heads, bq, bk),
        grid_spec=pltpu.PrefetchScalarGridSpec(
            num_scalar_prefetch=2,
            grid=(rows // bq,),
            in_specs=[
                pl.BlockSpec((heads, bq, LANES), lambda i, lo, hi: (0, i, 0)),
                pl.BlockSpec((heads, rows, LANES), full),
                pl.BlockSpec((heads, VT, rows), full),
                pl.BlockSpec((1, bq), lambda i, lo, hi: (0, i)),
            ],
            out_specs=[
                pl.BlockSpec((bq, heads * HD), lambda i, lo, hi: (i, 0)),
                pl.BlockSpec((heads, bq, LANES), lambda i, lo, hi: (0, i, 0)),
            ],
            scratch_shapes=[
                pltpu.VMEM((heads, 1, bq), F32),
                pltpu.VMEM((heads, VT, bq), F32),
            ],
        ),
        out_shape=[
            jax.ShapeDtypeStruct((rows, heads * HD), BF),
            jax.ShapeDtypeStruct((heads, rows, LANES), BF),
        ],
        compiler_params=pltpu.CompilerParams(vmem_limit_bytes=60 << 20),
        name="attend",
    )(lo, hi, qe, ke, vt, padw)


def bwd_kernel(heads, bq, bk, lo_ref, hi_ref, qb_ref, ke_ref, ve_ref, go_ref, att_ref, out_ref, ge_ref, dqt_ref, kt_ref, qt_ref, got_ref, dkt_ref, dvt_ref):
    j = pl.program_id(0)
    rows = qb_ref.shape[1]

    @pl.when(j == 0)
    def _():
        for h in range(heads):
            dqt_ref[h] = jnp.zeros_like(dqt_ref[h])
            for c in range(rows // 512):
                sl = pl.ds(c * 512, 512)
                go = go_ref[sl, h * HD : (h + 1) * HD]
                at = att_ref[sl, h * HD : (h + 1) * HD]
                delta = jnp.sum(go.astype(F32) * at.astype(F32), axis=1, keepdims=True)
                wide = jnp.concatenate([go, jnp.zeros_like(go)], axis=1)
                ge_ref[h, sl, :] = put3(wide, -delta, HD)
                got_ref[h, :, c * 512 : (c + 1) * 512] = wide.T[:HD]
                qt_ref[h, :, c * 512 : (c + 1) * 512] = qb_ref[h, sl, :].T[:HD]

    for h in range(heads):
        kt_ref[h] = ke_ref[h].T[:HD]

    zero = jnp.zeros((HD, bk), F32)

    def step(at, bq):
        row0 = pl.multiple_of(at, UNIT)
        work = [(h, pl.ds(row0 + c, QB)) for c in range(0, bq, QB) for h in range(heads)]
        score = lambda h, c: (nt(ke_ref[h], qb_ref[h, c, :]), nt(ve_ref[h], ge_ref[h, c, :]))
        ss = [score(*w) for w in work[:BAHEAD]]
        for n, (h, c) in enumerate(work):
            if n + BAHEAD < len(work):
                ss.append(score(*work[n + BAHEAD]))
            st, dt = ss[n]
            p = jnp.exp(st)
            ds = (p * dt).astype(BF)
            pb = p.astype(BF)
            dvt_ref[h] += nt(got_ref[h, :, c], pb)
            dkt_ref[h] += nt(qt_ref[h, :, c], ds)
            dqt_ref[h, :, c] += nn(kt_ref[h], ds)

    for h in range(heads):
        dkt_ref[h] = zero
        dvt_ref[h] = zero
    in_steps(lo_ref[j], hi_ref[j], bq, step)
    for h in range(heads):
        for part, ref in ((1, dkt_ref), (2, dvt_ref)):
            at = (part * heads + h) * HD
            out_ref[pl.ds(pl.multiple_of(j * bk, bk), bk), at : at + HD] = ref[h].T.astype(BF)

    @pl.when(j == pl.num_programs(0) - 1)
    def _():
        for h in range(heads):
            for c in range(rows // 512):
                sl = pl.ds(c * 512, 512)
                out_ref[sl, h * HD : (h + 1) * HD] = (dqt_ref[h, :, c * 512 : (c + 1) * 512].T * (HD ** -0.5)).astype(BF)


def attend_back(qb, ke, ve, go, att, lo, hi, bq, bk):
    heads, rows, _ = qb.shape
    full3 = lambda i, lo, hi: (0, 0, 0)
    full2 = lambda i, lo, hi: (0, 0)
    blk3 = lambda i, lo, hi: (0, i, 0)
    wide = heads * HD
    return pl.pallas_call(
        functools.partial(bwd_kernel, heads, bq, bk),
        grid_spec=pltpu.PrefetchScalarGridSpec(
            num_scalar_prefetch=2,
            grid=(rows // bk,),
            in_specs=[
                pl.BlockSpec((heads, rows, LANES), full3),
                pl.BlockSpec((heads, bk, LANES), blk3),
                pl.BlockSpec((heads, bk, LANES), blk3),
                pl.BlockSpec((rows, wide), full2),
                pl.BlockSpec((rows, wide), full2),
            ],
            out_specs=pl.BlockSpec((rows, 3 * wide), full2),
            scratch_shapes=[
                pltpu.VMEM((heads, rows, LANES), BF),
                pltpu.VMEM((heads, HD, rows), F32),
                pltpu.VMEM((heads, HD, bk), BF),
                pltpu.VMEM((heads, HD, rows), BF),
                pltpu.VMEM((heads, HD, rows), BF),
                pltpu.VMEM((heads, HD, bk), F32),
                pltpu.VMEM((heads, HD, bk), F32),
            ],
        ),
        out_shape=jax.ShapeDtypeStruct((rows, 3 * wide), BF),
        compiler_params=pltpu.CompilerParams(vmem_limit_bytes=60 << 20),
        name="attend_back",
    )(lo, hi, qb, ke, ve, go, att)


def dot_f32(a, b, dims):
    return lax.dot_general(a, b, ((dims[:1], dims[1:]), ((), ())), precision=highest, preferred_element_type=F32)


def soap_group(base, group, gr_ref, w_ref, m1_ref, m2_ref, av_ref, st_ref, ba_ref,
               nw_ref, n1_ref, n2_ref, na_ref, ns_ref, nb_ref, aug_ref):
    size = w_ref.shape[-1]
    half = size // 2
    panel = 8
    every = range(group)
    grads, firsts = [], []
    for s in every:
        rows = slice((base + s) * half, (base + s + 1) * half)
        wire = gr_ref[rows, :]
        grads.append(jnp.concatenate([wire[:, :size], wire[:, size:]], axis=0))
        firsts.append(beta_one * m1_ref[0, base + s] + (1.0 - beta_one) * grads[s])
        n1_ref[0, base + s] = firsts[s]
    sides = [(s, side) for s in every for side in range(2)]
    outers = [dot_f32(grads[s], grads[s], (1, 1) if side == 0 else (0, 0)) for s, side in sides]
    both = [dot_f32(jnp.concatenate([grads[s], firsts[s]], axis=0), ba_ref[0, base + s, 1], (1, 0)) for s in every]
    stats = []
    for (s, side), outer in zip(sides, outers):
        stats.append(beta_two * st_ref[0, base + s, side] + (1.0 - beta_two) * outer)
        ns_ref[0, base + s, side] = stats[-1]
    pairs = [dot_f32(ba_ref[0, base + s, 0], jnp.concatenate([both[s][:size], both[s][size:]], axis=1), (0, 0)) for s in every]
    mts = [dot_f32(ba_ref[0, base + s, side], stat, (0, 1)) for (s, side), stat in zip(sides, stats)]
    scaled = []
    for s in every:
        rotated, moment = pairs[s][:, :size], pairs[s][:, size:]
        second = beta_two * m2_ref[0, base + s] + (1.0 - beta_two) * rotated * rotated
        n2_ref[0, base + s] = second
        scaled.append(moment / (jnp.sqrt(second) + step_eps))
    grams = [dot_f32(mt, mt, (1, 1)) for mt in mts]
    inner = [dot_f32(scaled[s], ba_ref[0, base + s, 1], (1, 1)) for s in every]
    for m, (gram, mt) in enumerate(zip(grams, mts)):
        aug_ref[m] = jnp.concatenate([gram, mt], axis=1)
    directions = [dot_f32(ba_ref[0, base + s, 0], inner[s], (1, 0)) for s in every]
    for s in every:
        weight = w_ref[0, base + s]
        fresh = weight - step_rate * (directions[s] + weight_decay * weight)
        nw_ref[0, base + s] = fresh
        na_ref[0, base + s] = average_keep * av_ref[0, base + s] + (1.0 - average_keep) * fresh
    count = 2 * group
    row = lax.broadcasted_iota(jnp.int32, (count, panel, LANES), 1)
    for p in range(size // panel):
        top = p * panel
        part = aug_ref[:, top : top + panel, :]
        for r in range(panel):
            pivot = lax.rsqrt(part[:, r : r + 1, top + r : top + r + 1])
            lead = part[:, r : r + 1, :] * pivot
            column = jnp.where(row > r, part[:, :, top + r : top + r + 1] * pivot, 0.0)
            part = jnp.where(row == r, lead, part - column * lead)
        aug_ref[:, top : top + panel, :] = part
        below = top + panel
        if below < size:
            high = part.astype(BF).astype(F32)
            rest = part - high
            mid = rest.astype(BF).astype(F32)
            low = rest - mid
            first = jnp.concatenate([high, high, mid, high, mid, low], axis=1).astype(BF)
            other = jnp.concatenate([high, mid, high, low, mid, high], axis=1).astype(BF)
            for m in range(count):
                aug_ref[m, below:, :] -= lax.dot_general(
                    first[m][:, below:size], other[m], (((0,), (0,)), ((), ())), preferred_element_type=F32
                )
    for s in range(group):
        for side in range(2):
            nb_ref[0, base + s, side] = aug_ref[2 * s + side][:, size:].T


MESH = pl.DeviceIdType.MESH


def normalize(values):
    center = jnp.mean(values, axis=-1, keepdims=True)
    centered = values - center
    variance = jnp.mean(centered * centered, axis=-1, keepdims=True)
    scale = lax.rsqrt(variance + norm_eps)
    return centered * scale, scale


def norm_back(grad, xhat, scale):
    along = jnp.mean(grad * xhat, axis=-1, keepdims=True)
    return (grad - jnp.mean(grad, axis=-1, keepdims=True) - xhat * along) * scale


TAIL = 0.305
TAIL_FIT = (
    0.1216397411342051,
    0.12246669816059132,
    0.10342157025713879,
    0.1210193967312446,
    -0.037972477455618554,
    0.18571204369074895,
    -0.15298537812807472,
    0.036698452375741396,
)


def gelu_pair(u):
    size = jnp.abs(u)
    bell = jnp.exp(-0.5 * u * u)
    t = 1.0 / (1.0 + TAIL * size)
    poly = jnp.full_like(t, TAIL_FIT[-1])
    for c in TAIL_FIT[-2::-1]:
        poly = poly * t + c
    upper = poly * t * bell
    cdf = jnp.where(u > 0.0, 1.0 - upper, upper)
    return u * cdf, cdf + (0.3989422804014327 * u) * bell


def project_kernel(heads, shards, wide, gain_row, gains_dev, unit_ref, weight_ref, gains_ref, tok_ref, seg_ref, pad_ref,
                   norm_ref, qe_ref, ke_ref, ve_ref, vt_ref, mix_ref, line_ref, along_ref,
                   wide_ref, wire_ref, all_ref, near_ref, gain_ref, send_w, recv_w, send_z, recv_z):
    width = tok_ref.shape[1]
    half = HD // 2
    cols = 3 * heads
    units = wire_ref.shape[0]

    @pl.when(pl.program_id(0) == 0)
    def _():
        z = lax.axis_index("narrow")
        w = lax.axis_index("wide")
        twin = w + 1 - 2 * lax.rem(w, 2)
        chips = wide // 2
        barrier = pltpu.get_barrier_semaphore()
        pl.semaphore_signal(barrier, inc=1, device_id={"wide": twin}, device_id_type=MESH)
        for d in range(1, chips):
            pl.semaphore_signal(barrier, inc=1, device_id={"wide": lax.rem(w + 2 * d, wide)}, device_id_type=MESH)
        for d in range(1, shards):
            pl.semaphore_signal(barrier, inc=1, device_id={"narrow": lax.rem(z + d, shards)}, device_id_type=MESH)
        for s in range(gain_row // half):
            low = weight_ref[0, s].astype(BF)
            t = jnp.concatenate([low[:half], low[half:]], axis=1)
            wire_ref[2 * s] = t[:16]
            wire_ref[2 * s + 1] = t[16:]
        line = gains_ref[...]
        if gains_dev < LANES:
            line = jnp.concatenate([line, jnp.zeros((1, LANES - gains_dev), F32)], axis=1)
        first = lax.broadcasted_iota(jnp.int32, (16, LANES), 0) == 0
        wire_ref[gain_row // 16] = jnp.where(first, line, 0.0).astype(BF)
        pl.semaphore_wait(barrier, chips + shards - 1)

        def slot(s):
            return all_ref.at[pl.ds(s * units, units)]

        def to_chip(d, mine):
            peer = lax.rem(w + 2 * d, wide)
            return pltpu.make_async_remote_copy(
                src_ref=wire_ref,
                dst_ref=slot(w if mine else peer),
                send_sem=send_w.at[d],
                recv_sem=recv_w.at[w if mine else peer],
                device_id={"wide": peer},
                device_id_type=MESH,
            )

        def to_twin(d, mine):
            owner = lax.rem((w if mine else twin) + 2 * d, wide)
            return pltpu.make_async_remote_copy(
                src_ref=wire_ref if d == 0 else slot(owner),
                dst_ref=slot(owner),
                send_sem=send_w.at[chips + d],
                recv_sem=recv_w.at[owner],
                device_id={"wide": twin},
                device_id_type=MESH,
            )

        def to_shard(d, mine):
            peer = lax.rem(z + d, shards)
            return pltpu.make_async_remote_copy(
                src_ref=wire_ref,
                dst_ref=near_ref.at[z if mine else peer],
                send_sem=send_z.at[d - 1],
                recv_sem=recv_z.at[z if mine else peer],
                device_id={"narrow": peer},
                device_id_type=MESH,
            )

        for d in range(1, chips):
            to_chip(d, True).start()
        to_twin(0, True).start()
        for d in range(1, shards):
            to_shard(d, True).start()
        all_ref[pl.ds(w * units, units)] = wire_ref[...]
        near_ref[z] = wire_ref[...]
        for d in range(1, chips):
            to_chip(d, False).wait_recv()
            to_twin(d, True).start()
        for d in range(chips):
            to_twin(d, False).wait_recv()

        for v in range(wide):
            line_ref[v] = all_ref[v * units + gain_row // 16]
        pieces = [line_ref[v].astype(F32)[:1, :gains_dev] for v in range(wide // 2)]
        gain_ref[...] = jnp.concatenate(pieces, axis=1)
        zero = jnp.zeros((half, HD), BF)

        def fill(r, _):
            low = pl.multiple_of(r * HD, HD)
            for c in range(cols):
                unit = unit_ref[r * cols + c]
                t = jnp.concatenate([all_ref[unit], all_ref[unit + 1]], axis=0)
                for part in range(2):
                    piece = t[:, part * HD : (part + 1) * HD]
                    at = pl.ds(low + part * half, half)
                    wide_ref[at, c * LANES : (c + 1) * LANES] = jnp.concatenate([piece, zero], axis=1)
                    mix_ref[at, c * HD : (c + 1) * HD] = piece
            return 0

        lax.fori_loop(0, width // HD, fill, 0)
        for d in range(1, shards):
            to_shard(d, False).wait_recv()
            to_shard(d, True).wait_send()
        along_ref[...] = near_ref[...]
        for d in range(1, chips):
            to_chip(d, True).wait_send()
        for d in range(chips):
            to_twin(d, True).wait_send()

    xhat, _ = normalize(tok_ref[...].astype(F32))
    normed = (xhat * gain_ref[...]).astype(BF)
    norm_ref[...] = normed
    count = tok_ref.shape[0]
    lane = lax.broadcasted_iota(jnp.int32, (LANES, count), 0)
    seg = seg_ref[...]
    same = lane - HD == seg
    in_segs = (lane >= HD) & (lane < HD + SEGS)
    ones = (lane >= HD + SEGS) & (lane < HD + SEGS + 3)
    ext_q = jnp.where(same, 1.0, 0.0).T
    ext_k = jnp.where(in_segs, jnp.where(same & (pad_ref[...] > 0), 0.0, NEG), jnp.where(ones, 1.0, 0.0)).T
    side = lax.broadcasted_iota(jnp.int32, (count, LANES), 1)
    ext_v = jnp.where((side >= HD) & (side < HD + 3), 1.0, 0.0)
    whole = nn(normed, wide_ref[...]).astype(BF)
    for h in range(heads):
        for ref, part, scale, ext in ((qe_ref, 0, HD ** -0.5, ext_q), (ke_ref, 1, 1.0, ext_k), (ve_ref, 2, 1.0, ext_v)):
            c = part * heads + h
            mixed = whole[:, c * LANES : (c + 1) * LANES]
            out = (mixed.astype(F32) * scale + ext).astype(BF)
            ref[h] = out
            if part == 2:
                vt_ref[h] = out.T[:VT]


def project(weights, gains, unit, tokens, seg, pad, heads, shards, wide, gain_row, gains_dev):
    rows, width = tokens.shape
    tb = min(512, rows)
    full = lambda i, r: (0, 0)
    full3 = lambda i, r: (0, 0, 0)
    blk = lambda i, r: (i, 0)
    col = lambda i, r: (0, i)
    ext = lambda i, r: (0, i, 0)
    out = lambda *s: jax.ShapeDtypeStruct(s, BF)
    dma = pltpu.SemaphoreType.DMA
    units = gain_row // 16 + 1
    return pl.pallas_call(
        functools.partial(project_kernel, heads, shards, wide, gain_row, gains_dev),
        grid_spec=pltpu.PrefetchScalarGridSpec(
            num_scalar_prefetch=1,
            grid=(rows // tb,),
            in_specs=[
                pl.BlockSpec(weights.shape, lambda i, r: (0, 0, 0, 0)),
                pl.BlockSpec((1, gains_dev), full),
                pl.BlockSpec((tb, width), blk),
                pl.BlockSpec((1, tb), col),
                pl.BlockSpec((1, tb), col),
            ],
            out_specs=[
                pl.BlockSpec((tb, width), blk),
                pl.BlockSpec((heads, tb, LANES), ext),
                pl.BlockSpec((heads, tb, LANES), ext),
                pl.BlockSpec((heads, tb, LANES), ext),
                pl.BlockSpec((heads, VT, tb), lambda i, r: (0, 0, i)),
                pl.BlockSpec((width, 3 * heads * HD), full),
                pl.BlockSpec((wide, 16, LANES), full3),
                pl.BlockSpec((shards, units, 16, LANES), lambda i, r: (0, 0, 0, 0)),
            ],
            scratch_shapes=[
                pltpu.VMEM((width, 3 * heads * LANES), BF),
                pltpu.VMEM((units, 16, LANES), BF),
                pltpu.VMEM((wide * units, 16, LANES), BF),
                pltpu.VMEM((shards, units, 16, LANES), BF),
                pltpu.VMEM((1, width), F32),
                dma((wide,)),
                dma((wide,)),
                dma((shards - 1,)),
                dma((shards,)),
            ],
        ),
        out_shape=[
            out(rows, width),
            out(heads, rows, LANES),
            out(heads, rows, LANES),
            out(heads, rows, LANES),
            out(heads, VT, rows),
            out(width, 3 * heads * HD),
            out(wide, 16, LANES),
            out(shards, units, 16, LANES),
        ],
        compiler_params=pltpu.CompilerParams(vmem_limit_bytes=60 << 20, collective_id=3, has_side_effects=True),
        name="project",
    )(unit, weights, gains, tokens, seg, pad)


def middle_kernel(shards, span, units, wide, gain_row, gains_dev, inside,
                  unit_ref, sel_ref, gain_ref, pad_ref, wire_ref, att_ref, tok_ref, cot_ref,
                  outa_ref, outb_ref, back_ref, res_ref, grads_ref, mix_ref,
                  tokens_ref, cots_ref, got_ref, give_ref, wo_ref, wu_ref, wd_ref, go_ref, gu_ref, gd_ref, gg_ref, blk_ref,
                  hold_ref, resv_ref, mixv_ref, gradv_ref, local_sem, send_i, recv_i, send_b, recv_b, send_a, recv_a):
    own, width = tokens_ref.shape
    parts = recv_i.shape[1]
    tb = own // parts
    half = HD // 2
    rows_dev = gradv_ref.shape[1]
    z = lax.axis_index("narrow")
    kinds = (
        (mixv_ref, None, width, 3 * span),
        (wo_ref, go_ref, span, width),
        (wu_ref, gu_ref, width, units),
        (wd_ref, gd_ref, units, width),
    )
    mix_blocks = width // HD * (3 * span // HD)
    per = blk_ref.shape[0] // shards

    barrier = pltpu.get_barrier_semaphore()
    for d in range(1, shards):
        pl.semaphore_signal(barrier, inc=1, device_id={"narrow": lax.rem(z + d, shards)}, device_id_type=MESH)
    pl.semaphore_wait(barrier, shards - 1)

    def bring(d, t, mine):
        peer = lax.rem(z + d, shards)
        slot = z if mine else peer
        return pltpu.make_async_remote_copy(
            src_ref=att_ref.at[pl.ds(pl.multiple_of(peer * own + t * tb, tb), tb), :],
            dst_ref=got_ref.at[slot, pl.ds(pl.multiple_of(t * tb, tb), tb), :],
            send_sem=send_i.at[d - 1, t],
            recv_sem=recv_i.at[slot, t],
            device_id={"narrow": peer},
            device_id_type=MESH,
        )

    def give(d, t, mine):
        peer = lax.rem(z + d, shards)
        slot = z if mine else peer
        return pltpu.make_async_remote_copy(
            src_ref=give_ref.at[peer, pl.ds(pl.multiple_of(t * tb, tb), tb), :],
            dst_ref=back_ref.at[pl.ds(pl.multiple_of(slot * own + t * tb, tb), tb), :],
            send_sem=send_b.at[d - 1, t],
            recv_sem=recv_b.at[slot, t],
            device_id={"narrow": peer},
            device_id_type=MESH,
        )

    def hop_copy(c, t, step):
        at = pl.ds(pl.multiple_of(t * tb, tb), tb)
        return pltpu.make_async_remote_copy(
            src_ref=outa_ref.at[c, at, :],
            dst_ref=outa_ref.at[c, at, :],
            send_sem=send_a.at[step, c, t],
            recv_sem=recv_a.at[c, t],
            device_id={"narrow": lax.rem(z + (1 if step == 0 else shards - 1), shards)},
            device_id_type=MESH,
        )

    room = (z < shards - 1, z > 0)
    for t in range(parts):
        for d in range(1, shards):
            bring(d, t, True).start()
    mine = pl.ds(pl.multiple_of(z * own, own), own)
    copies = [
        pltpu.make_async_copy(att_ref.at[mine, :], got_ref.at[z], local_sem.at[0]),
        pltpu.make_async_copy(tok_ref.at[mine, :], tokens_ref, local_sem.at[1]),
        pltpu.make_async_copy(cot_ref.at[mine, :], cots_ref, local_sem.at[2]),
    ]
    fetch = pltpu.make_async_copy(wire_ref, hold_ref, local_sem.at[3])
    fetch.start()
    for copy in copies:
        copy.start()
    fetch.wait()

    base = 0
    for ref, acc, rows, cols in kinds:
        grid_cols = cols // HD

        def fill(r, _, ref=ref, base=base, grid_cols=grid_cols):
            low = pl.multiple_of(r * HD, HD)
            for n in range(shards):
                for c in range(grid_cols):
                    unit = unit_ref[base + r * grid_cols + c] + n * (rows_dev // 16)
                    t = jnp.concatenate([hold_ref[unit], hold_ref[unit + 1]], axis=0)
                    for part in range(2):
                        ref[n, pl.ds(low + part * half, half), c * HD : (c + 1) * HD] = t[:, part * HD : (part + 1) * HD]
            return 0

        lax.fori_loop(0, rows // HD, fill, 0)
        base += rows // HD * grid_cols
        if acc is not None:
            acc[...] = jnp.zeros_like(acc)
    gg_ref[...] = jnp.zeros_like(gg_ref)
    stores = [
        pltpu.make_async_copy(mixv_ref, mix_ref, local_sem.at[4]),
        pltpu.make_async_copy(resv_ref, res_ref, local_sem.at[5]),
        pltpu.make_async_copy(gradv_ref, grads_ref, local_sem.at[6]),
    ]
    stores[0].start()
    for copy in copies:
        copy.wait()

    def block(t, _):
        at = pl.ds(pl.multiple_of(t * tb, tb), tb)
        for d in range(1, shards):
            bring(d, t, False).wait_recv()
        tokens = tokens_ref[at, :].astype(F32)
        cot = cots_ref[at, :]
        branch = nn(got_ref[0, at, :], wo_ref[0])
        for n in range(1, shards):
            branch += nn(got_ref[n, at, :], wo_ref[n])
        residual = tokens + branch
        xhat, scale = normalize(residual)
        gain = gain_ref[...]
        normed = (xhat * gain).astype(BF)
        ups = [nn(normed, wu_ref[n]) for n in range(shards)]
        downs = [nt(cot, wd_ref[n]) for n in range(shards)]
        actives, back_ups = [], []
        for n in range(shards):
            value, slope = gelu_pair(ups[n])
            actives.append(value.astype(BF))
            back_ups.append((slope * downs[n]).astype(BF))
        mlp = nn(actives[0], wd_ref[0])
        back = nt(back_ups[0], wu_ref[0])
        for n in range(1, shards):
            mlp += nn(actives[n], wd_ref[n])
            back += nt(back_ups[n], wu_ref[n])
        out = (residual + mlp).astype(BF)

        @pl.when(t < inside)
        def _():
            outa_ref[z, at, :] = out
            for step in range(2):

                @pl.when(room[step])
                def _(step=step):
                    hop_copy(z, t, step).start()

        @pl.when(t >= inside)
        def _():
            outb_ref[pl.ds(pl.multiple_of((t - inside) * tb, tb), tb), :] = out

        gg_ref[...] += jnp.sum(back * xhat, axis=0, keepdims=True)
        back_res = cot.astype(F32) + norm_back(back * gain, xhat, scale)
        resv_ref[at, :] = back_res
        branch_low = back_res.astype(BF)
        line = pad_ref[:, pl.ds(pl.multiple_of(z * own + t * tb, LANES), tb)]
        pad = jnp.broadcast_to(line.astype(F32), (8, tb)).T[:, :1]
        for n in range(shards):
            give_ref[n, at, :] = (nt(branch_low, wo_ref[n]) * pad).astype(BF)
        for d in range(1, shards):
            give(d, t, True).start()
        for n in range(shards):
            gd_ref[n] += tn(actives[n], cot)
            gu_ref[n] += tn(normed, back_ups[n])
            go_ref[n] += tn(got_ref[n, at, :], branch_low)
        return 0

    lax.fori_loop(0, parts, block, 0)
    stores[1].start()
    back_ref[mine, :] = give_ref[z]
    base = 0
    for ref, acc, rows, cols in kinds:
        grid_cols = cols // HD
        if acc is not None:

            def cut(r, _, acc=acc, base=base, grid_cols=grid_cols):
                low = pl.multiple_of(r * HD, HD)
                for n in range(shards):
                    for c in range(grid_cols):
                        lanes = slice(c * HD, (c + 1) * HD)
                        value = jnp.concatenate([acc[n, pl.ds(low, half), lanes], acc[n, pl.ds(low + half, half), lanes]], axis=1)
                        blk_ref[n * per + base - mix_blocks + r * grid_cols + c] = value.astype(BF)
                return 0

            lax.fori_loop(0, rows // HD, cut, 0)
        base += rows // HD * grid_cols
    for n in range(shards):
        blk_ref[(n + 1) * per - 1] = jnp.zeros((half, LANES), BF)
    slots = gain_row // half
    top = lax.broadcasted_iota(jnp.int32, (16, LANES), 0) == 0

    def place(v, _):
        for n in range(shards):
            for i in range(slots):
                gradv_ref[v * shards + n, i * half : (i + 1) * half, :] = blk_ref[sel_ref[v * slots + i] + n * per]
        return 0

    lax.fori_loop(0, wide, place, 0)
    for v in range(wide):
        piece = v * gains_dev // LANES - width // LANES
        for n in range(shards):
            if piece >= 0:
                value = jnp.where(top, gg_ref[:, piece * LANES : (piece + 1) * LANES], 0.0).astype(BF)
            else:
                value = jnp.zeros((16, LANES), BF)
            gradv_ref[v * shards + n, gain_row:, :] = value
    stores[2].start()

    hops = [(s, t, step) for s in range(1, shards) for t in range(inside) for step in range(2)]
    for s, t, step in hops:
        chunk = z - s if step == 0 else z + s
        there = chunk >= 0 if step == 0 else chunk < shards

        @pl.when(there)
        def _(chunk=chunk, t=t, step=step):
            hop_copy(chunk, t, step).wait_recv()

        @pl.when(there & room[step])
        def _(chunk=chunk, t=t, step=step):
            hop_copy(chunk, t, step).start()

    for t in range(parts):
        for d in range(1, shards):
            give(d, t, False).wait_recv()
    for copy in stores:
        copy.wait()
    for t in range(parts):
        for d in range(1, shards):
            bring(d, t, True).wait_send()
            give(d, t, True).wait_send()
    for t in range(inside):
        for step in range(2):

            @pl.when(room[step])
            def _(t=t, step=step):
                hop_copy(z, t, step).wait_send()

    for s, t, step in hops:
        chunk = z - s if step == 0 else z + s
        there = chunk >= 0 if step == 0 else chunk < shards

        @pl.when(there & room[step])
        def _(chunk=chunk, t=t, step=step):
            hop_copy(chunk, t, step).wait_send()


def middle(unit, sel, wire, gain_two, pad, att, tokens, cotangent, shards, wide, rows_dev, gain_row, gains_dev):
    rows, span = att.shape
    width = tokens.shape[1]
    units = FF // shards
    own = rows // shards
    tb = min(256, own)
    parts = own // tb
    inside = max(1, parts // 4)
    blocks = unit.shape[0] - width // HD * (3 * span // HD)
    vmem = pl.BlockSpec(memory_space=pltpu.VMEM)
    smem = pl.BlockSpec(memory_space=pltpu.SMEM)
    hbm = pl.BlockSpec(memory_space=pl.ANY)
    dma = pltpu.SemaphoreType.DMA
    return pl.pallas_call(
        functools.partial(middle_kernel, shards, span, units, wide, gain_row, gains_dev, inside),
        in_specs=[smem, smem, vmem, vmem, hbm, hbm, hbm, hbm],
        out_specs=[vmem] * 3 + [hbm] * 3,
        out_shape=[
            jax.ShapeDtypeStruct((shards, inside * tb, width), BF),
            jax.ShapeDtypeStruct((own - inside * tb, width), BF),
            jax.ShapeDtypeStruct((rows, span), BF),
            jax.ShapeDtypeStruct((own, width), F32),
            jax.ShapeDtypeStruct((wide * shards, rows_dev, LANES), BF),
            jax.ShapeDtypeStruct((shards, width, 3 * span), BF),
        ],
        scratch_shapes=[
            pltpu.VMEM((own, width), BF),
            pltpu.VMEM((own, width), BF),
            pltpu.VMEM((shards, own, span), BF),
            pltpu.VMEM((shards, own, span), BF),
            pltpu.VMEM((shards, span, width), BF),
            pltpu.VMEM((shards, width, units), BF),
            pltpu.VMEM((shards, units, width), BF),
            pltpu.VMEM((shards, span, width), F32),
            pltpu.VMEM((shards, width, units), F32),
            pltpu.VMEM((shards, units, width), F32),
            pltpu.VMEM((1, width), F32),
            pltpu.VMEM((shards * (blocks + 1), HD // 2, LANES), BF),
            pltpu.VMEM(wire.shape, BF),
            pltpu.VMEM((own, width), F32),
            pltpu.VMEM((shards, width, 3 * span), BF),
            pltpu.VMEM((wide * shards, rows_dev, LANES), BF),
            dma((7,)),
            dma((shards - 1, parts)),
            dma((shards, parts)),
            dma((shards - 1, parts)),
            dma((shards, parts)),
            dma((2, shards, inside)),
            dma((shards, inside)),
        ],
        compiler_params=pltpu.CompilerParams(vmem_limit_bytes=63 << 20, collective_id=2, has_side_effects=True),
        name="middle",
    )(unit, sel, gain_two, pad, wire, att, tokens, cotangent)


PARTS = 4


def finish_kernel(shards, wide, gain_row, gains_dev, group, sel_ref, mix_ref, gain_ref, fullh_ref, resh_ref, bm_ref, norm_ref, tok_ref, *refs):
    given, taken = refs[1:7], refs[9:15]
    states, outs, (full_ref, res_ref) = refs[15:21], refs[21:27], refs[27:29]
    first_ref, grad_ref, line_ref = refs[0], refs[7], refs[8]
    (own_ref, normed_ref, tokens_ref, got_ref, acc_ref, blk_ref, grads_ref, sums_ref, firsts_ref, part_ref, aug_ref,
     local_sem, send_z, recv_z, send_w, recv_w, send_a, recv_a, send_g, recv_g, send_f, recv_f) = refs[29:]
    width = norm_ref.shape[1]
    rows, cols = bm_ref.shape
    own = rows // shards
    hold = own // PARTS
    half = HD // 2
    grid_cols = cols // HD
    blocks = width // HD * grid_cols
    slots = gain_row // half
    z = lax.axis_index("narrow")
    w = lax.axis_index("wide")

    barrier = pltpu.get_barrier_semaphore()
    for d in range(1, shards):
        pl.semaphore_signal(barrier, inc=1, device_id={"narrow": lax.rem(z + d, shards)}, device_id_type=MESH)
    for d in range(1, wide):
        pl.semaphore_signal(barrier, inc=1, device_id={"wide": lax.rem(w + d, wide)}, device_id_type=MESH)
    pl.semaphore_wait(barrier, shards + wide - 2)

    def to_peer(d, part, mine):
        peer = lax.rem(z + d, shards)
        slot = z if mine else peer
        at = pl.multiple_of(peer * own + part * hold, hold)
        return pltpu.make_async_remote_copy(
            src_ref=bm_ref.at[pl.ds(at, hold), :],
            dst_ref=got_ref.at[slot, pl.ds(part * hold, hold), :],
            send_sem=send_z.at[d - 1, part],
            recv_sem=recv_z.at[slot, part],
            device_id={"narrow": peer},
            device_id_type=MESH,
        )

    def to_owner(d, mine):
        peer = lax.rem(w + d, wide)
        slot = w if mine else peer
        return pltpu.make_async_remote_copy(
            src_ref=grads_ref.at[peer],
            dst_ref=sums_ref.at[slot],
            send_sem=send_w.at[d - 1],
            recv_sem=recv_w.at[slot],
            device_id={"wide": peer},
            device_id_type=MESH,
        )

    def hop_copy(c, part, step):
        at = pl.ds(pl.multiple_of(c * own + part * hold, hold), hold)
        return pltpu.make_async_remote_copy(
            src_ref=grad_ref.at[at, :],
            dst_ref=grad_ref.at[at, :],
            send_sem=send_a.at[step, c, part],
            recv_sem=recv_a.at[c, part],
            device_id={"narrow": lax.rem(z + (1 if step == 0 else shards - 1), shards)},
            device_id_type=MESH,
        )

    def pass_on(c, part, act):
        for step, there in ((0, z < shards - 1), (1, z > 0)):
            if c is None or step == c[0]:
                chunk = z if c is None else c[1]
                ok = there if c is None else there & c[2]

                @pl.when(ok)
                def _(chunk=chunk, step=step):
                    act(hop_copy(chunk, part, step))

    def line_to(d, mine):
        peer = lax.rem(z + d, shards)
        slot = z if mine else peer
        return pltpu.make_async_remote_copy(
            src_ref=line_ref.at[z],
            dst_ref=line_ref.at[slot],
            send_sem=send_g.at[d - 1],
            recv_sem=recv_g.at[slot],
            device_id={"narrow": peer},
            device_id_type=MESH,
        )

    rows_dev = part_ref.shape[0]

    def first_to(d, mine):
        peer = lax.rem(z + d, shards)
        slot = z if mine else peer
        return pltpu.make_async_remote_copy(
            src_ref=first_ref.at[pl.ds(pl.multiple_of(peer * rows_dev, 16), rows_dev), :],
            dst_ref=firsts_ref.at[slot],
            send_sem=send_f.at[d - 1],
            recv_sem=recv_f.at[slot],
            device_id={"narrow": peer},
            device_id_type=MESH,
        )

    for d in range(1, shards):
        first_to(d, True).start()
    for part in range(PARTS):
        for d in range(1, shards):
            to_peer(d, part, True).start()
    mine = pl.ds(pl.multiple_of(z * own, own), own)
    copies = [
        pltpu.make_async_copy(bm_ref, own_ref, local_sem.at[0]),
        pltpu.make_async_copy(norm_ref, normed_ref, local_sem.at[1]),
        pltpu.make_async_copy(tok_ref.at[mine, :], tokens_ref, local_sem.at[2]),
        pltpu.make_async_copy(bm_ref.at[mine, :], got_ref.at[z], local_sem.at[3]),
        pltpu.make_async_copy(
            first_ref.at[pl.ds(pl.multiple_of(z * rows_dev, 16), rows_dev), :], firsts_ref.at[z], local_sem.at[4]
        ),
    ]
    late = [
        pltpu.make_async_copy(a, b, local_sem.at[5 + k])
        for k, (a, b) in enumerate(zip((fullh_ref, resh_ref, *given), (full_ref, res_ref, *states)))
    ]
    for copy in copies + late:
        copy.start()
    for copy in copies:
        copy.wait()

    acc_ref[...] = jnp.zeros_like(acc_ref)
    tb = min(512, rows)

    def add(i, _):
        at = pl.ds(pl.multiple_of(i * tb, tb), tb)
        acc_ref[...] += tn(normed_ref[at, :], own_ref[at, :])
        return 0

    lax.fori_loop(0, rows // tb, add, 0)
    blk_ref[blocks] = jnp.zeros((half, LANES), BF)

    def cut(r, _):
        low = pl.multiple_of(r * HD, HD)
        for c in range(grid_cols):
            lanes = slice(c * HD, (c + 1) * HD)
            value = jnp.concatenate([acc_ref[pl.ds(low, half), lanes], acc_ref[pl.ds(low + half, half), lanes]], axis=1)
            blk_ref[r * grid_cols + c] = value.astype(BF)
        return 0

    lax.fori_loop(0, width // HD, cut, 0)
    along = jnp.sum(acc_ref[...] * mix_ref[...].astype(F32), axis=1, keepdims=True)
    line = jnp.broadcast_to(along, (width, LANES)).T[:16] / gain_ref[...]
    top = lax.broadcasted_iota(jnp.int32, (16, LANES), 0) == 0
    for v in range(wide):

        def place(i, _, v=v):
            grads_ref[v, pl.ds(pl.multiple_of(i * half, half), half), :] = blk_ref[sel_ref[v * slots + i]]
            return 0

        lax.fori_loop(0, slots, place, 0)
        piece = v * gains_dev // LANES
        if piece < width // LANES:
            value = jnp.where(top, line[:, piece * LANES : (piece + 1) * LANES], 0.0).astype(BF)
        else:
            value = jnp.zeros((16, LANES), BF)
        grads_ref[v, gain_row : gain_row + 16, :] = value
    for d in range(1, wide):
        to_owner(d, True).start()
    part_ref[...] = grads_ref[w].astype(F32)

    tile = min(256, hold)

    def norm_rows(i, _):
        at = pl.ds(pl.multiple_of(i * tile, tile), tile)
        back = nt(got_ref[0, at, :], full_ref[0])
        for n in range(1, shards):
            back += nt(got_ref[n, at, :], full_ref[n])
        xhat, scale = normalize(tokens_ref[at, :].astype(F32))
        grad = res_ref[at, :] + norm_back(back * gain_ref[...], xhat, scale)
        grad_ref[pl.ds(pl.multiple_of(z * own + i * tile, tile), tile), :] = grad.astype(BF)
        return 0

    def norm_part(part):
        for d in range(1, shards):
            to_peer(d, part, False).wait_recv()
        lax.fori_loop(part * hold // tile, (part + 1) * hold // tile, norm_rows, 0)
        pass_on(None, part, lambda copy: copy.start())

    for d in range(1, wide):
        to_owner(d, False).wait_recv()
    for d in range(1, wide):
        part_ref[...] += sums_ref[lax.rem(w + d, wide)].astype(F32)
    line_ref[z] = part_ref[gain_row : gain_row + 16, :]
    for d in range(1, shards):
        line_to(d, True).start()
    for d in range(1, shards):
        first_to(d, False).wait_recv()
    total = firsts_ref[0].astype(F32)
    for n in range(1, shards):
        total += firsts_ref[n].astype(F32)
    line_ref[shards] = total[gain_row : gain_row + 16, :]
    part_ref[...] += total
    for copy in late:
        copy.wait()
    stores = [pltpu.make_async_copy(a, b, local_sem.at[13 + k]) for k, (a, b) in enumerate(zip(outs, taken))]
    ready = 0
    rounds = slots // group
    for g in range(rounds):
        soap_group(g * group, group, part_ref, *states, *outs, aug_ref)
        upto = PARTS * (g + 1) // rounds
        while ready < upto:
            norm_part(ready)
            ready += 1
    for copy in stores:
        copy.start()
    hops = [(s, part, step) for s in range(1, shards) for part in range(PARTS) for step in range(2)]
    for s, part, step in hops:
        chunk = z - s if step == 0 else z + s
        there = chunk >= 0 if step == 0 else chunk < shards

        @pl.when(there)
        def _(chunk=chunk, part=part, step=step):
            hop_copy(chunk, part, step).wait_recv()

        pass_on((step, chunk, there), part, lambda copy: copy.start())
    for copy in stores:
        copy.wait()
    for d in range(1, shards):
        line_to(d, False).wait_recv()
    for part in range(PARTS):
        pass_on(None, part, lambda copy: copy.wait_send())
    for s, part, step in hops:
        chunk = z - s if step == 0 else z + s
        there = chunk >= 0 if step == 0 else chunk < shards
        pass_on((step, chunk, there), part, lambda copy: copy.wait_send())
    for d in range(1, shards):
        line_to(d, True).wait_send()
        first_to(d, True).wait_send()
    for part in range(PARTS):
        for d in range(1, shards):
            to_peer(d, part, True).wait_send()
    for d in range(1, wide):
        to_owner(d, True).wait_send()


def finish(sel, mix, mix_full, gain_one, res, bm, normed, tokens, states, group, wide, rows_dev, gain_row, gains_dev):
    shards = mix_full.shape[0]
    rows, cols = bm.shape
    width = normed.shape[1]
    own = rows // shards
    half = HD // 2
    blocks = width // HD * (cols // HD)
    vmem = pl.BlockSpec(memory_space=pltpu.VMEM)
    smem = pl.BlockSpec(memory_space=pltpu.SMEM)
    hbm = pl.BlockSpec(memory_space=pl.ANY)
    dma = pltpu.SemaphoreType.DMA
    return pl.pallas_call(
        functools.partial(finish_kernel, shards, wide, gain_row, gains_dev, group),
        in_specs=[smem, vmem, vmem, hbm, hbm, hbm, hbm, hbm, hbm] + [hbm] * 6,
        out_specs=[vmem] * 2 + [hbm] * 6,
        out_shape=[jax.ShapeDtypeStruct((rows, width), BF), jax.ShapeDtypeStruct((shards + 1, 16, LANES), F32)]
        + [jax.ShapeDtypeStruct(a.shape, a.dtype) for a in states[1:]],
        scratch_shapes=[pltpu.VMEM(a.shape, a.dtype) for a in states[1:]] * 2
        + [
            pltpu.VMEM(mix_full.shape, BF),
            pltpu.VMEM(res.shape, F32),
            pltpu.VMEM((rows, cols), BF),
            pltpu.VMEM((rows, width), BF),
            pltpu.VMEM((own, width), BF),
            pltpu.VMEM((shards, own, cols), BF),
            pltpu.VMEM((width, cols), F32),
            pltpu.VMEM((blocks + 1, half, LANES), BF),
            pltpu.VMEM((wide, rows_dev, LANES), BF),
            pltpu.VMEM((wide, rows_dev, LANES), BF),
            pltpu.VMEM((shards, rows_dev, LANES), BF),
            pltpu.VMEM((rows_dev, LANES), F32),
            pltpu.VMEM((2 * group, HD, LANES), F32),
            dma((19,)),
            dma((shards - 1, PARTS)),
            dma((shards, PARTS)),
            dma((wide - 1,)),
            dma((wide,)),
            dma((2, shards, PARTS)),
            dma((shards, PARTS)),
            dma((shards - 1,)),
            dma((shards,)),
            dma((shards - 1,)),
            dma((shards,)),
        ],
        compiler_params=pltpu.CompilerParams(vmem_limit_bytes=62 << 20, collective_id=1, has_side_effects=True),
        name="finish",
    )(sel, mix, gain_one, mix_full, res, bm, normed, tokens, *states)


def wrap_kernel(count, per, grad_ref, outa_ref, outb_ref, *refs):
    olds, wide_ref, out_ref, news = refs[:count], refs[count], refs[count + 1], refs[count + 2 :]
    for old, new in zip(olds, news):
        new[...] = old[...]
    wide_ref[...] = grad_ref[...].astype(F32)
    place = lax.rem(pl.program_id(0), per)

    @pl.when(place == 0)
    def _():
        out_ref[...] = outa_ref[0]

    @pl.when(place > 0)
    def _():
        out_ref[...] = outb_ref[0]


def wrap(grad, out_a, out_b, olds):
    rows, width = grad.shape
    tb = out_a.shape[1]
    per = 1 + out_b.shape[1] // tb
    steps = rows // tb
    slots = olds[0].shape[1]
    group = next(g for g in range(1, slots + 1) if slots % g == 0 and slots // g <= steps)
    last = slots // group - 1
    blk = pl.BlockSpec((tb, width), lambda i: (i, 0))
    part_a = pl.BlockSpec((1, tb, width), lambda i: (i // per, 0, 0))
    part_b = pl.BlockSpec((1, tb, width), lambda i: (i // per, jnp.maximum(i % per - 1, 0), 0))
    states = [
        pl.BlockSpec((1, group, *a.shape[2:]), lambda i, k=a.ndim: (0, jnp.minimum(i, last)) + (0,) * (k - 2)) for a in olds
    ]
    return pl.pallas_call(
        functools.partial(wrap_kernel, len(olds), per),
        grid=(steps,),
        in_specs=[blk, part_a, part_b] + states,
        out_specs=[blk, blk] + states,
        out_shape=[jax.ShapeDtypeStruct((rows, width), F32), jax.ShapeDtypeStruct((rows, width), BF)]
        + [jax.ShapeDtypeStruct(a.shape, a.dtype) for a in olds],
        compiler_params=pltpu.CompilerParams(vmem_limit_bytes=60 << 20),
        name="wrap",
    )(grad, out_a, out_b, *olds)


def adam_gains(grad, gain, first, second, average):
    new_first = beta_one * first + (1.0 - beta_one) * grad
    new_second = beta_two * second + (1.0 - beta_two) * grad * grad
    new_gain = gain - gain_rate * new_first / (jnp.sqrt(new_second) + step_eps)
    new_average = average_keep * average + (1.0 - average_keep) * new_gain
    return (new_gain, new_first, new_second, new_average)


def body(
    tokens,
    cotangent,
    segment_ids,
    pad_mask,
    owner_order,
    weights,
    first_moment,
    second_moment,
    average,
    stats,
    bases,
    gains,
    gain_first,
    gain_second,
    gain_average,
):
    narrow = lax.axis_size("narrow")
    wide = lax.axis_size("wide")
    heads = HEADS // narrow
    rows, width = tokens.shape
    span = heads * HD
    own = rows // narrow
    slots, size = weights.shape[1], weights.shape[2]
    half = size // 2
    block_count = owner_order.shape[0]
    gains_dev = gains.shape[0]
    gain_row = slots * half
    rows_dev = gain_row + 16

    ids = jnp.arange(block_count, dtype=jnp.int32)
    slot_of = jnp.sum(jnp.where(owner_order[None, :] == ids[:, None], ids[None, :], 0), axis=1)
    device, place = slot_of // slots, slot_of % slots
    row_own = device * rows_dev + place * half
    row_full = device * (narrow * rows_dev) + place * half

    seg = segment_ids
    seg_row = segment_ids[0]
    pad = pad_mask
    block = min(512, rows)
    low_seg = seg_row[::block]
    high_seg = seg_row[block - 1 :: block]
    begin = jnp.sum((seg_row[None, :] < low_seg[:, None]).astype(jnp.int32), axis=1) // UNIT
    end = (jnp.sum((seg_row[None, :] <= high_seg[:, None]).astype(jnp.int32), axis=1) + UNIT - 1) // UNIT

    normed, qe, ke, ve, vt, mix, lines, along = project(
        weights, gains[None], row_own // 16, tokens, seg, pad, heads, narrow, wide, gain_row, gains_dev
    )
    wire_full = lax.all_gather(along.reshape(-1, LANES), "wide", axis=0, tiled=True)
    gain_all = lines[:, 0, :gains_dev].astype(F32).reshape(1, 2 * width)
    gain_one, gain_two = gain_all[:, :width], gain_all[:, width:]
    attended, qb = attend(qe, ke, vt, pad, begin, end, block, block)
    unit = row_full // 16
    mix_blocks = width // size * 3 * heads
    sel_rest = jnp.where(owner_order >= mix_blocks, owner_order - mix_blocks, block_count - mix_blocks)
    out_a, out_b, back_att, back_res, grads, mix_full = middle(
        unit, sel_rest, wire_full.reshape(-1, 16, LANES), gain_two, pad, attended, tokens, cotangent,
        narrow, wide, rows_dev, gain_row, gains_dev,
    )
    part_a = lax.psum_scatter(grads.reshape(-1, LANES), "wide", scatter_dimension=0, tiled=True)
    out_b = lax.all_to_all(jnp.broadcast_to(out_b, (narrow, *out_b.shape)), "narrow", 0, 0)
    bm = attend_back(qb, ke, ve, back_att, attended, begin, end, block, block)
    bm, part_a, out_b = lax.optimization_barrier((bm, part_a, out_b))
    sel = jnp.minimum(owner_order, mix_blocks)
    group = next(g for g in range(min(12, slots), 0, -1) if slots % g == 0)
    states = (part_a, weights, first_moment, second_moment, average, stats, bases)
    grad_all, lines, *fresh = finish(
        sel, mix, mix_full, gain_one, back_res, bm, normed, tokens, states, group, wide, rows_dev, gain_row, gains_dev
    )
    input_grad, output, new_weight, new_first, new_second, new_average, new_stats, new_bases = wrap(
        grad_all, out_a, out_b, fresh
    )
    line = jnp.sum(lines[:, 0], axis=0)
    offset = lax.axis_index("wide") * gains_dev % LANES
    own_gain = lax.dynamic_slice_in_dim(line, offset, gains_dev, 0)
    new_gains, gain_moment, gain_square, gain_mean = adam_gains(own_gain, gains, gain_first, gain_second, gain_average)
    return (
        output,
        input_grad,
        new_weight,
        new_first,
        new_second,
        new_average,
        new_stats,
        new_bases,
        new_gains,
        gain_moment,
        gain_square,
        gain_mean,
    )


def solution(mesh):
    block = P("narrow", "wide", None, None)
    pair = P("narrow", "wide", None, None, None)
    rows = P("wide", None)
    line = P("wide")
    return jax.shard_map(
        body,
        mesh=mesh,
        in_specs=(rows, rows, rows, rows, P(), block, block, block, block, pair, pair, line, line, line, line),
        out_specs=(rows, rows, block, block, block, block, pair, pair, line, line, line, line),
        check_vma=False,
    )
```

```python
import functools

import jax
import jax.numpy as jnp
from jax import lax
from jax.experimental import pallas as pl
from jax.experimental.pallas import tpu as pltpu
from jax.sharding import PartitionSpec as P

HEADS = 8
HD = 64
FF = 2048
LANES = 128
SEGS = 4
NEG = -1e30
F32 = jnp.float32
BF = jnp.bfloat16
highest = lax.Precision.HIGHEST

beta_one = 0.9
beta_two = 0.95
step_rate = 0.1
gain_rate = 0.75
weight_decay = 0.01
average_keep = 0.5
norm_eps = 1e-05
step_eps = 1e-08


def nt(a, b):
    return lax.dot_general(a, b, (((1,), (1,)), ((), ())), preferred_element_type=F32)


def nn(a, b):
    return lax.dot_general(a, b, (((1,), (0,)), ((), ())), preferred_element_type=F32)


def tn(a, b):
    return lax.dot_general(a, b, (((0,), (0,)), ((), ())), preferred_element_type=F32)


def split3(x):
    hi = x.astype(BF)
    r = x - hi.astype(F32)
    mid = r.astype(BF)
    lo = (r - mid.astype(F32)).astype(BF)
    return hi, mid, lo


def put3(base, x, lane0):
    lane = lax.broadcasted_iota(jnp.int32, base.shape, 1)
    hi, mid, lo = split3(x)
    out = jnp.where(lane == lane0, hi.astype(F32), base.astype(F32))
    out = jnp.where(lane == lane0 + 1, mid.astype(F32), out)
    out = jnp.where(lane == lane0 + 2, lo.astype(F32), out)
    return out.astype(BF)


VT = 80
UNIT = 256


def in_steps(begin, end, block, step):
    per = block // UNIT
    count = end - begin
    whole = count // per

    def long(i, _):
        step((begin + i * per) * UNIT, block)
        return 0

    def short(i, _):
        step((begin + whole * per + i) * UNIT, UNIT)
        return 0

    lax.fori_loop(0, whole, long, 0)
    lax.fori_loop(0, count - whole * per, short, 0)


QC, AHEAD, QB, BAHEAD = 512, 1, 256, 1


def fwd_kernel(heads, bq, bk, lo_ref, hi_ref, qe_ref, ke_ref, vt_ref, pad_ref, att_ref, qb_ref, m_ref, acc_ref):
    i = pl.program_id(0)
    row0 = pl.multiple_of(i * bq, bq)
    real = pad_ref[...] > 0
    for h in range(heads):
        qt = qe_ref[h].astype(F32).T[:HD]
        kt = ke_ref[h, pl.ds(row0, bq), :].astype(F32).T[:HD]
        own = jnp.sum(qt * kt, axis=0, keepdims=True)
        m_ref[h] = jnp.where(real, NEG, own)
        acc_ref[h] = jnp.where(real, 0.0, vt_ref[h, :, pl.ds(row0, bq)].astype(F32))

    def step(at, bk):
        col0 = pl.multiple_of(at, UNIT)
        work = [(h, slice(c, c + QC)) for c in range(0, bq, QC) for h in range(heads)]
        score = lambda h, c: nt(ke_ref[h, pl.ds(col0, bk), :], qe_ref[h, c, :])
        ss = [score(*w) for w in work[:AHEAD]]
        for n, (h, c) in enumerate(work):
            if n + AHEAD < len(work):
                ss.append(score(*work[n + AHEAD]))
            s = ss[n]
            m_old = m_ref[h, :, c]
            m_new = jnp.maximum(m_old, jnp.max(s, axis=0, keepdims=True))
            p = jnp.exp(s - m_new).astype(BF)
            alpha = jnp.exp(m_old - m_new)
            acc_ref[h, :, c] = acc_ref[h, :, c] * alpha + nn(vt_ref[h, :, pl.ds(col0, bk)], p)
            m_ref[h, :, c] = m_new

    in_steps(lo_ref[i], hi_ref[i], bk, step)
    outs = []
    for h in range(heads):
        acc = acc_ref[h]
        total = acc[HD : HD + 1]
        outs.append(jnp.where(real, acc[:HD] / total, 0.0))
        lse = jnp.broadcast_to(m_ref[h] + jnp.log(total), (8, bq)).T[:, :1]
        qb_ref[h] = put3(qe_ref[h], -lse, HD + 4)
    att_ref[...] = (jnp.concatenate(outs, axis=0) if heads > 1 else outs[0]).T.astype(BF)


def attend(qe, ke, vt, padw, lo, hi, bq, bk):
    heads, rows, _ = qe.shape
    full = lambda i, lo, hi: (0, 0, 0)
    return pl.pallas_call(
        functools.partial(fwd_kernel, heads, bq, bk),
        grid_spec=pltpu.PrefetchScalarGridSpec(
            num_scalar_prefetch=2,
            grid=(rows // bq,),
            in_specs=[
                pl.BlockSpec((heads, bq, LANES), lambda i, lo, hi: (0, i, 0)),
                pl.BlockSpec((heads, rows, LANES), full),
                pl.BlockSpec((heads, VT, rows), full),
                pl.BlockSpec((1, bq), lambda i, lo, hi: (0, i)),
            ],
            out_specs=[
                pl.BlockSpec((bq, heads * HD), lambda i, lo, hi: (i, 0)),
                pl.BlockSpec((heads, bq, LANES), lambda i, lo, hi: (0, i, 0)),
            ],
            scratch_shapes=[
                pltpu.VMEM((heads, 1, bq), F32),
                pltpu.VMEM((heads, VT, bq), F32),
            ],
        ),
        out_shape=[
            jax.ShapeDtypeStruct((rows, heads * HD), BF),
            jax.ShapeDtypeStruct((heads, rows, LANES), BF),
        ],
        compiler_params=pltpu.CompilerParams(vmem_limit_bytes=60 << 20),
        name="attend",
    )(lo, hi, qe, ke, vt, padw)


def bwd_kernel(heads, bq, bk, lo_ref, hi_ref, qb_ref, ke_ref, ve_ref, go_ref, att_ref, out_ref, ge_ref, dqt_ref, kt_ref, qt_ref, got_ref, dkt_ref, dvt_ref):
    j = pl.program_id(0)
    rows = qb_ref.shape[1]

    @pl.when(j == 0)
    def _():
        for h in range(heads):
            dqt_ref[h] = jnp.zeros_like(dqt_ref[h])
            for c in range(rows // 512):
                sl = pl.ds(c * 512, 512)
                go = go_ref[sl, h * HD : (h + 1) * HD]
                at = att_ref[sl, h * HD : (h + 1) * HD]
                delta = jnp.sum(go.astype(F32) * at.astype(F32), axis=1, keepdims=True)
                wide = jnp.concatenate([go, jnp.zeros_like(go)], axis=1)
                ge_ref[h, sl, :] = put3(wide, -delta, HD)
                got_ref[h, :, c * 512 : (c + 1) * 512] = wide.T[:HD]
                qt_ref[h, :, c * 512 : (c + 1) * 512] = qb_ref[h, sl, :].T[:HD]

    for h in range(heads):
        kt_ref[h] = ke_ref[h].T[:HD]

    zero = jnp.zeros((HD, bk), F32)

    def step(at, bq):
        row0 = pl.multiple_of(at, UNIT)
        work = [(h, pl.ds(row0 + c, QB)) for c in range(0, bq, QB) for h in range(heads)]
        score = lambda h, c: (nt(ke_ref[h], qb_ref[h, c, :]), nt(ve_ref[h], ge_ref[h, c, :]))
        ss = [score(*w) for w in work[:BAHEAD]]
        for n, (h, c) in enumerate(work):
            if n + BAHEAD < len(work):
                ss.append(score(*work[n + BAHEAD]))
            st, dt = ss[n]
            p = jnp.exp(st)
            ds = (p * dt).astype(BF)
            pb = p.astype(BF)
            dvt_ref[h] += nt(got_ref[h, :, c], pb)
            dkt_ref[h] += nt(qt_ref[h, :, c], ds)
            dqt_ref[h, :, c] += nn(kt_ref[h], ds)

    for h in range(heads):
        dkt_ref[h] = zero
        dvt_ref[h] = zero
    in_steps(lo_ref[j], hi_ref[j], bq, step)
    for h in range(heads):
        for part, ref in ((1, dkt_ref), (2, dvt_ref)):
            at = (part * heads + h) * HD
            out_ref[pl.ds(pl.multiple_of(j * bk, bk), bk), at : at + HD] = ref[h].T.astype(BF)

    @pl.when(j == pl.num_programs(0) - 1)
    def _():
        for h in range(heads):
            for c in range(rows // 512):
                sl = pl.ds(c * 512, 512)
                out_ref[sl, h * HD : (h + 1) * HD] = (dqt_ref[h, :, c * 512 : (c + 1) * 512].T * (HD ** -0.5)).astype(BF)


def attend_back(qb, ke, ve, go, att, lo, hi, bq, bk):
    heads, rows, _ = qb.shape
    full3 = lambda i, lo, hi: (0, 0, 0)
    full2 = lambda i, lo, hi: (0, 0)
    blk3 = lambda i, lo, hi: (0, i, 0)
    wide = heads * HD
    return pl.pallas_call(
        functools.partial(bwd_kernel, heads, bq, bk),
        grid_spec=pltpu.PrefetchScalarGridSpec(
            num_scalar_prefetch=2,
            grid=(rows // bk,),
            in_specs=[
                pl.BlockSpec((heads, rows, LANES), full3),
                pl.BlockSpec((heads, bk, LANES), blk3),
                pl.BlockSpec((heads, bk, LANES), blk3),
                pl.BlockSpec((rows, wide), full2),
                pl.BlockSpec((rows, wide), full2),
            ],
            out_specs=pl.BlockSpec((rows, 3 * wide), full2),
            scratch_shapes=[
                pltpu.VMEM((heads, rows, LANES), BF),
                pltpu.VMEM((heads, HD, rows), F32),
                pltpu.VMEM((heads, HD, bk), BF),
                pltpu.VMEM((heads, HD, rows), BF),
                pltpu.VMEM((heads, HD, rows), BF),
                pltpu.VMEM((heads, HD, bk), F32),
                pltpu.VMEM((heads, HD, bk), F32),
            ],
        ),
        out_shape=jax.ShapeDtypeStruct((rows, 3 * wide), BF),
        compiler_params=pltpu.CompilerParams(vmem_limit_bytes=60 << 20),
        name="attend_back",
    )(lo, hi, qb, ke, ve, go, att)


def dot_f32(a, b, dims):
    return lax.dot_general(a, b, ((dims[:1], dims[1:]), ((), ())), precision=highest, preferred_element_type=F32)


def soap_group(base, group, gr_ref, w_ref, m1_ref, m2_ref, av_ref, st_ref, ba_ref,
               nw_ref, n1_ref, n2_ref, na_ref, ns_ref, nb_ref, aug_ref):
    size = w_ref.shape[-1]
    half = size // 2
    panel = 8
    every = range(group)
    grads, firsts = [], []
    for s in every:
        rows = slice((base + s) * half, (base + s + 1) * half)
        wire = gr_ref[rows, :]
        grads.append(jnp.concatenate([wire[:, :size], wire[:, size:]], axis=0))
        firsts.append(beta_one * m1_ref[0, base + s] + (1.0 - beta_one) * grads[s])
        n1_ref[0, base + s] = firsts[s]
    sides = [(s, side) for s in every for side in range(2)]
    outers = [dot_f32(grads[s], grads[s], (1, 1) if side == 0 else (0, 0)) for s, side in sides]
    both = [dot_f32(jnp.concatenate([grads[s], firsts[s]], axis=0), ba_ref[0, base + s, 1], (1, 0)) for s in every]
    stats = []
    for (s, side), outer in zip(sides, outers):
        stats.append(beta_two * st_ref[0, base + s, side] + (1.0 - beta_two) * outer)
        ns_ref[0, base + s, side] = stats[-1]
    pairs = [dot_f32(ba_ref[0, base + s, 0], jnp.concatenate([both[s][:size], both[s][size:]], axis=1), (0, 0)) for s in every]
    mts = [dot_f32(ba_ref[0, base + s, side], stat, (0, 1)) for (s, side), stat in zip(sides, stats)]
    scaled = []
    for s in every:
        rotated, moment = pairs[s][:, :size], pairs[s][:, size:]
        second = beta_two * m2_ref[0, base + s] + (1.0 - beta_two) * rotated * rotated
        n2_ref[0, base + s] = second
        scaled.append(moment / (jnp.sqrt(second) + step_eps))
    grams = [dot_f32(mt, mt, (1, 1)) for mt in mts]
    inner = [dot_f32(scaled[s], ba_ref[0, base + s, 1], (1, 1)) for s in every]
    for m, (gram, mt) in enumerate(zip(grams, mts)):
        aug_ref[m] = jnp.concatenate([gram, mt], axis=1)
    directions = [dot_f32(ba_ref[0, base + s, 0], inner[s], (1, 0)) for s in every]
    for s in every:
        weight = w_ref[0, base + s]
        fresh = weight - step_rate * (directions[s] + weight_decay * weight)
        nw_ref[0, base + s] = fresh
        na_ref[0, base + s] = average_keep * av_ref[0, base + s] + (1.0 - average_keep) * fresh
    count = 2 * group
    row = lax.broadcasted_iota(jnp.int32, (count, panel, LANES), 1)
    for p in range(size // panel):
        top = p * panel
        part = aug_ref[:, top : top + panel, :]
        for r in range(panel):
            pivot = lax.rsqrt(part[:, r : r + 1, top + r : top + r + 1])
            lead = part[:, r : r + 1, :] * pivot
            column = jnp.where(row > r, part[:, :, top + r : top + r + 1] * pivot, 0.0)
            part = jnp.where(row == r, lead, part - column * lead)
        aug_ref[:, top : top + panel, :] = part
        below = top + panel
        if below < size:
            high = part.astype(BF).astype(F32)
            rest = part - high
            mid = rest.astype(BF).astype(F32)
            low = rest - mid
            first = jnp.concatenate([high, high, mid, high, mid, low], axis=1).astype(BF)
            other = jnp.concatenate([high, mid, high, low, mid, high], axis=1).astype(BF)
            for m in range(count):
                aug_ref[m, below:, :] -= lax.dot_general(
                    first[m][:, below:size], other[m], (((0,), (0,)), ((), ())), preferred_element_type=F32
                )
    for s in range(group):
        for side in range(2):
            nb_ref[0, base + s, side] = aug_ref[2 * s + side][:, size:].T


MESH = pl.DeviceIdType.MESH


def normalize(values):
    center = jnp.mean(values, axis=-1, keepdims=True)
    centered = values - center
    variance = jnp.mean(centered * centered, axis=-1, keepdims=True)
    scale = lax.rsqrt(variance + norm_eps)
    return centered * scale, scale


def norm_back(grad, xhat, scale):
    along = jnp.mean(grad * xhat, axis=-1, keepdims=True)
    return (grad - jnp.mean(grad, axis=-1, keepdims=True) - xhat * along) * scale


TAIL = 0.305
TAIL_FIT = (
    0.1216397411342051,
    0.12246669816059132,
    0.10342157025713879,
    0.1210193967312446,
    -0.037972477455618554,
    0.18571204369074895,
    -0.15298537812807472,
    0.036698452375741396,
)


def gelu_pair(u):
    size = jnp.abs(u)
    bell = jnp.exp(-0.5 * u * u)
    t = 1.0 / (1.0 + TAIL * size)
    poly = jnp.full_like(t, TAIL_FIT[-1])
    for c in TAIL_FIT[-2::-1]:
        poly = poly * t + c
    upper = poly * t * bell
    cdf = jnp.where(u > 0.0, 1.0 - upper, upper)
    return u * cdf, cdf + (0.3989422804014327 * u) * bell


def project_kernel(heads, shards, wide, gain_row, gains_dev, unit_ref, weight_ref, gains_ref, tok_ref, seg_ref, pad_ref,
                   norm_ref, qe_ref, ke_ref, ve_ref, vt_ref, mix_ref, line_ref, along_ref,
                   wide_ref, wire_ref, all_ref, near_ref, gain_ref, send_w, recv_w, send_z, recv_z):
    width = tok_ref.shape[1]
    half = HD // 2
    cols = 3 * heads
    units = wire_ref.shape[0]

    @pl.when(pl.program_id(0) == 0)
    def _():
        z = lax.axis_index("narrow")
        w = lax.axis_index("wide")
        twin = w + 1 - 2 * lax.rem(w, 2)
        chips = wide // 2
        barrier = pltpu.get_barrier_semaphore()
        pl.semaphore_signal(barrier, inc=1, device_id={"wide": twin}, device_id_type=MESH)
        for d in range(1, chips):
            pl.semaphore_signal(barrier, inc=1, device_id={"wide": lax.rem(w + 2 * d, wide)}, device_id_type=MESH)
        for d in range(1, shards):
            pl.semaphore_signal(barrier, inc=1, device_id={"narrow": lax.rem(z + d, shards)}, device_id_type=MESH)
        for s in range(gain_row // half):
            low = weight_ref[0, s].astype(BF)
            t = jnp.concatenate([low[:half], low[half:]], axis=1)
            wire_ref[2 * s] = t[:16]
            wire_ref[2 * s + 1] = t[16:]
        line = gains_ref[...]
        if gains_dev < LANES:
            line = jnp.concatenate([line, jnp.zeros((1, LANES - gains_dev), F32)], axis=1)
        first = lax.broadcasted_iota(jnp.int32, (16, LANES), 0) == 0
        wire_ref[gain_row // 16] = jnp.where(first, line, 0.0).astype(BF)
        pl.semaphore_wait(barrier, chips + shards - 1)

        def slot(s):
            return all_ref.at[pl.ds(s * units, units)]

        def to_chip(d, mine):
            peer = lax.rem(w + 2 * d, wide)
            return pltpu.make_async_remote_copy(
                src_ref=wire_ref,
                dst_ref=slot(w if mine else peer),
                send_sem=send_w.at[d],
                recv_sem=recv_w.at[w if mine else peer],
                device_id={"wide": peer},
                device_id_type=MESH,
            )

        def to_twin(d, mine):
            owner = lax.rem((w if mine else twin) + 2 * d, wide)
            return pltpu.make_async_remote_copy(
                src_ref=wire_ref if d == 0 else slot(owner),
                dst_ref=slot(owner),
                send_sem=send_w.at[chips + d],
                recv_sem=recv_w.at[owner],
                device_id={"wide": twin},
                device_id_type=MESH,
            )

        def to_shard(d, mine):
            peer = lax.rem(z + d, shards)
            return pltpu.make_async_remote_copy(
                src_ref=wire_ref,
                dst_ref=near_ref.at[z if mine else peer],
                send_sem=send_z.at[d - 1],
                recv_sem=recv_z.at[z if mine else peer],
                device_id={"narrow": peer},
                device_id_type=MESH,
            )

        for d in range(1, chips):
            to_chip(d, True).start()
        to_twin(0, True).start()
        for d in range(1, shards):
            to_shard(d, True).start()
        all_ref[pl.ds(w * units, units)] = wire_ref[...]
        near_ref[z] = wire_ref[...]
        for d in range(1, chips):
            to_chip(d, False).wait_recv()
            to_twin(d, True).start()
        for d in range(chips):
            to_twin(d, False).wait_recv()

        for v in range(wide):
            line_ref[v] = all_ref[v * units + gain_row // 16]
        pieces = [line_ref[v].astype(F32)[:1, :gains_dev] for v in range(wide // 2)]
        gain_ref[...] = jnp.concatenate(pieces, axis=1)
        zero = jnp.zeros((half, HD), BF)

        def fill(r, _):
            low = pl.multiple_of(r * HD, HD)
            for c in range(cols):
                unit = unit_ref[r * cols + c]
                t = jnp.concatenate([all_ref[unit], all_ref[unit + 1]], axis=0)
                for part in range(2):
                    piece = t[:, part * HD : (part + 1) * HD]
                    at = pl.ds(low + part * half, half)
                    wide_ref[at, c * LANES : (c + 1) * LANES] = jnp.concatenate([piece, zero], axis=1)
                    mix_ref[at, c * HD : (c + 1) * HD] = piece
            return 0

        lax.fori_loop(0, width // HD, fill, 0)
        for d in range(1, shards):
            to_shard(d, False).wait_recv()
            to_shard(d, True).wait_send()
        along_ref[...] = near_ref[...]
        for d in range(1, chips):
            to_chip(d, True).wait_send()
        for d in range(chips):
            to_twin(d, True).wait_send()

    xhat, _ = normalize(tok_ref[...].astype(F32))
    normed = (xhat * gain_ref[...]).astype(BF)
    norm_ref[...] = normed
    count = tok_ref.shape[0]
    lane = lax.broadcasted_iota(jnp.int32, (LANES, count), 0)
    seg = seg_ref[...]
    same = lane - HD == seg
    in_segs = (lane >= HD) & (lane < HD + SEGS)
    ones = (lane >= HD + SEGS) & (lane < HD + SEGS + 3)
    ext_q = jnp.where(same, 1.0, 0.0).T
    ext_k = jnp.where(in_segs, jnp.where(same & (pad_ref[...] > 0), 0.0, NEG), jnp.where(ones, 1.0, 0.0)).T
    side = lax.broadcasted_iota(jnp.int32, (count, LANES), 1)
    ext_v = jnp.where((side >= HD) & (side < HD + 3), 1.0, 0.0)
    whole = nn(normed, wide_ref[...]).astype(BF)
    for h in range(heads):
        for ref, part, scale, ext in ((qe_ref, 0, HD ** -0.5, ext_q), (ke_ref, 1, 1.0, ext_k), (ve_ref, 2, 1.0, ext_v)):
            c = part * heads + h
            mixed = whole[:, c * LANES : (c + 1) * LANES]
            out = (mixed.astype(F32) * scale + ext).astype(BF)
            ref[h] = out
            if part == 2:
                vt_ref[h] = out.T[:VT]


def project(weights, gains, unit, tokens, seg, pad, heads, shards, wide, gain_row, gains_dev):
    rows, width = tokens.shape
    tb = min(512, rows)
    full = lambda i, r: (0, 0)
    full3 = lambda i, r: (0, 0, 0)
    blk = lambda i, r: (i, 0)
    col = lambda i, r: (0, i)
    ext = lambda i, r: (0, i, 0)
    out = lambda *s: jax.ShapeDtypeStruct(s, BF)
    dma = pltpu.SemaphoreType.DMA
    units = gain_row // 16 + 1
    return pl.pallas_call(
        functools.partial(project_kernel, heads, shards, wide, gain_row, gains_dev),
        grid_spec=pltpu.PrefetchScalarGridSpec(
            num_scalar_prefetch=1,
            grid=(rows // tb,),
            in_specs=[
                pl.BlockSpec(weights.shape, lambda i, r: (0, 0, 0, 0)),
                pl.BlockSpec((1, gains_dev), full),
                pl.BlockSpec((tb, width), blk),
                pl.BlockSpec((1, tb), col),
                pl.BlockSpec((1, tb), col),
            ],
            out_specs=[
                pl.BlockSpec((tb, width), blk),
                pl.BlockSpec((heads, tb, LANES), ext),
                pl.BlockSpec((heads, tb, LANES), ext),
                pl.BlockSpec((heads, tb, LANES), ext),
                pl.BlockSpec((heads, VT, tb), lambda i, r: (0, 0, i)),
                pl.BlockSpec((width, 3 * heads * HD), full),
                pl.BlockSpec((wide, 16, LANES), full3),
                pl.BlockSpec((shards, units, 16, LANES), lambda i, r: (0, 0, 0, 0)),
            ],
            scratch_shapes=[
                pltpu.VMEM((width, 3 * heads * LANES), BF),
                pltpu.VMEM((units, 16, LANES), BF),
                pltpu.VMEM((wide * units, 16, LANES), BF),
                pltpu.VMEM((shards, units, 16, LANES), BF),
                pltpu.VMEM((1, width), F32),
                dma((wide,)),
                dma((wide,)),
                dma((shards - 1,)),
                dma((shards,)),
            ],
        ),
        out_shape=[
            out(rows, width),
            out(heads, rows, LANES),
            out(heads, rows, LANES),
            out(heads, rows, LANES),
            out(heads, VT, rows),
            out(width, 3 * heads * HD),
            out(wide, 16, LANES),
            out(shards, units, 16, LANES),
        ],
        compiler_params=pltpu.CompilerParams(vmem_limit_bytes=60 << 20, collective_id=3, has_side_effects=True),
        name="project",
    )(unit, weights, gains, tokens, seg, pad)


def middle_kernel(shards, span, units, wide, gain_row, gains_dev, inside,
                  unit_ref, sel_ref, gain_ref, pad_ref, wire_ref, att_ref, tok_ref, cot_ref,
                  outa_ref, back_ref, outs_ref, res_ref, grads_ref, mix_ref,
                  tokens_ref, cots_ref, got_ref, give_ref, wo_ref, wu_ref, wd_ref, go_ref, gu_ref, gd_ref, gg_ref, blk_ref,
                  hold_ref, resv_ref, mixv_ref, gradv_ref, outb_ref, local_sem, send_i, recv_i, send_b, recv_b, send_a, recv_a):
    own, width = tokens_ref.shape
    parts = recv_i.shape[1]
    tb = own // parts
    half = HD // 2
    rows_dev = gradv_ref.shape[1]
    z = lax.axis_index("narrow")
    kinds = (
        (mixv_ref, None, width, 3 * span),
        (wo_ref, go_ref, span, width),
        (wu_ref, gu_ref, width, units),
        (wd_ref, gd_ref, units, width),
    )
    mix_blocks = width // HD * (3 * span // HD)
    per = blk_ref.shape[0] // shards

    barrier = pltpu.get_barrier_semaphore()
    for d in range(1, shards):
        pl.semaphore_signal(barrier, inc=1, device_id={"narrow": lax.rem(z + d, shards)}, device_id_type=MESH)
    pl.semaphore_wait(barrier, shards - 1)

    def bring(d, t, mine):
        peer = lax.rem(z + d, shards)
        slot = z if mine else peer
        return pltpu.make_async_remote_copy(
            src_ref=att_ref.at[pl.ds(pl.multiple_of(peer * own + t * tb, tb), tb), :],
            dst_ref=got_ref.at[slot, pl.ds(pl.multiple_of(t * tb, tb), tb), :],
            send_sem=send_i.at[d - 1, t],
            recv_sem=recv_i.at[slot, t],
            device_id={"narrow": peer},
            device_id_type=MESH,
        )

    def give(d, t, mine):
        peer = lax.rem(z + d, shards)
        slot = z if mine else peer
        return pltpu.make_async_remote_copy(
            src_ref=give_ref.at[peer, pl.ds(pl.multiple_of(t * tb, tb), tb), :],
            dst_ref=back_ref.at[pl.ds(pl.multiple_of(slot * own + t * tb, tb), tb), :],
            send_sem=send_b.at[d - 1, t],
            recv_sem=recv_b.at[slot, t],
            device_id={"narrow": peer},
            device_id_type=MESH,
        )

    def hop_copy(c, t, step):
        at = pl.ds(pl.multiple_of(t * tb, tb), tb)
        return pltpu.make_async_remote_copy(
            src_ref=outa_ref.at[c, at, :],
            dst_ref=outa_ref.at[c, at, :],
            send_sem=send_a.at[step, c, t],
            recv_sem=recv_a.at[c, t],
            device_id={"narrow": lax.rem(z + (1 if step == 0 else shards - 1), shards)},
            device_id_type=MESH,
        )

    room = (z < shards - 1, z > 0)
    for t in range(parts):
        for d in range(1, shards):
            bring(d, t, True).start()
    mine = pl.ds(pl.multiple_of(z * own, own), own)
    copies = [
        pltpu.make_async_copy(att_ref.at[mine, :], got_ref.at[z], local_sem.at[0]),
        pltpu.make_async_copy(tok_ref.at[mine, :], tokens_ref, local_sem.at[1]),
        pltpu.make_async_copy(cot_ref.at[mine, :], cots_ref, local_sem.at[2]),
    ]
    fetch = pltpu.make_async_copy(wire_ref, hold_ref, local_sem.at[3])
    fetch.start()
    for copy in copies:
        copy.start()
    fetch.wait()

    base = 0
    for ref, acc, rows, cols in kinds:
        grid_cols = cols // HD

        def fill(r, _, ref=ref, base=base, grid_cols=grid_cols):
            low = pl.multiple_of(r * HD, HD)
            for n in range(shards):
                for c in range(grid_cols):
                    unit = unit_ref[base + r * grid_cols + c] + n * (rows_dev // 16)
                    t = jnp.concatenate([hold_ref[unit], hold_ref[unit + 1]], axis=0)
                    for part in range(2):
                        ref[n, pl.ds(low + part * half, half), c * HD : (c + 1) * HD] = t[:, part * HD : (part + 1) * HD]
            return 0

        lax.fori_loop(0, rows // HD, fill, 0)
        base += rows // HD * grid_cols
        if acc is not None:
            acc[...] = jnp.zeros_like(acc)
    gg_ref[...] = jnp.zeros_like(gg_ref)
    stores = [
        pltpu.make_async_copy(mixv_ref, mix_ref, local_sem.at[4]),
        pltpu.make_async_copy(resv_ref, res_ref, local_sem.at[5]),
        pltpu.make_async_copy(gradv_ref, grads_ref, local_sem.at[6]),
    ]
    stores += [pltpu.make_async_copy(outb_ref, outs_ref.at[n], local_sem.at[7 + n]) for n in range(shards)]
    stores[0].start()
    for copy in copies:
        copy.wait()

    def block(t, _):
        at = pl.ds(pl.multiple_of(t * tb, tb), tb)
        for d in range(1, shards):
            bring(d, t, False).wait_recv()
        tokens = tokens_ref[at, :].astype(F32)
        cot = cots_ref[at, :]
        branch = nn(got_ref[0, at, :], wo_ref[0])
        for n in range(1, shards):
            branch += nn(got_ref[n, at, :], wo_ref[n])
        residual = tokens + branch
        xhat, scale = normalize(residual)
        gain = gain_ref[...]
        normed = (xhat * gain).astype(BF)
        ups = [nn(normed, wu_ref[n]) for n in range(shards)]
        downs = [nt(cot, wd_ref[n]) for n in range(shards)]
        actives, back_ups = [], []
        for n in range(shards):
            value, slope = gelu_pair(ups[n])
            actives.append(value.astype(BF))
            back_ups.append((slope * downs[n]).astype(BF))
        mlp = nn(actives[0], wd_ref[0])
        back = nt(back_ups[0], wu_ref[0])
        for n in range(1, shards):
            mlp += nn(actives[n], wd_ref[n])
            back += nt(back_ups[n], wu_ref[n])
        out = (residual + mlp).astype(BF)

        @pl.when(t < inside)
        def _():
            outa_ref[z, at, :] = out
            for step in range(2):

                @pl.when(room[step])
                def _(step=step):
                    hop_copy(z, t, step).start()

        @pl.when(t >= inside)
        def _():
            outb_ref[pl.ds(pl.multiple_of((t - inside) * tb, tb), tb), :] = out

        gg_ref[...] += jnp.sum(back * xhat, axis=0, keepdims=True)
        back_res = cot.astype(F32) + norm_back(back * gain, xhat, scale)
        resv_ref[at, :] = back_res
        branch_low = back_res.astype(BF)
        line = pad_ref[:, pl.ds(pl.multiple_of(z * own + t * tb, LANES), tb)]
        pad = jnp.broadcast_to(line.astype(F32), (8, tb)).T[:, :1]
        for n in range(shards):
            give_ref[n, at, :] = (nt(branch_low, wo_ref[n]) * pad).astype(BF)
        for d in range(1, shards):
            give(d, t, True).start()
        for n in range(shards):
            gd_ref[n] += tn(actives[n], cot)
            gu_ref[n] += tn(normed, back_ups[n])
            go_ref[n] += tn(got_ref[n, at, :], branch_low)
        return 0

    lax.fori_loop(0, parts, block, 0)
    for copy in stores[1:2] + stores[3:]:
        copy.start()
    back_ref[mine, :] = give_ref[z]
    base = 0
    for ref, acc, rows, cols in kinds:
        grid_cols = cols // HD
        if acc is not None:

            def cut(r, _, acc=acc, base=base, grid_cols=grid_cols):
                low = pl.multiple_of(r * HD, HD)
                for n in range(shards):
                    for c in range(grid_cols):
                        lanes = slice(c * HD, (c + 1) * HD)
                        value = jnp.concatenate([acc[n, pl.ds(low, half), lanes], acc[n, pl.ds(low + half, half), lanes]], axis=1)
                        blk_ref[n * per + base - mix_blocks + r * grid_cols + c] = value.astype(BF)
                return 0

            lax.fori_loop(0, rows // HD, cut, 0)
        base += rows // HD * grid_cols
    for n in range(shards):
        blk_ref[(n + 1) * per - 1] = jnp.zeros((half, LANES), BF)
    slots = gain_row // half
    top = lax.broadcasted_iota(jnp.int32, (16, LANES), 0) == 0

    def place(v, _):
        for n in range(shards):
            for i in range(slots):
                gradv_ref[v * shards + n, i * half : (i + 1) * half, :] = blk_ref[sel_ref[v * slots + i] + n * per]
        return 0

    lax.fori_loop(0, wide, place, 0)
    for v in range(wide):
        piece = v * gains_dev // LANES - width // LANES
        for n in range(shards):
            if piece >= 0:
                value = jnp.where(top, gg_ref[:, piece * LANES : (piece + 1) * LANES], 0.0).astype(BF)
            else:
                value = jnp.zeros((16, LANES), BF)
            gradv_ref[v * shards + n, gain_row:, :] = value
    stores[2].start()

    hops = [(s, t, step) for s in range(1, shards) for t in range(inside) for step in range(2)]
    for s, t, step in hops:
        chunk = z - s if step == 0 else z + s
        there = chunk >= 0 if step == 0 else chunk < shards

        @pl.when(there)
        def _(chunk=chunk, t=t, step=step):
            hop_copy(chunk, t, step).wait_recv()

        @pl.when(there & room[step])
        def _(chunk=chunk, t=t, step=step):
            hop_copy(chunk, t, step).start()

    for t in range(parts):
        for d in range(1, shards):
            give(d, t, False).wait_recv()
    for copy in stores:
        copy.wait()
    for t in range(parts):
        for d in range(1, shards):
            bring(d, t, True).wait_send()
            give(d, t, True).wait_send()
    for t in range(inside):
        for step in range(2):

            @pl.when(room[step])
            def _(t=t, step=step):
                hop_copy(z, t, step).wait_send()

    for s, t, step in hops:
        chunk = z - s if step == 0 else z + s
        there = chunk >= 0 if step == 0 else chunk < shards

        @pl.when(there & room[step])
        def _(chunk=chunk, t=t, step=step):
            hop_copy(chunk, t, step).wait_send()


def middle(unit, sel, wire, gain_two, pad, att, tokens, cotangent, shards, wide, rows_dev, gain_row, gains_dev):
    rows, span = att.shape
    width = tokens.shape[1]
    units = FF // shards
    own = rows // shards
    tb = min(256, own)
    parts = own // tb
    inside = max(1, parts // 4)
    blocks = unit.shape[0] - width // HD * (3 * span // HD)
    vmem = pl.BlockSpec(memory_space=pltpu.VMEM)
    smem = pl.BlockSpec(memory_space=pltpu.SMEM)
    hbm = pl.BlockSpec(memory_space=pl.ANY)
    dma = pltpu.SemaphoreType.DMA
    return pl.pallas_call(
        functools.partial(middle_kernel, shards, span, units, wide, gain_row, gains_dev, inside),
        in_specs=[smem, smem, vmem, vmem, hbm, hbm, hbm, hbm],
        out_specs=[vmem] * 2 + [hbm] * 4,
        out_shape=[
            jax.ShapeDtypeStruct((shards, inside * tb, width), BF),
            jax.ShapeDtypeStruct((rows, span), BF),
            jax.ShapeDtypeStruct((shards, own - inside * tb, width), BF),
            jax.ShapeDtypeStruct((own, width), F32),
            jax.ShapeDtypeStruct((wide * shards, rows_dev, LANES), BF),
            jax.ShapeDtypeStruct((shards, width, 3 * span), BF),
        ],
        scratch_shapes=[
            pltpu.VMEM((own, width), BF),
            pltpu.VMEM((own, width), BF),
            pltpu.VMEM((shards, own, span), BF),
            pltpu.VMEM((shards, own, span), BF),
            pltpu.VMEM((shards, span, width), BF),
            pltpu.VMEM((shards, width, units), BF),
            pltpu.VMEM((shards, units, width), BF),
            pltpu.VMEM((shards, span, width), F32),
            pltpu.VMEM((shards, width, units), F32),
            pltpu.VMEM((shards, units, width), F32),
            pltpu.VMEM((1, width), F32),
            pltpu.VMEM((shards * (blocks + 1), HD // 2, LANES), BF),
            pltpu.VMEM(wire.shape, BF),
            pltpu.VMEM((own, width), F32),
            pltpu.VMEM((shards, width, 3 * span), BF),
            pltpu.VMEM((wide * shards, rows_dev, LANES), BF),
            pltpu.VMEM((own - inside * tb, width), BF),
            dma((7 + shards,)),
            dma((shards - 1, parts)),
            dma((shards, parts)),
            dma((shards - 1, parts)),
            dma((shards, parts)),
            dma((2, shards, inside)),
            dma((shards, inside)),
        ],
        compiler_params=pltpu.CompilerParams(vmem_limit_bytes=63 << 20, collective_id=2, has_side_effects=True),
        name="middle",
    )(unit, sel, gain_two, pad, wire, att, tokens, cotangent)


PARTS = 4


def finish_kernel(shards, wide, gain_row, gains_dev, group, sel_ref, mix_ref, gain_ref, fullh_ref, resh_ref, bm_ref, norm_ref, tok_ref, *refs):
    given, taken = refs[1:7], refs[9:15]
    states, outs, (full_ref, res_ref) = refs[15:21], refs[21:27], refs[27:29]
    first_ref, grad_ref, line_ref = refs[0], refs[7], refs[8]
    (own_ref, normed_ref, tokens_ref, got_ref, acc_ref, blk_ref, grads_ref, sums_ref, firsts_ref, part_ref, aug_ref,
     local_sem, send_z, recv_z, send_w, recv_w, send_a, recv_a, send_g, recv_g, send_f, recv_f) = refs[29:]
    width = norm_ref.shape[1]
    rows, cols = bm_ref.shape
    own = rows // shards
    hold = own // PARTS
    half = HD // 2
    grid_cols = cols // HD
    blocks = width // HD * grid_cols
    slots = gain_row // half
    z = lax.axis_index("narrow")
    w = lax.axis_index("wide")

    barrier = pltpu.get_barrier_semaphore()
    for d in range(1, shards):
        pl.semaphore_signal(barrier, inc=1, device_id={"narrow": lax.rem(z + d, shards)}, device_id_type=MESH)
    for d in range(1, wide):
        pl.semaphore_signal(barrier, inc=1, device_id={"wide": lax.rem(w + d, wide)}, device_id_type=MESH)
    pl.semaphore_wait(barrier, shards + wide - 2)

    def to_peer(d, part, mine):
        peer = lax.rem(z + d, shards)
        slot = z if mine else peer
        at = pl.multiple_of(peer * own + part * hold, hold)
        return pltpu.make_async_remote_copy(
            src_ref=bm_ref.at[pl.ds(at, hold), :],
            dst_ref=got_ref.at[slot, pl.ds(part * hold, hold), :],
            send_sem=send_z.at[d - 1, part],
            recv_sem=recv_z.at[slot, part],
            device_id={"narrow": peer},
            device_id_type=MESH,
        )

    def to_owner(d, mine):
        peer = lax.rem(w + d, wide)
        slot = w if mine else peer
        return pltpu.make_async_remote_copy(
            src_ref=grads_ref.at[peer],
            dst_ref=sums_ref.at[slot],
            send_sem=send_w.at[d - 1],
            recv_sem=recv_w.at[slot],
            device_id={"wide": peer},
            device_id_type=MESH,
        )

    def hop_copy(c, part, step):
        at = pl.ds(pl.multiple_of(c * own + part * hold, hold), hold)
        return pltpu.make_async_remote_copy(
            src_ref=grad_ref.at[at, :],
            dst_ref=grad_ref.at[at, :],
            send_sem=send_a.at[step, c, part],
            recv_sem=recv_a.at[c, part],
            device_id={"narrow": lax.rem(z + (1 if step == 0 else shards - 1), shards)},
            device_id_type=MESH,
        )

    def pass_on(c, part, act):
        for step, there in ((0, z < shards - 1), (1, z > 0)):
            if c is None or step == c[0]:
                chunk = z if c is None else c[1]
                ok = there if c is None else there & c[2]

                @pl.when(ok)
                def _(chunk=chunk, step=step):
                    act(hop_copy(chunk, part, step))

    def line_to(d, mine):
        peer = lax.rem(z + d, shards)
        slot = z if mine else peer
        return pltpu.make_async_remote_copy(
            src_ref=line_ref.at[z],
            dst_ref=line_ref.at[slot],
            send_sem=send_g.at[d - 1],
            recv_sem=recv_g.at[slot],
            device_id={"narrow": peer},
            device_id_type=MESH,
        )

    rows_dev = part_ref.shape[0]

    def first_to(d, mine):
        peer = lax.rem(z + d, shards)
        slot = z if mine else peer
        return pltpu.make_async_remote_copy(
            src_ref=first_ref.at[pl.ds(pl.multiple_of(peer * rows_dev, 16), rows_dev), :],
            dst_ref=firsts_ref.at[slot],
            send_sem=send_f.at[d - 1],
            recv_sem=recv_f.at[slot],
            device_id={"narrow": peer},
            device_id_type=MESH,
        )

    for d in range(1, shards):
        first_to(d, True).start()
    for part in range(PARTS):
        for d in range(1, shards):
            to_peer(d, part, True).start()
    mine = pl.ds(pl.multiple_of(z * own, own), own)
    copies = [
        pltpu.make_async_copy(bm_ref, own_ref, local_sem.at[0]),
        pltpu.make_async_copy(norm_ref, normed_ref, local_sem.at[1]),
        pltpu.make_async_copy(tok_ref.at[mine, :], tokens_ref, local_sem.at[2]),
        pltpu.make_async_copy(bm_ref.at[mine, :], got_ref.at[z], local_sem.at[3]),
        pltpu.make_async_copy(
            first_ref.at[pl.ds(pl.multiple_of(z * rows_dev, 16), rows_dev), :], firsts_ref.at[z], local_sem.at[4]
        ),
    ]
    late = [
        pltpu.make_async_copy(a, b, local_sem.at[5 + k])
        for k, (a, b) in enumerate(zip((fullh_ref, resh_ref, *given), (full_ref, res_ref, *states)))
    ]
    for copy in copies + late:
        copy.start()
    for copy in copies:
        copy.wait()

    acc_ref[...] = jnp.zeros_like(acc_ref)
    tb = min(512, rows)

    def add(i, _):
        at = pl.ds(pl.multiple_of(i * tb, tb), tb)
        acc_ref[...] += tn(normed_ref[at, :], own_ref[at, :])
        return 0

    lax.fori_loop(0, rows // tb, add, 0)
    blk_ref[blocks] = jnp.zeros((half, LANES), BF)

    def cut(r, _):
        low = pl.multiple_of(r * HD, HD)
        for c in range(grid_cols):
            lanes = slice(c * HD, (c + 1) * HD)
            value = jnp.concatenate([acc_ref[pl.ds(low, half), lanes], acc_ref[pl.ds(low + half, half), lanes]], axis=1)
            blk_ref[r * grid_cols + c] = value.astype(BF)
        return 0

    lax.fori_loop(0, width // HD, cut, 0)
    along = jnp.sum(acc_ref[...] * mix_ref[...].astype(F32), axis=1, keepdims=True)
    line = jnp.broadcast_to(along, (width, LANES)).T[:16] / gain_ref[...]
    top = lax.broadcasted_iota(jnp.int32, (16, LANES), 0) == 0
    for v in range(wide):

        def place(i, _, v=v):
            grads_ref[v, pl.ds(pl.multiple_of(i * half, half), half), :] = blk_ref[sel_ref[v * slots + i]]
            return 0

        lax.fori_loop(0, slots, place, 0)
        piece = v * gains_dev // LANES
        if piece < width // LANES:
            value = jnp.where(top, line[:, piece * LANES : (piece + 1) * LANES], 0.0).astype(BF)
        else:
            value = jnp.zeros((16, LANES), BF)
        grads_ref[v, gain_row : gain_row + 16, :] = value
    for d in range(1, wide):
        to_owner(d, True).start()
    part_ref[...] = grads_ref[w].astype(F32)

    tile = min(256, hold)

    def norm_rows(i, _):
        at = pl.ds(pl.multiple_of(i * tile, tile), tile)
        back = nt(got_ref[0, at, :], full_ref[0])
        for n in range(1, shards):
            back += nt(got_ref[n, at, :], full_ref[n])
        xhat, scale = normalize(tokens_ref[at, :].astype(F32))
        grad = res_ref[at, :] + norm_back(back * gain_ref[...], xhat, scale)
        grad_ref[pl.ds(pl.multiple_of(z * own + i * tile, tile), tile), :] = grad.astype(BF)
        return 0

    def norm_part(part):
        for d in range(1, shards):
            to_peer(d, part, False).wait_recv()
        lax.fori_loop(part * hold // tile, (part + 1) * hold // tile, norm_rows, 0)
        pass_on(None, part, lambda copy: copy.start())

    for d in range(1, wide):
        to_owner(d, False).wait_recv()
    for d in range(1, wide):
        part_ref[...] += sums_ref[lax.rem(w + d, wide)].astype(F32)
    line_ref[z] = part_ref[gain_row : gain_row + 16, :]
    for d in range(1, shards):
        line_to(d, True).start()
    for d in range(1, shards):
        first_to(d, False).wait_recv()
    total = firsts_ref[0].astype(F32)
    for n in range(1, shards):
        total += firsts_ref[n].astype(F32)
    line_ref[shards] = total[gain_row : gain_row + 16, :]
    part_ref[...] += total
    for copy in late:
        copy.wait()
    stores = [pltpu.make_async_copy(a, b, local_sem.at[13 + k]) for k, (a, b) in enumerate(zip(outs, taken))]
    ready = 0
    rounds = slots // group
    for g in range(rounds):
        soap_group(g * group, group, part_ref, *states, *outs, aug_ref)
        upto = PARTS * (g + 1) // rounds
        while ready < upto:
            norm_part(ready)
            ready += 1
    for copy in stores:
        copy.start()
    hops = [(s, part, step) for s in range(1, shards) for part in range(PARTS) for step in range(2)]
    for s, part, step in hops:
        chunk = z - s if step == 0 else z + s
        there = chunk >= 0 if step == 0 else chunk < shards

        @pl.when(there)
        def _(chunk=chunk, part=part, step=step):
            hop_copy(chunk, part, step).wait_recv()

        pass_on((step, chunk, there), part, lambda copy: copy.start())
    for copy in stores:
        copy.wait()
    for d in range(1, shards):
        line_to(d, False).wait_recv()
    for part in range(PARTS):
        pass_on(None, part, lambda copy: copy.wait_send())
    for s, part, step in hops:
        chunk = z - s if step == 0 else z + s
        there = chunk >= 0 if step == 0 else chunk < shards
        pass_on((step, chunk, there), part, lambda copy: copy.wait_send())
    for d in range(1, shards):
        line_to(d, True).wait_send()
        first_to(d, True).wait_send()
    for part in range(PARTS):
        for d in range(1, shards):
            to_peer(d, part, True).wait_send()
    for d in range(1, wide):
        to_owner(d, True).wait_send()


def finish(sel, mix, mix_full, gain_one, res, bm, normed, tokens, states, group, wide, rows_dev, gain_row, gains_dev):
    shards = mix_full.shape[0]
    rows, cols = bm.shape
    width = normed.shape[1]
    own = rows // shards
    half = HD // 2
    blocks = width // HD * (cols // HD)
    vmem = pl.BlockSpec(memory_space=pltpu.VMEM)
    smem = pl.BlockSpec(memory_space=pltpu.SMEM)
    hbm = pl.BlockSpec(memory_space=pl.ANY)
    dma = pltpu.SemaphoreType.DMA
    return pl.pallas_call(
        functools.partial(finish_kernel, shards, wide, gain_row, gains_dev, group),
        in_specs=[smem, vmem, vmem, hbm, hbm, hbm, hbm, hbm, hbm] + [hbm] * 6,
        out_specs=[vmem] * 2 + [hbm] * 6,
        out_shape=[jax.ShapeDtypeStruct((rows, width), BF), jax.ShapeDtypeStruct((shards + 1, 16, LANES), F32)]
        + [jax.ShapeDtypeStruct(a.shape, a.dtype) for a in states[1:]],
        scratch_shapes=[pltpu.VMEM(a.shape, a.dtype) for a in states[1:]] * 2
        + [
            pltpu.VMEM(mix_full.shape, BF),
            pltpu.VMEM(res.shape, F32),
            pltpu.VMEM((rows, cols), BF),
            pltpu.VMEM((rows, width), BF),
            pltpu.VMEM((own, width), BF),
            pltpu.VMEM((shards, own, cols), BF),
            pltpu.VMEM((width, cols), F32),
            pltpu.VMEM((blocks + 1, half, LANES), BF),
            pltpu.VMEM((wide, rows_dev, LANES), BF),
            pltpu.VMEM((wide, rows_dev, LANES), BF),
            pltpu.VMEM((shards, rows_dev, LANES), BF),
            pltpu.VMEM((rows_dev, LANES), F32),
            pltpu.VMEM((2 * group, HD, LANES), F32),
            dma((19,)),
            dma((shards - 1, PARTS)),
            dma((shards, PARTS)),
            dma((wide - 1,)),
            dma((wide,)),
            dma((2, shards, PARTS)),
            dma((shards, PARTS)),
            dma((shards - 1,)),
            dma((shards,)),
            dma((shards - 1,)),
            dma((shards,)),
        ],
        compiler_params=pltpu.CompilerParams(vmem_limit_bytes=46 << 20, collective_id=1, has_side_effects=True),
        name="finish",
    )(sel, mix, gain_one, mix_full, res, bm, normed, tokens, *states)


def wrap_kernel(count, per, grad_ref, outa_ref, outb_ref, *refs):
    olds, wide_ref, out_ref, news = refs[:count], refs[count], refs[count + 1], refs[count + 2 :]
    for old, new in zip(olds, news):
        new[...] = old[...]
    wide_ref[...] = grad_ref[...].astype(F32)
    place = lax.rem(pl.program_id(0), per)

    @pl.when(place == 0)
    def _():
        out_ref[...] = outa_ref[0]

    @pl.when(place > 0)
    def _():
        out_ref[...] = outb_ref[0]


def wrap(grad, out_a, out_b, olds):
    rows, width = grad.shape
    tb = out_a.shape[1]
    per = 1 + out_b.shape[1] // tb
    steps = rows // tb
    slots = olds[0].shape[1]
    group = next(g for g in range(1, slots + 1) if slots % g == 0 and slots // g <= steps)
    last = slots // group - 1
    blk = pl.BlockSpec((tb, width), lambda i: (i, 0))
    part_a = pl.BlockSpec((1, tb, width), lambda i: (i // per, 0, 0))
    part_b = pl.BlockSpec((1, tb, width), lambda i: (i // per, jnp.maximum(i % per - 1, 0), 0))
    states = [
        pl.BlockSpec((1, group, *a.shape[2:]), lambda i, k=a.ndim: (0, jnp.minimum(i, last)) + (0,) * (k - 2)) for a in olds
    ]
    return pl.pallas_call(
        functools.partial(wrap_kernel, len(olds), per),
        grid=(steps,),
        in_specs=[blk, part_a, part_b] + states,
        out_specs=[blk, blk] + states,
        out_shape=[jax.ShapeDtypeStruct((rows, width), F32), jax.ShapeDtypeStruct((rows, width), BF)]
        + [jax.ShapeDtypeStruct(a.shape, a.dtype) for a in olds],
        compiler_params=pltpu.CompilerParams(vmem_limit_bytes=48 << 20),
        name="wrap",
    )(grad, out_a, out_b, *olds)


def adam_gains(grad, gain, first, second, average):
    new_first = beta_one * first + (1.0 - beta_one) * grad
    new_second = beta_two * second + (1.0 - beta_two) * grad * grad
    new_gain = gain - gain_rate * new_first / (jnp.sqrt(new_second) + step_eps)
    new_average = average_keep * average + (1.0 - average_keep) * new_gain
    return (new_gain, new_first, new_second, new_average)


def body(
    tokens,
    cotangent,
    segment_ids,
    pad_mask,
    owner_order,
    weights,
    first_moment,
    second_moment,
    average,
    stats,
    bases,
    gains,
    gain_first,
    gain_second,
    gain_average,
):
    narrow = lax.axis_size("narrow")
    wide = lax.axis_size("wide")
    heads = HEADS // narrow
    rows, width = tokens.shape
    span = heads * HD
    own = rows // narrow
    slots, size = weights.shape[1], weights.shape[2]
    half = size // 2
    block_count = owner_order.shape[0]
    gains_dev = gains.shape[0]
    gain_row = slots * half
    rows_dev = gain_row + 16

    ids = jnp.arange(block_count, dtype=jnp.int32)
    slot_of = jnp.sum(jnp.where(owner_order[None, :] == ids[:, None], ids[None, :], 0), axis=1)
    device, place = slot_of // slots, slot_of % slots
    row_own = device * rows_dev + place * half
    row_full = device * (narrow * rows_dev) + place * half

    seg = segment_ids
    seg_row = segment_ids[0]
    pad = pad_mask
    block = min(512, rows)
    low_seg = seg_row[::block]
    high_seg = seg_row[block - 1 :: block]
    begin = jnp.sum((seg_row[None, :] < low_seg[:, None]).astype(jnp.int32), axis=1) // UNIT
    end = (jnp.sum((seg_row[None, :] <= high_seg[:, None]).astype(jnp.int32), axis=1) + UNIT - 1) // UNIT

    normed, qe, ke, ve, vt, mix, lines, along = project(
        weights, gains[None], row_own // 16, tokens, seg, pad, heads, narrow, wide, gain_row, gains_dev
    )
    wire_full = lax.all_gather(along.reshape(-1, LANES), "wide", axis=0, tiled=True)
    gain_all = lines[:, 0, :gains_dev].astype(F32).reshape(1, 2 * width)
    gain_one, gain_two = gain_all[:, :width], gain_all[:, width:]
    attended, qb = attend(qe, ke, vt, pad, begin, end, block, block)
    unit = row_full // 16
    mix_blocks = width // size * 3 * heads
    sel_rest = jnp.where(owner_order >= mix_blocks, owner_order - mix_blocks, block_count - mix_blocks)
    out_a, back_att, out_b, back_res, grads, mix_full = middle(
        unit, sel_rest, wire_full.reshape(-1, 16, LANES), gain_two, pad, attended, tokens, cotangent,
        narrow, wide, rows_dev, gain_row, gains_dev,
    )
    part_a = lax.psum_scatter(grads.reshape(-1, LANES), "wide", scatter_dimension=0, tiled=True)
    out_b = lax.all_to_all(out_b, "narrow", 0, 0)
    bm = attend_back(qb, ke, ve, back_att, attended, begin, end, block, block)
    bm, part_a, out_b = lax.optimization_barrier((bm, part_a, out_b))
    sel = jnp.minimum(owner_order, mix_blocks)
    group = next(g for g in range(min(12, slots), 0, -1) if slots % g == 0)
    states = (part_a, weights, first_moment, second_moment, average, stats, bases)
    grad_all, lines, *fresh = finish(
        sel, mix, mix_full, gain_one, back_res, bm, normed, tokens, states, group, wide, rows_dev, gain_row, gains_dev
    )
    input_grad, output, new_weight, new_first, new_second, new_average, new_stats, new_bases = wrap(
        grad_all, out_a, out_b, fresh
    )
    line = jnp.sum(lines[:, 0], axis=0)
    offset = lax.axis_index("wide") * gains_dev % LANES
    own_gain = lax.dynamic_slice_in_dim(line, offset, gains_dev, 0)
    new_gains, gain_moment, gain_square, gain_mean = adam_gains(own_gain, gains, gain_first, gain_second, gain_average)
    return (
        output,
        input_grad,
        new_weight,
        new_first,
        new_second,
        new_average,
        new_stats,
        new_bases,
        new_gains,
        gain_moment,
        gain_square,
        gain_mean,
    )


def solution(mesh):
    block = P("narrow", "wide", None, None)
    pair = P("narrow", "wide", None, None, None)
    rows = P("wide", None)
    line = P("wide")
    return jax.shard_map(
        body,
        mesh=mesh,
        in_specs=(rows, rows, rows, rows, P(), block, block, block, block, pair, pair, line, line, line, line),
        out_specs=(rows, rows, block, block, block, block, pair, pair, line, line, line, line),
        check_vma=False,
    )
```

```python
import functools

import jax
import jax.numpy as jnp
from jax import lax
from jax.experimental import pallas as pl
from jax.experimental.pallas import tpu as pltpu
from jax.sharding import PartitionSpec as P

HEADS = 8
HD = 64
FF = 2048
LANES = 128
SEGS = 4
NEG = -1e30
F32 = jnp.float32
BF = jnp.bfloat16
highest = lax.Precision.HIGHEST

beta_one = 0.9
beta_two = 0.95
step_rate = 0.1
gain_rate = 0.75
weight_decay = 0.01
average_keep = 0.5
norm_eps = 1e-05
step_eps = 1e-08


def nt(a, b):
    return lax.dot_general(a, b, (((1,), (1,)), ((), ())), preferred_element_type=F32)


def nn(a, b):
    return lax.dot_general(a, b, (((1,), (0,)), ((), ())), preferred_element_type=F32)


def tn(a, b):
    return lax.dot_general(a, b, (((0,), (0,)), ((), ())), preferred_element_type=F32)


def split3(x):
    hi = x.astype(BF)
    r = x - hi.astype(F32)
    mid = r.astype(BF)
    lo = (r - mid.astype(F32)).astype(BF)
    return hi, mid, lo


def put3(base, x, lane0):
    lane = lax.broadcasted_iota(jnp.int32, base.shape, 1)
    hi, mid, lo = split3(x)
    out = jnp.where(lane == lane0, hi.astype(F32), base.astype(F32))
    out = jnp.where(lane == lane0 + 1, mid.astype(F32), out)
    out = jnp.where(lane == lane0 + 2, lo.astype(F32), out)
    return out.astype(BF)


VT = 80
UNIT = 256


def in_steps(begin, end, block, step):
    per = block // UNIT
    count = end - begin
    whole = count // per

    def long(i, _):
        step((begin + i * per) * UNIT, block)
        return 0

    def short(i, _):
        step((begin + whole * per + i) * UNIT, UNIT)
        return 0

    lax.fori_loop(0, whole, long, 0)
    lax.fori_loop(0, count - whole * per, short, 0)


QC, AHEAD, QB, BAHEAD = 512, 1, 256, 1


def fwd_kernel(heads, bq, bk, lo_ref, hi_ref, qe_ref, ke_ref, vt_ref, pad_ref, att_ref, qb_ref, m_ref, acc_ref):
    i = pl.program_id(0)
    row0 = pl.multiple_of(i * bq, bq)
    real = pad_ref[...] > 0
    for h in range(heads):
        qt = qe_ref[h].astype(F32).T[:HD]
        kt = ke_ref[h, pl.ds(row0, bq), :].astype(F32).T[:HD]
        own = jnp.sum(qt * kt, axis=0, keepdims=True)
        m_ref[h] = jnp.where(real, NEG, own)
        acc_ref[h] = jnp.where(real, 0.0, vt_ref[h, :, pl.ds(row0, bq)].astype(F32))

    def step(at, bk):
        col0 = pl.multiple_of(at, UNIT)
        work = [(h, slice(c, c + QC)) for c in range(0, bq, QC) for h in range(heads)]
        score = lambda h, c: nt(ke_ref[h, pl.ds(col0, bk), :], qe_ref[h, c, :])
        ss = [score(*w) for w in work[:AHEAD]]
        for n, (h, c) in enumerate(work):
            if n + AHEAD < len(work):
                ss.append(score(*work[n + AHEAD]))
            s = ss[n]
            m_old = m_ref[h, :, c]
            m_new = jnp.maximum(m_old, jnp.max(s, axis=0, keepdims=True))
            p = jnp.exp(s - m_new).astype(BF)
            alpha = jnp.exp(m_old - m_new)
            acc_ref[h, :, c] = acc_ref[h, :, c] * alpha + nn(vt_ref[h, :, pl.ds(col0, bk)], p)
            m_ref[h, :, c] = m_new

    in_steps(lo_ref[i], hi_ref[i], bk, step)
    outs = []
    for h in range(heads):
        acc = acc_ref[h]
        total = acc[HD : HD + 1]
        outs.append(jnp.where(real, acc[:HD] / total, 0.0))
        lse = jnp.broadcast_to(m_ref[h] + jnp.log(total), (8, bq)).T[:, :1]
        qb_ref[h] = put3(qe_ref[h], -lse, HD + 4)
    att_ref[...] = (jnp.concatenate(outs, axis=0) if heads > 1 else outs[0]).T.astype(BF)


def attend(qe, ke, vt, padw, lo, hi, bq, bk):
    heads, rows, _ = qe.shape
    full = lambda i, lo, hi: (0, 0, 0)
    return pl.pallas_call(
        functools.partial(fwd_kernel, heads, bq, bk),
        grid_spec=pltpu.PrefetchScalarGridSpec(
            num_scalar_prefetch=2,
            grid=(rows // bq,),
            in_specs=[
                pl.BlockSpec((heads, bq, LANES), lambda i, lo, hi: (0, i, 0)),
                pl.BlockSpec((heads, rows, LANES), full),
                pl.BlockSpec((heads, VT, rows), full),
                pl.BlockSpec((1, bq), lambda i, lo, hi: (0, i)),
            ],
            out_specs=[
                pl.BlockSpec((bq, heads * HD), lambda i, lo, hi: (i, 0)),
                pl.BlockSpec((heads, bq, LANES), lambda i, lo, hi: (0, i, 0)),
            ],
            scratch_shapes=[
                pltpu.VMEM((heads, 1, bq), F32),
                pltpu.VMEM((heads, VT, bq), F32),
            ],
        ),
        out_shape=[
            jax.ShapeDtypeStruct((rows, heads * HD), BF),
            jax.ShapeDtypeStruct((heads, rows, LANES), BF),
        ],
        compiler_params=pltpu.CompilerParams(vmem_limit_bytes=60 << 20),
        name="attend",
    )(lo, hi, qe, ke, vt, padw)


def bwd_kernel(heads, bq, bk, lo_ref, hi_ref, qb_ref, ke_ref, ve_ref, go_ref, att_ref, out_ref, ge_ref, dqt_ref, kt_ref, qt_ref, got_ref, dkt_ref, dvt_ref):
    j = pl.program_id(0)
    rows = qb_ref.shape[1]

    @pl.when(j == 0)
    def _():
        for h in range(heads):
            dqt_ref[h] = jnp.zeros_like(dqt_ref[h])
            for c in range(rows // 512):
                sl = pl.ds(c * 512, 512)
                go = go_ref[sl, h * HD : (h + 1) * HD]
                at = att_ref[sl, h * HD : (h + 1) * HD]
                delta = jnp.sum(go.astype(F32) * at.astype(F32), axis=1, keepdims=True)
                wide = jnp.concatenate([go, jnp.zeros_like(go)], axis=1)
                ge_ref[h, sl, :] = put3(wide, -delta, HD)
                got_ref[h, :, c * 512 : (c + 1) * 512] = wide.T[:HD]
                qt_ref[h, :, c * 512 : (c + 1) * 512] = qb_ref[h, sl, :].T[:HD]

    for h in range(heads):
        kt_ref[h] = ke_ref[h].T[:HD]

    zero = jnp.zeros((HD, bk), F32)

    def step(at, bq):
        row0 = pl.multiple_of(at, UNIT)
        work = [(h, pl.ds(row0 + c, QB)) for c in range(0, bq, QB) for h in range(heads)]
        score = lambda h, c: (nt(ke_ref[h], qb_ref[h, c, :]), nt(ve_ref[h], ge_ref[h, c, :]))
        ss = [score(*w) for w in work[:BAHEAD]]
        for n, (h, c) in enumerate(work):
            if n + BAHEAD < len(work):
                ss.append(score(*work[n + BAHEAD]))
            st, dt = ss[n]
            p = jnp.exp(st)
            ds = (p * dt).astype(BF)
            pb = p.astype(BF)
            dvt_ref[h] += nt(got_ref[h, :, c], pb)
            dkt_ref[h] += nt(qt_ref[h, :, c], ds)
            dqt_ref[h, :, c] += nn(kt_ref[h], ds)

    for h in range(heads):
        dkt_ref[h] = zero
        dvt_ref[h] = zero
    in_steps(lo_ref[j], hi_ref[j], bq, step)
    for h in range(heads):
        for part, ref in ((1, dkt_ref), (2, dvt_ref)):
            at = (part * heads + h) * HD
            out_ref[pl.ds(pl.multiple_of(j * bk, bk), bk), at : at + HD] = ref[h].T.astype(BF)

    @pl.when(j == pl.num_programs(0) - 1)
    def _():
        for h in range(heads):
            for c in range(rows // 512):
                sl = pl.ds(c * 512, 512)
                out_ref[sl, h * HD : (h + 1) * HD] = (dqt_ref[h, :, c * 512 : (c + 1) * 512].T * (HD ** -0.5)).astype(BF)


def attend_back(qb, ke, ve, go, att, lo, hi, bq, bk):
    heads, rows, _ = qb.shape
    full3 = lambda i, lo, hi: (0, 0, 0)
    full2 = lambda i, lo, hi: (0, 0)
    blk3 = lambda i, lo, hi: (0, i, 0)
    wide = heads * HD
    return pl.pallas_call(
        functools.partial(bwd_kernel, heads, bq, bk),
        grid_spec=pltpu.PrefetchScalarGridSpec(
            num_scalar_prefetch=2,
            grid=(rows // bk,),
            in_specs=[
                pl.BlockSpec((heads, rows, LANES), full3),
                pl.BlockSpec((heads, bk, LANES), blk3),
                pl.BlockSpec((heads, bk, LANES), blk3),
                pl.BlockSpec((rows, wide), full2),
                pl.BlockSpec((rows, wide), full2),
            ],
            out_specs=pl.BlockSpec((rows, 3 * wide), full2),
            scratch_shapes=[
                pltpu.VMEM((heads, rows, LANES), BF),
                pltpu.VMEM((heads, HD, rows), F32),
                pltpu.VMEM((heads, HD, bk), BF),
                pltpu.VMEM((heads, HD, rows), BF),
                pltpu.VMEM((heads, HD, rows), BF),
                pltpu.VMEM((heads, HD, bk), F32),
                pltpu.VMEM((heads, HD, bk), F32),
            ],
        ),
        out_shape=jax.ShapeDtypeStruct((rows, 3 * wide), BF),
        compiler_params=pltpu.CompilerParams(vmem_limit_bytes=60 << 20),
        name="attend_back",
    )(lo, hi, qb, ke, ve, go, att)


def dot_f32(a, b, dims):
    return lax.dot_general(a, b, ((dims[:1], dims[1:]), ((), ())), precision=highest, preferred_element_type=F32)


def soap_group(base, group, gr_ref, w_ref, m1_ref, m2_ref, av_ref, st_ref, ba_ref,
               nw_ref, n1_ref, n2_ref, na_ref, ns_ref, nb_ref, aug_ref):
    size = w_ref.shape[-1]
    half = size // 2
    panel = 8
    every = range(group)
    grads, firsts = [], []
    for s in every:
        rows = slice((base + s) * half, (base + s + 1) * half)
        wire = gr_ref[rows, :]
        grads.append(jnp.concatenate([wire[:, :size], wire[:, size:]], axis=0))
        firsts.append(beta_one * m1_ref[0, base + s] + (1.0 - beta_one) * grads[s])
        n1_ref[0, base + s] = firsts[s]
    sides = [(s, side) for s in every for side in range(2)]
    outers = [dot_f32(grads[s], grads[s], (1, 1) if side == 0 else (0, 0)) for s, side in sides]
    both = [dot_f32(jnp.concatenate([grads[s], firsts[s]], axis=0), ba_ref[0, base + s, 1], (1, 0)) for s in every]
    stats = []
    for (s, side), outer in zip(sides, outers):
        stats.append(beta_two * st_ref[0, base + s, side] + (1.0 - beta_two) * outer)
        ns_ref[0, base + s, side] = stats[-1]
    pairs = [dot_f32(ba_ref[0, base + s, 0], jnp.concatenate([both[s][:size], both[s][size:]], axis=1), (0, 0)) for s in every]
    mts = [dot_f32(ba_ref[0, base + s, side], stat, (0, 1)) for (s, side), stat in zip(sides, stats)]
    scaled = []
    for s in every:
        rotated, moment = pairs[s][:, :size], pairs[s][:, size:]
        second = beta_two * m2_ref[0, base + s] + (1.0 - beta_two) * rotated * rotated
        n2_ref[0, base + s] = second
        scaled.append(moment / (jnp.sqrt(second) + step_eps))
    grams = [dot_f32(mt, mt, (1, 1)) for mt in mts]
    inner = [dot_f32(scaled[s], ba_ref[0, base + s, 1], (1, 1)) for s in every]
    for m, (gram, mt) in enumerate(zip(grams, mts)):
        aug_ref[m] = jnp.concatenate([gram, mt], axis=1)
    directions = [dot_f32(ba_ref[0, base + s, 0], inner[s], (1, 0)) for s in every]
    for s in every:
        weight = w_ref[0, base + s]
        fresh = weight - step_rate * (directions[s] + weight_decay * weight)
        nw_ref[0, base + s] = fresh
        na_ref[0, base + s] = average_keep * av_ref[0, base + s] + (1.0 - average_keep) * fresh
    count = 2 * group
    row = lax.broadcasted_iota(jnp.int32, (count, panel, LANES), 1)
    for p in range(size // panel):
        top = p * panel
        part = aug_ref[:, top : top + panel, :]
        for r in range(panel):
            pivot = lax.rsqrt(part[:, r : r + 1, top + r : top + r + 1])
            lead = part[:, r : r + 1, :] * pivot
            column = jnp.where(row > r, part[:, :, top + r : top + r + 1] * pivot, 0.0)
            part = jnp.where(row == r, lead, part - column * lead)
        aug_ref[:, top : top + panel, :] = part
        below = top + panel
        if below < size:
            high = part.astype(BF).astype(F32)
            rest = part - high
            mid = rest.astype(BF).astype(F32)
            low = rest - mid
            first = jnp.concatenate([high, high, mid, high, mid, low], axis=1).astype(BF)
            other = jnp.concatenate([high, mid, high, low, mid, high], axis=1).astype(BF)
            for m in range(count):
                aug_ref[m, below:, :] -= lax.dot_general(
                    first[m][:, below:size], other[m], (((0,), (0,)), ((), ())), preferred_element_type=F32
                )
    for s in range(group):
        for side in range(2):
            nb_ref[0, base + s, side] = aug_ref[2 * s + side][:, size:].T


MESH = pl.DeviceIdType.MESH


def normalize(values):
    center = jnp.mean(values, axis=-1, keepdims=True)
    centered = values - center
    variance = jnp.mean(centered * centered, axis=-1, keepdims=True)
    scale = lax.rsqrt(variance + norm_eps)
    return centered * scale, scale


def norm_back(grad, xhat, scale):
    along = jnp.mean(grad * xhat, axis=-1, keepdims=True)
    return (grad - jnp.mean(grad, axis=-1, keepdims=True) - xhat * along) * scale


TAIL = 0.305
TAIL_FIT = (
    0.1216397411342051,
    0.12246669816059132,
    0.10342157025713879,
    0.1210193967312446,
    -0.037972477455618554,
    0.18571204369074895,
    -0.15298537812807472,
    0.036698452375741396,
)


def gelu_pair(u):
    size = jnp.abs(u)
    bell = jnp.exp(-0.5 * u * u)
    t = 1.0 / (1.0 + TAIL * size)
    poly = jnp.full_like(t, TAIL_FIT[-1])
    for c in TAIL_FIT[-2::-1]:
        poly = poly * t + c
    upper = poly * t * bell
    cdf = jnp.where(u > 0.0, 1.0 - upper, upper)
    return u * cdf, cdf + (0.3989422804014327 * u) * bell


def project_kernel(heads, shards, wide, gain_row, gains_dev, unit_ref, weight_ref, gains_ref, tok_ref, seg_ref, pad_ref,
                   norm_ref, qe_ref, ke_ref, ve_ref, vt_ref, mix_ref, line_ref, along_ref,
                   wide_ref, wire_ref, all_ref, near_ref, gain_ref, send_w, recv_w, send_z, recv_z):
    width = tok_ref.shape[1]
    half = HD // 2
    cols = 3 * heads
    units = wire_ref.shape[0]

    @pl.when(pl.program_id(0) == 0)
    def _():
        z = lax.axis_index("narrow")
        w = lax.axis_index("wide")
        twin = w + 1 - 2 * lax.rem(w, 2)
        chips = wide // 2
        barrier = pltpu.get_barrier_semaphore()
        pl.semaphore_signal(barrier, inc=1, device_id={"wide": twin}, device_id_type=MESH)
        for d in range(1, chips):
            pl.semaphore_signal(barrier, inc=1, device_id={"wide": lax.rem(w + 2 * d, wide)}, device_id_type=MESH)
        for d in range(1, shards):
            pl.semaphore_signal(barrier, inc=1, device_id={"narrow": lax.rem(z + d, shards)}, device_id_type=MESH)
        for s in range(gain_row // half):
            low = weight_ref[0, s].astype(BF)
            t = jnp.concatenate([low[:half], low[half:]], axis=1)
            wire_ref[2 * s] = t[:16]
            wire_ref[2 * s + 1] = t[16:]
        line = gains_ref[...]
        if gains_dev < LANES:
            line = jnp.concatenate([line, jnp.zeros((1, LANES - gains_dev), F32)], axis=1)
        first = lax.broadcasted_iota(jnp.int32, (16, LANES), 0) == 0
        wire_ref[gain_row // 16] = jnp.where(first, line, 0.0).astype(BF)
        pl.semaphore_wait(barrier, chips + shards - 1)

        def slot(s):
            return all_ref.at[pl.ds(s * units, units)]

        def to_chip(d, mine):
            peer = lax.rem(w + 2 * d, wide)
            return pltpu.make_async_remote_copy(
                src_ref=wire_ref,
                dst_ref=slot(w if mine else peer),
                send_sem=send_w.at[d],
                recv_sem=recv_w.at[w if mine else peer],
                device_id={"wide": peer},
                device_id_type=MESH,
            )

        def to_twin(d, mine):
            owner = lax.rem((w if mine else twin) + 2 * d, wide)
            return pltpu.make_async_remote_copy(
                src_ref=wire_ref if d == 0 else slot(owner),
                dst_ref=slot(owner),
                send_sem=send_w.at[chips + d],
                recv_sem=recv_w.at[owner],
                device_id={"wide": twin},
                device_id_type=MESH,
            )

        def to_shard(d, mine):
            peer = lax.rem(z + d, shards)
            return pltpu.make_async_remote_copy(
                src_ref=wire_ref,
                dst_ref=near_ref.at[z if mine else peer],
                send_sem=send_z.at[d - 1],
                recv_sem=recv_z.at[z if mine else peer],
                device_id={"narrow": peer},
                device_id_type=MESH,
            )

        for d in range(1, chips):
            to_chip(d, True).start()
        to_twin(0, True).start()
        for d in range(1, shards):
            to_shard(d, True).start()
        all_ref[pl.ds(w * units, units)] = wire_ref[...]
        near_ref[z] = wire_ref[...]
        for d in range(1, chips):
            to_chip(d, False).wait_recv()
            to_twin(d, True).start()
        for d in range(chips):
            to_twin(d, False).wait_recv()

        for v in range(wide):
            line_ref[v] = all_ref[v * units + gain_row // 16]
        pieces = [line_ref[v].astype(F32)[:1, :gains_dev] for v in range(wide // 2)]
        gain_ref[...] = jnp.concatenate(pieces, axis=1)
        zero = jnp.zeros((half, HD), BF)

        def fill(r, _):
            low = pl.multiple_of(r * HD, HD)
            for c in range(cols):
                unit = unit_ref[r * cols + c]
                t = jnp.concatenate([all_ref[unit], all_ref[unit + 1]], axis=0)
                for part in range(2):
                    piece = t[:, part * HD : (part + 1) * HD]
                    at = pl.ds(low + part * half, half)
                    wide_ref[at, c * LANES : (c + 1) * LANES] = jnp.concatenate([piece, zero], axis=1)
                    mix_ref[at, c * HD : (c + 1) * HD] = piece
            return 0

        lax.fori_loop(0, width // HD, fill, 0)
        for d in range(1, shards):
            to_shard(d, False).wait_recv()
            to_shard(d, True).wait_send()
        along_ref[...] = near_ref[...]
        for d in range(1, chips):
            to_chip(d, True).wait_send()
        for d in range(chips):
            to_twin(d, True).wait_send()

    xhat, _ = normalize(tok_ref[...].astype(F32))
    normed = (xhat * gain_ref[...]).astype(BF)
    norm_ref[...] = normed
    count = tok_ref.shape[0]
    lane = lax.broadcasted_iota(jnp.int32, (LANES, count), 0)
    seg = seg_ref[...]
    same = lane - HD == seg
    in_segs = (lane >= HD) & (lane < HD + SEGS)
    ones = (lane >= HD + SEGS) & (lane < HD + SEGS + 3)
    ext_q = jnp.where(same, 1.0, 0.0).T
    ext_k = jnp.where(in_segs, jnp.where(same & (pad_ref[...] > 0), 0.0, NEG), jnp.where(ones, 1.0, 0.0)).T
    side = lax.broadcasted_iota(jnp.int32, (count, LANES), 1)
    ext_v = jnp.where((side >= HD) & (side < HD + 3), 1.0, 0.0)
    whole = nn(normed, wide_ref[...]).astype(BF)
    for h in range(heads):
        for ref, part, scale, ext in ((qe_ref, 0, HD ** -0.5, ext_q), (ke_ref, 1, 1.0, ext_k), (ve_ref, 2, 1.0, ext_v)):
            c = part * heads + h
            mixed = whole[:, c * LANES : (c + 1) * LANES]
            out = (mixed.astype(F32) * scale + ext).astype(BF)
            ref[h] = out
            if part == 2:
                vt_ref[h] = out.T[:VT]


def project(weights, gains, unit, tokens, seg, pad, heads, shards, wide, gain_row, gains_dev):
    rows, width = tokens.shape
    tb = min(512, rows)
    full = lambda i, r: (0, 0)
    full3 = lambda i, r: (0, 0, 0)
    blk = lambda i, r: (i, 0)
    col = lambda i, r: (0, i)
    ext = lambda i, r: (0, i, 0)
    out = lambda *s: jax.ShapeDtypeStruct(s, BF)
    dma = pltpu.SemaphoreType.DMA
    units = gain_row // 16 + 1
    return pl.pallas_call(
        functools.partial(project_kernel, heads, shards, wide, gain_row, gains_dev),
        grid_spec=pltpu.PrefetchScalarGridSpec(
            num_scalar_prefetch=1,
            grid=(rows // tb,),
            in_specs=[
                pl.BlockSpec(weights.shape, lambda i, r: (0, 0, 0, 0)),
                pl.BlockSpec((1, gains_dev), full),
                pl.BlockSpec((tb, width), blk),
                pl.BlockSpec((1, tb), col),
                pl.BlockSpec((1, tb), col),
            ],
            out_specs=[
                pl.BlockSpec((tb, width), blk),
                pl.BlockSpec((heads, tb, LANES), ext),
                pl.BlockSpec((heads, tb, LANES), ext),
                pl.BlockSpec((heads, tb, LANES), ext),
                pl.BlockSpec((heads, VT, tb), lambda i, r: (0, 0, i)),
                pl.BlockSpec((width, 3 * heads * HD), full),
                pl.BlockSpec((wide, 16, LANES), full3),
                pl.BlockSpec((shards, units, 16, LANES), lambda i, r: (0, 0, 0, 0)),
            ],
            scratch_shapes=[
                pltpu.VMEM((width, 3 * heads * LANES), BF),
                pltpu.VMEM((units, 16, LANES), BF),
                pltpu.VMEM((wide * units, 16, LANES), BF),
                pltpu.VMEM((shards, units, 16, LANES), BF),
                pltpu.VMEM((1, width), F32),
                dma((wide,)),
                dma((wide,)),
                dma((shards - 1,)),
                dma((shards,)),
            ],
        ),
        out_shape=[
            out(rows, width),
            out(heads, rows, LANES),
            out(heads, rows, LANES),
            out(heads, rows, LANES),
            out(heads, VT, rows),
            out(width, 3 * heads * HD),
            out(wide, 16, LANES),
            out(shards, units, 16, LANES),
        ],
        compiler_params=pltpu.CompilerParams(vmem_limit_bytes=60 << 20, collective_id=3, has_side_effects=True),
        name="project",
    )(unit, weights, gains, tokens, seg, pad)


def middle_kernel(shards, span, units, wide, gain_row, gains_dev, inside,
                  unit_ref, sel_ref, gain_ref, pad_ref, wire_ref, att_ref, tok_ref, cot_ref,
                  outa_ref, back_ref, outs_ref, res_ref, grads_ref, mix_ref,
                  tokens_ref, cots_ref, got_ref, give_ref, wo_ref, wu_ref, wd_ref, go_ref, gu_ref, gd_ref, gg_ref, blk_ref,
                  hold_ref, resv_ref, mixv_ref, gradv_ref, outb_ref, local_sem, send_i, recv_i, send_b, recv_b, send_a, recv_a):
    own, width = tokens_ref.shape
    parts = recv_i.shape[1]
    tb = own // parts
    half = HD // 2
    rows_dev = gradv_ref.shape[1]
    z = lax.axis_index("narrow")
    kinds = (
        (mixv_ref, None, width, 3 * span),
        (wo_ref, go_ref, span, width),
        (wu_ref, gu_ref, width, units),
        (wd_ref, gd_ref, units, width),
    )
    mix_blocks = width // HD * (3 * span // HD)
    per = blk_ref.shape[0] // shards

    barrier = pltpu.get_barrier_semaphore()
    for d in range(1, shards):
        pl.semaphore_signal(barrier, inc=1, device_id={"narrow": lax.rem(z + d, shards)}, device_id_type=MESH)
    pl.semaphore_wait(barrier, shards - 1)

    def bring(d, t, mine):
        peer = lax.rem(z + d, shards)
        slot = z if mine else peer
        return pltpu.make_async_remote_copy(
            src_ref=att_ref.at[pl.ds(pl.multiple_of(peer * own + t * tb, tb), tb), :],
            dst_ref=got_ref.at[slot, pl.ds(pl.multiple_of(t * tb, tb), tb), :],
            send_sem=send_i.at[d - 1, t],
            recv_sem=recv_i.at[slot, t],
            device_id={"narrow": peer},
            device_id_type=MESH,
        )

    def give(d, t, mine):
        peer = lax.rem(z + d, shards)
        slot = z if mine else peer
        return pltpu.make_async_remote_copy(
            src_ref=give_ref.at[peer, pl.ds(pl.multiple_of(t * tb, tb), tb), :],
            dst_ref=back_ref.at[pl.ds(pl.multiple_of(slot * own + t * tb, tb), tb), :],
            send_sem=send_b.at[d - 1, t],
            recv_sem=recv_b.at[slot, t],
            device_id={"narrow": peer},
            device_id_type=MESH,
        )

    def hop_copy(c, t, step):
        at = pl.ds(pl.multiple_of(t * tb, tb), tb)
        return pltpu.make_async_remote_copy(
            src_ref=outa_ref.at[c, at, :],
            dst_ref=outa_ref.at[c, at, :],
            send_sem=send_a.at[step, c, t],
            recv_sem=recv_a.at[c, t],
            device_id={"narrow": lax.rem(z + (1 if step == 0 else shards - 1), shards)},
            device_id_type=MESH,
        )

    room = (z < shards - 1, z > 0)
    for t in range(parts):
        for d in range(1, shards):
            bring(d, t, True).start()
    mine = pl.ds(pl.multiple_of(z * own, own), own)
    copies = [
        pltpu.make_async_copy(att_ref.at[mine, :], got_ref.at[z], local_sem.at[0]),
        pltpu.make_async_copy(tok_ref.at[mine, :], tokens_ref, local_sem.at[1]),
        pltpu.make_async_copy(cot_ref.at[mine, :], cots_ref, local_sem.at[2]),
    ]
    fetch = pltpu.make_async_copy(wire_ref, hold_ref, local_sem.at[3])
    fetch.start()
    for copy in copies:
        copy.start()
    fetch.wait()

    def gather_blocks(kinds, base):
        for ref, acc, rows, cols in kinds:
            grid_cols = cols // HD

            def fill(r, _, ref=ref, base=base, grid_cols=grid_cols):
                low = pl.multiple_of(r * HD, HD)
                for n in range(shards):
                    for c in range(grid_cols):
                        unit = unit_ref[base + r * grid_cols + c] + n * (rows_dev // 16)
                        t = jnp.concatenate([hold_ref[unit], hold_ref[unit + 1]], axis=0)
                        for part in range(2):
                            ref[n, pl.ds(low + part * half, half), c * HD : (c + 1) * HD] = t[:, part * HD : (part + 1) * HD]
                return 0

            lax.fori_loop(0, rows // HD, fill, 0)
            base += rows // HD * grid_cols
            if acc is not None:
                acc[...] = jnp.zeros_like(acc)

    gather_blocks(kinds[1:], mix_blocks)
    gg_ref[...] = jnp.zeros_like(gg_ref)
    stores = [
        pltpu.make_async_copy(mixv_ref, mix_ref, local_sem.at[4]),
        pltpu.make_async_copy(resv_ref, res_ref, local_sem.at[5]),
        pltpu.make_async_copy(gradv_ref, grads_ref, local_sem.at[6]),
    ]
    stores += [pltpu.make_async_copy(outb_ref, outs_ref.at[n], local_sem.at[7 + n]) for n in range(shards)]
    for copy in copies:
        copy.wait()

    def block(t, _):
        at = pl.ds(pl.multiple_of(t * tb, tb), tb)
        for d in range(1, shards):
            bring(d, t, False).wait_recv()
        tokens = tokens_ref[at, :].astype(F32)
        cot = cots_ref[at, :]
        branch = nn(got_ref[0, at, :], wo_ref[0])
        for n in range(1, shards):
            branch += nn(got_ref[n, at, :], wo_ref[n])
        residual = tokens + branch
        xhat, scale = normalize(residual)
        gain = gain_ref[...]
        normed = (xhat * gain).astype(BF)
        ups = [nn(normed, wu_ref[n]) for n in range(shards)]
        downs = [nt(cot, wd_ref[n]) for n in range(shards)]
        actives, back_ups = [], []
        for n in range(shards):
            value, slope = gelu_pair(ups[n])
            actives.append(value.astype(BF))
            back_ups.append((slope * downs[n]).astype(BF))
        mlp = nn(actives[0], wd_ref[0])
        back = nt(back_ups[0], wu_ref[0])
        for n in range(1, shards):
            mlp += nn(actives[n], wd_ref[n])
            back += nt(back_ups[n], wu_ref[n])
        out = (residual + mlp).astype(BF)

        @pl.when(t < inside)
        def _():
            outa_ref[z, at, :] = out
            for step in range(2):

                @pl.when(room[step])
                def _(step=step):
                    hop_copy(z, t, step).start()

        @pl.when(t >= inside)
        def _():
            outb_ref[pl.ds(pl.multiple_of((t - inside) * tb, tb), tb), :] = out

        gg_ref[...] += jnp.sum(back * xhat, axis=0, keepdims=True)
        back_res = cot.astype(F32) + norm_back(back * gain, xhat, scale)
        resv_ref[at, :] = back_res
        branch_low = back_res.astype(BF)
        line = pad_ref[:, pl.ds(pl.multiple_of(z * own + t * tb, LANES), tb)]
        pad = jnp.broadcast_to(line.astype(F32), (8, tb)).T[:, :1]
        for n in range(shards):
            give_ref[n, at, :] = (nt(branch_low, wo_ref[n]) * pad).astype(BF)
        for d in range(1, shards):
            give(d, t, True).start()
        for n in range(shards):
            gd_ref[n] += tn(actives[n], cot)
            gu_ref[n] += tn(normed, back_ups[n])
            go_ref[n] += tn(got_ref[n, at, :], branch_low)
        return 0

    lax.fori_loop(0, parts, block, 0)
    for copy in stores[1:2] + stores[3:]:
        copy.start()
    gather_blocks(kinds[:1], 0)
    stores[0].start()
    back_ref[mine, :] = give_ref[z]
    base = 0
    for ref, acc, rows, cols in kinds:
        grid_cols = cols // HD
        if acc is not None:

            def cut(r, _, acc=acc, base=base, grid_cols=grid_cols):
                low = pl.multiple_of(r * HD, HD)
                for n in range(shards):
                    for c in range(grid_cols):
                        lanes = slice(c * HD, (c + 1) * HD)
                        value = jnp.concatenate([acc[n, pl.ds(low, half), lanes], acc[n, pl.ds(low + half, half), lanes]], axis=1)
                        blk_ref[n * per + base - mix_blocks + r * grid_cols + c] = value.astype(BF)
                return 0

            lax.fori_loop(0, rows // HD, cut, 0)
        base += rows // HD * grid_cols
    for n in range(shards):
        blk_ref[(n + 1) * per - 1] = jnp.zeros((half, LANES), BF)
    slots = gain_row // half
    top = lax.broadcasted_iota(jnp.int32, (16, LANES), 0) == 0

    def place(v, _):
        for n in range(shards):
            for i in range(slots):
                gradv_ref[v * shards + n, i * half : (i + 1) * half, :] = blk_ref[sel_ref[v * slots + i] + n * per]
        return 0

    lax.fori_loop(0, wide, place, 0)
    for v in range(wide):
        piece = v * gains_dev // LANES - width // LANES
        for n in range(shards):
            if piece >= 0:
                value = jnp.where(top, gg_ref[:, piece * LANES : (piece + 1) * LANES], 0.0).astype(BF)
            else:
                value = jnp.zeros((16, LANES), BF)
            gradv_ref[v * shards + n, gain_row:, :] = value
    stores[2].start()

    hops = [(s, t, step) for s in range(1, shards) for t in range(inside) for step in range(2)]
    for s, t, step in hops:
        chunk = z - s if step == 0 else z + s
        there = chunk >= 0 if step == 0 else chunk < shards

        @pl.when(there)
        def _(chunk=chunk, t=t, step=step):
            hop_copy(chunk, t, step).wait_recv()

        @pl.when(there & room[step])
        def _(chunk=chunk, t=t, step=step):
            hop_copy(chunk, t, step).start()

    for t in range(parts):
        for d in range(1, shards):
            give(d, t, False).wait_recv()
    for copy in stores:
        copy.wait()
    for t in range(parts):
        for d in range(1, shards):
            bring(d, t, True).wait_send()
            give(d, t, True).wait_send()
    for t in range(inside):
        for step in range(2):

            @pl.when(room[step])
            def _(t=t, step=step):
                hop_copy(z, t, step).wait_send()

    for s, t, step in hops:
        chunk = z - s if step == 0 else z + s
        there = chunk >= 0 if step == 0 else chunk < shards

        @pl.when(there & room[step])
        def _(chunk=chunk, t=t, step=step):
            hop_copy(chunk, t, step).wait_send()


def middle(unit, sel, wire, gain_two, pad, att, tokens, cotangent, shards, wide, rows_dev, gain_row, gains_dev):
    rows, span = att.shape
    width = tokens.shape[1]
    units = FF // shards
    own = rows // shards
    tb = min(256, own)
    parts = own // tb
    inside = max(1, parts // 4)
    blocks = unit.shape[0] - width // HD * (3 * span // HD)
    vmem = pl.BlockSpec(memory_space=pltpu.VMEM)
    smem = pl.BlockSpec(memory_space=pltpu.SMEM)
    hbm = pl.BlockSpec(memory_space=pl.ANY)
    dma = pltpu.SemaphoreType.DMA
    return pl.pallas_call(
        functools.partial(middle_kernel, shards, span, units, wide, gain_row, gains_dev, inside),
        in_specs=[smem, smem, vmem, vmem, hbm, hbm, hbm, hbm],
        out_specs=[vmem] * 2 + [hbm] * 4,
        out_shape=[
            jax.ShapeDtypeStruct((shards, inside * tb, width), BF),
            jax.ShapeDtypeStruct((rows, span), BF),
            jax.ShapeDtypeStruct((shards, own - inside * tb, width), BF),
            jax.ShapeDtypeStruct((own, width), F32),
            jax.ShapeDtypeStruct((wide * shards, rows_dev, LANES), BF),
            jax.ShapeDtypeStruct((shards, width, 3 * span), BF),
        ],
        scratch_shapes=[
            pltpu.VMEM((own, width), BF),
            pltpu.VMEM((own, width), BF),
            pltpu.VMEM((shards, own, span), BF),
            pltpu.VMEM((shards, own, span), BF),
            pltpu.VMEM((shards, span, width), BF),
            pltpu.VMEM((shards, width, units), BF),
            pltpu.VMEM((shards, units, width), BF),
            pltpu.VMEM((shards, span, width), F32),
            pltpu.VMEM((shards, width, units), F32),
            pltpu.VMEM((shards, units, width), F32),
            pltpu.VMEM((1, width), F32),
            pltpu.VMEM((shards * (blocks + 1), HD // 2, LANES), BF),
            pltpu.VMEM(wire.shape, BF),
            pltpu.VMEM((own, width), F32),
            pltpu.VMEM((shards, width, 3 * span), BF),
            pltpu.VMEM((wide * shards, rows_dev, LANES), BF),
            pltpu.VMEM((own - inside * tb, width), BF),
            dma((7 + shards,)),
            dma((shards - 1, parts)),
            dma((shards, parts)),
            dma((shards - 1, parts)),
            dma((shards, parts)),
            dma((2, shards, inside)),
            dma((shards, inside)),
        ],
        compiler_params=pltpu.CompilerParams(vmem_limit_bytes=63 << 20, collective_id=2, has_side_effects=True),
        name="middle",
    )(unit, sel, gain_two, pad, wire, att, tokens, cotangent)


PARTS = 8


def finish_kernel(shards, wide, gain_row, gains_dev, group, sel_ref, mix_ref, gain_ref, fullh_ref, resh_ref, bm_ref, norm_ref, tok_ref, *refs):
    given, taken = refs[1:7], refs[9:15]
    states, outs, (full_ref, res_ref) = refs[15:21], refs[21:27], refs[27:29]
    first_ref, grad_ref, line_ref = refs[0], refs[7], refs[8]
    (own_ref, normed_ref, tokens_ref, got_ref, acc_ref, blk_ref, grads_ref, sums_ref, firsts_ref, part_ref, aug_ref,
     local_sem, send_z, recv_z, send_w, recv_w, send_a, recv_a, send_g, recv_g, send_f, recv_f) = refs[29:]
    width = norm_ref.shape[1]
    rows, cols = bm_ref.shape
    own = rows // shards
    hold = own // PARTS
    half = HD // 2
    grid_cols = cols // HD
    blocks = width // HD * grid_cols
    slots = gain_row // half
    z = lax.axis_index("narrow")
    w = lax.axis_index("wide")

    barrier = pltpu.get_barrier_semaphore()
    for d in range(1, shards):
        pl.semaphore_signal(barrier, inc=1, device_id={"narrow": lax.rem(z + d, shards)}, device_id_type=MESH)
    for d in range(1, wide):
        pl.semaphore_signal(barrier, inc=1, device_id={"wide": lax.rem(w + d, wide)}, device_id_type=MESH)
    pl.semaphore_wait(barrier, shards + wide - 2)

    def to_peer(d, part, mine):
        peer = lax.rem(z + d, shards)
        slot = z if mine else peer
        at = pl.multiple_of(peer * own + part * hold, hold)
        return pltpu.make_async_remote_copy(
            src_ref=bm_ref.at[pl.ds(at, hold), :],
            dst_ref=got_ref.at[slot, pl.ds(part * hold, hold), :],
            send_sem=send_z.at[d - 1, part],
            recv_sem=recv_z.at[slot, part],
            device_id={"narrow": peer},
            device_id_type=MESH,
        )

    def to_owner(d, mine):
        peer = lax.rem(w + d, wide)
        slot = w if mine else peer
        return pltpu.make_async_remote_copy(
            src_ref=grads_ref.at[peer],
            dst_ref=sums_ref.at[slot],
            send_sem=send_w.at[d - 1],
            recv_sem=recv_w.at[slot],
            device_id={"wide": peer},
            device_id_type=MESH,
        )

    def hop_copy(c, part, step):
        at = pl.ds(pl.multiple_of(c * own + part * hold, hold), hold)
        return pltpu.make_async_remote_copy(
            src_ref=grad_ref.at[at, :],
            dst_ref=grad_ref.at[at, :],
            send_sem=send_a.at[step, c, part],
            recv_sem=recv_a.at[c, part],
            device_id={"narrow": lax.rem(z + (1 if step == 0 else shards - 1), shards)},
            device_id_type=MESH,
        )

    def pass_on(c, part, act):
        for step, there in ((0, z < shards - 1), (1, z > 0)):
            if c is None or step == c[0]:
                chunk = z if c is None else c[1]
                ok = there if c is None else there & c[2]

                @pl.when(ok)
                def _(chunk=chunk, step=step):
                    act(hop_copy(chunk, part, step))

    def line_to(d, mine):
        peer = lax.rem(z + d, shards)
        slot = z if mine else peer
        return pltpu.make_async_remote_copy(
            src_ref=line_ref.at[z],
            dst_ref=line_ref.at[slot],
            send_sem=send_g.at[d - 1],
            recv_sem=recv_g.at[slot],
            device_id={"narrow": peer},
            device_id_type=MESH,
        )

    rows_dev = part_ref.shape[0]

    def first_to(d, mine):
        peer = lax.rem(z + d, shards)
        slot = z if mine else peer
        return pltpu.make_async_remote_copy(
            src_ref=first_ref.at[pl.ds(pl.multiple_of(peer * rows_dev, 16), rows_dev), :],
            dst_ref=firsts_ref.at[slot],
            send_sem=send_f.at[d - 1],
            recv_sem=recv_f.at[slot],
            device_id={"narrow": peer},
            device_id_type=MESH,
        )

    for d in range(1, shards):
        first_to(d, True).start()
    for part in range(PARTS):
        for d in range(1, shards):
            to_peer(d, part, True).start()
    mine = pl.ds(pl.multiple_of(z * own, own), own)
    copies = [
        pltpu.make_async_copy(bm_ref, own_ref, local_sem.at[0]),
        pltpu.make_async_copy(norm_ref, normed_ref, local_sem.at[1]),
        pltpu.make_async_copy(tok_ref.at[mine, :], tokens_ref, local_sem.at[2]),
        pltpu.make_async_copy(bm_ref.at[mine, :], got_ref.at[z], local_sem.at[3]),
        pltpu.make_async_copy(
            first_ref.at[pl.ds(pl.multiple_of(z * rows_dev, 16), rows_dev), :], firsts_ref.at[z], local_sem.at[4]
        ),
    ]
    late = [
        pltpu.make_async_copy(a, b, local_sem.at[5 + k])
        for k, (a, b) in enumerate(zip((fullh_ref, resh_ref, *given), (full_ref, res_ref, *states)))
    ]
    for copy in copies + late:
        copy.start()
    for copy in copies:
        copy.wait()

    acc_ref[...] = jnp.zeros_like(acc_ref)
    tb = min(512, rows)

    def add(i, _):
        at = pl.ds(pl.multiple_of(i * tb, tb), tb)
        acc_ref[...] += tn(normed_ref[at, :], own_ref[at, :])
        return 0

    lax.fori_loop(0, rows // tb, add, 0)
    blk_ref[blocks] = jnp.zeros((half, LANES), BF)

    def cut(r, _):
        low = pl.multiple_of(r * HD, HD)
        for c in range(grid_cols):
            lanes = slice(c * HD, (c + 1) * HD)
            value = jnp.concatenate([acc_ref[pl.ds(low, half), lanes], acc_ref[pl.ds(low + half, half), lanes]], axis=1)
            blk_ref[r * grid_cols + c] = value.astype(BF)
        return 0

    lax.fori_loop(0, width // HD, cut, 0)
    along = jnp.sum(acc_ref[...] * mix_ref[...].astype(F32), axis=1, keepdims=True)
    line = jnp.broadcast_to(along, (width, LANES)).T[:16] / gain_ref[...]
    top = lax.broadcasted_iota(jnp.int32, (16, LANES), 0) == 0
    for v in range(wide):

        def place(i, _, v=v):
            grads_ref[v, pl.ds(pl.multiple_of(i * half, half), half), :] = blk_ref[sel_ref[v * slots + i]]
            return 0

        lax.fori_loop(0, slots, place, 0)
        piece = v * gains_dev // LANES
        if piece < width // LANES:
            value = jnp.where(top, line[:, piece * LANES : (piece + 1) * LANES], 0.0).astype(BF)
        else:
            value = jnp.zeros((16, LANES), BF)
        grads_ref[v, gain_row : gain_row + 16, :] = value
    for d in range(1, wide):
        to_owner(d, True).start()
    part_ref[...] = grads_ref[w].astype(F32)

    tile = min(256, hold)

    def norm_rows(i, _):
        at = pl.ds(pl.multiple_of(i * tile, tile), tile)
        back = nt(got_ref[0, at, :], full_ref[0])
        for n in range(1, shards):
            back += nt(got_ref[n, at, :], full_ref[n])
        xhat, scale = normalize(tokens_ref[at, :].astype(F32))
        grad = res_ref[at, :] + norm_back(back * gain_ref[...], xhat, scale)
        grad_ref[pl.ds(pl.multiple_of(z * own + i * tile, tile), tile), :] = grad.astype(BF)
        return 0

    def norm_part(part):
        for d in range(1, shards):
            to_peer(d, part, False).wait_recv()
        lax.fori_loop(part * hold // tile, (part + 1) * hold // tile, norm_rows, 0)
        pass_on(None, part, lambda copy: copy.start())

    for d in range(1, wide):
        to_owner(d, False).wait_recv()
    for d in range(1, wide):
        part_ref[...] += sums_ref[lax.rem(w + d, wide)].astype(F32)
    line_ref[z] = part_ref[gain_row : gain_row + 16, :]
    for d in range(1, shards):
        line_to(d, True).start()
    for d in range(1, shards):
        first_to(d, False).wait_recv()
    total = firsts_ref[0].astype(F32)
    for n in range(1, shards):
        total += firsts_ref[n].astype(F32)
    line_ref[shards] = total[gain_row : gain_row + 16, :]
    part_ref[...] += total
    for copy in late:
        copy.wait()
    stores = [pltpu.make_async_copy(a, b, local_sem.at[13 + k]) for k, (a, b) in enumerate(zip(outs, taken))]
    ready = 0
    rounds = slots // group
    for g in range(rounds):
        soap_group(g * group, group, part_ref, *states, *outs, aug_ref)
        upto = PARTS if g == rounds - 1 else 0
        while ready < upto:
            norm_part(ready)
            ready += 1
    for copy in stores:
        copy.start()
    hops = [(s, part, step) for s in range(1, shards) for part in range(PARTS) for step in range(2)]
    for s, part, step in hops:
        chunk = z - s if step == 0 else z + s
        there = chunk >= 0 if step == 0 else chunk < shards

        @pl.when(there)
        def _(chunk=chunk, part=part, step=step):
            hop_copy(chunk, part, step).wait_recv()

        pass_on((step, chunk, there), part, lambda copy: copy.start())
    for copy in stores:
        copy.wait()
    for d in range(1, shards):
        line_to(d, False).wait_recv()
    for part in range(PARTS):
        pass_on(None, part, lambda copy: copy.wait_send())
    for s, part, step in hops:
        chunk = z - s if step == 0 else z + s
        there = chunk >= 0 if step == 0 else chunk < shards
        pass_on((step, chunk, there), part, lambda copy: copy.wait_send())
    for d in range(1, shards):
        line_to(d, True).wait_send()
        first_to(d, True).wait_send()
    for part in range(PARTS):
        for d in range(1, shards):
            to_peer(d, part, True).wait_send()
    for d in range(1, wide):
        to_owner(d, True).wait_send()


def finish(sel, mix, mix_full, gain_one, res, bm, normed, tokens, states, group, wide, rows_dev, gain_row, gains_dev):
    shards = mix_full.shape[0]
    rows, cols = bm.shape
    width = normed.shape[1]
    own = rows // shards
    half = HD // 2
    blocks = width // HD * (cols // HD)
    vmem = pl.BlockSpec(memory_space=pltpu.VMEM)
    smem = pl.BlockSpec(memory_space=pltpu.SMEM)
    hbm = pl.BlockSpec(memory_space=pl.ANY)
    dma = pltpu.SemaphoreType.DMA
    return pl.pallas_call(
        functools.partial(finish_kernel, shards, wide, gain_row, gains_dev, group),
        in_specs=[smem, vmem, vmem, hbm, hbm, hbm, hbm, hbm, hbm] + [hbm] * 6,
        out_specs=[vmem] * 2 + [hbm] * 6,
        out_shape=[jax.ShapeDtypeStruct((rows, width), BF), jax.ShapeDtypeStruct((shards + 1, 16, LANES), F32)]
        + [jax.ShapeDtypeStruct(a.shape, a.dtype) for a in states[1:]],
        scratch_shapes=[pltpu.VMEM(a.shape, a.dtype) for a in states[1:]] * 2
        + [
            pltpu.VMEM(mix_full.shape, BF),
            pltpu.VMEM(res.shape, F32),
            pltpu.VMEM((rows, cols), BF),
            pltpu.VMEM((rows, width), BF),
            pltpu.VMEM((own, width), BF),
            pltpu.VMEM((shards, own, cols), BF),
            pltpu.VMEM((width, cols), F32),
            pltpu.VMEM((blocks + 1, half, LANES), BF),
            pltpu.VMEM((wide, rows_dev, LANES), BF),
            pltpu.VMEM((wide, rows_dev, LANES), BF),
            pltpu.VMEM((shards, rows_dev, LANES), BF),
            pltpu.VMEM((rows_dev, LANES), F32),
            pltpu.VMEM((2 * group, HD, LANES), F32),
            dma((19,)),
            dma((shards - 1, PARTS)),
            dma((shards, PARTS)),
            dma((wide - 1,)),
            dma((wide,)),
            dma((2, shards, PARTS)),
            dma((shards, PARTS)),
            dma((shards - 1,)),
            dma((shards,)),
            dma((shards - 1,)),
            dma((shards,)),
        ],
        compiler_params=pltpu.CompilerParams(vmem_limit_bytes=43 << 20, collective_id=1, has_side_effects=True),
        name="finish",
    )(sel, mix, gain_one, mix_full, res, bm, normed, tokens, *states)


def wrap_kernel(count, per, grad_ref, outa_ref, outb_ref, *refs):
    olds, wide_ref, out_ref, news = refs[:count], refs[count], refs[count + 1], refs[count + 2 :]
    for old, new in zip(olds, news):
        new[...] = old[...]
    wide_ref[...] = grad_ref[...].astype(F32)
    place = lax.rem(pl.program_id(0), per)

    @pl.when(place == 0)
    def _():
        out_ref[...] = outa_ref[0]

    @pl.when(place > 0)
    def _():
        out_ref[...] = outb_ref[0]


def wrap(grad, out_a, out_b, olds):
    rows, width = grad.shape
    tb = out_a.shape[1]
    per = 1 + out_b.shape[1] // tb
    steps = rows // tb
    slots = olds[0].shape[1]
    group = next(g for g in range(1, slots + 1) if slots % g == 0 and slots // g <= steps)
    last = slots // group - 1
    blk = pl.BlockSpec((tb, width), lambda i: (i, 0))
    part_a = pl.BlockSpec((1, tb, width), lambda i: (i // per, 0, 0))
    part_b = pl.BlockSpec((1, tb, width), lambda i: (i // per, jnp.maximum(i % per - 1, 0), 0))
    states = [
        pl.BlockSpec((1, group, *a.shape[2:]), lambda i, k=a.ndim: (0, jnp.minimum(i, last)) + (0,) * (k - 2)) for a in olds
    ]
    return pl.pallas_call(
        functools.partial(wrap_kernel, len(olds), per),
        grid=(steps,),
        in_specs=[blk, part_a, part_b] + states,
        out_specs=[blk, blk] + states,
        out_shape=[jax.ShapeDtypeStruct((rows, width), F32), jax.ShapeDtypeStruct((rows, width), BF)]
        + [jax.ShapeDtypeStruct(a.shape, a.dtype) for a in olds],
        compiler_params=pltpu.CompilerParams(vmem_limit_bytes=44 << 20),
        name="wrap",
    )(grad, out_a, out_b, *olds)


def adam_gains(grad, gain, first, second, average):
    new_first = beta_one * first + (1.0 - beta_one) * grad
    new_second = beta_two * second + (1.0 - beta_two) * grad * grad
    new_gain = gain - gain_rate * new_first / (jnp.sqrt(new_second) + step_eps)
    new_average = average_keep * average + (1.0 - average_keep) * new_gain
    return (new_gain, new_first, new_second, new_average)


def body(
    tokens,
    cotangent,
    segment_ids,
    pad_mask,
    owner_order,
    weights,
    first_moment,
    second_moment,
    average,
    stats,
    bases,
    gains,
    gain_first,
    gain_second,
    gain_average,
):
    narrow = lax.axis_size("narrow")
    wide = lax.axis_size("wide")
    heads = HEADS // narrow
    rows, width = tokens.shape
    span = heads * HD
    own = rows // narrow
    slots, size = weights.shape[1], weights.shape[2]
    half = size // 2
    block_count = owner_order.shape[0]
    gains_dev = gains.shape[0]
    gain_row = slots * half
    rows_dev = gain_row + 16

    ids = jnp.arange(block_count, dtype=jnp.int32)
    slot_of = jnp.sum(jnp.where(owner_order[None, :] == ids[:, None], ids[None, :], 0), axis=1)
    device, place = slot_of // slots, slot_of % slots
    row_own = device * rows_dev + place * half
    row_full = device * (narrow * rows_dev) + place * half

    seg = segment_ids
    seg_row = segment_ids[0]
    pad = pad_mask
    block = min(512, rows)
    low_seg = seg_row[::block]
    high_seg = seg_row[block - 1 :: block]
    begin = jnp.sum((seg_row[None, :] < low_seg[:, None]).astype(jnp.int32), axis=1) // UNIT
    end = (jnp.sum((seg_row[None, :] <= high_seg[:, None]).astype(jnp.int32), axis=1) + UNIT - 1) // UNIT

    normed, qe, ke, ve, vt, mix, lines, along = project(
        weights, gains[None], row_own // 16, tokens, seg, pad, heads, narrow, wide, gain_row, gains_dev
    )
    wire_full = lax.all_gather(along.reshape(-1, LANES), "wide", axis=0, tiled=True)
    gain_all = lines[:, 0, :gains_dev].astype(F32).reshape(1, 2 * width)
    gain_one, gain_two = gain_all[:, :width], gain_all[:, width:]
    attended, qb = attend(qe, ke, vt, pad, begin, end, block, block)
    unit = row_full // 16
    mix_blocks = width // size * 3 * heads
    sel_rest = jnp.where(owner_order >= mix_blocks, owner_order - mix_blocks, block_count - mix_blocks)
    out_a, back_att, out_b, back_res, grads, mix_full = middle(
        unit, sel_rest, wire_full.reshape(-1, 16, LANES), gain_two, pad, attended, tokens, cotangent,
        narrow, wide, rows_dev, gain_row, gains_dev,
    )
    part_a = lax.psum_scatter(grads.reshape(-1, LANES), "wide", scatter_dimension=0, tiled=True)
    out_b = lax.all_to_all(out_b, "narrow", 0, 0)
    bm = attend_back(qb, ke, ve, back_att, attended, begin, end, block, block)
    bm, part_a, out_b = lax.optimization_barrier((bm, part_a, out_b))
    sel = jnp.minimum(owner_order, mix_blocks)
    group = next(g for g in range(min(12, slots), 0, -1) if slots % g == 0)
    states = (part_a, weights, first_moment, second_moment, average, stats, bases)
    grad_all, lines, *fresh = finish(
        sel, mix, mix_full, gain_one, back_res, bm, normed, tokens, states, group, wide, rows_dev, gain_row, gains_dev
    )
    input_grad, output, new_weight, new_first, new_second, new_average, new_stats, new_bases = wrap(
        grad_all, out_a, out_b, fresh
    )
    line = jnp.sum(lines[:, 0], axis=0)
    offset = lax.axis_index("wide") * gains_dev % LANES
    own_gain = lax.dynamic_slice_in_dim(line, offset, gains_dev, 0)
    new_gains, gain_moment, gain_square, gain_mean = adam_gains(own_gain, gains, gain_first, gain_second, gain_average)
    return (
        output,
        input_grad,
        new_weight,
        new_first,
        new_second,
        new_average,
        new_stats,
        new_bases,
        new_gains,
        gain_moment,
        gain_square,
        gain_mean,
    )


def solution(mesh):
    block = P("narrow", "wide", None, None)
    pair = P("narrow", "wide", None, None, None)
    rows = P("wide", None)
    line = P("wide")
    return jax.shard_map(
        body,
        mesh=mesh,
        in_specs=(rows, rows, rows, rows, P(), block, block, block, block, pair, pair, line, line, line, line),
        out_specs=(rows, rows, block, block, block, block, pair, pair, line, line, line, line),
        check_vma=False,
    )
```

```python
import functools

import jax
import jax.numpy as jnp
from jax import lax
from jax.experimental import pallas as pl
from jax.experimental.pallas import tpu as pltpu
from jax.sharding import PartitionSpec as P

HEADS = 8
HD = 64
FF = 2048
LANES = 128
SEGS = 4
NEG = -1e30
F32 = jnp.float32
BF = jnp.bfloat16
highest = lax.Precision.HIGHEST

beta_one = 0.9
beta_two = 0.95
step_rate = 0.1
gain_rate = 0.75
weight_decay = 0.01
average_keep = 0.5
norm_eps = 1e-05
step_eps = 1e-08


def nt(a, b):
    return lax.dot_general(a, b, (((1,), (1,)), ((), ())), preferred_element_type=F32)


def nn(a, b):
    return lax.dot_general(a, b, (((1,), (0,)), ((), ())), preferred_element_type=F32)


def tn(a, b):
    return lax.dot_general(a, b, (((0,), (0,)), ((), ())), preferred_element_type=F32)


def split3(x):
    hi = x.astype(BF)
    r = x - hi.astype(F32)
    mid = r.astype(BF)
    lo = (r - mid.astype(F32)).astype(BF)
    return hi, mid, lo


def put3(base, x, lane0):
    lane = lax.broadcasted_iota(jnp.int32, base.shape, 1)
    hi, mid, lo = split3(x)
    out = jnp.where(lane == lane0, hi.astype(F32), base.astype(F32))
    out = jnp.where(lane == lane0 + 1, mid.astype(F32), out)
    out = jnp.where(lane == lane0 + 2, lo.astype(F32), out)
    return out.astype(BF)


VT = 80
UNIT = 256


def in_steps(begin, end, block, step):
    per = block // UNIT
    count = end - begin
    whole = count // per

    def long(i, _):
        step((begin + i * per) * UNIT, block)
        return 0

    def short(i, _):
        step((begin + whole * per + i) * UNIT, UNIT)
        return 0

    lax.fori_loop(0, whole, long, 0)
    lax.fori_loop(0, count - whole * per, short, 0)


QC, AHEAD, QB, BAHEAD = 512, 1, 256, 1


def fwd_kernel(heads, bq, bk, lo_ref, hi_ref, qe_ref, ke_ref, vt_ref, pad_ref, att_ref, qb_ref, m_ref, acc_ref):
    i = pl.program_id(0)
    row0 = pl.multiple_of(i * bq, bq)
    real = pad_ref[...] > 0
    for h in range(heads):
        qt = qe_ref[h].astype(F32).T[:HD]
        kt = ke_ref[h, pl.ds(row0, bq), :].astype(F32).T[:HD]
        own = jnp.sum(qt * kt, axis=0, keepdims=True)
        m_ref[h] = jnp.where(real, NEG, own)
        acc_ref[h] = jnp.where(real, 0.0, vt_ref[h, :, pl.ds(row0, bq)].astype(F32))

    def step(at, bk):
        col0 = pl.multiple_of(at, UNIT)
        work = [(h, slice(c, c + QC)) for c in range(0, bq, QC) for h in range(heads)]
        score = lambda h, c: nt(ke_ref[h, pl.ds(col0, bk), :], qe_ref[h, c, :])
        ss = [score(*w) for w in work[:AHEAD]]
        for n, (h, c) in enumerate(work):
            if n + AHEAD < len(work):
                ss.append(score(*work[n + AHEAD]))
            s = ss[n]
            m_old = m_ref[h, :, c]
            m_new = jnp.maximum(m_old, jnp.max(s, axis=0, keepdims=True))
            p = jnp.exp(s - m_new).astype(BF)
            alpha = jnp.exp(m_old - m_new)
            acc_ref[h, :, c] = acc_ref[h, :, c] * alpha + nn(vt_ref[h, :, pl.ds(col0, bk)], p)
            m_ref[h, :, c] = m_new

    in_steps(lo_ref[i], hi_ref[i], bk, step)
    outs = []
    for h in range(heads):
        acc = acc_ref[h]
        total = acc[HD : HD + 1]
        outs.append(jnp.where(real, acc[:HD] / total, 0.0))
        lse = jnp.broadcast_to(m_ref[h] + jnp.log(total), (8, bq)).T[:, :1]
        qb_ref[h] = put3(qe_ref[h], -lse, HD + 4)
    att_ref[...] = (jnp.concatenate(outs, axis=0) if heads > 1 else outs[0]).T.astype(BF)


def attend(qe, ke, vt, padw, lo, hi, bq, bk):
    heads, rows, _ = qe.shape
    full = lambda i, lo, hi: (0, 0, 0)
    return pl.pallas_call(
        functools.partial(fwd_kernel, heads, bq, bk),
        grid_spec=pltpu.PrefetchScalarGridSpec(
            num_scalar_prefetch=2,
            grid=(rows // bq,),
            in_specs=[
                pl.BlockSpec((heads, bq, LANES), lambda i, lo, hi: (0, i, 0)),
                pl.BlockSpec((heads, rows, LANES), full),
                pl.BlockSpec((heads, VT, rows), full),
                pl.BlockSpec((1, bq), lambda i, lo, hi: (0, i)),
            ],
            out_specs=[
                pl.BlockSpec((bq, heads * HD), lambda i, lo, hi: (i, 0)),
                pl.BlockSpec((heads, bq, LANES), lambda i, lo, hi: (0, i, 0)),
            ],
            scratch_shapes=[
                pltpu.VMEM((heads, 1, bq), F32),
                pltpu.VMEM((heads, VT, bq), F32),
            ],
        ),
        out_shape=[
            jax.ShapeDtypeStruct((rows, heads * HD), BF),
            jax.ShapeDtypeStruct((heads, rows, LANES), BF),
        ],
        compiler_params=pltpu.CompilerParams(vmem_limit_bytes=60 << 20),
        name="attend",
    )(lo, hi, qe, ke, vt, padw)


def bwd_kernel(heads, bq, bk, lo_ref, hi_ref, qb_ref, ke_ref, ve_ref, go_ref, att_ref, out_ref, ge_ref, dqt_ref, kt_ref, qt_ref, got_ref, dkt_ref, dvt_ref):
    j = pl.program_id(0)
    rows = qb_ref.shape[1]

    @pl.when(j == 0)
    def _():
        for h in range(heads):
            dqt_ref[h] = jnp.zeros_like(dqt_ref[h])
            for c in range(rows // 512):
                sl = pl.ds(c * 512, 512)
                go = go_ref[sl, h * HD : (h + 1) * HD]
                at = att_ref[sl, h * HD : (h + 1) * HD]
                delta = jnp.sum(go.astype(F32) * at.astype(F32), axis=1, keepdims=True)
                wide = jnp.concatenate([go, jnp.zeros_like(go)], axis=1)
                ge_ref[h, sl, :] = put3(wide, -delta, HD)
                got_ref[h, :, c * 512 : (c + 1) * 512] = wide.T[:HD]
                qt_ref[h, :, c * 512 : (c + 1) * 512] = qb_ref[h, sl, :].T[:HD]

    for h in range(heads):
        kt_ref[h] = ke_ref[h].T[:HD]

    zero = jnp.zeros((HD, bk), F32)

    def step(at, bq):
        row0 = pl.multiple_of(at, UNIT)
        work = [(h, pl.ds(row0 + c, QB)) for c in range(0, bq, QB) for h in range(heads)]
        score = lambda h, c: (nt(ke_ref[h], qb_ref[h, c, :]), nt(ve_ref[h], ge_ref[h, c, :]))
        ss = [score(*w) for w in work[:BAHEAD]]
        for n, (h, c) in enumerate(work):
            if n + BAHEAD < len(work):
                ss.append(score(*work[n + BAHEAD]))
            st, dt = ss[n]
            p = jnp.exp(st)
            ds = (p * dt).astype(BF)
            pb = p.astype(BF)
            dvt_ref[h] += nt(got_ref[h, :, c], pb)
            dkt_ref[h] += nt(qt_ref[h, :, c], ds)
            dqt_ref[h, :, c] += nn(kt_ref[h], ds)

    for h in range(heads):
        dkt_ref[h] = zero
        dvt_ref[h] = zero
    in_steps(lo_ref[j], hi_ref[j], bq, step)
    for h in range(heads):
        for part, ref in ((1, dkt_ref), (2, dvt_ref)):
            at = (part * heads + h) * HD
            out_ref[pl.ds(pl.multiple_of(j * bk, bk), bk), at : at + HD] = ref[h].T.astype(BF)

    @pl.when(j == pl.num_programs(0) - 1)
    def _():
        for h in range(heads):
            for c in range(rows // 512):
                sl = pl.ds(c * 512, 512)
                out_ref[sl, h * HD : (h + 1) * HD] = (dqt_ref[h, :, c * 512 : (c + 1) * 512].T * (HD ** -0.5)).astype(BF)


def attend_back(qb, ke, ve, go, att, lo, hi, bq, bk):
    heads, rows, _ = qb.shape
    full3 = lambda i, lo, hi: (0, 0, 0)
    full2 = lambda i, lo, hi: (0, 0)
    blk3 = lambda i, lo, hi: (0, i, 0)
    wide = heads * HD
    return pl.pallas_call(
        functools.partial(bwd_kernel, heads, bq, bk),
        grid_spec=pltpu.PrefetchScalarGridSpec(
            num_scalar_prefetch=2,
            grid=(rows // bk,),
            in_specs=[
                pl.BlockSpec((heads, rows, LANES), full3),
                pl.BlockSpec((heads, bk, LANES), blk3),
                pl.BlockSpec((heads, bk, LANES), blk3),
                pl.BlockSpec((rows, wide), full2),
                pl.BlockSpec((rows, wide), full2),
            ],
            out_specs=pl.BlockSpec((rows, 3 * wide), full2),
            scratch_shapes=[
                pltpu.VMEM((heads, rows, LANES), BF),
                pltpu.VMEM((heads, HD, rows), F32),
                pltpu.VMEM((heads, HD, bk), BF),
                pltpu.VMEM((heads, HD, rows), BF),
                pltpu.VMEM((heads, HD, rows), BF),
                pltpu.VMEM((heads, HD, bk), F32),
                pltpu.VMEM((heads, HD, bk), F32),
            ],
        ),
        out_shape=jax.ShapeDtypeStruct((rows, 3 * wide), BF),
        compiler_params=pltpu.CompilerParams(vmem_limit_bytes=60 << 20),
        name="attend_back",
    )(lo, hi, qb, ke, ve, go, att)


def dot_f32(a, b, dims):
    return lax.dot_general(a, b, ((dims[:1], dims[1:]), ((), ())), precision=highest, preferred_element_type=F32)


def soap_group(base, group, gr_ref, w_ref, m1_ref, m2_ref, av_ref, st_ref, ba_ref,
               nw_ref, n1_ref, n2_ref, na_ref, ns_ref, nb_ref, aug_ref):
    size = w_ref.shape[-1]
    half = size // 2
    panel = 8
    every = range(group)
    grads, firsts = [], []
    for s in every:
        rows = slice((base + s) * half, (base + s + 1) * half)
        wire = gr_ref[rows, :]
        grads.append(jnp.concatenate([wire[:, :size], wire[:, size:]], axis=0))
        firsts.append(beta_one * m1_ref[0, base + s] + (1.0 - beta_one) * grads[s])
        n1_ref[0, base + s] = firsts[s]
    sides = [(s, side) for s in every for side in range(2)]
    outers = [dot_f32(grads[s], grads[s], (1, 1) if side == 0 else (0, 0)) for s, side in sides]
    both = [dot_f32(jnp.concatenate([grads[s], firsts[s]], axis=0), ba_ref[0, base + s, 1], (1, 0)) for s in every]
    stats = []
    for (s, side), outer in zip(sides, outers):
        stats.append(beta_two * st_ref[0, base + s, side] + (1.0 - beta_two) * outer)
        ns_ref[0, base + s, side] = stats[-1]
    pairs = [dot_f32(ba_ref[0, base + s, 0], jnp.concatenate([both[s][:size], both[s][size:]], axis=1), (0, 0)) for s in every]
    mts = [dot_f32(ba_ref[0, base + s, side], stat, (0, 1)) for (s, side), stat in zip(sides, stats)]
    scaled = []
    for s in every:
        rotated, moment = pairs[s][:, :size], pairs[s][:, size:]
        second = beta_two * m2_ref[0, base + s] + (1.0 - beta_two) * rotated * rotated
        n2_ref[0, base + s] = second
        scaled.append(moment / (jnp.sqrt(second) + step_eps))
    grams = [dot_f32(mt, mt, (1, 1)) for mt in mts]
    inner = [dot_f32(scaled[s], ba_ref[0, base + s, 1], (1, 1)) for s in every]
    for m, (gram, mt) in enumerate(zip(grams, mts)):
        aug_ref[m] = jnp.concatenate([gram, mt], axis=1)
    directions = [dot_f32(ba_ref[0, base + s, 0], inner[s], (1, 0)) for s in every]
    for s in every:
        weight = w_ref[0, base + s]
        fresh = weight - step_rate * (directions[s] + weight_decay * weight)
        nw_ref[0, base + s] = fresh
        na_ref[0, base + s] = average_keep * av_ref[0, base + s] + (1.0 - average_keep) * fresh
    count = 2 * group
    row = lax.broadcasted_iota(jnp.int32, (count, panel, LANES), 1)
    for p in range(size // panel):
        top = p * panel
        part = aug_ref[:, top : top + panel, :]
        for r in range(panel):
            pivot = lax.rsqrt(part[:, r : r + 1, top + r : top + r + 1])
            lead = part[:, r : r + 1, :] * pivot
            column = jnp.where(row > r, part[:, :, top + r : top + r + 1] * pivot, 0.0)
            part = jnp.where(row == r, lead, part - column * lead)
        aug_ref[:, top : top + panel, :] = part
        below = top + panel
        if below < size:
            high = part.astype(BF).astype(F32)
            rest = part - high
            mid = rest.astype(BF).astype(F32)
            low = rest - mid
            first = jnp.concatenate([high, high, mid, high, mid, low], axis=1).astype(BF)
            other = jnp.concatenate([high, mid, high, low, mid, high], axis=1).astype(BF)
            for m in range(count):
                aug_ref[m, below:, :] -= lax.dot_general(
                    first[m][:, below:size], other[m], (((0,), (0,)), ((), ())), preferred_element_type=F32
                )
    for s in range(group):
        for side in range(2):
            nb_ref[0, base + s, side] = aug_ref[2 * s + side][:, size:].T


MESH = pl.DeviceIdType.MESH


def normalize(values):
    center = jnp.mean(values, axis=-1, keepdims=True)
    centered = values - center
    variance = jnp.mean(centered * centered, axis=-1, keepdims=True)
    scale = lax.rsqrt(variance + norm_eps)
    return centered * scale, scale


def norm_back(grad, xhat, scale):
    along = jnp.mean(grad * xhat, axis=-1, keepdims=True)
    return (grad - jnp.mean(grad, axis=-1, keepdims=True) - xhat * along) * scale


TAIL = 0.305
TAIL_FIT = (
    0.1216397411342051,
    0.12246669816059132,
    0.10342157025713879,
    0.1210193967312446,
    -0.037972477455618554,
    0.18571204369074895,
    -0.15298537812807472,
    0.036698452375741396,
)


def gelu_pair(u):
    size = jnp.abs(u)
    bell = jnp.exp(-0.5 * u * u)
    t = 1.0 / (1.0 + TAIL * size)
    poly = jnp.full_like(t, TAIL_FIT[-1])
    for c in TAIL_FIT[-2::-1]:
        poly = poly * t + c
    upper = poly * t * bell
    cdf = jnp.where(u > 0.0, 1.0 - upper, upper)
    return u * cdf, cdf + (0.3989422804014327 * u) * bell


def project_kernel(heads, shards, wide, gain_row, gains_dev, unit_ref, weight_ref, gains_ref, tok_ref, seg_ref, pad_ref,
                   norm_ref, qe_ref, ke_ref, ve_ref, vt_ref, mix_ref, line_ref, along_ref,
                   wide_ref, wire_ref, all_ref, near_ref, gain_ref, send_w, recv_w, send_z, recv_z):
    width = tok_ref.shape[1]
    half = HD // 2
    cols = 3 * heads
    units = wire_ref.shape[0]

    @pl.when(pl.program_id(0) == 0)
    def _():
        z = lax.axis_index("narrow")
        w = lax.axis_index("wide")
        twin = w + 1 - 2 * lax.rem(w, 2)
        chips = wide // 2
        barrier = pltpu.get_barrier_semaphore()
        pl.semaphore_signal(barrier, inc=1, device_id={"wide": twin}, device_id_type=MESH)
        for d in range(1, chips):
            pl.semaphore_signal(barrier, inc=1, device_id={"wide": lax.rem(w + 2 * d, wide)}, device_id_type=MESH)
        for d in range(1, shards):
            pl.semaphore_signal(barrier, inc=1, device_id={"narrow": lax.rem(z + d, shards)}, device_id_type=MESH)
        for s in range(gain_row // half):
            low = weight_ref[0, s].astype(BF)
            t = jnp.concatenate([low[:half], low[half:]], axis=1)
            wire_ref[2 * s] = t[:16]
            wire_ref[2 * s + 1] = t[16:]
        line = gains_ref[...]
        if gains_dev < LANES:
            line = jnp.concatenate([line, jnp.zeros((1, LANES - gains_dev), F32)], axis=1)
        first = lax.broadcasted_iota(jnp.int32, (16, LANES), 0) == 0
        wire_ref[gain_row // 16] = jnp.where(first, line, 0.0).astype(BF)
        pl.semaphore_wait(barrier, chips + shards - 1)

        def slot(s):
            return all_ref.at[pl.ds(s * units, units)]

        def to_chip(d, mine):
            peer = lax.rem(w + 2 * d, wide)
            return pltpu.make_async_remote_copy(
                src_ref=wire_ref,
                dst_ref=slot(w if mine else peer),
                send_sem=send_w.at[d],
                recv_sem=recv_w.at[w if mine else peer],
                device_id={"wide": peer},
                device_id_type=MESH,
            )

        def to_twin(d, mine):
            owner = lax.rem((w if mine else twin) + 2 * d, wide)
            return pltpu.make_async_remote_copy(
                src_ref=wire_ref if d == 0 else slot(owner),
                dst_ref=slot(owner),
                send_sem=send_w.at[chips + d],
                recv_sem=recv_w.at[owner],
                device_id={"wide": twin},
                device_id_type=MESH,
            )

        def to_shard(d, mine):
            peer = lax.rem(z + d, shards)
            return pltpu.make_async_remote_copy(
                src_ref=wire_ref,
                dst_ref=near_ref.at[z if mine else peer],
                send_sem=send_z.at[d - 1],
                recv_sem=recv_z.at[z if mine else peer],
                device_id={"narrow": peer},
                device_id_type=MESH,
            )

        for d in range(1, chips):
            to_chip(d, True).start()
        to_twin(0, True).start()
        for d in range(1, shards):
            to_shard(d, True).start()
        all_ref[pl.ds(w * units, units)] = wire_ref[...]
        near_ref[z] = wire_ref[...]
        for d in range(1, chips):
            to_chip(d, False).wait_recv()
            to_twin(d, True).start()
        for d in range(chips):
            to_twin(d, False).wait_recv()

        for v in range(wide):
            line_ref[v] = all_ref[v * units + gain_row // 16]
        pieces = [line_ref[v].astype(F32)[:1, :gains_dev] for v in range(wide // 2)]
        gain_ref[...] = jnp.concatenate(pieces, axis=1)
        zero = jnp.zeros((half, HD), BF)

        def fill(r, _):
            low = pl.multiple_of(r * HD, HD)
            for c in range(cols):
                unit = unit_ref[r * cols + c]
                t = jnp.concatenate([all_ref[unit], all_ref[unit + 1]], axis=0)
                for part in range(2):
                    piece = t[:, part * HD : (part + 1) * HD]
                    at = pl.ds(low + part * half, half)
                    wide_ref[at, c * LANES : (c + 1) * LANES] = jnp.concatenate([piece, zero], axis=1)
                    mix_ref[at, c * HD : (c + 1) * HD] = piece
            return 0

        lax.fori_loop(0, width // HD, fill, 0)
        for d in range(1, shards):
            to_shard(d, False).wait_recv()
            to_shard(d, True).wait_send()
        along_ref[...] = near_ref[...]
        for d in range(1, chips):
            to_chip(d, True).wait_send()
        for d in range(chips):
            to_twin(d, True).wait_send()

    xhat, _ = normalize(tok_ref[...].astype(F32))
    normed = (xhat * gain_ref[...]).astype(BF)
    norm_ref[...] = normed
    count = tok_ref.shape[0]
    lane = lax.broadcasted_iota(jnp.int32, (LANES, count), 0)
    seg = seg_ref[...]
    same = lane - HD == seg
    in_segs = (lane >= HD) & (lane < HD + SEGS)
    ones = (lane >= HD + SEGS) & (lane < HD + SEGS + 3)
    ext_q = jnp.where(same, 1.0, 0.0).T
    ext_k = jnp.where(in_segs, jnp.where(same & (pad_ref[...] > 0), 0.0, NEG), jnp.where(ones, 1.0, 0.0)).T
    side = lax.broadcasted_iota(jnp.int32, (count, LANES), 1)
    ext_v = jnp.where((side >= HD) & (side < HD + 3), 1.0, 0.0)
    whole = nn(normed, wide_ref[...]).astype(BF)
    for h in range(heads):
        for ref, part, scale, ext in ((qe_ref, 0, HD ** -0.5, ext_q), (ke_ref, 1, 1.0, ext_k), (ve_ref, 2, 1.0, ext_v)):
            c = part * heads + h
            mixed = whole[:, c * LANES : (c + 1) * LANES]
            out = (mixed.astype(F32) * scale + ext).astype(BF)
            ref[h] = out
            if part == 2:
                vt_ref[h] = out.T[:VT]


def project(weights, gains, unit, tokens, seg, pad, heads, shards, wide, gain_row, gains_dev):
    rows, width = tokens.shape
    tb = min(1024, rows)
    full = lambda i, r: (0, 0)
    full3 = lambda i, r: (0, 0, 0)
    blk = lambda i, r: (i, 0)
    col = lambda i, r: (0, i)
    ext = lambda i, r: (0, i, 0)
    out = lambda *s: jax.ShapeDtypeStruct(s, BF)
    dma = pltpu.SemaphoreType.DMA
    units = gain_row // 16 + 1
    return pl.pallas_call(
        functools.partial(project_kernel, heads, shards, wide, gain_row, gains_dev),
        grid_spec=pltpu.PrefetchScalarGridSpec(
            num_scalar_prefetch=1,
            grid=(rows // tb,),
            in_specs=[
                pl.BlockSpec(weights.shape, lambda i, r: (0, 0, 0, 0)),
                pl.BlockSpec((1, gains_dev), full),
                pl.BlockSpec((tb, width), blk),
                pl.BlockSpec((1, tb), col),
                pl.BlockSpec((1, tb), col),
            ],
            out_specs=[
                pl.BlockSpec((tb, width), blk),
                pl.BlockSpec((heads, tb, LANES), ext),
                pl.BlockSpec((heads, tb, LANES), ext),
                pl.BlockSpec((heads, tb, LANES), ext),
                pl.BlockSpec((heads, VT, tb), lambda i, r: (0, 0, i)),
                pl.BlockSpec((width, 3 * heads * HD), full),
                pl.BlockSpec((wide, 16, LANES), full3),
                pl.BlockSpec((shards, units, 16, LANES), lambda i, r: (0, 0, 0, 0)),
            ],
            scratch_shapes=[
                pltpu.VMEM((width, 3 * heads * LANES), BF),
                pltpu.VMEM((units, 16, LANES), BF),
                pltpu.VMEM((wide * units, 16, LANES), BF),
                pltpu.VMEM((shards, units, 16, LANES), BF),
                pltpu.VMEM((1, width), F32),
                dma((wide,)),
                dma((wide,)),
                dma((shards - 1,)),
                dma((shards,)),
            ],
        ),
        out_shape=[
            out(rows, width),
            out(heads, rows, LANES),
            out(heads, rows, LANES),
            out(heads, rows, LANES),
            out(heads, VT, rows),
            out(width, 3 * heads * HD),
            out(wide, 16, LANES),
            out(shards, units, 16, LANES),
        ],
        compiler_params=pltpu.CompilerParams(vmem_limit_bytes=60 << 20, collective_id=3, has_side_effects=True),
        name="project",
    )(unit, weights, gains, tokens, seg, pad)


def middle_kernel(shards, span, units, wide, gain_row, gains_dev, inside,
                  unit_ref, sel_ref, gain_ref, pad_ref, wire_ref, att_ref, tok_ref, cot_ref,
                  outa_ref, back_ref, outs_ref, res_ref, grads_ref, mix_ref,
                  tokens_ref, cots_ref, got_ref, give_ref, wo_ref, wu_ref, wd_ref, go_ref, gu_ref, gd_ref, gg_ref, blk_ref,
                  hold_ref, resv_ref, mixv_ref, gradv_ref, outb_ref, local_sem, send_i, recv_i, send_b, recv_b, send_a, recv_a):
    own, width = tokens_ref.shape
    parts = recv_i.shape[1]
    tb = own // parts
    half = HD // 2
    rows_dev = gradv_ref.shape[1]
    z = lax.axis_index("narrow")
    kinds = (
        (mixv_ref, None, width, 3 * span),
        (wo_ref, go_ref, span, width),
        (wu_ref, gu_ref, width, units),
        (wd_ref, gd_ref, units, width),
    )
    mix_blocks = width // HD * (3 * span // HD)
    per = blk_ref.shape[0] // shards

    barrier = pltpu.get_barrier_semaphore()
    for d in range(1, shards):
        pl.semaphore_signal(barrier, inc=1, device_id={"narrow": lax.rem(z + d, shards)}, device_id_type=MESH)
    pl.semaphore_wait(barrier, shards - 1)

    def bring(d, t, mine):
        peer = lax.rem(z + d, shards)
        slot = z if mine else peer
        return pltpu.make_async_remote_copy(
            src_ref=att_ref.at[pl.ds(pl.multiple_of(peer * own + t * tb, tb), tb), :],
            dst_ref=got_ref.at[slot, pl.ds(pl.multiple_of(t * tb, tb), tb), :],
            send_sem=send_i.at[d - 1, t],
            recv_sem=recv_i.at[slot, t],
            device_id={"narrow": peer},
            device_id_type=MESH,
        )

    def give(d, t, mine):
        peer = lax.rem(z + d, shards)
        slot = z if mine else peer
        return pltpu.make_async_remote_copy(
            src_ref=give_ref.at[peer, pl.ds(pl.multiple_of(t * tb, tb), tb), :],
            dst_ref=back_ref.at[pl.ds(pl.multiple_of(slot * own + t * tb, tb), tb), :],
            send_sem=send_b.at[d - 1, t],
            recv_sem=recv_b.at[slot, t],
            device_id={"narrow": peer},
            device_id_type=MESH,
        )

    def hop_copy(c, t, step):
        at = pl.ds(pl.multiple_of(t * tb, tb), tb)
        return pltpu.make_async_remote_copy(
            src_ref=outa_ref.at[c, at, :],
            dst_ref=outa_ref.at[c, at, :],
            send_sem=send_a.at[step, c, t],
            recv_sem=recv_a.at[c, t],
            device_id={"narrow": lax.rem(z + (1 if step == 0 else shards - 1), shards)},
            device_id_type=MESH,
        )

    room = (z < shards - 1, z > 0)
    for t in range(parts):
        for d in range(1, shards):
            bring(d, t, True).start()
    mine = pl.ds(pl.multiple_of(z * own, own), own)
    copies = [
        pltpu.make_async_copy(att_ref.at[mine, :], got_ref.at[z], local_sem.at[0]),
        pltpu.make_async_copy(tok_ref.at[mine, :], tokens_ref, local_sem.at[1]),
        pltpu.make_async_copy(cot_ref.at[mine, :], cots_ref, local_sem.at[2]),
    ]
    fetch = pltpu.make_async_copy(wire_ref, hold_ref, local_sem.at[3])
    fetch.start()
    for copy in copies:
        copy.start()
    fetch.wait()

    def gather_blocks(kinds, base):
        for ref, acc, rows, cols in kinds:
            grid_cols = cols // HD

            def fill(r, _, ref=ref, base=base, grid_cols=grid_cols):
                low = pl.multiple_of(r * HD, HD)
                for n in range(shards):
                    for c in range(grid_cols):
                        unit = unit_ref[base + r * grid_cols + c] + n * (rows_dev // 16)
                        t = jnp.concatenate([hold_ref[unit], hold_ref[unit + 1]], axis=0)
                        for part in range(2):
                            ref[n, pl.ds(low + part * half, half), c * HD : (c + 1) * HD] = t[:, part * HD : (part + 1) * HD]
                return 0

            lax.fori_loop(0, rows // HD, fill, 0)
            base += rows // HD * grid_cols
            if acc is not None:
                acc[...] = jnp.zeros_like(acc)

    gather_blocks(kinds[1:], mix_blocks)
    gg_ref[...] = jnp.zeros_like(gg_ref)
    stores = [
        pltpu.make_async_copy(mixv_ref, mix_ref, local_sem.at[4]),
        pltpu.make_async_copy(resv_ref, res_ref, local_sem.at[5]),
        pltpu.make_async_copy(gradv_ref, grads_ref, local_sem.at[6]),
    ]
    stores += [pltpu.make_async_copy(outb_ref, outs_ref.at[n], local_sem.at[7 + n]) for n in range(shards)]
    for copy in copies:
        copy.wait()

    def block(t, _):
        at = pl.ds(pl.multiple_of(t * tb, tb), tb)
        for d in range(1, shards):
            bring(d, t, False).wait_recv()
        tokens = tokens_ref[at, :].astype(F32)
        cot = cots_ref[at, :]
        branch = nn(got_ref[0, at, :], wo_ref[0])
        for n in range(1, shards):
            branch += nn(got_ref[n, at, :], wo_ref[n])
        residual = tokens + branch
        xhat, scale = normalize(residual)
        gain = gain_ref[...]
        normed = (xhat * gain).astype(BF)
        ups = [nn(normed, wu_ref[n]) for n in range(shards)]
        downs = [nt(cot, wd_ref[n]) for n in range(shards)]
        actives, back_ups = [], []
        for n in range(shards):
            value, slope = gelu_pair(ups[n])
            actives.append(value.astype(BF))
            back_ups.append((slope * downs[n]).astype(BF))
        mlp = nn(actives[0], wd_ref[0])
        back = nt(back_ups[0], wu_ref[0])
        for n in range(1, shards):
            mlp += nn(actives[n], wd_ref[n])
            back += nt(back_ups[n], wu_ref[n])
        out = (residual + mlp).astype(BF)

        @pl.when(t < inside)
        def _():
            outa_ref[z, at, :] = out
            for step in range(2):

                @pl.when(room[step])
                def _(step=step):
                    hop_copy(z, t, step).start()

        @pl.when(t >= inside)
        def _():
            outb_ref[pl.ds(pl.multiple_of((t - inside) * tb, tb), tb), :] = out

        gg_ref[...] += jnp.sum(back * xhat, axis=0, keepdims=True)
        back_res = cot.astype(F32) + norm_back(back * gain, xhat, scale)
        resv_ref[at, :] = back_res
        branch_low = back_res.astype(BF)
        line = pad_ref[:, pl.ds(pl.multiple_of(z * own + t * tb, LANES), tb)]
        pad = jnp.broadcast_to(line.astype(F32), (8, tb)).T[:, :1]
        for n in range(shards):
            give_ref[n, at, :] = (nt(branch_low, wo_ref[n]) * pad).astype(BF)
        for d in range(1, shards):
            give(d, t, True).start()
        for n in range(shards):
            gd_ref[n] += tn(actives[n], cot)
            gu_ref[n] += tn(normed, back_ups[n])
            go_ref[n] += tn(got_ref[n, at, :], branch_low)
        return 0

    lax.fori_loop(0, parts, block, 0)
    for copy in stores[1:2] + stores[3:]:
        copy.start()
    gather_blocks(kinds[:1], 0)
    stores[0].start()
    back_ref[mine, :] = give_ref[z]
    base = 0
    for ref, acc, rows, cols in kinds:
        grid_cols = cols // HD
        if acc is not None:

            def cut(r, _, acc=acc, base=base, grid_cols=grid_cols):
                low = pl.multiple_of(r * HD, HD)
                for n in range(shards):
                    for c in range(grid_cols):
                        lanes = slice(c * HD, (c + 1) * HD)
                        value = jnp.concatenate([acc[n, pl.ds(low, half), lanes], acc[n, pl.ds(low + half, half), lanes]], axis=1)
                        blk_ref[n * per + base - mix_blocks + r * grid_cols + c] = value.astype(BF)
                return 0

            lax.fori_loop(0, rows // HD, cut, 0)
        base += rows // HD * grid_cols
    for n in range(shards):
        blk_ref[(n + 1) * per - 1] = jnp.zeros((half, LANES), BF)
    slots = gain_row // half
    top = lax.broadcasted_iota(jnp.int32, (16, LANES), 0) == 0

    def place(v, _):
        for n in range(shards):
            for i in range(slots):
                gradv_ref[v * shards + n, i * half : (i + 1) * half, :] = blk_ref[sel_ref[v * slots + i] + n * per]
        return 0

    lax.fori_loop(0, wide, place, 0)
    for v in range(wide):
        piece = v * gains_dev // LANES - width // LANES
        for n in range(shards):
            if piece >= 0:
                value = jnp.where(top, gg_ref[:, piece * LANES : (piece + 1) * LANES], 0.0).astype(BF)
            else:
                value = jnp.zeros((16, LANES), BF)
            gradv_ref[v * shards + n, gain_row:, :] = value
    stores[2].start()

    hops = [(s, t, step) for s in range(1, shards) for t in range(inside) for step in range(2)]
    for s, t, step in hops:
        chunk = z - s if step == 0 else z + s
        there = chunk >= 0 if step == 0 else chunk < shards

        @pl.when(there)
        def _(chunk=chunk, t=t, step=step):
            hop_copy(chunk, t, step).wait_recv()

        @pl.when(there & room[step])
        def _(chunk=chunk, t=t, step=step):
            hop_copy(chunk, t, step).start()

    for t in range(parts):
        for d in range(1, shards):
            give(d, t, False).wait_recv()
    for copy in stores:
        copy.wait()
    for t in range(parts):
        for d in range(1, shards):
            bring(d, t, True).wait_send()
            give(d, t, True).wait_send()
    for t in range(inside):
        for step in range(2):

            @pl.when(room[step])
            def _(t=t, step=step):
                hop_copy(z, t, step).wait_send()

    for s, t, step in hops:
        chunk = z - s if step == 0 else z + s
        there = chunk >= 0 if step == 0 else chunk < shards

        @pl.when(there & room[step])
        def _(chunk=chunk, t=t, step=step):
            hop_copy(chunk, t, step).wait_send()


def middle(unit, sel, wire, gain_two, pad, att, tokens, cotangent, shards, wide, rows_dev, gain_row, gains_dev):
    rows, span = att.shape
    width = tokens.shape[1]
    units = FF // shards
    own = rows // shards
    tb = min(256, own)
    parts = own // tb
    inside = max(1, parts // 4)
    blocks = unit.shape[0] - width // HD * (3 * span // HD)
    vmem = pl.BlockSpec(memory_space=pltpu.VMEM)
    smem = pl.BlockSpec(memory_space=pltpu.SMEM)
    hbm = pl.BlockSpec(memory_space=pl.ANY)
    dma = pltpu.SemaphoreType.DMA
    return pl.pallas_call(
        functools.partial(middle_kernel, shards, span, units, wide, gain_row, gains_dev, inside),
        in_specs=[smem, smem, vmem, vmem, hbm, hbm, hbm, hbm],
        out_specs=[vmem] * 2 + [hbm] * 4,
        out_shape=[
            jax.ShapeDtypeStruct((shards, inside * tb, width), BF),
            jax.ShapeDtypeStruct((rows, span), BF),
            jax.ShapeDtypeStruct((shards, own - inside * tb, width), BF),
            jax.ShapeDtypeStruct((own, width), F32),
            jax.ShapeDtypeStruct((wide * shards, rows_dev, LANES), BF),
            jax.ShapeDtypeStruct((shards, width, 3 * span), BF),
        ],
        scratch_shapes=[
            pltpu.VMEM((own, width), BF),
            pltpu.VMEM((own, width), BF),
            pltpu.VMEM((shards, own, span), BF),
            pltpu.VMEM((shards, own, span), BF),
            pltpu.VMEM((shards, span, width), BF),
            pltpu.VMEM((shards, width, units), BF),
            pltpu.VMEM((shards, units, width), BF),
            pltpu.VMEM((shards, span, width), F32),
            pltpu.VMEM((shards, width, units), F32),
            pltpu.VMEM((shards, units, width), F32),
            pltpu.VMEM((1, width), F32),
            pltpu.VMEM((shards * (blocks + 1), HD // 2, LANES), BF),
            pltpu.VMEM(wire.shape, BF),
            pltpu.VMEM((own, width), F32),
            pltpu.VMEM((shards, width, 3 * span), BF),
            pltpu.VMEM((wide * shards, rows_dev, LANES), BF),
            pltpu.VMEM((own - inside * tb, width), BF),
            dma((7 + shards,)),
            dma((shards - 1, parts)),
            dma((shards, parts)),
            dma((shards - 1, parts)),
            dma((shards, parts)),
            dma((2, shards, inside)),
            dma((shards, inside)),
        ],
        compiler_params=pltpu.CompilerParams(vmem_limit_bytes=63 << 20, collective_id=2, has_side_effects=True),
        name="middle",
    )(unit, sel, gain_two, pad, wire, att, tokens, cotangent)


PARTS = 8


def finish_kernel(shards, wide, gain_row, gains_dev, group, sel_ref, mix_ref, gain_ref, fullh_ref, resh_ref, bm_ref, norm_ref, tok_ref, *refs):
    given, taken = refs[1:7], refs[9:15]
    states, outs, (full_ref, res_ref) = refs[15:21], refs[21:27], refs[27:29]
    first_ref, grad_ref, line_ref = refs[0], refs[7], refs[8]
    (own_ref, normed_ref, tokens_ref, got_ref, acc_ref, blk_ref, grads_ref, sums_ref, firsts_ref, part_ref, aug_ref,
     local_sem, send_z, recv_z, send_w, recv_w, send_a, recv_a, send_g, recv_g, send_f, recv_f) = refs[29:]
    width = norm_ref.shape[1]
    rows, cols = bm_ref.shape
    own = rows // shards
    hold = own // PARTS
    half = HD // 2
    grid_cols = cols // HD
    blocks = width // HD * grid_cols
    slots = gain_row // half
    z = lax.axis_index("narrow")
    w = lax.axis_index("wide")

    barrier = pltpu.get_barrier_semaphore()
    for d in range(1, shards):
        pl.semaphore_signal(barrier, inc=1, device_id={"narrow": lax.rem(z + d, shards)}, device_id_type=MESH)
    for d in range(1, wide):
        pl.semaphore_signal(barrier, inc=1, device_id={"wide": lax.rem(w + d, wide)}, device_id_type=MESH)
    pl.semaphore_wait(barrier, shards + wide - 2)

    def to_peer(d, part, mine):
        peer = lax.rem(z + d, shards)
        slot = z if mine else peer
        at = pl.multiple_of(peer * own + part * hold, hold)
        return pltpu.make_async_remote_copy(
            src_ref=bm_ref.at[pl.ds(at, hold), :],
            dst_ref=got_ref.at[slot, pl.ds(part * hold, hold), :],
            send_sem=send_z.at[d - 1, part],
            recv_sem=recv_z.at[slot, part],
            device_id={"narrow": peer},
            device_id_type=MESH,
        )

    def to_owner(d, mine):
        peer = lax.rem(w + d, wide)
        slot = w if mine else peer
        return pltpu.make_async_remote_copy(
            src_ref=grads_ref.at[peer],
            dst_ref=sums_ref.at[slot],
            send_sem=send_w.at[d - 1],
            recv_sem=recv_w.at[slot],
            device_id={"wide": peer},
            device_id_type=MESH,
        )

    def hop_copy(c, part, step):
        at = pl.ds(pl.multiple_of(c * own + part * hold, hold), hold)
        return pltpu.make_async_remote_copy(
            src_ref=grad_ref.at[at, :],
            dst_ref=grad_ref.at[at, :],
            send_sem=send_a.at[step, c, part],
            recv_sem=recv_a.at[c, part],
            device_id={"narrow": lax.rem(z + (1 if step == 0 else shards - 1), shards)},
            device_id_type=MESH,
        )

    def pass_on(c, part, act):
        for step, there in ((0, z < shards - 1), (1, z > 0)):
            if c is None or step == c[0]:
                chunk = z if c is None else c[1]
                ok = there if c is None else there & c[2]

                @pl.when(ok)
                def _(chunk=chunk, step=step):
                    act(hop_copy(chunk, part, step))

    def line_to(d, mine):
        peer = lax.rem(z + d, shards)
        slot = z if mine else peer
        return pltpu.make_async_remote_copy(
            src_ref=line_ref.at[z],
            dst_ref=line_ref.at[slot],
            send_sem=send_g.at[d - 1],
            recv_sem=recv_g.at[slot],
            device_id={"narrow": peer},
            device_id_type=MESH,
        )

    rows_dev = part_ref.shape[0]

    def first_to(d, mine):
        peer = lax.rem(z + d, shards)
        slot = z if mine else peer
        return pltpu.make_async_remote_copy(
            src_ref=first_ref.at[pl.ds(pl.multiple_of(peer * rows_dev, 16), rows_dev), :],
            dst_ref=firsts_ref.at[slot],
            send_sem=send_f.at[d - 1],
            recv_sem=recv_f.at[slot],
            device_id={"narrow": peer},
            device_id_type=MESH,
        )

    for d in range(1, shards):
        first_to(d, True).start()
    for part in range(PARTS):
        for d in range(1, shards):
            to_peer(d, part, True).start()
    mine = pl.ds(pl.multiple_of(z * own, own), own)
    copies = [
        pltpu.make_async_copy(bm_ref, own_ref, local_sem.at[0]),
        pltpu.make_async_copy(norm_ref, normed_ref, local_sem.at[1]),
        pltpu.make_async_copy(tok_ref.at[mine, :], tokens_ref, local_sem.at[2]),
        pltpu.make_async_copy(bm_ref.at[mine, :], got_ref.at[z], local_sem.at[3]),
        pltpu.make_async_copy(
            first_ref.at[pl.ds(pl.multiple_of(z * rows_dev, 16), rows_dev), :], firsts_ref.at[z], local_sem.at[4]
        ),
    ]
    late = [
        pltpu.make_async_copy(a, b, local_sem.at[5 + k])
        for k, (a, b) in enumerate(zip((fullh_ref, resh_ref, *given), (full_ref, res_ref, *states)))
    ]
    for copy in copies + late:
        copy.start()
    for copy in copies:
        copy.wait()

    acc_ref[...] = jnp.zeros_like(acc_ref)
    tb = min(512, rows)

    def add(i, _):
        at = pl.ds(pl.multiple_of(i * tb, tb), tb)
        acc_ref[...] += tn(normed_ref[at, :], own_ref[at, :])
        return 0

    lax.fori_loop(0, rows // tb, add, 0)
    blk_ref[blocks] = jnp.zeros((half, LANES), BF)

    def cut(r, _):
        low = pl.multiple_of(r * HD, HD)
        for c in range(grid_cols):
            lanes = slice(c * HD, (c + 1) * HD)
            value = jnp.concatenate([acc_ref[pl.ds(low, half), lanes], acc_ref[pl.ds(low + half, half), lanes]], axis=1)
            blk_ref[r * grid_cols + c] = value.astype(BF)
        return 0

    lax.fori_loop(0, width // HD, cut, 0)
    along = jnp.sum(acc_ref[...] * mix_ref[...].astype(F32), axis=1, keepdims=True)
    line = jnp.broadcast_to(along, (width, LANES)).T[:16] / gain_ref[...]
    top = lax.broadcasted_iota(jnp.int32, (16, LANES), 0) == 0
    for v in range(wide):

        def place(i, _, v=v):
            grads_ref[v, pl.ds(pl.multiple_of(i * half, half), half), :] = blk_ref[sel_ref[v * slots + i]]
            return 0

        lax.fori_loop(0, slots, place, 0)
        piece = v * gains_dev // LANES
        if piece < width // LANES:
            value = jnp.where(top, line[:, piece * LANES : (piece + 1) * LANES], 0.0).astype(BF)
        else:
            value = jnp.zeros((16, LANES), BF)
        grads_ref[v, gain_row : gain_row + 16, :] = value
    for d in range(1, wide):
        to_owner(d, True).start()
    part_ref[...] = grads_ref[w].astype(F32)

    tile = min(256, hold)

    def norm_rows(i, _):
        at = pl.ds(pl.multiple_of(i * tile, tile), tile)
        back = nt(got_ref[0, at, :], full_ref[0])
        for n in range(1, shards):
            back += nt(got_ref[n, at, :], full_ref[n])
        xhat, scale = normalize(tokens_ref[at, :].astype(F32))
        grad = res_ref[at, :] + norm_back(back * gain_ref[...], xhat, scale)
        grad_ref[pl.ds(pl.multiple_of(z * own + i * tile, tile), tile), :] = grad.astype(BF)
        return 0

    def norm_part(part):
        for d in range(1, shards):
            to_peer(d, part, False).wait_recv()
        lax.fori_loop(part * hold // tile, (part + 1) * hold // tile, norm_rows, 0)
        pass_on(None, part, lambda copy: copy.start())

    for d in range(1, wide):
        to_owner(d, False).wait_recv()
    for d in range(1, wide):
        part_ref[...] += sums_ref[lax.rem(w + d, wide)].astype(F32)
    line_ref[z] = part_ref[gain_row : gain_row + 16, :]
    for d in range(1, shards):
        line_to(d, True).start()
    for d in range(1, shards):
        first_to(d, False).wait_recv()
    total = firsts_ref[0].astype(F32)
    for n in range(1, shards):
        total += firsts_ref[n].astype(F32)
    line_ref[shards] = total[gain_row : gain_row + 16, :]
    part_ref[...] += total
    for copy in late:
        copy.wait()
    stores = [pltpu.make_async_copy(a, b, local_sem.at[13 + k]) for k, (a, b) in enumerate(zip(outs, taken))]
    ready = 0
    rounds = slots // group
    for g in range(rounds):
        soap_group(g * group, group, part_ref, *states, *outs, aug_ref)
        upto = PARTS if g == rounds - 1 else 0
        while ready < upto:
            norm_part(ready)
            ready += 1
    for copy in stores:
        copy.start()
    hops = [(s, part, step) for s in range(1, shards) for part in range(PARTS) for step in range(2)]
    for s, part, step in hops:
        chunk = z - s if step == 0 else z + s
        there = chunk >= 0 if step == 0 else chunk < shards

        @pl.when(there)
        def _(chunk=chunk, part=part, step=step):
            hop_copy(chunk, part, step).wait_recv()

        pass_on((step, chunk, there), part, lambda copy: copy.start())
    for copy in stores:
        copy.wait()
    for d in range(1, shards):
        line_to(d, False).wait_recv()
    for part in range(PARTS):
        pass_on(None, part, lambda copy: copy.wait_send())
    for s, part, step in hops:
        chunk = z - s if step == 0 else z + s
        there = chunk >= 0 if step == 0 else chunk < shards
        pass_on((step, chunk, there), part, lambda copy: copy.wait_send())
    for d in range(1, shards):
        line_to(d, True).wait_send()
        first_to(d, True).wait_send()
    for part in range(PARTS):
        for d in range(1, shards):
            to_peer(d, part, True).wait_send()
    for d in range(1, wide):
        to_owner(d, True).wait_send()


def finish(sel, mix, mix_full, gain_one, res, bm, normed, tokens, states, group, wide, rows_dev, gain_row, gains_dev):
    shards = mix_full.shape[0]
    rows, cols = bm.shape
    width = normed.shape[1]
    own = rows // shards
    half = HD // 2
    blocks = width // HD * (cols // HD)
    vmem = pl.BlockSpec(memory_space=pltpu.VMEM)
    smem = pl.BlockSpec(memory_space=pltpu.SMEM)
    hbm = pl.BlockSpec(memory_space=pl.ANY)
    dma = pltpu.SemaphoreType.DMA
    return pl.pallas_call(
        functools.partial(finish_kernel, shards, wide, gain_row, gains_dev, group),
        in_specs=[smem, vmem, vmem, hbm, hbm, hbm, hbm, hbm, hbm] + [hbm] * 6,
        out_specs=[vmem] * 2 + [hbm] * 6,
        out_shape=[jax.ShapeDtypeStruct((rows, width), BF), jax.ShapeDtypeStruct((shards + 1, 16, LANES), F32)]
        + [jax.ShapeDtypeStruct(a.shape, a.dtype) for a in states[1:]],
        scratch_shapes=[pltpu.VMEM(a.shape, a.dtype) for a in states[1:]] * 2
        + [
            pltpu.VMEM(mix_full.shape, BF),
            pltpu.VMEM(res.shape, F32),
            pltpu.VMEM((rows, cols), BF),
            pltpu.VMEM((rows, width), BF),
            pltpu.VMEM((own, width), BF),
            pltpu.VMEM((shards, own, cols), BF),
            pltpu.VMEM((width, cols), F32),
            pltpu.VMEM((blocks + 1, half, LANES), BF),
            pltpu.VMEM((wide, rows_dev, LANES), BF),
            pltpu.VMEM((wide, rows_dev, LANES), BF),
            pltpu.VMEM((shards, rows_dev, LANES), BF),
            pltpu.VMEM((rows_dev, LANES), F32),
            pltpu.VMEM((2 * group, HD, LANES), F32),
            dma((19,)),
            dma((shards - 1, PARTS)),
            dma((shards, PARTS)),
            dma((wide - 1,)),
            dma((wide,)),
            dma((2, shards, PARTS)),
            dma((shards, PARTS)),
            dma((shards - 1,)),
            dma((shards,)),
            dma((shards - 1,)),
            dma((shards,)),
        ],
        compiler_params=pltpu.CompilerParams(vmem_limit_bytes=43 << 20, collective_id=1, has_side_effects=True),
        name="finish",
    )(sel, mix, gain_one, mix_full, res, bm, normed, tokens, *states)


def wrap_kernel(count, per, grad_ref, outa_ref, outb_ref, *refs):
    olds, wide_ref, out_ref, news = refs[:count], refs[count], refs[count + 1], refs[count + 2 :]
    for old, new in zip(olds, news):
        new[...] = old[...]
    wide_ref[...] = grad_ref[...].astype(F32)
    place = lax.rem(pl.program_id(0), per)

    @pl.when(place == 0)
    def _():
        out_ref[...] = outa_ref[0]

    @pl.when(place > 0)
    def _():
        out_ref[...] = outb_ref[0]


def wrap(grad, out_a, out_b, olds):
    rows, width = grad.shape
    tb = out_a.shape[1]
    per = 1 + out_b.shape[1] // tb
    steps = rows // tb
    slots = olds[0].shape[1]
    group = next(g for g in range(1, slots + 1) if slots % g == 0 and slots // g <= steps)
    last = slots // group - 1
    blk = pl.BlockSpec((tb, width), lambda i: (i, 0))
    part_a = pl.BlockSpec((1, tb, width), lambda i: (i // per, 0, 0))
    part_b = pl.BlockSpec((1, tb, width), lambda i: (i // per, jnp.maximum(i % per - 1, 0), 0))
    states = [
        pl.BlockSpec((1, group, *a.shape[2:]), lambda i, k=a.ndim: (0, jnp.minimum(i, last)) + (0,) * (k - 2)) for a in olds
    ]
    return pl.pallas_call(
        functools.partial(wrap_kernel, len(olds), per),
        grid=(steps,),
        in_specs=[blk, part_a, part_b] + states,
        out_specs=[blk, blk] + states,
        out_shape=[jax.ShapeDtypeStruct((rows, width), F32), jax.ShapeDtypeStruct((rows, width), BF)]
        + [jax.ShapeDtypeStruct(a.shape, a.dtype) for a in olds],
        compiler_params=pltpu.CompilerParams(vmem_limit_bytes=44 << 20),
        name="wrap",
    )(grad, out_a, out_b, *olds)


def adam_gains(grad, gain, first, second, average):
    new_first = beta_one * first + (1.0 - beta_one) * grad
    new_second = beta_two * second + (1.0 - beta_two) * grad * grad
    new_gain = gain - gain_rate * new_first / (jnp.sqrt(new_second) + step_eps)
    new_average = average_keep * average + (1.0 - average_keep) * new_gain
    return (new_gain, new_first, new_second, new_average)


def body(
    tokens,
    cotangent,
    segment_ids,
    pad_mask,
    owner_order,
    weights,
    first_moment,
    second_moment,
    average,
    stats,
    bases,
    gains,
    gain_first,
    gain_second,
    gain_average,
):
    narrow = lax.axis_size("narrow")
    wide = lax.axis_size("wide")
    heads = HEADS // narrow
    rows, width = tokens.shape
    span = heads * HD
    own = rows // narrow
    slots, size = weights.shape[1], weights.shape[2]
    half = size // 2
    block_count = owner_order.shape[0]
    gains_dev = gains.shape[0]
    gain_row = slots * half
    rows_dev = gain_row + 16

    ids = jnp.arange(block_count, dtype=jnp.int32)
    slot_of = jnp.sum(jnp.where(owner_order[None, :] == ids[:, None], ids[None, :], 0), axis=1)
    device, place = slot_of // slots, slot_of % slots
    row_own = device * rows_dev + place * half
    row_full = device * (narrow * rows_dev) + place * half

    seg = segment_ids
    seg_row = segment_ids[0]
    pad = pad_mask
    block = min(512, rows)
    low_seg = seg_row[::block]
    high_seg = seg_row[block - 1 :: block]
    begin = jnp.sum((seg_row[None, :] < low_seg[:, None]).astype(jnp.int32), axis=1) // UNIT
    end = (jnp.sum((seg_row[None, :] <= high_seg[:, None]).astype(jnp.int32), axis=1) + UNIT - 1) // UNIT

    normed, qe, ke, ve, vt, mix, lines, along = project(
        weights, gains[None], row_own // 16, tokens, seg, pad, heads, narrow, wide, gain_row, gains_dev
    )
    wire_full = lax.all_gather(along.reshape(-1, LANES), "wide", axis=0, tiled=True)
    gain_all = lines[:, 0, :gains_dev].astype(F32).reshape(1, 2 * width)
    gain_one, gain_two = gain_all[:, :width], gain_all[:, width:]
    attended, qb = attend(qe, ke, vt, pad, begin, end, block, block)
    unit = row_full // 16
    mix_blocks = width // size * 3 * heads
    sel_rest = jnp.where(owner_order >= mix_blocks, owner_order - mix_blocks, block_count - mix_blocks)
    out_a, back_att, out_b, back_res, grads, mix_full = middle(
        unit, sel_rest, wire_full.reshape(-1, 16, LANES), gain_two, pad, attended, tokens, cotangent,
        narrow, wide, rows_dev, gain_row, gains_dev,
    )
    part_a = lax.psum_scatter(grads.reshape(-1, LANES), "wide", scatter_dimension=0, tiled=True)
    out_b = lax.all_to_all(out_b, "narrow", 0, 0)
    bm = attend_back(qb, ke, ve, back_att, attended, begin, end, block, block)
    bm, part_a, out_b = lax.optimization_barrier((bm, part_a, out_b))
    sel = jnp.minimum(owner_order, mix_blocks)
    group = next(g for g in range(min(12, slots), 0, -1) if slots % g == 0)
    states = (part_a, weights, first_moment, second_moment, average, stats, bases)
    grad_all, lines, *fresh = finish(
        sel, mix, mix_full, gain_one, back_res, bm, normed, tokens, states, group, wide, rows_dev, gain_row, gains_dev
    )
    input_grad, output, new_weight, new_first, new_second, new_average, new_stats, new_bases = wrap(
        grad_all, out_a, out_b, fresh
    )
    line = jnp.sum(lines[:, 0], axis=0)
    offset = lax.axis_index("wide") * gains_dev % LANES
    own_gain = lax.dynamic_slice_in_dim(line, offset, gains_dev, 0)
    new_gains, gain_moment, gain_square, gain_mean = adam_gains(own_gain, gains, gain_first, gain_second, gain_average)
    return (
        output,
        input_grad,
        new_weight,
        new_first,
        new_second,
        new_average,
        new_stats,
        new_bases,
        new_gains,
        gain_moment,
        gain_square,
        gain_mean,
    )


def solution(mesh):
    block = P("narrow", "wide", None, None)
    pair = P("narrow", "wide", None, None, None)
    rows = P("wide", None)
    line = P("wide")
    return jax.shard_map(
        body,
        mesh=mesh,
        in_specs=(rows, rows, rows, rows, P(), block, block, block, block, pair, pair, line, line, line, line),
        out_specs=(rows, rows, block, block, block, block, pair, pair, line, line, line, line),
        check_vma=False,
    )
```
